32 devices in a mesh: fsdp: 8 (over z, y), dp: 4 (over x, core).
Axes of the slice: x: 2, y: 2, z: 4, core: 2. Of those that a mesh axis runs over, the one named last changes fastest.
Arguments:
- hidden_in: bfloat16 [128, 128, 768], P(('fsdp', 'dp')), may hold values from -6 to 6
- query_key_value_weight: bfloat16 [768, 2304], P('fsdp'), may hold values from -0.21875 to 0.21875
- attention_output_weight: bfloat16 [768, 768], P('fsdp'), may hold values from -0.625 to 0.625
- gate_up_weight: bfloat16 [768, 6144], P('fsdp'), may hold values from -0.21875 to 0.21875
- down_weight: bfloat16 [3072, 768], P('fsdp'), may hold values from -0.109375 to 0.109375
- gain_attn: bfloat16 [768], P('fsdp'), may hold values from 0.25 to 1.75
- shift_attn: bfloat16 [768], P('fsdp'), may hold values from -3 to 3
- gain_ffn: bfloat16 [768], P('fsdp'), may hold values from 0.25 to 1.75
- shift_ffn: bfloat16 [768], P('fsdp'), may hold values from -3 to 3
- masked_output_gradient: bfloat16 [128, 32, 768], P(('fsdp', 'dp')), may hold values from -6 to 6
- positions: int32 [128, 32], P(('fsdp', 'dp')), may hold values from 0 to 127, as said below
- mask_counts: int32 [128], P(('fsdp', 'dp')), may hold values from 8 to 32
Outputs:
- layer_out: bfloat16 [128, 128, 768], P(('fsdp', 'dp'))
- grad_in: float32 [128, 128, 768], P(('fsdp', 'dp'))
- grad_qkv: float32 [768, 2304], P('fsdp')
- grad_out_proj: float32 [768, 768], P('fsdp')
- grad_up: float32 [768, 6144], P('fsdp')
- grad_down: float32 [3072, 768], P('fsdp')
- grad_gain_attn: float32 [768], P('fsdp')
- grad_shift_attn: float32 [768], P('fsdp')
- grad_gain_ffn: float32 [768], P('fsdp')
- grad_shift_ffn: float32 [768], P('fsdp')
The draws below stay inside these ranges and needn't reach their ends.
Inputs may be any that keep to these rules, and one draw needn't show every extreme that they name: Within one sequence the listed positions are distinct.
All inputs are finite; a program needn't handle non-finite values.
Results may differ from the reference program's by a relative error of at most 0.015.
Values may be sent and summed in bfloat16 or wider, within the bound.
No kernel may reach another device: no remote copies, remote signals or barrier semaphores. Data moves between devices by JAX's collectives and lax.ppermute only.
A program may use at most 192 MiB of HBM per device.

```python
import math
import jax
import jax.numpy as jnp
from jax import lax

D = 768
HEADS = 12
HEAD_DIM = 64
FF = 3072
SEQ_LEN = 128
MASK_MOST = 32
SEQS = 128


def draw_positions(key, part):
    seq_keys = jax.random.split(jax.random.fold_in(key, 11), SEQS)

    def single(seq_key):
        return jax.random.permutation(seq_key, SEQ_LEN)[:MASK_MOST]
    return jax.vmap(single)(seq_keys).astype(jnp.int32)


def draw_mask_counts(key, part):
    least = max(1, MASK_MOST // 4)
    drawn = jax.random.randint(jax.random.fold_in(key, 23), (SEQS,), least, MASK_MOST + 1)
    fullest = jax.random.randint(jax.random.fold_in(key, 37), (), 0, SEQS)
    return drawn.at[fullest].set(MASK_MOST).astype(jnp.int32)


def raised(values, own_key, source, target, parts, factor):
    def block_of(dim):
        return (jnp.arange(values.shape[dim]) // (values.shape[dim] // parts)).reshape((-1,) + (1,) * (values.ndim - 1 - dim))

    first = jax.random.permutation(own_key, parts)[block_of(target)]
    far = (block_of(target) + parts // 2) % parts
    return jnp.where((block_of(source) == first) | (block_of(source) == far), factor * values, values)


def shard_levels(key, shape, shards, low, largest):
    level = 1.0
    for axis_at, parts in shards:
        draws = jax.random.uniform(jax.random.fold_in(jax.random.fold_in(key, 6), axis_at), (parts,), jnp.float32, low / len(shards), largest / len(shards))
        level = level * jnp.repeat(jnp.exp(draws), shape[axis_at] // parts).reshape((-1,) + (1,) * (len(shape) - 1 - axis_at))
    return level


def gaussian(stream_key, shape, width, limit, cuts=(), held_as=jnp.bfloat16):
    array = width * jax.random.normal(stream_key, shape, jnp.float32)
    if cuts:
        array = array * shard_levels(stream_key, shape, cuts, -0.22, 0.18)
    return jnp.clip(array, -limit, limit).astype(held_as)


def heavy_noise(key, shape, scale, most, pieces, heavy, held_as=jnp.bfloat16):
    values = scale * jax.random.normal(key, shape, jnp.float32)
    if pieces:
        values = values * shard_levels(key, shape, pieces, -0.22, 0.18)
    return jnp.clip(raised(values, jax.random.fold_in(key, 3), *heavy), -most, most).astype(held_as)


def setup_inputs(seed: int = 0) -> dict:
    streams_of = jax.random.split(jax.random.key(seed), 13)
    hidden_in = gaussian(streams_of[0], (SEQS, SEQ_LEN, D), 1.0, 6.0, ((0, 32),))
    query_key_value_weight = gaussian(streams_of[1], (D, 3 * D), D ** -0.5, 0.21875, ((0, 8),))
    attention_output_weight = gaussian(streams_of[2], (D, D), (D // 8) ** -0.5, 0.625, ((0, 8),))
    gate_up_weight = gaussian(streams_of[3], (D, 2 * FF), D ** -0.5, 0.21875, ((0, 8),))
    down_weight = gaussian(streams_of[4], (FF, D), FF ** -0.5, 0.109375, ((0, 8),))
    gain_attn = jnp.clip(1.0 + 0.15 * jax.random.normal(streams_of[5], (D,), jnp.float32), 0.25, 1.75).astype(jnp.bfloat16)
    shift_attn = gaussian(streams_of[6], (D,), 0.5, 3.0, ((0, 8),))
    gain_ffn = jnp.clip(1.0 + 0.15 * jax.random.normal(streams_of[7], (D,), jnp.float32), 0.25, 1.75).astype(jnp.bfloat16)
    shift_ffn = gaussian(streams_of[8], (D,), 0.5, 3.0, ((0, 8),))
    masked_output_gradient = heavy_noise(streams_of[9], (SEQS, MASK_MOST, D), 1.0, 6.0, ((0, 32),), (0, 2, 32, 2.75))
    positions = draw_positions(jax.random.fold_in(streams_of[12], 71), 0)
    mask_counts = draw_mask_counts(jax.random.fold_in(streams_of[12], 71), 0)
    return {"hidden_in": hidden_in, "query_key_value_weight": query_key_value_weight, "attention_output_weight": attention_output_weight, "gate_up_weight": gate_up_weight, "down_weight": down_weight, "gain_attn": gain_attn, "shift_attn": shift_attn, "gain_ffn": gain_ffn, "shift_ffn": shift_ffn, "masked_output_gradient": masked_output_gradient, "positions": positions, "mask_counts": mask_counts}


@jax.custom_vjp
def low(v):
    return lax.optimization_barrier(v.astype(jnp.bfloat16)).astype(jnp.float32)

@jax.custom_vjp
def low_back(v):
    return v

def low_keep(v):
    return (low(v), None)

def low_pass(kept, grad):
    return (grad,)

def back_keep(v):
    return (v, None)

def back_low(kept, grad):
    return (low(grad),)
low.defvjp(low_keep, low_pass)
low_back.defvjp(back_keep, back_low)
norm_eps = 1e-12
highest_precision = lax.Precision.HIGHEST

def layer_norm(value, gain, shift):
    center = value - lax.optimization_barrier(jnp.mean(value, axis=-1, keepdims=True))
    spread = lax.optimization_barrier(jnp.mean(center * center, axis=-1, keepdims=True))
    return center * lax.rsqrt(spread + norm_eps) * gain + shift

def alibi_table():
    head_index = jnp.arange(HEADS, dtype=jnp.float32)
    slopes = jnp.exp2(-8.0 * (head_index + 1.0) / HEADS)
    places = jnp.arange(SEQ_LEN)
    distance = jnp.abs(places[:, None] - places[None, :]).astype(jnp.float32)
    return -slopes[:, None, None] * distance[None, :, :]

def block_layer(grouped_token_rows, params):
    query_key_value_weight, attention_output_weight, gate_up_weight, down_weight, gain_attn, shift_attn, gain_ffn, shift_ffn = params
    count = grouped_token_rows.shape[0]
    projected = low(low_back(jnp.einsum('jkf,fw->jkw', grouped_token_rows, query_key_value_weight, precision=highest_precision)))
    queries = projected[:, :, :D].reshape(count, SEQ_LEN, HEADS, HEAD_DIM)
    key_rows = projected[:, :, D:2 * D].reshape(count, SEQ_LEN, HEADS, HEAD_DIM)
    value_rows = projected[:, :, 2 * D:].reshape(count, SEQ_LEN, HEADS, HEAD_DIM)
    raw = jnp.einsum('sqhc,skhc->shqk', queries, key_rows, precision=highest_precision)
    scores = low_back(raw * HEAD_DIM ** (-0.5) + alibi_table()[None])
    soft = low(jax.nn.softmax(scores, axis=-1))
    mixed = jnp.einsum('shqk,skhc->sqhc', soft, value_rows, precision=highest_precision)
    context = low_back(low(mixed)).reshape(count, SEQ_LEN, D)
    first_branch = low_back(jnp.einsum('jkf,fw->jkw', context, attention_output_weight, precision=highest_precision))
    normed_one = layer_norm(grouped_token_rows + first_branch, gain_attn, shift_attn)
    normed_low = low(normed_one)
    lifted = low_back(jnp.einsum('irb,bn->irn', normed_low, gate_up_weight, precision=highest_precision))
    gated_hidden = low(jax.nn.gelu(lifted[:, :, :FF], approximate=False) * lifted[:, :, FF:])
    second_branch = low_back(jnp.einsum('jvq,qw->jvw', gated_hidden, down_weight, precision=highest_precision))
    return layer_norm(normed_one + second_branch, gain_ffn, shift_ffn)

def run_all(stacked, params):

    def step(running, grouped_token_rows):
        return (running, jax.checkpoint(block_layer)(grouped_token_rows, params))
    _, results = lax.scan(step, jnp.zeros((), jnp.float32), stacked)
    return results

def reference(hidden_in, query_key_value_weight, attention_output_weight, gate_up_weight, down_weight, gain_attn, shift_attn, gain_ffn, shift_ffn, masked_output_gradient, positions, mask_counts):
    seq_total = hidden_in.shape[0]
    group = math.gcd(seq_total, max(1, 4096 // SEQ_LEN))
    groups = seq_total // group
    stacked = hidden_in.astype(jnp.float32).reshape(groups, group, SEQ_LEN, D)
    params = (query_key_value_weight.astype(jnp.float32), attention_output_weight.astype(jnp.float32), gate_up_weight.astype(jnp.float32), down_weight.astype(jnp.float32), gain_attn.astype(jnp.float32), shift_attn.astype(jnp.float32), gain_ffn.astype(jnp.float32), shift_ffn.astype(jnp.float32))
    outputs, pull = jax.vjp(run_all, stacked, params)
    slots = jnp.arange(MASK_MOST, dtype=jnp.int32)
    live = (slots[None, :] < mask_counts[:, None]).astype(jnp.float32)
    weighted = masked_output_gradient.astype(jnp.float32) * live[:, :, None]
    seq_index = jnp.broadcast_to(jnp.arange(seq_total, dtype=jnp.int32)[:, None], positions.shape)
    grad_out = jnp.zeros((seq_total, SEQ_LEN, D), jnp.float32).at[seq_index, positions].add(weighted)
    grad_stack, grad_params = pull(grad_out.reshape(groups, group, SEQ_LEN, D))
    layer_out = outputs.reshape(seq_total, SEQ_LEN, D).astype(jnp.bfloat16)
    grad_in = grad_stack.reshape(seq_total, SEQ_LEN, D)
    return (layer_out, grad_in, grad_params[0], grad_params[1], grad_params[2], grad_params[3], grad_params[4], grad_params[5], grad_params[6], grad_params[7])
```

```python
import jax
import jax.numpy as jnp
from jax import lax
from jax.sharding import PartitionSpec as P

HEADS = 12
HEAD_DIM = 64
FF = 3072
EPS = 1e-12
F32 = jnp.float32
LOW = jnp.bfloat16
AXES = ("fsdp", "dp")


def mm(a, b):
    return jnp.dot(a, b, preferred_element_type=F32)


def slopes():
    return jnp.exp2(-8.0 * (jnp.arange(HEADS, dtype=F32) + 1.0) / HEADS)


def norm_parts(value):
    center = value - jnp.mean(value, axis=-1, keepdims=True)
    rstd = lax.rsqrt(jnp.mean(center * center, axis=-1, keepdims=True) + EPS)
    return center * rstd, rstd


def norm_back(grad, unit, rstd, gain):
    scaled = grad * gain
    return rstd * (
        scaled
        - jnp.mean(scaled, axis=-1, keepdims=True)
        - unit * jnp.mean(scaled * unit, axis=-1, keepdims=True)
    )


def pick(onehot, rows):
    if rows.dtype == LOW:
        return jnp.einsum("svj,sjd->svd", onehot.astype(LOW), rows, preferred_element_type=F32).astype(LOW)
    return jnp.einsum("svj,sjd->svd", onehot, rows, precision=lax.Precision.HIGHEST)


def gather_weights(w_qkv, w_out, w_up, w_down):
    fsdp = lax.axis_size("fsdp")
    dp = lax.axis_size("dp")
    rows, width = w_out.shape
    if rows % (8 * dp):
        return (
            lax.all_gather(w_qkv, "fsdp", axis=0, tiled=True),
            lax.all_gather(w_out, "fsdp", axis=0, tiled=True),
            lax.all_gather(w_up, "fsdp", axis=0, tiled=True),
            lax.all_gather(w_down, "fsdp", axis=0, tiled=True),
        )
    mine = lax.axis_index("dp")
    part = rows // dp
    group = w_down.shape[0] // rows
    joined = jnp.concatenate([w_qkv, w_out, w_up], axis=1)
    joined = lax.dynamic_slice_in_dim(joined, mine * part, part, axis=0)
    down = lax.dynamic_slice_in_dim(w_down, mine * part * group, part * group, axis=0)
    down = jnp.concatenate([down[k * part : (k + 1) * part] for k in range(group)], axis=1)
    full = lax.all_gather(jnp.concatenate([joined, down], axis=1), AXES, axis=0, tiled=True)
    a, b = w_qkv.shape[1], w_qkv.shape[1] + w_out.shape[1]
    c = b + w_up.shape[1]
    full_down = full[:, c:].reshape(fsdp * dp, part, group, width)
    full_down = full_down.transpose(0, 2, 1, 3).reshape(fsdp * dp * part * group, width)
    return full[:, :a], full[:, a:b], full[:, b:c], full_down


def scatter_grads(g_qkv, g_out, g_up, g_down):
    fsdp = lax.axis_size("fsdp")
    dp = lax.axis_size("dp")
    width = g_out.shape[1]
    rows = g_out.shape[0] // fsdp
    if rows % (8 * dp):
        return tuple(
            lax.psum(lax.psum_scatter(g, "fsdp", scatter_dimension=0, tiled=True), "dp")
            for g in (g_qkv, g_out, g_up, g_down)
        )
    part = rows // dp
    group = g_down.shape[0] // g_out.shape[0]
    down = g_down.reshape(fsdp * dp, group, part, width).transpose(0, 2, 1, 3)
    down = down.reshape(fsdp * rows, group * width)
    joined = jnp.concatenate([g_qkv, g_out, g_up, down], axis=1).astype(LOW)
    mine = lax.psum_scatter(joined, AXES, scatter_dimension=0, tiled=True)
    full = lax.all_gather(mine, "dp", axis=0, tiled=True).astype(F32)
    a, b = g_qkv.shape[1], g_qkv.shape[1] + width
    c = b + g_up.shape[1]
    full_down = full[:, c:].reshape(dp, part, group, width).transpose(0, 2, 1, 3)
    return full[:, :a], full[:, a:b], full[:, b:c], full_down.reshape(rows * group, width)


def on_device(hidden_in, w_qkv, w_out, w_up, w_down, gain_attn, shift_attn, gain_ffn, shift_ffn, grad_listed, positions, counts):
    seqs, length, width = hidden_in.shape
    tokens = seqs * length
    most = positions.shape[1]
    norms = jnp.stack([gain_attn, shift_attn, gain_ffn, shift_ffn])
    norms = lax.all_gather(norms, "fsdp", axis=1, tiled=True).astype(F32)
    w_qkv, w_out, w_up, w_down = gather_weights(w_qkv, w_out, w_up, w_down)
    live = jnp.arange(most, dtype=jnp.int32)[None, :] < counts[:, None]
    onehot = (positions[:, :, None] == jnp.arange(length, dtype=jnp.int32)).astype(F32)
    rows_in = hidden_in.reshape(tokens, width)
    slope = slopes()
    scale = HEAD_DIM**-0.5
    qkv = mm(rows_in, w_qkv).astype(LOW)
    split = qkv.reshape(seqs, length, 3, HEADS, HEAD_DIM)
    q, k, v = split[:, :, 0], split[:, :, 1], split[:, :, 2]
    place = jnp.arange(length, dtype=F32)
    bias = -slope[:, None, None] * jnp.abs(place[:, None] - place[None, :])
    s = jnp.einsum("sqhc,skhc->shqk", q, k, preferred_element_type=F32) * scale + bias
    p = jax.nn.softmax(s, axis=-1).astype(LOW)
    att = jnp.einsum("shqk,skhc->sqhc", p, v, preferred_element_type=F32).astype(LOW)
    att = att.reshape(tokens, width)
    r1 = rows_in.astype(F32) + mm(att, w_out)
    unit1, _ = norm_parts(r1)
    h1 = unit1 * norms[0] + norms[1]
    h1_low = h1.astype(LOW)
    u = mm(h1_low, w_up)
    act = (jax.nn.gelu(u[:, :FF], approximate=False) * u[:, FF:]).astype(LOW)
    r2 = h1 + mm(act, w_down)
    unit2, _ = norm_parts(r2)
    layer_out = (unit2 * norms[2] + norms[3]).astype(LOW).reshape(seqs, length, width)
    def listed(a):
        return pick(onehot, a.reshape(seqs, length, -1)).reshape(seqs * most, -1)

    dy = jnp.where(live[:, :, None], grad_listed, 0).astype(F32).reshape(seqs * most, width)
    unit2_m, rstd2_m = norm_parts(listed(r2))
    g_gain_ffn = jnp.sum(dy * unit2_m, axis=0)
    g_shift_ffn = jnp.sum(dy, axis=0)
    dr2 = norm_back(dy, unit2_m, rstd2_m, norms[2])
    e2 = dr2.astype(LOW)
    h1_m = listed(h1_low)
    u_m = mm(h1_m, w_up)
    gate, up = u_m[:, :FF], u_m[:, FF:]
    cdf = 0.5 * (1.0 + lax.erf(gate * (0.5**0.5)))
    pdf = jnp.exp(-0.5 * gate * gate) * ((2.0 * jnp.pi) ** -0.5)
    gelu = gate * cdf
    act_m = (gelu * up).astype(LOW)
    g_down = jnp.einsum("nf,nd->fd", act_m, e2, preferred_element_type=F32)
    dact = jnp.einsum("nd,fd->nf", e2, w_down, preferred_element_type=F32)
    du = jnp.concatenate([dact * up * (cdf + gate * pdf), dact * gelu], axis=1).astype(LOW)
    g_up = jnp.einsum("nd,nf->df", h1_m, du, preferred_element_type=F32)
    dh1 = dr2 + jnp.einsum("nf,df->nd", du, w_up, preferred_element_type=F32)
    unit1_m, rstd1_m = norm_parts(listed(r1))
    g_gain_attn = jnp.sum(dh1 * unit1_m, axis=0)
    g_shift_attn = jnp.sum(dh1, axis=0)
    dr1 = norm_back(dh1, unit1_m, rstd1_m, norms[0])
    e1 = dr1.astype(LOW)
    g_out = jnp.einsum("nd,ne->de", listed(att), e1, preferred_element_type=F32)
    datt = jnp.einsum("ne,de->nd", e1, w_out, preferred_element_type=F32).astype(LOW)
    datt = datt.reshape(seqs, most, HEADS, HEAD_DIM)
    q_m = listed(qkv[:, :width]).reshape(seqs, most, HEADS, HEAD_DIM)
    away = jnp.abs(positions[:, :, None].astype(F32) - place[None, None, :])
    s_m = jnp.einsum("sqhc,skhc->shqk", q_m, k, preferred_element_type=F32) * scale
    p_m = jax.nn.softmax(s_m - slope[None, :, None, None] * away[:, None], axis=-1)
    dv = jnp.einsum("shqk,sqhc->skhc", p_m.astype(LOW), datt, preferred_element_type=F32)
    dp = jnp.einsum("sqhc,skhc->shqk", datt, v, preferred_element_type=F32)
    ds = (p_m * (dp - jnp.sum(dp * p_m, axis=-1, keepdims=True))).astype(LOW)
    dq_m = (jnp.einsum("shqk,skhc->sqhc", ds, k, preferred_element_type=F32) * scale).astype(LOW)
    dk = (jnp.einsum("shqk,sqhc->skhc", ds, q_m, preferred_element_type=F32) * scale).astype(LOW)
    put = (onehot * live[:, :, None]).astype(LOW)
    dq = jnp.einsum("svj,svd->sjd", put, dq_m.reshape(seqs, most, width), preferred_element_type=F32)
    dqkv = jnp.concatenate(
        [dq.astype(LOW).reshape(tokens, width), dk.reshape(tokens, width), dv.astype(LOW).reshape(tokens, width)], axis=1
    )
    g_qkv = jnp.einsum("nd,ne->de", rows_in, dqkv, preferred_element_type=F32)
    dr1_all = jnp.einsum("svj,svd->sjd", onehot * live[:, :, None], dr1.reshape(seqs, most, width), precision=lax.Precision.HIGHEST)
    grad_in = dr1_all.reshape(tokens, width) + jnp.einsum("ne,de->nd", dqkv, w_qkv, preferred_element_type=F32)
    owned = scatter_grads(g_qkv, g_out, g_up, g_down)
    small = lax.psum(jnp.stack([g_gain_attn, g_shift_attn, g_gain_ffn, g_shift_ffn]), AXES)
    share = width // lax.axis_size("fsdp")
    small = lax.dynamic_slice_in_dim(small, lax.axis_index("fsdp") * share, share, axis=1)
    return (
        layer_out,
        grad_in.reshape(seqs, length, width),
        *owned,
        small[0],
        small[1],
        small[2],
        small[3],
    )


def solution(mesh):
    rows3 = P(("fsdp", "dp"), None, None)
    rows2 = P("fsdp", None)
    rows1 = P("fsdp")
    return jax.shard_map(
        on_device,
        mesh=mesh,
        in_specs=(rows3, rows2, rows2, rows2, rows2, rows1, rows1, rows1, rows1, rows3, P(("fsdp", "dp"), None), P(("fsdp", "dp"))),
        out_specs=(rows3, rows3, rows2, rows2, rows2, rows2, rows1, rows1, rows1, rows1),
        check_vma=False,
    )
```

```python
import functools

import jax
import jax.numpy as jnp
from jax import lax
from jax.experimental import pallas as pl
from jax.experimental.pallas import tpu as pltpu
from jax.sharding import PartitionSpec as P

HEADS = 12
HEAD_DIM = 64
EPS = 1e-12
F32 = jnp.float32
LOW = jnp.bfloat16
AXES = ("fsdp", "dp")
D = 768
ROWS = 96
LINE = 4
SHARDS = D // ROWS
QUARTERS = 4
EXACT = lax.Precision.HIGHEST
SCALE = HEAD_DIM**-0.5
VMEM = pl.BlockSpec(memory_space=pltpu.VMEM)
SMEM = pl.BlockSpec(memory_space=pltpu.SMEM)
BIG = pltpu.CompilerParams(vmem_limit_bytes=60 * 1024 * 1024)


def out(shape, dtype):
    return jax.ShapeDtypeStruct(shape, dtype)


def cost(flops, size):
    return pl.CostEstimate(flops=int(flops), bytes_accessed=int(size), transcendentals=0)


def mm(a, b):
    return jnp.dot(a, b, preferred_element_type=F32)


def mm_nt(a, b):
    return lax.dot_general(a, b, (((1,), (1,)), ((), ())), preferred_element_type=F32)


def mm_tn(a, b):
    return lax.dot_general(a, b, (((0,), (0,)), ((), ())), preferred_element_type=F32)


def norm_parts(value):
    center = value - jnp.mean(value, axis=-1, keepdims=True)
    rstd = lax.rsqrt(jnp.mean(center * center, axis=-1, keepdims=True) + EPS)
    return center * rstd, rstd


def norm_back(grad, unit, rstd, gain):
    scaled = grad * gain
    return rstd * (
        scaled
        - jnp.mean(scaled, axis=-1, keepdims=True)
        - unit * jnp.mean(scaled * unit, axis=-1, keepdims=True)
    )


def onehot(pos_ref, seq, most, length):
    spots = lax.broadcasted_iota(jnp.int32, (most, length), 1)
    return spots == pos_ref[pl.ds(seq * most, most), :]


def gelu_parts(gate):
    cdf = 0.5 * (1.0 + lax.erf(gate * (0.5**0.5)))
    pdf = jnp.exp(-0.5 * gate * gate) * ((2.0 * jnp.pi) ** -0.5)
    return gate * cdf, cdf + gate * pdf


def slope_of(head):
    return 2.0 ** (-8.0 * (head + 1.0) / HEADS)


def block(ref, *index):
    value = ref[index] if index else ref[...]
    return value.reshape(-1, value.shape[-1])


def attention_kernel(seqs, most, slope_ref, x_ref, w_ref, norm_ref, pos_ref, qkv_ref, h1_ref, att_m_ref, h1_m_ref, q_m_ref, r1_m_ref, att_ref, r1_ref):
    length = x_ref.shape[0] // seqs
    step = 256

    @pl.loop(0, 3 * D // step)
    def _(n):
        j = n // (D // step)
        lane = pl.multiple_of((n - j * (D // step)) * step, step)
        w = w_ref[:, j, :, pl.ds(lane, step)].reshape(D, step)
        qkv_ref[:, pl.ds(pl.multiple_of(n * step, step), step)] = mm(x_ref[...], w).astype(LOW)

    first = lax.broadcasted_iota(jnp.int32, (length, 128), 1) < HEAD_DIM
    row = lax.broadcasted_iota(jnp.int32, (length, length), 0)
    col = lax.broadcasted_iota(jnp.int32, (length, length), 1)
    away = jnp.abs(row - col).astype(F32)

    @pl.loop(0, HEADS // 2)
    def _(t):
        lane = pl.multiple_of(t * 128, 128)
        for s in range(seqs):
            rows = slice(s * length, (s + 1) * length)
            q = qkv_ref[rows, pl.ds(lane, 128)]
            k = qkv_ref[rows, pl.ds(D + lane, 128)]
            v = qkv_ref[rows, pl.ds(2 * D + lane, 128)]
            mixed = []
            for h in range(2):
                mine = jnp.where(first if h == 0 else ~first, q, jnp.zeros_like(q))
                score = mm_nt(mine, k) * SCALE - slope_ref[2 * t + h] * away
                e = jnp.exp(score - jnp.max(score, axis=-1, keepdims=True))
                p = (e / jnp.sum(e, axis=-1, keepdims=True)).astype(LOW)
                mixed.append(mm(p, v))
            att_ref[rows, pl.ds(lane, 128)] = jnp.where(first, mixed[0], mixed[1]).astype(LOW)

    @pl.loop(0, D // step)
    def _(n):
        lane = pl.multiple_of(n * step, step)
        w = w_ref[:, 3, :, pl.ds(lane, step)].reshape(D, step)
        r1_ref[:, pl.ds(lane, step)] = x_ref[:, pl.ds(lane, step)].astype(F32) + mm(att_ref[...], w)

    for s in range(seqs):
        rows = slice(s * length, (s + 1) * length)
        listed = slice(s * most, (s + 1) * most)
        unit, _ = norm_parts(r1_ref[rows, :])
        h1 = unit * norm_ref[0:1, :] + norm_ref[1:2, :]
        h1_ref[rows, :] = h1
        hot = onehot(pos_ref, s, most, length)
        hot_low = hot.astype(LOW)
        r1_m_ref[listed, :] = jnp.dot(hot.astype(F32), r1_ref[rows, :], precision=EXACT, preferred_element_type=F32)
        h1_m_ref[listed, :] = mm(hot_low, h1.astype(LOW)).astype(LOW)
        att_m_ref[listed, :] = mm(hot_low, att_ref[rows, :]).astype(LOW)
        q_m_ref[listed, :] = mm(hot_low, qkv_ref[rows, 0:D]).astype(LOW)


def attention_forward(x, w_attn, norms, pos, slopes, seqs):
    tokens = x.shape[0]
    listed = pos.shape[0]
    return pl.pallas_call(
        functools.partial(attention_kernel, seqs, listed // seqs),
        out_shape=(
            out((tokens, 3 * D), LOW),
            out((tokens, D), F32),
            out((listed, D), LOW),
            out((listed, D), LOW),
            out((listed, D), LOW),
            out((listed, D), F32),
        ),
        in_specs=[SMEM, VMEM, VMEM, VMEM, VMEM],
        out_specs=(VMEM,) * 6,
        scratch_shapes=[pltpu.VMEM((tokens, D), LOW), pltpu.VMEM((tokens, D), F32)],
        compiler_params=BIG,
        cost_estimate=cost(2 * tokens * D * 4 * D, 8e6),
        name="attention_forward",
    )(slopes, x, w_attn, norms, pos)


def ffn_kernel(seqs, most, h1_ref, gate_ref, up_ref, down_ref, norm_ref, pos_ref, dy_ref, y_ref, dr2_ref, e2_ref, small_ref, low_ref, act_ref, acc_ref):
    j = pl.program_id(0)
    tokens = h1_ref.shape[0]
    length = tokens // seqs
    step = 256

    @pl.when(j == 0)
    def _():
        low_ref[...] = h1_ref[...].astype(LOW)
        acc_ref[...] = h1_ref[...]

    @pl.loop(0, D // step)
    def _(n):
        lane = pl.multiple_of(n * step, step)
        gate = mm(low_ref[...], gate_ref[:, :, pl.ds(lane, step)].reshape(D, step))
        up = mm(low_ref[...], up_ref[:, :, pl.ds(lane, step)].reshape(D, step))
        cdf = 0.5 * (1.0 + lax.erf(gate * (0.5**0.5)))
        act_ref[:, pl.ds(lane, step)] = (gate * cdf * up).astype(LOW)

    @pl.loop(0, D // step)
    def _(n):
        lane = pl.multiple_of(n * step, step)
        acc_ref[:, pl.ds(lane, step)] += mm(act_ref[...], down_ref[:, :, :, pl.ds(lane, step)].reshape(D, step))

    @pl.when(j == QUARTERS - 1)
    def _():
        gain = norm_ref[2:3, :]
        small = [jnp.zeros((1, D), F32)] * 2
        for s in range(seqs):
            rows = slice(s * length, (s + 1) * length)
            listed = slice(s * most, (s + 1) * most)
            unit, _ = norm_parts(acc_ref[rows, :])
            y_ref[rows, :] = (unit * gain + norm_ref[3:4, :]).astype(LOW)
            hot = onehot(pos_ref, s, most, length).astype(F32)
            picked = jnp.dot(hot, acc_ref[rows, :], precision=EXACT, preferred_element_type=F32)
            unit_m, rstd_m = norm_parts(picked)
            dy = dy_ref[listed, :].astype(F32)
            small = [small[0] + jnp.sum(dy * unit_m, axis=0, keepdims=True), small[1] + jnp.sum(dy, axis=0, keepdims=True)]
            dr2 = norm_back(dy, unit_m, rstd_m, gain)
            dr2_ref[listed, :] = dr2
            e2_ref[listed, :] = dr2.astype(LOW)
        small_ref[...] = jnp.concatenate(small, axis=0)


def ffn_forward(h1, w_ffn, norms, pos, dy, seqs):
    tokens = h1.shape[0]
    listed = pos.shape[0]
    whole = lambda shape: pl.BlockSpec(shape, lambda j: (0,) * len(shape), pipeline_mode=pl.Buffered(1))
    return pl.pallas_call(
        functools.partial(ffn_kernel, seqs, listed // seqs),
        out_shape=(out((tokens, D), LOW), out((listed, D), F32), out((listed, D), LOW), out((2, D), F32)),
        grid=(QUARTERS,),
        in_specs=[
            whole((tokens, D)),
            pl.BlockSpec((SHARDS, None, None, ROWS, D), lambda j: (0, j, 0, 0, 0)),
            pl.BlockSpec((SHARDS, None, None, ROWS, D), lambda j: (0, j, 1, 0, 0)),
            pl.BlockSpec((SHARDS // QUARTERS, QUARTERS, None, ROWS, D), lambda j: (j, 0, 2, 0, 0)),
            whole(norms.shape),
            whole(pos.shape),
            whole(dy.shape),
        ],
        out_specs=(
            pl.BlockSpec((tokens, D), lambda j: (0, 0)),
            pl.BlockSpec((listed, D), lambda j: (0, 0)),
            pl.BlockSpec((listed, D), lambda j: (0, 0)),
            pl.BlockSpec((2, D), lambda j: (0, 0)),
        ),
        scratch_shapes=[pltpu.VMEM((tokens, D), LOW), pltpu.VMEM((tokens, D), LOW), pltpu.VMEM((tokens, D), F32)],
        compiler_params=BIG,
        cost_estimate=cost(2 * tokens * D * 12 * D, 18e6),
        name="ffn_forward",
    )(h1, w_ffn, w_ffn, w_ffn, norms, pos, dy)


def ffn_again_kernel(where_ref, h_ref, gate_ref, up_ref, act_ref, to_gate_ref, to_up_ref):
    step = 256

    @pl.loop(0, D // step)
    def _(n):
        lane = pl.multiple_of(n * step, step)
        rows = block(h_ref)
        gate = mm(rows, gate_ref[:, :, pl.ds(lane, step)].reshape(D, step))
        up = mm(rows, up_ref[:, :, pl.ds(lane, step)].reshape(D, step))
        value, slope = gelu_parts(gate)
        act_ref[:, pl.ds(lane, step)] = (value * up).astype(LOW)
        to_gate_ref[:, pl.ds(lane, step)] = slope * up
        to_up_ref[:, pl.ds(lane, step)] = value


def quarter_specs(which):
    specs = {
        "gate": pl.BlockSpec((SHARDS, None, None, ROWS, D), lambda g, w: (0, w[4], 0, 0, 0)),
        "up": pl.BlockSpec((SHARDS, None, None, ROWS, D), lambda g, w: (0, w[4], 1, 0, 0)),
        "down": pl.BlockSpec((SHARDS // QUARTERS, QUARTERS, None, ROWS, D), lambda g, w: (w[4], 0, 2, 0, 0)),
    }
    return [specs[name] for name in which]


def at_once(shape):
    return pl.BlockSpec(shape, lambda g, w: (0,) * len(shape))


def ffn_again(where, h_all, w_ffn):
    rows = h_all.shape[0] * h_all.shape[1]
    return pl.pallas_call(
        ffn_again_kernel,
        out_shape=(out((rows, D), LOW), out((rows, D), F32), out((rows, D), F32)),
        grid_spec=pltpu.PrefetchScalarGridSpec(
            num_scalar_prefetch=1,
            grid=(1,),
            in_specs=[at_once(h_all.shape), *quarter_specs(["gate", "up"])],
            out_specs=(at_once((rows, D)),) * 3,
        ),
        compiler_params=BIG,
        cost_estimate=cost(4 * rows * D * D, 8e6),
        name="ffn_again",
    )(where, h_all, w_ffn, w_ffn)


def ffn_back_kernel(where_ref, e_ref, to_gate_ref, to_up_ref, gate_ref, up_ref, down_ref, dgate_ref, dup_ref, keep_ref, send_ref):
    listed = e_ref.shape[1]
    half = QUARTERS // 2
    for n in range(SHARDS // QUARTERS):
        lanes = slice(n * QUARTERS * ROWS, (n + 1) * QUARTERS * ROWS)
        dact = mm_nt(block(e_ref), block(down_ref, n))
        dgate_ref[:, lanes] = (dact * to_gate_ref[:, lanes]).astype(LOW)
        dup_ref[:, lanes] = (dact * to_up_ref[:, lanes]).astype(LOW)
    for n in range(2):
        shards = slice(n * SHARDS // 2, (n + 1) * SHARDS // 2)
        lanes = slice(n * D // 2, (n + 1) * D // 2)
        part = mm_nt(dgate_ref[...], block(gate_ref, shards)) + mm_nt(dup_ref[...], block(up_ref, shards))
        for r in range(half):
            keep_ref[r, :, lanes] = part[2 * r * listed : (2 * r + 1) * listed]
            send_ref[r, :, lanes] = part[(2 * r + 1) * listed : (2 * r + 2) * listed].astype(LOW)


def ffn_back(where, e_all, to_gate, to_up, w_ffn):
    count, listed, _ = e_all.shape
    rows = count * listed
    return pl.pallas_call(
        ffn_back_kernel,
        out_shape=(out((rows, D), LOW), out((rows, D), LOW), out((count // 2, listed, D), F32), out((count // 2, listed, D), LOW)),
        grid_spec=pltpu.PrefetchScalarGridSpec(
            num_scalar_prefetch=1,
            grid=(1,),
            in_specs=[at_once(e_all.shape), at_once((rows, D)), at_once((rows, D)), *quarter_specs(["gate", "up", "down"])],
            out_specs=(at_once((rows, D)), at_once((rows, D)), at_once((count // 2, listed, D)), at_once((count // 2, listed, D))),
        ),
        compiler_params=BIG,
        cost_estimate=cost(6 * rows * D * D, 12e6),
        name="ffn_back",
    )(where, e_all, to_gate, to_up, w_ffn, w_ffn, w_ffn)


def weight_grad_kernel(where_ref, a_ref, b_ref, keep_ref, send_ref, full_ref):
    z, y = where_ref[0], where_ref[1]
    a = block(a_ref)
    step = 256

    @pl.loop(0, D // step)
    def _(n):
        lane = pl.multiple_of(n * step, step)
        full_ref[:, pl.ds(lane, step)] = mm_tn(a, block(b_ref, *([slice(None)] * (len(b_ref.shape) - 1)), pl.ds(lane, step)))

    for r in range(LINE):
        base = 2 * lax.rem(z + r, LINE)
        for other, ref in ((0, keep_ref), (1, send_ref)):
            start = (base + (y if other == 0 else 1 - y)) * ROWS
            ref[r] = full_ref[pl.ds(pl.multiple_of(start, 8), ROWS), :].astype(LOW)


def weight_grad(where, a, b):
    shape = (LINE, ROWS, D)
    rows = a.size // D
    return pl.pallas_call(
        weight_grad_kernel,
        out_shape=(out(shape, LOW), out(shape, LOW)),
        in_specs=[SMEM, VMEM, VMEM],
        out_specs=(VMEM, VMEM),
        scratch_shapes=[pltpu.VMEM((D, D), F32)],
        compiler_params=BIG,
        cost_estimate=cost(2 * rows * D * D, 4e6),
        name="weight_grad",
    )(where, a, b)


def attention_back_kernel(seqs, most, slope_ref, dr2_ref, part_ref, came_ref, r1_ref, q_ref, qkv_ref, att_ref, w_ref, norm_ref, pos_ref, dr1_ref, rhs_ref, lhs_ref, small_ref, datt_ref):
    length = qkv_ref.shape[0] // seqs
    listed = seqs * most
    dh1 = dr2_ref[...] + part_ref[...] + came_ref[...].astype(F32)
    unit, rstd = norm_parts(r1_ref[...])
    small_ref[0:1, :] = jnp.sum(dh1 * unit, axis=0, keepdims=True)
    small_ref[1:2, :] = jnp.sum(dh1, axis=0, keepdims=True)
    dr1 = norm_back(dh1, unit, rstd, norm_ref[0:1, :])
    dr1_ref[...] = dr1
    low = dr1.astype(LOW)
    rhs_ref[0:listed, 3 * D : 4 * D] = low
    rhs_ref[listed:, 3 * D : 4 * D] = jnp.zeros((seqs * length - listed, D), LOW)
    lhs_ref[0:listed, :] = att_ref[...]
    lhs_ref[listed:, :] = jnp.zeros((seqs * length - listed, D), LOW)
    for n in range(2):
        lanes = slice(n * D // 2, (n + 1) * D // 2)
        datt_ref[:, lanes] = mm_nt(low, block(w_ref, slice(n * SHARDS // 2, (n + 1) * SHARDS // 2), 3)).astype(LOW)
    first = lax.broadcasted_iota(jnp.int32, (length, 128), 1) < HEAD_DIM
    first_m = lax.broadcasted_iota(jnp.int32, (most, 128), 1) < HEAD_DIM
    spots = lax.broadcasted_iota(jnp.int32, (most, length), 1)

    @pl.loop(0, HEADS // 2)
    def _(t):
        lane = pl.multiple_of(t * 128, 128)
        for s in range(seqs):
            rows = slice(s * length, (s + 1) * length)
            mine = slice(s * most, (s + 1) * most)
            at = pos_ref[mine, :]
            away = jnp.abs(at - spots).astype(F32)
            hot = (spots == at).astype(LOW)
            q = q_ref[mine, pl.ds(lane, 128)]
            da = datt_ref[mine, pl.ds(lane, 128)]
            k = qkv_ref[rows, pl.ds(D + lane, 128)]
            v = qkv_ref[rows, pl.ds(2 * D + lane, 128)]
            dq, dk, dv = [], [], []
            for h in range(2):
                pick = first_m if h == 0 else ~first_m
                score = mm_nt(jnp.where(pick, q, jnp.zeros_like(q)), k) * SCALE - slope_ref[2 * t + h] * away
                e = jnp.exp(score - jnp.max(score, axis=-1, keepdims=True))
                p = e / jnp.sum(e, axis=-1, keepdims=True)
                dp = mm_nt(jnp.where(pick, da, jnp.zeros_like(da)), v)
                ds = (p * (dp - jnp.sum(dp * p, axis=-1, keepdims=True))).astype(LOW)
                dv.append(mm_tn(p.astype(LOW), da))
                dq.append(mm(ds, k))
                dk.append(mm_tn(ds, q))
            dq = (jnp.where(first_m, dq[0], dq[1]) * SCALE).astype(LOW)
            rhs_ref[rows, pl.ds(lane, 128)] = mm_tn(hot, dq).astype(LOW)
            rhs_ref[rows, pl.ds(D + lane, 128)] = (jnp.where(first, dk[0], dk[1]) * SCALE).astype(LOW)
            rhs_ref[rows, pl.ds(2 * D + lane, 128)] = jnp.where(first, dv[0], dv[1]).astype(LOW)


def attention_back(dr2, part, came, r1_m, q_m, qkv, att_m, w_attn, norms, pos, slopes, seqs):
    tokens = qkv.shape[0]
    listed = pos.shape[0]
    return pl.pallas_call(
        functools.partial(attention_back_kernel, seqs, listed // seqs),
        out_shape=(out((listed, D), F32), out((tokens, 4 * D), LOW), out((tokens, D), LOW), out((2, D), F32)),
        in_specs=[SMEM] + [VMEM] * 10,
        out_specs=(VMEM,) * 4,
        scratch_shapes=[pltpu.VMEM((listed, D), LOW)],
        compiler_params=BIG,
        cost_estimate=cost(2 * listed * D * D * 2, 12e6),
        name="attention_back",
    )(slopes, dr2, part, came, r1_m, q_m, qkv, att_m, w_attn, norms, pos)


def attention_grads_kernel(where_ref, x_ref, lhs_ref, rhs_ref, keep0_ref, keep1_ref, send0_ref, send1_ref, full_ref):
    z, y, mine = where_ref[0], where_ref[1], where_ref[4]
    half = ROWS // 2
    step = 256
    for rc in (1, 0):
        for rx in (0, 1):
            r = 2 * rx + rc
            j = (mine + r) if False else jnp.bitwise_xor(mine, r)
            is_out = j == 3

            def fill(a_ref):
                @pl.loop(0, D // step)
                def _(n):
                    lane = pl.multiple_of(n * step, step)
                    cols = pl.ds(pl.multiple_of(j * D + n * step, step), step)
                    full_ref[:, pl.ds(lane, step)] = mm_tn(a_ref[...], rhs_ref[:, cols])

            @pl.when(is_out)
            def _():
                fill(lhs_ref)

            @pl.when(jnp.logical_not(is_out))
            def _():
                fill(x_ref)

            refs = (keep0_ref, keep1_ref) if rc == 0 else (send0_ref, send1_ref)
            for rz in range(LINE):
                base = 2 * lax.rem(z + rz, LINE)
                for ry in (0, 1):
                    start = (base + (y if ry == 0 else 1 - y)) * ROWS
                    for part in (0, 1):
                        rows = pl.ds(pl.multiple_of(start + part * half, 8), half)
                        value = full_ref[rows, :].astype(LOW)
                        if part == 0:
                            refs[0][rx, ry, rz] = value
                        else:
                            refs[1][ry, rx, rz] = value


def attention_grads(where, x, lhs, rhs):
    shape = (2, 2, LINE, ROWS // 2, D)
    return pl.pallas_call(
        attention_grads_kernel,
        out_shape=(out(shape, LOW),) * 4,
        in_specs=[SMEM, VMEM, VMEM, VMEM],
        out_specs=(VMEM,) * 4,
        scratch_shapes=[pltpu.VMEM((D, D), F32)],
        compiler_params=BIG,
        cost_estimate=cost(2 * x.shape[0] * D * 4 * D, 10e6),
        name="attention_grads",
    )(where, x, lhs, rhs)


def input_grad_kernel(seqs, rhs_ref, w_ref, dr1_ref, pos_ref, out_ref):
    length = out_ref.shape[0] // seqs
    most = dr1_ref.shape[0] // seqs
    for n in range(2):
        lanes = slice(n * D // 2, (n + 1) * D // 2)
        shards = slice(n * SHARDS // 2, (n + 1) * SHARDS // 2)
        total = mm_nt(rhs_ref[:, 0:D], block(w_ref, shards, 0))
        total += mm_nt(rhs_ref[:, D : 2 * D], block(w_ref, shards, 1))
        total += mm_nt(rhs_ref[:, 2 * D : 3 * D], block(w_ref, shards, 2))
        for s in range(seqs):
            rows = slice(s * length, (s + 1) * length)
            hot = (lax.broadcasted_iota(jnp.int32, (length, most), 0) == pos_ref[s : s + 1, :]).astype(F32)
            spread = jnp.dot(hot, dr1_ref[s * most : (s + 1) * most, lanes], precision=EXACT, preferred_element_type=F32)
            out_ref[rows, lanes] = total[rows] + spread


def input_grad(rhs, w_attn, dr1, positions):
    tokens = rhs.shape[0]
    return pl.pallas_call(
        functools.partial(input_grad_kernel, positions.shape[0]),
        out_shape=out((tokens, D), F32),
        in_specs=[VMEM] * 4,
        out_specs=VMEM,
        compiler_params=BIG,
        cost_estimate=cost(2 * tokens * D * 3 * D, 10e6),
        name="input_grad",
    )(rhs, w_attn, dr1, positions)


def place(z, y, x, c):
    return (2 * z + y) * 4 + 2 * x + c


def grid_perm(move):
    return [
        (place(z, y, x, c), place(*move(z, y, x, c)))
        for z in range(4)
        for y in range(2)
        for x in range(2)
        for c in range(2)
    ]


MOVES = {
    "x": grid_perm(lambda z, y, x, c: (z, y, 1 - x, c)),
    "y": grid_perm(lambda z, y, x, c: (z, 1 - y, x, c)),
    "c": grid_perm(lambda z, y, x, c: (z, y, x, 1 - c)),
    1: grid_perm(lambda z, y, x, c: ((z + 1) % 4, y, x, c)),
    2: grid_perm(lambda z, y, x, c: ((z + 2) % 4, y, x, c)),
    3: grid_perm(lambda z, y, x, c: ((z + 3) % 4, y, x, c)),
    "down": [(m * 4 + q, (2 * q + m // 4) * 4 + m % 4) for m in range(8) for q in range(4)],
}


def send(value, move):
    return lax.ppermute(value, AXES, MOVES[move])


def share_dp(value):
    core = send(value, "c")
    return value, core, send(value, "x"), send(core, "x")


def line_sum(block_list, kept):
    total = kept.astype(F32)
    for r, value in block_list:
        total = total + send(value, r).astype(F32)
    return total


def reduce_quarter(keep, away):
    got = send(away, "y")
    total = keep.astype(F32) + got.astype(F32)
    return line_sum([(r, total[r].astype(LOW)) for r in (1, 2, 3)], total[0]).astype(LOW)


def reduce_attention(keep, away, first, second):
    total = keep.astype(F32) + send(away, "c").astype(F32)
    total = total[0] + send(total[1].astype(LOW), first).astype(F32)
    total = total[0] + send(total[1].astype(LOW), second).astype(F32)
    return line_sum([(r, total[r].astype(LOW)) for r in (1, 2, 3)], total[0]).astype(LOW)


def finish_kernel(rows_out, where_ref, a_ref, b_ref, c_ref, d_ref, *rest):
    outs, held = rest[:-1], rest[-1]
    mine = where_ref[4]
    for r, ref in enumerate((a_ref, b_ref, c_ref, d_ref)):
        held[jnp.bitwise_xor(mine, r)] = ref[...].astype(F32)
    if rows_out:
        for j in range(QUARTERS):
            outs[0][j * ROWS : (j + 1) * ROWS, :] = held[j]
    else:
        at = 0
        for ref in outs:
            for j in range(ref.shape[1] // D):
                ref[:, j * D : (j + 1) * D] = held[at]
                at += 1


def finish(where, pieces, widths, rows_out=False):
    shapes = [out((QUARTERS * ROWS, D), F32)] if rows_out else [out((ROWS, n * D), F32) for n in widths]
    return pl.pallas_call(
        functools.partial(finish_kernel, rows_out),
        out_shape=tuple(shapes),
        in_specs=[SMEM] + [VMEM] * 4,
        out_specs=(VMEM,) * len(shapes),
        scratch_shapes=[pltpu.VMEM((QUARTERS, ROWS, D), F32)],
        compiler_params=BIG,
        cost_estimate=cost(1e5, 2e6),
        name="finish",
    )(where, *pieces)


def on_block(hidden_in, w_qkv, w_out, w_up, w_down, gain_attn, shift_attn, gain_ffn, shift_ffn, grad_listed, positions, counts):
    seqs, length, width = hidden_in.shape
    tokens = seqs * length
    most = positions.shape[1]
    i, j = lax.axis_index("fsdp"), lax.axis_index("dp")
    where = jnp.stack([i // 2, i % 2, j // 2, j % 2, j]).astype(jnp.int32)
    ff = w_down.shape[0] * SHARDS
    attn_piece = lax.dynamic_slice_in_dim(jnp.concatenate([w_qkv, w_out], axis=1), j * D, D, axis=1)
    w_attn = lax.all_gather(attn_piece, AXES, axis=0, tiled=False).reshape(SHARDS, QUARTERS, ROWS, D)
    ffn_piece = jnp.stack(
        [
            lax.dynamic_slice_in_dim(w_up, j * D, D, axis=1),
            lax.dynamic_slice_in_dim(w_up, ff + j * D, D, axis=1),
            lax.dynamic_slice_in_dim(w_down, j * ROWS, ROWS, axis=0),
        ]
    )
    w_ffn = lax.all_gather(ffn_piece, AXES, axis=0, tiled=False).reshape(SHARDS, QUARTERS, 3, ROWS, D)
    norms = jnp.stack([gain_attn, shift_attn, gain_ffn, shift_ffn])
    norms = lax.all_gather(norms, "fsdp", axis=1, tiled=True).astype(F32)
    slopes = jnp.exp2(-8.0 * (jnp.arange(HEADS, dtype=F32) + 1.0) / HEADS)
    x = hidden_in.reshape(tokens, width)
    pos = positions.reshape(seqs * most, 1)
    live = jnp.arange(most, dtype=jnp.int32)[None, :] < counts[:, None]
    dy = jnp.where(live[:, :, None], grad_listed, jnp.zeros_like(grad_listed)).reshape(seqs * most, width)

    qkv, h1, att_m, h1_m, q_m, r1_m = attention_forward(x, w_attn, norms, pos, slopes, seqs)
    h_all = jnp.stack(share_dp(h1_m))
    layer_out, dr2, e2, small_ffn = ffn_forward(h1, w_ffn, norms, pos, dy, seqs)
    act, to_gate, to_up = ffn_again(where, h_all, w_ffn)
    e_all = jnp.stack(share_dp(e2))
    dgate, dup, keep, away = ffn_back(where, e_all, to_gate, to_up, w_ffn)
    total = keep + send(away, "c").astype(F32)
    came = send(total[1].astype(LOW), "x")
    g_down = reduce_quarter(*weight_grad(where, act, e_all))
    g_gate = reduce_quarter(*weight_grad(where, h_all, dgate))
    g_up = reduce_quarter(*weight_grad(where, h_all, dup))
    dr1, rhs, lhs, small_attn = attention_back(dr2, total[0], came, r1_m, q_m, qkv, att_m, w_attn, norms, pos, slopes, seqs)
    keep0, keep1, away0, away1 = attention_grads(where, x, lhs, rhs)
    g_attn = jnp.concatenate(
        [reduce_attention(keep0, away0, "x", "y"), reduce_attention(keep1, away1, "y", "x")], axis=0
    )
    grad_in = input_grad(rhs, w_attn, dr1, positions)
    (grad_down,) = finish(where, share_dp(send(g_down, "down")), (), rows_out=True)
    (grad_gate,) = finish(where, share_dp(g_gate), (QUARTERS,))
    (grad_up,) = finish(where, share_dp(g_up), (QUARTERS,))
    grad_qkv, grad_out = finish(where, share_dp(g_attn), (3, 1))
    small = lax.psum(jnp.concatenate([small_attn, small_ffn]), AXES)
    small = lax.dynamic_slice_in_dim(small, i * ROWS, ROWS, axis=1)
    return (
        layer_out.reshape(seqs, length, width),
        grad_in.reshape(seqs, length, width),
        grad_qkv,
        grad_out,
        jnp.concatenate([grad_gate, grad_up], axis=1),
        grad_down,
        small[0],
        small[1],
        small[2],
        small[3],
    )


FF = 3072


def slopes():
    return jnp.exp2(-8.0 * (jnp.arange(HEADS, dtype=F32) + 1.0) / HEADS)


def pick(onehot, rows):
    if rows.dtype == LOW:
        return jnp.einsum("svj,sjd->svd", onehot.astype(LOW), rows, preferred_element_type=F32).astype(LOW)
    return jnp.einsum("svj,sjd->svd", onehot, rows, precision=lax.Precision.HIGHEST)


def gather_weights(w_qkv, w_out, w_up, w_down):
    fsdp = lax.axis_size("fsdp")
    dp = lax.axis_size("dp")
    rows, width = w_out.shape
    if rows % (8 * dp):
        return (
            lax.all_gather(w_qkv, "fsdp", axis=0, tiled=True),
            lax.all_gather(w_out, "fsdp", axis=0, tiled=True),
            lax.all_gather(w_up, "fsdp", axis=0, tiled=True),
            lax.all_gather(w_down, "fsdp", axis=0, tiled=True),
        )
    mine = lax.axis_index("dp")
    part = rows // dp
    group = w_down.shape[0] // rows
    joined = jnp.concatenate([w_qkv, w_out, w_up], axis=1)
    joined = lax.dynamic_slice_in_dim(joined, mine * part, part, axis=0)
    down = lax.dynamic_slice_in_dim(w_down, mine * part * group, part * group, axis=0)
    down = jnp.concatenate([down[k * part : (k + 1) * part] for k in range(group)], axis=1)
    full = lax.all_gather(jnp.concatenate([joined, down], axis=1), AXES, axis=0, tiled=True)
    a, b = w_qkv.shape[1], w_qkv.shape[1] + w_out.shape[1]
    c = b + w_up.shape[1]
    full_down = full[:, c:].reshape(fsdp * dp, part, group, width)
    full_down = full_down.transpose(0, 2, 1, 3).reshape(fsdp * dp * part * group, width)
    return full[:, :a], full[:, a:b], full[:, b:c], full_down


def scatter_grads(g_qkv, g_out, g_up, g_down):
    fsdp = lax.axis_size("fsdp")
    dp = lax.axis_size("dp")
    width = g_out.shape[1]
    rows = g_out.shape[0] // fsdp
    if rows % (8 * dp):
        return tuple(
            lax.psum(lax.psum_scatter(g, "fsdp", scatter_dimension=0, tiled=True), "dp")
            for g in (g_qkv, g_out, g_up, g_down)
        )
    part = rows // dp
    group = g_down.shape[0] // g_out.shape[0]
    down = g_down.reshape(fsdp * dp, group, part, width).transpose(0, 2, 1, 3)
    down = down.reshape(fsdp * rows, group * width)
    joined = jnp.concatenate([g_qkv, g_out, g_up, down], axis=1).astype(LOW)
    mine = lax.psum_scatter(joined, AXES, scatter_dimension=0, tiled=True)
    full = lax.all_gather(mine, "dp", axis=0, tiled=True).astype(F32)
    a, b = g_qkv.shape[1], g_qkv.shape[1] + width
    c = b + g_up.shape[1]
    full_down = full[:, c:].reshape(dp, part, group, width).transpose(0, 2, 1, 3)
    return full[:, :a], full[:, a:b], full[:, b:c], full_down.reshape(rows * group, width)


def on_device(hidden_in, w_qkv, w_out, w_up, w_down, gain_attn, shift_attn, gain_ffn, shift_ffn, grad_listed, positions, counts):
    seqs, length, width = hidden_in.shape
    tokens = seqs * length
    most = positions.shape[1]
    norms = jnp.stack([gain_attn, shift_attn, gain_ffn, shift_ffn])
    norms = lax.all_gather(norms, "fsdp", axis=1, tiled=True).astype(F32)
    w_qkv, w_out, w_up, w_down = gather_weights(w_qkv, w_out, w_up, w_down)
    live = jnp.arange(most, dtype=jnp.int32)[None, :] < counts[:, None]
    onehot = (positions[:, :, None] == jnp.arange(length, dtype=jnp.int32)).astype(F32)
    rows_in = hidden_in.reshape(tokens, width)
    slope = slopes()
    scale = HEAD_DIM**-0.5
    qkv = mm(rows_in, w_qkv).astype(LOW)
    split = qkv.reshape(seqs, length, 3, HEADS, HEAD_DIM)
    q, k, v = split[:, :, 0], split[:, :, 1], split[:, :, 2]
    place = jnp.arange(length, dtype=F32)
    bias = -slope[:, None, None] * jnp.abs(place[:, None] - place[None, :])
    s = jnp.einsum("sqhc,skhc->shqk", q, k, preferred_element_type=F32) * scale + bias
    p = jax.nn.softmax(s, axis=-1).astype(LOW)
    att = jnp.einsum("shqk,skhc->sqhc", p, v, preferred_element_type=F32).astype(LOW)
    att = att.reshape(tokens, width)
    r1 = rows_in.astype(F32) + mm(att, w_out)
    unit1, _ = norm_parts(r1)
    h1 = unit1 * norms[0] + norms[1]
    h1_low = h1.astype(LOW)
    u = mm(h1_low, w_up)
    act = (jax.nn.gelu(u[:, :FF], approximate=False) * u[:, FF:]).astype(LOW)
    r2 = h1 + mm(act, w_down)
    unit2, _ = norm_parts(r2)
    layer_out = (unit2 * norms[2] + norms[3]).astype(LOW).reshape(seqs, length, width)
    def listed(a):
        return pick(onehot, a.reshape(seqs, length, -1)).reshape(seqs * most, -1)

    dy = jnp.where(live[:, :, None], grad_listed, 0).astype(F32).reshape(seqs * most, width)
    unit2_m, rstd2_m = norm_parts(listed(r2))
    g_gain_ffn = jnp.sum(dy * unit2_m, axis=0)
    g_shift_ffn = jnp.sum(dy, axis=0)
    dr2 = norm_back(dy, unit2_m, rstd2_m, norms[2])
    e2 = dr2.astype(LOW)
    h1_m = listed(h1_low)
    u_m = mm(h1_m, w_up)
    gate, up = u_m[:, :FF], u_m[:, FF:]
    cdf = 0.5 * (1.0 + lax.erf(gate * (0.5**0.5)))
    pdf = jnp.exp(-0.5 * gate * gate) * ((2.0 * jnp.pi) ** -0.5)
    gelu = gate * cdf
    act_m = (gelu * up).astype(LOW)
    g_down = jnp.einsum("nf,nd->fd", act_m, e2, preferred_element_type=F32)
    dact = jnp.einsum("nd,fd->nf", e2, w_down, preferred_element_type=F32)
    du = jnp.concatenate([dact * up * (cdf + gate * pdf), dact * gelu], axis=1).astype(LOW)
    g_up = jnp.einsum("nd,nf->df", h1_m, du, preferred_element_type=F32)
    dh1 = dr2 + jnp.einsum("nf,df->nd", du, w_up, preferred_element_type=F32)
    unit1_m, rstd1_m = norm_parts(listed(r1))
    g_gain_attn = jnp.sum(dh1 * unit1_m, axis=0)
    g_shift_attn = jnp.sum(dh1, axis=0)
    dr1 = norm_back(dh1, unit1_m, rstd1_m, norms[0])
    e1 = dr1.astype(LOW)
    g_out = jnp.einsum("nd,ne->de", listed(att), e1, preferred_element_type=F32)
    datt = jnp.einsum("ne,de->nd", e1, w_out, preferred_element_type=F32).astype(LOW)
    datt = datt.reshape(seqs, most, HEADS, HEAD_DIM)
    q_m = listed(qkv[:, :width]).reshape(seqs, most, HEADS, HEAD_DIM)
    away = jnp.abs(positions[:, :, None].astype(F32) - place[None, None, :])
    s_m = jnp.einsum("sqhc,skhc->shqk", q_m, k, preferred_element_type=F32) * scale
    p_m = jax.nn.softmax(s_m - slope[None, :, None, None] * away[:, None], axis=-1)
    dv = jnp.einsum("shqk,sqhc->skhc", p_m.astype(LOW), datt, preferred_element_type=F32)
    dp = jnp.einsum("sqhc,skhc->shqk", datt, v, preferred_element_type=F32)
    ds = (p_m * (dp - jnp.sum(dp * p_m, axis=-1, keepdims=True))).astype(LOW)
    dq_m = (jnp.einsum("shqk,skhc->sqhc", ds, k, preferred_element_type=F32) * scale).astype(LOW)
    dk = (jnp.einsum("shqk,sqhc->skhc", ds, q_m, preferred_element_type=F32) * scale).astype(LOW)
    put = (onehot * live[:, :, None]).astype(LOW)
    dq = jnp.einsum("svj,svd->sjd", put, dq_m.reshape(seqs, most, width), preferred_element_type=F32)
    dqkv = jnp.concatenate(
        [dq.astype(LOW).reshape(tokens, width), dk.reshape(tokens, width), dv.astype(LOW).reshape(tokens, width)], axis=1
    )
    g_qkv = jnp.einsum("nd,ne->de", rows_in, dqkv, preferred_element_type=F32)
    dr1_all = jnp.einsum("svj,svd->sjd", onehot * live[:, :, None], dr1.reshape(seqs, most, width), precision=lax.Precision.HIGHEST)
    grad_in = dr1_all.reshape(tokens, width) + jnp.einsum("ne,de->nd", dqkv, w_qkv, preferred_element_type=F32)
    owned = scatter_grads(g_qkv, g_out, g_up, g_down)
    small = lax.psum(jnp.stack([g_gain_attn, g_shift_attn, g_gain_ffn, g_shift_ffn]), AXES)
    share = width // lax.axis_size("fsdp")
    small = lax.dynamic_slice_in_dim(small, lax.axis_index("fsdp") * share, share, axis=1)
    return (
        layer_out,
        grad_in.reshape(seqs, length, width),
        *owned,
        small[0],
        small[1],
        small[2],
        small[3],
    )


def solution(mesh):
    rows3 = P(("fsdp", "dp"), None, None)
    rows2 = P("fsdp", None)
    rows1 = P("fsdp")
    shape = dict(mesh.shape)
    step = on_block if shape == {"fsdp": SHARDS, "dp": QUARTERS} else on_device
    return jax.shard_map(
        step,
        mesh=mesh,
        in_specs=(rows3, rows2, rows2, rows2, rows2, rows1, rows1, rows1, rows1, rows3, P(("fsdp", "dp"), None), P(("fsdp", "dp"))),
        out_specs=(rows3, rows3, rows2, rows2, rows2, rows2, rows1, rows1, rows1, rows1),
        check_vma=False,
    )
```

```python
import functools

import jax
import jax.numpy as jnp
from jax import lax
from jax.experimental import pallas as pl
from jax.experimental.pallas import tpu as pltpu
from jax.sharding import PartitionSpec as P

HEADS = 12
HEAD_DIM = 64
EPS = 1e-12
F32 = jnp.float32
LOW = jnp.bfloat16
AXES = ("fsdp", "dp")
D = 768
ROWS = 96
LINE = 4
SHARDS = D // ROWS
QUARTERS = 4
EXACT = lax.Precision.HIGHEST
SCALE = HEAD_DIM**-0.5
VMEM = pl.BlockSpec(memory_space=pltpu.VMEM)
SMEM = pl.BlockSpec(memory_space=pltpu.SMEM)
BIG = pltpu.CompilerParams(vmem_limit_bytes=60 * 1024 * 1024)


def out(shape, dtype):
    return jax.ShapeDtypeStruct(shape, dtype)


def cost(us):
    return pl.CostEstimate(flops=0, bytes_accessed=int(us * 3.0e6), transcendentals=0)


def mm(a, b):
    return jnp.dot(a, b, preferred_element_type=F32)


def mm_nt(a, b):
    return lax.dot_general(a, b, (((1,), (1,)), ((), ())), preferred_element_type=F32)


def mm_tn(a, b):
    return lax.dot_general(a, b, (((0,), (0,)), ((), ())), preferred_element_type=F32)


def norm_parts(value):
    center = value - jnp.mean(value, axis=-1, keepdims=True)
    rstd = lax.rsqrt(jnp.mean(center * center, axis=-1, keepdims=True) + EPS)
    return center * rstd, rstd


def norm_back(grad, unit, rstd, gain):
    scaled = grad * gain
    return rstd * (
        scaled
        - jnp.mean(scaled, axis=-1, keepdims=True)
        - unit * jnp.mean(scaled * unit, axis=-1, keepdims=True)
    )


def onehot(pos_ref, seq, most, length):
    spots = lax.broadcasted_iota(jnp.int32, (most, length), 1)
    return spots == pos_ref[pl.ds(seq * most, most), :]


def gelu_parts(gate):
    cdf = 0.5 * (1.0 + lax.erf(gate * (0.5**0.5)))
    pdf = jnp.exp(-0.5 * gate * gate) * ((2.0 * jnp.pi) ** -0.5)
    return gate * cdf, cdf + gate * pdf


def slope_of(head):
    return 2.0 ** (-8.0 * (head + 1.0) / HEADS)


def block(ref, *index):
    value = ref[index] if index else ref[...]
    return value.reshape(-1, value.shape[-1])


EXTRA = 8
HALVES = ((0, 48), (48, 56))
KEYS = [(ry, rx, rc) for rc in (0, 1) for rx in (0, 1) for ry in (0, 1)]


def attention_kernel(seqs, most, where_ref, slope_ref, x_ref, norm_ref, pos_ref, *rest):
    lines, rest = rest[:16], rest[16:]
    qkv_ref, h1_ref, att_m_ref, h1_m_ref, q_m_ref, r1_m_ref, w_ref, att_ref, r1_ref, sem = rest
    z, y, c_x = where_ref[0], where_ref[1], where_ref[4]
    copies = []
    for n, (ry, rx, rc) in enumerate(KEYS):
        j = jnp.bitwise_xor(c_x, 2 * rx + rc)
        for r in range(LINE):
            shard = 2 * lax.rem(z + LINE - r, LINE) + jnp.bitwise_xor(y, ry)
            for half, (start, size) in enumerate(HALVES):
                size = min(size, ROWS - start)
                copies.append(
                    pltpu.make_async_copy(
                        lines[2 * n + half].at[r, pl.ds(0, size)], w_ref.at[shard, j, pl.ds(start, size)], sem
                    )
                )
    for copy in copies:
        copy.start()
    for copy in copies:
        copy.wait()
    length = x_ref.shape[0] // seqs
    step = 256

    @pl.loop(0, 3 * D // step)
    def _(n):
        j = n // (D // step)
        lane = pl.multiple_of((n - j * (D // step)) * step, step)
        w = w_ref[:, j, :, pl.ds(lane, step)].reshape(D, step)
        qkv_ref[:, pl.ds(pl.multiple_of(n * step, step), step)] = mm(x_ref[...], w).astype(LOW)

    first = lax.broadcasted_iota(jnp.int32, (length, 128), 1) < HEAD_DIM
    row = lax.broadcasted_iota(jnp.int32, (length, length), 0)
    col = lax.broadcasted_iota(jnp.int32, (length, length), 1)
    away = jnp.abs(row - col).astype(F32)

    @pl.loop(0, HEADS // 2)
    def _(t):
        lane = pl.multiple_of(t * 128, 128)
        bias = jnp.concatenate([slope_ref[2 * t] * away, slope_ref[2 * t + 1] * away], axis=0)
        for s in range(seqs):
            rows = slice(s * length, (s + 1) * length)
            q = qkv_ref[rows, pl.ds(lane, 128)]
            k = qkv_ref[rows, pl.ds(D + lane, 128)]
            v = qkv_ref[rows, pl.ds(2 * D + lane, 128)]
            zero = jnp.zeros_like(q)
            both = jnp.concatenate([jnp.where(first, q, zero), jnp.where(first, zero, q)], axis=0)
            score = mm_nt(both, k) * SCALE - bias
            e = jnp.exp(score - jnp.max(score, axis=-1, keepdims=True))
            p = (e * (1.0 / jnp.sum(e, axis=-1, keepdims=True))).astype(LOW)
            mixed = mm(p, v)
            att_ref[rows, pl.ds(lane, 128)] = jnp.where(first, mixed[:length], mixed[length:]).astype(LOW)

    @pl.loop(0, D // step)
    def _(n):
        lane = pl.multiple_of(n * step, step)
        w = w_ref[:, 3, :, pl.ds(lane, step)].reshape(D, step)
        r1_ref[:, pl.ds(lane, step)] = x_ref[:, pl.ds(lane, step)].astype(F32) + mm(att_ref[...], w)

    for s in range(seqs):
        rows = slice(s * length, (s + 1) * length)
        listed = slice(s * most, (s + 1) * most)
        unit, _ = norm_parts(r1_ref[rows, :])
        h1 = unit * norm_ref[0:1, :] + norm_ref[1:2, :]
        h1_ref[rows, :] = h1
        hot = onehot(pos_ref, s, most, length)
        hot_low = hot.astype(LOW)
        r1_m_ref[listed, :] = jnp.dot(hot.astype(F32), r1_ref[rows, :], precision=EXACT, preferred_element_type=F32)
        h1_m_ref[listed, :] = mm(hot_low, h1.astype(LOW)).astype(LOW)
        att_m_ref[listed, :] = mm(hot_low, att_ref[rows, :]).astype(LOW)
        q_m_ref[listed, :] = mm(hot_low, qkv_ref[rows, 0:D]).astype(LOW)


def attention_forward(where, x, lines, norms, pos, slopes, seqs):
    tokens = x.shape[0]
    listed = pos.shape[0]
    return pl.pallas_call(
        functools.partial(attention_kernel, seqs, listed // seqs),
        out_shape=(
            out((tokens, 3 * D), LOW),
            out((tokens, D), F32),
            out((listed, D), LOW),
            out((listed, D), LOW),
            out((listed, D), LOW),
            out((listed, D), F32),
            out((SHARDS, QUARTERS, ROWS, D), LOW),
        ),
        in_specs=[SMEM, SMEM, VMEM, VMEM, VMEM] + [pl.BlockSpec(memory_space=pl.ANY)] * 16,
        out_specs=(VMEM,) * 7,
        scratch_shapes=[pltpu.VMEM((tokens, D), LOW), pltpu.VMEM((tokens, D), F32), pltpu.SemaphoreType.DMA],
        compiler_params=BIG,
        cost_estimate=cost(20),
        name="attention_forward",
    )(where, slopes, x, norms, pos, *lines)


def ffn_kernel(seqs, most, h1_ref, gate_ref, up_ref, down_ref, norm_ref, pos_ref, dy_ref, y_ref, dr2_ref, e2_ref, small_ref, low_ref, act_ref, acc_ref):
    j = pl.program_id(0)
    tokens = h1_ref.shape[0]
    length = tokens // seqs
    step = 256

    @pl.when(j == 0)
    def _():
        low_ref[...] = h1_ref[...].astype(LOW)
        acc_ref[...] = h1_ref[...]

    @pl.loop(0, D // step)
    def _(n):
        lane = pl.multiple_of(n * step, step)
        gate = mm(low_ref[...], gate_ref[:, :, pl.ds(lane, step)].reshape(D, step))
        up = mm(low_ref[...], up_ref[:, :, pl.ds(lane, step)].reshape(D, step))
        cdf = 0.5 * (1.0 + lax.erf(gate * (0.5**0.5)))
        act_ref[:, pl.ds(lane, step)] = (gate * cdf * up).astype(LOW)

    @pl.loop(0, D // step)
    def _(n):
        lane = pl.multiple_of(n * step, step)
        acc_ref[:, pl.ds(lane, step)] += mm(act_ref[...], down_ref[:, :, :, pl.ds(lane, step)].reshape(D, step))

    @pl.when(j == QUARTERS - 1)
    def _():
        gain = norm_ref[2:3, :]
        small = [jnp.zeros((1, D), F32)] * 2
        for s in range(seqs):
            rows = slice(s * length, (s + 1) * length)
            listed = slice(s * most, (s + 1) * most)
            unit, _ = norm_parts(acc_ref[rows, :])
            y_ref[rows, :] = (unit * gain + norm_ref[3:4, :]).astype(LOW)
            hot = onehot(pos_ref, s, most, length).astype(F32)
            picked = jnp.dot(hot, acc_ref[rows, :], precision=EXACT, preferred_element_type=F32)
            unit_m, rstd_m = norm_parts(picked)
            dy = dy_ref[listed, :].astype(F32)
            small = [small[0] + jnp.sum(dy * unit_m, axis=0, keepdims=True), small[1] + jnp.sum(dy, axis=0, keepdims=True)]
            dr2 = norm_back(dy, unit_m, rstd_m, gain)
            dr2_ref[listed, :] = dr2
            e2_ref[listed, :] = dr2.astype(LOW)
        small_ref[...] = jnp.concatenate(small, axis=0)


def ffn_forward(h1, w_ffn, norms, pos, dy, seqs):
    tokens = h1.shape[0]
    listed = pos.shape[0]
    whole = lambda shape: pl.BlockSpec(shape, lambda j: (0,) * len(shape), pipeline_mode=pl.Buffered(1))
    return pl.pallas_call(
        functools.partial(ffn_kernel, seqs, listed // seqs),
        out_shape=(out((tokens, D), LOW), out((listed, D), F32), out((listed, D), LOW), out((2, D), F32)),
        grid=(QUARTERS,),
        in_specs=[
            whole((tokens, D)),
            pl.BlockSpec((SHARDS, None, None, ROWS, D), lambda j: (0, j, 0, 0, 0)),
            pl.BlockSpec((SHARDS, None, None, ROWS, D), lambda j: (0, j, 1, 0, 0)),
            pl.BlockSpec((SHARDS // QUARTERS, QUARTERS, None, ROWS, D), lambda j: (j, 0, 2, 0, 0)),
            whole(norms.shape),
            whole(pos.shape),
            whole(dy.shape),
        ],
        out_specs=(
            pl.BlockSpec((tokens, D), lambda j: (0, 0)),
            pl.BlockSpec((listed, D), lambda j: (0, 0)),
            pl.BlockSpec((listed, D), lambda j: (0, 0)),
            pl.BlockSpec((2, D), lambda j: (0, 0)),
        ),
        scratch_shapes=[pltpu.VMEM((tokens, D), LOW), pltpu.VMEM((tokens, D), LOW), pltpu.VMEM((tokens, D), F32)],
        compiler_params=BIG,
        cost_estimate=cost(16),
        name="ffn_forward",
    )(h1, w_ffn, w_ffn, w_ffn, norms, pos, dy)


def ffn_again_kernel(where_ref, h_ref, gate_ref, up_ref, act_ref, to_gate_ref, to_up_ref):
    step = 256

    @pl.loop(0, D // step)
    def _(n):
        lane = pl.multiple_of(n * step, step)
        rows = block(h_ref)
        gate = mm(rows, gate_ref[:, :, pl.ds(lane, step)].reshape(D, step))
        up = mm(rows, up_ref[:, :, pl.ds(lane, step)].reshape(D, step))
        value, slope = gelu_parts(gate)
        act_ref[:, pl.ds(lane, step)] = (value * up).astype(LOW)
        to_gate_ref[:, pl.ds(lane, step)] = slope * up
        to_up_ref[:, pl.ds(lane, step)] = value


def quarter_specs(which):
    specs = {
        "gate": pl.BlockSpec((SHARDS, None, None, ROWS, D), lambda g, w: (0, w[4], 0, 0, 0)),
        "up": pl.BlockSpec((SHARDS, None, None, ROWS, D), lambda g, w: (0, w[4], 1, 0, 0)),
        "down": pl.BlockSpec((SHARDS // QUARTERS, QUARTERS, None, ROWS, D), lambda g, w: (w[4], 0, 2, 0, 0)),
    }
    return [specs[name] for name in which]


def at_once(shape):
    return pl.BlockSpec(shape, lambda g, w: (0,) * len(shape))


def ffn_again(where, h_all, w_ffn):
    rows = h_all.shape[0] * h_all.shape[1]
    return pl.pallas_call(
        ffn_again_kernel,
        out_shape=(out((rows, D), LOW), out((rows, D), F32), out((rows, D), F32)),
        grid_spec=pltpu.PrefetchScalarGridSpec(
            num_scalar_prefetch=1,
            grid=(1,),
            in_specs=[at_once(h_all.shape), *quarter_specs(["gate", "up"])],
            out_specs=(at_once((rows, D)),) * 3,
        ),
        compiler_params=BIG,
        cost_estimate=cost(6),
        name="ffn_again",
    )(where, h_all, w_ffn, w_ffn)


def ffn_back_kernel(where_ref, e_ref, to_gate_ref, to_up_ref, gate_ref, up_ref, down_ref, dgate_ref, dup_ref, keep_ref, send_ref):
    listed = e_ref.shape[1]
    half = QUARTERS // 2
    for n in range(SHARDS // QUARTERS):
        lanes = slice(n * QUARTERS * ROWS, (n + 1) * QUARTERS * ROWS)
        dact = mm_nt(block(e_ref), block(down_ref, n))
        dgate_ref[:, lanes] = (dact * to_gate_ref[:, lanes]).astype(LOW)
        dup_ref[:, lanes] = (dact * to_up_ref[:, lanes]).astype(LOW)
    for n in range(2):
        shards = slice(n * SHARDS // 2, (n + 1) * SHARDS // 2)
        lanes = slice(n * D // 2, (n + 1) * D // 2)
        part = mm_nt(dgate_ref[...], block(gate_ref, shards)) + mm_nt(dup_ref[...], block(up_ref, shards))
        for r in range(half):
            keep_ref[r, :, lanes] = part[2 * r * listed : (2 * r + 1) * listed]
            send_ref[r, :, lanes] = part[(2 * r + 1) * listed : (2 * r + 2) * listed].astype(LOW)


def ffn_back(where, e_all, to_gate, to_up, w_ffn):
    count, listed, _ = e_all.shape
    rows = count * listed
    return pl.pallas_call(
        ffn_back_kernel,
        out_shape=(out((rows, D), LOW), out((rows, D), LOW), out((count // 2, listed, D), F32), out((count // 2, listed, D), LOW)),
        grid_spec=pltpu.PrefetchScalarGridSpec(
            num_scalar_prefetch=1,
            grid=(1,),
            in_specs=[at_once(e_all.shape), at_once((rows, D)), at_once((rows, D)), *quarter_specs(["gate", "up", "down"])],
            out_specs=(at_once((rows, D)), at_once((rows, D)), at_once((count // 2, listed, D)), at_once((count // 2, listed, D))),
        ),
        compiler_params=BIG,
        cost_estimate=cost(7),
        name="ffn_back",
    )(where, e_all, to_gate, to_up, w_ffn, w_ffn, w_ffn)


def weight_grad_kernel(where_ref, a_ref, b_ref, keep_ref, send_ref, full_ref):
    z, y = where_ref[0], where_ref[1]
    a = block(a_ref)
    step = 256

    @pl.loop(0, D // step)
    def _(n):
        lane = pl.multiple_of(n * step, step)
        full_ref[:, pl.ds(lane, step)] = mm_tn(a, block(b_ref, *([slice(None)] * (len(b_ref.shape) - 1)), pl.ds(lane, step)))

    for r in range(LINE):
        base = 2 * lax.rem(z + r, LINE)
        for other, ref in ((0, keep_ref), (1, send_ref)):
            start = (base + (y if other == 0 else 1 - y)) * ROWS
            ref[r] = full_ref[pl.ds(pl.multiple_of(start, 8), ROWS), :].astype(LOW)


def weight_grad(where, a, b):
    shape = (LINE, ROWS, D)
    rows = a.size // D
    return pl.pallas_call(
        weight_grad_kernel,
        out_shape=(out(shape, LOW), out(shape, LOW)),
        in_specs=[SMEM, VMEM, VMEM],
        out_specs=(VMEM, VMEM),
        scratch_shapes=[pltpu.VMEM((D, D), F32)],
        compiler_params=BIG,
        cost_estimate=cost(4),
        name="weight_grad",
    )(where, a, b)


def attention_back_kernel(seqs, most, slope_ref, dr2_ref, part_ref, came_ref, r1_ref, q_ref, qkv_ref, att_ref, w_ref, norm_ref, pos_ref, dr1_ref, rhs_ref, lhs_ref, small_ref, datt_ref, away_ref, hot_ref):
    length = qkv_ref.shape[0] // seqs
    listed = seqs * most
    dh1 = dr2_ref[...] + part_ref[...] + came_ref[...].astype(F32)
    unit, rstd = norm_parts(r1_ref[...])
    small_ref[0:1, :] = jnp.sum(dh1 * unit, axis=0, keepdims=True)
    small_ref[1:2, :] = jnp.sum(dh1, axis=0, keepdims=True)
    dr1 = norm_back(dh1, unit, rstd, norm_ref[0:1, :])
    dr1_ref[...] = dr1
    low = dr1.astype(LOW)
    rhs_ref[0:listed, 3 * D : 4 * D] = low
    rhs_ref[listed:, 3 * D : 4 * D] = jnp.zeros((seqs * length - listed, D), LOW)
    lhs_ref[0:listed, :] = att_ref[...]
    lhs_ref[listed:, :] = jnp.zeros((seqs * length - listed, D), LOW)
    for n in range(2):
        lanes = slice(n * D // 2, (n + 1) * D // 2)
        datt_ref[:, lanes] = mm_nt(low, block(w_ref, slice(n * SHARDS // 2, (n + 1) * SHARDS // 2), 3)).astype(LOW)
    first_m = lax.broadcasted_iota(jnp.int32, (most, 128), 1) < HEAD_DIM
    spots = lax.broadcasted_iota(jnp.int32, (listed, length), 1)
    away_ref[...] = jnp.abs(pos_ref[...] - spots).astype(F32)
    hot_ref[...] = (spots == pos_ref[...]).astype(LOW)

    def both(value):
        zero = jnp.zeros_like(value)
        return jnp.concatenate([jnp.where(first_m, value, zero), jnp.where(first_m, zero, value)], axis=0)

    @pl.loop(0, HEADS // 2)
    def _(t):
        lane = pl.multiple_of(t * 128, 128)
        for s in range(seqs):
            rows = slice(s * length, (s + 1) * length)
            mine = slice(s * most, (s + 1) * most)
            away = away_ref[mine, :]
            q = both(q_ref[mine, pl.ds(lane, 128)])
            da = both(datt_ref[mine, pl.ds(lane, 128)])
            k = qkv_ref[rows, pl.ds(D + lane, 128)]
            v = qkv_ref[rows, pl.ds(2 * D + lane, 128)]
            bias = jnp.concatenate([slope_ref[2 * t] * away, slope_ref[2 * t + 1] * away], axis=0)
            score = mm_nt(q, k) * SCALE - bias
            e = jnp.exp(score - jnp.max(score, axis=-1, keepdims=True))
            p = e * (1.0 / jnp.sum(e, axis=-1, keepdims=True))
            dp = mm_nt(da, v)
            ds = (p * (dp - jnp.sum(dp * p, axis=-1, keepdims=True))).astype(LOW)
            dq = mm(ds, k)
            dq = (jnp.where(first_m, dq[:most], dq[most:]) * SCALE).astype(LOW)
            rhs_ref[rows, pl.ds(lane, 128)] = mm_tn(hot_ref[mine, :], dq).astype(LOW)
            rhs_ref[rows, pl.ds(D + lane, 128)] = (mm_tn(ds, q) * SCALE).astype(LOW)
            rhs_ref[rows, pl.ds(2 * D + lane, 128)] = mm_tn(p.astype(LOW), da).astype(LOW)


def attention_back(dr2, part, came, r1_m, q_m, qkv, att_m, w_attn, norms, pos, slopes, seqs):
    tokens = qkv.shape[0]
    listed = pos.shape[0]
    return pl.pallas_call(
        functools.partial(attention_back_kernel, seqs, listed // seqs),
        out_shape=(out((listed, D), F32), out((tokens, 4 * D), LOW), out((tokens, D), LOW), out((2, D), F32)),
        in_specs=[SMEM] + [VMEM] * 10,
        out_specs=(VMEM,) * 4,
        scratch_shapes=[pltpu.VMEM((listed, D), LOW), pltpu.VMEM((listed, tokens // seqs), F32), pltpu.VMEM((listed, tokens // seqs), LOW)],
        compiler_params=BIG,
        cost_estimate=cost(18),
        name="attention_back",
    )(slopes, dr2, part, came, r1_m, q_m, qkv, att_m, w_attn, norms, pos)


def attention_grads_kernel(where_ref, x_ref, lhs_ref, rhs_ref, keep0_ref, keep1_ref, send0_ref, send1_ref, full_ref):
    z, y, mine = where_ref[0], where_ref[1], where_ref[4]
    half = ROWS // 2
    step = 256
    for rc in (1, 0):
        for rx in (0, 1):
            r = 2 * rx + rc
            j = (mine + r) if False else jnp.bitwise_xor(mine, r)
            is_out = j == 3

            def fill(a_ref):
                @pl.loop(0, D // step)
                def _(n):
                    lane = pl.multiple_of(n * step, step)
                    cols = pl.ds(pl.multiple_of(j * D + n * step, step), step)
                    full_ref[:, pl.ds(lane, step)] = mm_tn(a_ref[...], rhs_ref[:, cols])

            @pl.when(is_out)
            def _():
                fill(lhs_ref)

            @pl.when(jnp.logical_not(is_out))
            def _():
                fill(x_ref)

            refs = (keep0_ref, keep1_ref) if rc == 0 else (send0_ref, send1_ref)
            for rz in range(LINE):
                base = 2 * lax.rem(z + rz, LINE)
                for ry in (0, 1):
                    start = (base + (y if ry == 0 else 1 - y)) * ROWS
                    for part in (0, 1):
                        rows = pl.ds(pl.multiple_of(start + part * half, 8), half)
                        value = full_ref[rows, :].astype(LOW)
                        if part == 0:
                            refs[0][rx, ry, rz] = value
                        else:
                            refs[1][ry, rx, rz] = value


def attention_grads(where, x, lhs, rhs):
    shape = (2, 2, LINE, ROWS // 2, D)
    return pl.pallas_call(
        attention_grads_kernel,
        out_shape=(out(shape, LOW),) * 4,
        in_specs=[SMEM, VMEM, VMEM, VMEM],
        out_specs=(VMEM,) * 4,
        scratch_shapes=[pltpu.VMEM((D, D), F32)],
        compiler_params=BIG,
        cost_estimate=cost(10),
        name="attention_grads",
    )(where, x, lhs, rhs)


def input_grad_kernel(seqs, rhs_ref, w_ref, dr1_ref, pos_ref, out_ref):
    length = out_ref.shape[0] // seqs
    most = dr1_ref.shape[0] // seqs
    for n in range(2):
        lanes = slice(n * D // 2, (n + 1) * D // 2)
        shards = slice(n * SHARDS // 2, (n + 1) * SHARDS // 2)
        total = mm_nt(rhs_ref[:, 0:D], block(w_ref, shards, 0))
        total += mm_nt(rhs_ref[:, D : 2 * D], block(w_ref, shards, 1))
        total += mm_nt(rhs_ref[:, 2 * D : 3 * D], block(w_ref, shards, 2))
        for s in range(seqs):
            rows = slice(s * length, (s + 1) * length)
            hot = (lax.broadcasted_iota(jnp.int32, (length, most), 0) == pos_ref[s : s + 1, :]).astype(F32)
            spread = jnp.dot(hot, dr1_ref[s * most : (s + 1) * most, lanes], precision=EXACT, preferred_element_type=F32)
            out_ref[rows, lanes] = total[rows] + spread


def input_grad(rhs, w_attn, dr1, positions):
    tokens = rhs.shape[0]
    return pl.pallas_call(
        functools.partial(input_grad_kernel, positions.shape[0]),
        out_shape=out((tokens, D), F32),
        in_specs=[VMEM] * 4,
        out_specs=VMEM,
        compiler_params=BIG,
        cost_estimate=cost(8),
        name="input_grad",
    )(rhs, w_attn, dr1, positions)


def place(z, y, x, c):
    return (2 * z + y) * 4 + 2 * x + c


def grid_perm(move):
    return [
        (place(z, y, x, c), place(*move(z, y, x, c)))
        for z in range(4)
        for y in range(2)
        for x in range(2)
        for c in range(2)
    ]


MOVES = {
    "x": grid_perm(lambda z, y, x, c: (z, y, 1 - x, c)),
    "y": grid_perm(lambda z, y, x, c: (z, 1 - y, x, c)),
    "c": grid_perm(lambda z, y, x, c: (z, y, x, 1 - c)),
    1: grid_perm(lambda z, y, x, c: ((z + 1) % 4, y, x, c)),
    2: grid_perm(lambda z, y, x, c: ((z + 2) % 4, y, x, c)),
    3: grid_perm(lambda z, y, x, c: ((z + 3) % 4, y, x, c)),
    "down": [(m * 4 + q, (2 * q + m // 4) * 4 + m % 4) for m in range(8) for q in range(4)],
}


def send(value, move):
    return lax.ppermute(value, AXES, MOVES[move])


def share_dp(value):
    core = send(value, "c")
    return value, core, send(value, "x"), send(core, "x")


def line_sum(block_list, kept):
    total = kept.astype(F32)
    for r, value in block_list:
        total = total + send(value, r).astype(F32)
    return total


def reduce_quarter(keep, away):
    got = send(away, "y")
    total = keep.astype(F32) + got.astype(F32)
    return line_sum([(r, total[r].astype(LOW)) for r in (1, 2, 3)], total[0]).astype(LOW)


def reduce_attention(keep, away, first, second):
    total = keep.astype(F32) + send(away, "c").astype(F32)
    total = total[0] + send(total[1].astype(LOW), first).astype(F32)
    total = total[0] + send(total[1].astype(LOW), second).astype(F32)
    return line_sum([(r, total[r].astype(LOW)) for r in (1, 2, 3)], total[0]).astype(LOW)


def finish_kernel(rows_out, where_ref, *rest):
    held = rest[-1]
    count = len(held.shape) and held.shape[0]
    pieces, outs = rest[: QUARTERS * count], rest[QUARTERS * count : -1]
    mine = where_ref[4]
    for n, ref in enumerate(pieces):
        held[n // QUARTERS, jnp.bitwise_xor(mine, n % QUARTERS)] = ref[...].astype(F32)
    if rows_out:
        for j in range(QUARTERS):
            outs[0][j * ROWS : (j + 1) * ROWS, :] = held[0, j]
        return
    at = 0
    for ref in outs:
        for j in range(ref.shape[1] // D):
            ref[:, j * D : (j + 1) * D] = held[at // QUARTERS, at % QUARTERS]
            at += 1


def finish(where, pieces, widths, rows_out=False):
    shapes = [out((QUARTERS * ROWS, D), F32)] if rows_out else [out((ROWS, n * D), F32) for n in widths]
    return pl.pallas_call(
        functools.partial(finish_kernel, rows_out),
        out_shape=tuple(shapes),
        in_specs=[SMEM] + [VMEM] * len(pieces),
        out_specs=(VMEM,) * len(shapes),
        scratch_shapes=[pltpu.VMEM((len(pieces) // QUARTERS, QUARTERS, ROWS, D), F32)],
        compiler_params=BIG,
        cost_estimate=cost(2),
        name="finish",
    )(where, *pieces)


def spread(piece, order):
    got = {frozenset(): piece}
    for step in (*order, "c"):
        for key in list(got):
            got[key | {step}] = send(got[key], step)
    return [got[frozenset(n for n, b in zip("yxc", key) if b)] for key in KEYS]


def sum_all(value):
    for step in ("c", "x", "y"):
        value = value + send(value, step)
    return value + send(value, 1) + send(value, 2) + send(value, 3)


def on_block(hidden_in, w_qkv, w_out, w_up, w_down, gain_attn, shift_attn, gain_ffn, shift_ffn, grad_listed, positions, counts):
    seqs, length, width = hidden_in.shape
    tokens = seqs * length
    most = positions.shape[1]
    i, j = lax.axis_index("fsdp"), lax.axis_index("dp")
    where = jnp.stack([i // 2, i % 2, j // 2, j % 2, j]).astype(jnp.int32)
    ff = w_down.shape[0] * SHARDS
    attn_piece = lax.dynamic_slice_in_dim(jnp.concatenate([w_qkv, w_out], axis=1), j * D, D, axis=1)
    norms = jnp.concatenate([gain_attn, shift_attn, gain_ffn, shift_ffn, jnp.zeros((D - 4 * ROWS,), LOW)])
    attn_piece = jnp.concatenate([attn_piece, jnp.broadcast_to(norms, (EXTRA, D))], axis=0)
    line = jnp.stack([attn_piece] + [send(attn_piece, r) for r in (1, 2, 3)])
    halves = [
        spread(line[:, start : start + size], order)
        for (start, size), order in zip(HALVES, (("y", "x"), ("x", "y")))
    ]
    lines = [half[n] for n in range(len(KEYS)) for half in halves]
    ffn_piece = jnp.stack(
        [
            lax.dynamic_slice_in_dim(w_up, j * D, D, axis=1),
            lax.dynamic_slice_in_dim(w_up, ff + j * D, D, axis=1),
            lax.dynamic_slice_in_dim(w_down, j * ROWS, ROWS, axis=0),
        ]
    )
    w_ffn = lax.all_gather(ffn_piece, AXES, axis=0, tiled=False).reshape(SHARDS, QUARTERS, 3, ROWS, D)
    tails = jnp.stack([halves[1][n][:, 48, : 4 * ROWS] for n in range(2)])
    tails = jnp.where(i % 2 == 0, tails, tails[::-1])
    tails = jnp.roll(tails[:, ::-1], i // 2 + 1, axis=1)
    norms = tails.transpose(1, 0, 2).reshape(SHARDS, 4, ROWS).transpose(1, 0, 2).reshape(4, D).astype(F32)
    slopes = jnp.exp2(-8.0 * (jnp.arange(HEADS, dtype=F32) + 1.0) / HEADS)
    x = hidden_in.reshape(tokens, width)
    pos = positions.reshape(seqs * most, 1)
    live = jnp.arange(most, dtype=jnp.int32)[None, :] < counts[:, None]
    dy = jnp.where(live[:, :, None], grad_listed, jnp.zeros_like(grad_listed)).reshape(seqs * most, width)

    qkv, h1, att_m, h1_m, q_m, r1_m, w_attn = attention_forward(where, x, lines, norms, pos, slopes, seqs)
    h_all = jnp.stack(share_dp(h1_m))
    h1, h_all = lax.optimization_barrier((h1, h_all))
    layer_out, dr2, e2, small_ffn = ffn_forward(h1, w_ffn, norms, pos, dy, seqs)
    act, to_gate, to_up = ffn_again(where, h_all, w_ffn)
    e_all = jnp.stack(share_dp(e2))
    dgate, dup, keep, away = ffn_back(where, e_all, to_gate, to_up, w_ffn)
    total = keep + send(away, "c").astype(F32)
    came = send(total[1].astype(LOW), "x")
    g_down = reduce_quarter(*weight_grad(where, act, e_all))
    g_gate = reduce_quarter(*weight_grad(where, h_all, dgate))
    g_up = reduce_quarter(*weight_grad(where, h_all, dup))
    dr1, rhs, lhs, small_attn = attention_back(dr2, total[0], came, r1_m, q_m, qkv, att_m, w_attn, norms, pos, slopes, seqs)
    keep0, keep1, away0, away1 = attention_grads(where, x, lhs, rhs)
    g_attn = jnp.concatenate(
        [reduce_attention(keep0, away0, "x", "y"), reduce_attention(keep1, away1, "y", "x")], axis=0
    )
    grad_in = input_grad(rhs, w_attn, dr1, positions)
    (grad_down,) = finish(where, share_dp(send(g_down, "down")), (), rows_out=True)
    (grad_up,) = finish(where, (*share_dp(g_gate), *share_dp(g_up)), (2 * QUARTERS,))
    grad_qkv, grad_out = finish(where, share_dp(g_attn), (3, 1))
    small = sum_all(jnp.concatenate([small_attn, small_ffn]))
    small = lax.dynamic_slice_in_dim(small, i * ROWS, ROWS, axis=1)
    return (
        layer_out.reshape(seqs, length, width),
        grad_in.reshape(seqs, length, width),
        grad_qkv,
        grad_out,
        grad_up,
        grad_down,
        small[0],
        small[1],
        small[2],
        small[3],
    )


FF = 3072


def slopes():
    return jnp.exp2(-8.0 * (jnp.arange(HEADS, dtype=F32) + 1.0) / HEADS)


def pick(onehot, rows):
    if rows.dtype == LOW:
        return jnp.einsum("svj,sjd->svd", onehot.astype(LOW), rows, preferred_element_type=F32).astype(LOW)
    return jnp.einsum("svj,sjd->svd", onehot, rows, precision=lax.Precision.HIGHEST)


def gather_weights(w_qkv, w_out, w_up, w_down):
    fsdp = lax.axis_size("fsdp")
    dp = lax.axis_size("dp")
    rows, width = w_out.shape
    if rows % (8 * dp):
        return (
            lax.all_gather(w_qkv, "fsdp", axis=0, tiled=True),
            lax.all_gather(w_out, "fsdp", axis=0, tiled=True),
            lax.all_gather(w_up, "fsdp", axis=0, tiled=True),
            lax.all_gather(w_down, "fsdp", axis=0, tiled=True),
        )
    mine = lax.axis_index("dp")
    part = rows // dp
    group = w_down.shape[0] // rows
    joined = jnp.concatenate([w_qkv, w_out, w_up], axis=1)
    joined = lax.dynamic_slice_in_dim(joined, mine * part, part, axis=0)
    down = lax.dynamic_slice_in_dim(w_down, mine * part * group, part * group, axis=0)
    down = jnp.concatenate([down[k * part : (k + 1) * part] for k in range(group)], axis=1)
    full = lax.all_gather(jnp.concatenate([joined, down], axis=1), AXES, axis=0, tiled=True)
    a, b = w_qkv.shape[1], w_qkv.shape[1] + w_out.shape[1]
    c = b + w_up.shape[1]
    full_down = full[:, c:].reshape(fsdp * dp, part, group, width)
    full_down = full_down.transpose(0, 2, 1, 3).reshape(fsdp * dp * part * group, width)
    return full[:, :a], full[:, a:b], full[:, b:c], full_down


def scatter_grads(g_qkv, g_out, g_up, g_down):
    fsdp = lax.axis_size("fsdp")
    dp = lax.axis_size("dp")
    width = g_out.shape[1]
    rows = g_out.shape[0] // fsdp
    if rows % (8 * dp):
        return tuple(
            lax.psum(lax.psum_scatter(g, "fsdp", scatter_dimension=0, tiled=True), "dp")
            for g in (g_qkv, g_out, g_up, g_down)
        )
    part = rows // dp
    group = g_down.shape[0] // g_out.shape[0]
    down = g_down.reshape(fsdp * dp, group, part, width).transpose(0, 2, 1, 3)
    down = down.reshape(fsdp * rows, group * width)
    joined = jnp.concatenate([g_qkv, g_out, g_up, down], axis=1).astype(LOW)
    mine = lax.psum_scatter(joined, AXES, scatter_dimension=0, tiled=True)
    full = lax.all_gather(mine, "dp", axis=0, tiled=True).astype(F32)
    a, b = g_qkv.shape[1], g_qkv.shape[1] + width
    c = b + g_up.shape[1]
    full_down = full[:, c:].reshape(dp, part, group, width).transpose(0, 2, 1, 3)
    return full[:, :a], full[:, a:b], full[:, b:c], full_down.reshape(rows * group, width)


def on_device(hidden_in, w_qkv, w_out, w_up, w_down, gain_attn, shift_attn, gain_ffn, shift_ffn, grad_listed, positions, counts):
    seqs, length, width = hidden_in.shape
    tokens = seqs * length
    most = positions.shape[1]
    norms = jnp.stack([gain_attn, shift_attn, gain_ffn, shift_ffn])
    norms = lax.all_gather(norms, "fsdp", axis=1, tiled=True).astype(F32)
    w_qkv, w_out, w_up, w_down = gather_weights(w_qkv, w_out, w_up, w_down)
    live = jnp.arange(most, dtype=jnp.int32)[None, :] < counts[:, None]
    onehot = (positions[:, :, None] == jnp.arange(length, dtype=jnp.int32)).astype(F32)
    rows_in = hidden_in.reshape(tokens, width)
    slope = slopes()
    scale = HEAD_DIM**-0.5
    qkv = mm(rows_in, w_qkv).astype(LOW)
    split = qkv.reshape(seqs, length, 3, HEADS, HEAD_DIM)
    q, k, v = split[:, :, 0], split[:, :, 1], split[:, :, 2]
    place = jnp.arange(length, dtype=F32)
    bias = -slope[:, None, None] * jnp.abs(place[:, None] - place[None, :])
    s = jnp.einsum("sqhc,skhc->shqk", q, k, preferred_element_type=F32) * scale + bias
    p = jax.nn.softmax(s, axis=-1).astype(LOW)
    att = jnp.einsum("shqk,skhc->sqhc", p, v, preferred_element_type=F32).astype(LOW)
    att = att.reshape(tokens, width)
    r1 = rows_in.astype(F32) + mm(att, w_out)
    unit1, _ = norm_parts(r1)
    h1 = unit1 * norms[0] + norms[1]
    h1_low = h1.astype(LOW)
    u = mm(h1_low, w_up)
    act = (jax.nn.gelu(u[:, :FF], approximate=False) * u[:, FF:]).astype(LOW)
    r2 = h1 + mm(act, w_down)
    unit2, _ = norm_parts(r2)
    layer_out = (unit2 * norms[2] + norms[3]).astype(LOW).reshape(seqs, length, width)
    def listed(a):
        return pick(onehot, a.reshape(seqs, length, -1)).reshape(seqs * most, -1)

    dy = jnp.where(live[:, :, None], grad_listed, 0).astype(F32).reshape(seqs * most, width)
    unit2_m, rstd2_m = norm_parts(listed(r2))
    g_gain_ffn = jnp.sum(dy * unit2_m, axis=0)
    g_shift_ffn = jnp.sum(dy, axis=0)
    dr2 = norm_back(dy, unit2_m, rstd2_m, norms[2])
    e2 = dr2.astype(LOW)
    h1_m = listed(h1_low)
    u_m = mm(h1_m, w_up)
    gate, up = u_m[:, :FF], u_m[:, FF:]
    cdf = 0.5 * (1.0 + lax.erf(gate * (0.5**0.5)))
    pdf = jnp.exp(-0.5 * gate * gate) * ((2.0 * jnp.pi) ** -0.5)
    gelu = gate * cdf
    act_m = (gelu * up).astype(LOW)
    g_down = jnp.einsum("nf,nd->fd", act_m, e2, preferred_element_type=F32)
    dact = jnp.einsum("nd,fd->nf", e2, w_down, preferred_element_type=F32)
    du = jnp.concatenate([dact * up * (cdf + gate * pdf), dact * gelu], axis=1).astype(LOW)
    g_up = jnp.einsum("nd,nf->df", h1_m, du, preferred_element_type=F32)
    dh1 = dr2 + jnp.einsum("nf,df->nd", du, w_up, preferred_element_type=F32)
    unit1_m, rstd1_m = norm_parts(listed(r1))
    g_gain_attn = jnp.sum(dh1 * unit1_m, axis=0)
    g_shift_attn = jnp.sum(dh1, axis=0)
    dr1 = norm_back(dh1, unit1_m, rstd1_m, norms[0])
    e1 = dr1.astype(LOW)
    g_out = jnp.einsum("nd,ne->de", listed(att), e1, preferred_element_type=F32)
    datt = jnp.einsum("ne,de->nd", e1, w_out, preferred_element_type=F32).astype(LOW)
    datt = datt.reshape(seqs, most, HEADS, HEAD_DIM)
    q_m = listed(qkv[:, :width]).reshape(seqs, most, HEADS, HEAD_DIM)
    away = jnp.abs(positions[:, :, None].astype(F32) - place[None, None, :])
    s_m = jnp.einsum("sqhc,skhc->shqk", q_m, k, preferred_element_type=F32) * scale
    p_m = jax.nn.softmax(s_m - slope[None, :, None, None] * away[:, None], axis=-1)
    dv = jnp.einsum("shqk,sqhc->skhc", p_m.astype(LOW), datt, preferred_element_type=F32)
    dp = jnp.einsum("sqhc,skhc->shqk", datt, v, preferred_element_type=F32)
    ds = (p_m * (dp - jnp.sum(dp * p_m, axis=-1, keepdims=True))).astype(LOW)
    dq_m = (jnp.einsum("shqk,skhc->sqhc", ds, k, preferred_element_type=F32) * scale).astype(LOW)
    dk = (jnp.einsum("shqk,sqhc->skhc", ds, q_m, preferred_element_type=F32) * scale).astype(LOW)
    put = (onehot * live[:, :, None]).astype(LOW)
    dq = jnp.einsum("svj,svd->sjd", put, dq_m.reshape(seqs, most, width), preferred_element_type=F32)
    dqkv = jnp.concatenate(
        [dq.astype(LOW).reshape(tokens, width), dk.reshape(tokens, width), dv.astype(LOW).reshape(tokens, width)], axis=1
    )
    g_qkv = jnp.einsum("nd,ne->de", rows_in, dqkv, preferred_element_type=F32)
    dr1_all = jnp.einsum("svj,svd->sjd", onehot * live[:, :, None], dr1.reshape(seqs, most, width), precision=lax.Precision.HIGHEST)
    grad_in = dr1_all.reshape(tokens, width) + jnp.einsum("ne,de->nd", dqkv, w_qkv, preferred_element_type=F32)
    owned = scatter_grads(g_qkv, g_out, g_up, g_down)
    small = lax.psum(jnp.stack([g_gain_attn, g_shift_attn, g_gain_ffn, g_shift_ffn]), AXES)
    share = width // lax.axis_size("fsdp")
    small = lax.dynamic_slice_in_dim(small, lax.axis_index("fsdp") * share, share, axis=1)
    return (
        layer_out,
        grad_in.reshape(seqs, length, width),
        *owned,
        small[0],
        small[1],
        small[2],
        small[3],
    )


def solution(mesh):
    rows3 = P(("fsdp", "dp"), None, None)
    rows2 = P("fsdp", None)
    rows1 = P("fsdp")
    shape = dict(mesh.shape)
    step = on_block if shape == {"fsdp": SHARDS, "dp": QUARTERS} else on_device
    return jax.shard_map(
        step,
        mesh=mesh,
        in_specs=(rows3, rows2, rows2, rows2, rows2, rows1, rows1, rows1, rows1, rows3, P(("fsdp", "dp"), None), P(("fsdp", "dp"))),
        out_specs=(rows3, rows3, rows2, rows2, rows2, rows2, rows1, rows1, rows1, rows1),
        check_vma=False,
    )
```

```python
import functools

import jax
import jax.numpy as jnp
from jax import lax
from jax.experimental import pallas as pl
from jax.experimental.pallas import tpu as pltpu
from jax.sharding import PartitionSpec as P

HEADS = 12
HEAD_DIM = 64
EPS = 1e-12
F32 = jnp.float32
LOW = jnp.bfloat16
AXES = ("fsdp", "dp")
D = 768
ROWS = 96
LINE = 4
SHARDS = D // ROWS
QUARTERS = 4
EXACT = lax.Precision.HIGHEST
SCALE = HEAD_DIM**-0.5
VMEM = pl.BlockSpec(memory_space=pltpu.VMEM)
SMEM = pl.BlockSpec(memory_space=pltpu.SMEM)
BIG = pltpu.CompilerParams(vmem_limit_bytes=60 * 1024 * 1024)


def out(shape, dtype):
    return jax.ShapeDtypeStruct(shape, dtype)


def cost(us):
    return pl.CostEstimate(flops=0, bytes_accessed=int(us * 3.0e6), transcendentals=0)


def mm(a, b):
    return jnp.dot(a, b, preferred_element_type=F32)


def mm_nt(a, b):
    return lax.dot_general(a, b, (((1,), (1,)), ((), ())), preferred_element_type=F32)


def mm_tn(a, b):
    return lax.dot_general(a, b, (((0,), (0,)), ((), ())), preferred_element_type=F32)


def norm_parts(value):
    center = value - jnp.mean(value, axis=-1, keepdims=True)
    rstd = lax.rsqrt(jnp.mean(center * center, axis=-1, keepdims=True) + EPS)
    return center * rstd, rstd


def norm_back(grad, unit, rstd, gain):
    scaled = grad * gain
    return rstd * (
        scaled
        - jnp.mean(scaled, axis=-1, keepdims=True)
        - unit * jnp.mean(scaled * unit, axis=-1, keepdims=True)
    )


def onehot(pos_ref, seq, most, length):
    spots = lax.broadcasted_iota(jnp.int32, (most, length), 1)
    return spots == pos_ref[pl.ds(seq * most, most), :]


def gelu_parts(gate):
    cdf = 0.5 * (1.0 + lax.erf(gate * (0.5**0.5)))
    pdf = jnp.exp(-0.5 * gate * gate) * ((2.0 * jnp.pi) ** -0.5)
    return gate * cdf, cdf + gate * pdf


def slope_of(head):
    return 2.0 ** (-8.0 * (head + 1.0) / HEADS)


def block(ref, *index):
    value = ref[index] if index else ref[...]
    return value.reshape(-1, value.shape[-1])


EXTRA = 8
HALVES = ((0, 48), (48, 56))
KEYS = [(ry, rx, rc) for rc in (0, 1) for rx in (0, 1) for ry in (0, 1)]


def attention_kernel(seqs, most, where_ref, slope_ref, x_ref, norm_ref, pos_ref, *rest):
    lines, rest = rest[:16], rest[16:]
    qkv_ref, h1_ref, att_m_ref, h1_m_ref, q_m_ref, r1_m_ref, w_ref, att_ref, r1_ref, sem = rest
    z, y, c_x = where_ref[0], where_ref[1], where_ref[4]
    copies = []
    for n, (ry, rx, rc) in enumerate(KEYS):
        j = jnp.bitwise_xor(c_x, 2 * rx + rc)
        for r in range(LINE):
            shard = 2 * lax.rem(z + LINE - r, LINE) + jnp.bitwise_xor(y, ry)
            for half, (start, size) in enumerate(HALVES):
                size = min(size, ROWS - start)
                copies.append(
                    pltpu.make_async_copy(
                        lines[2 * n + half].at[r, pl.ds(0, size)], w_ref.at[shard, j, pl.ds(start, size)], sem
                    )
                )
    for copy in copies:
        copy.start()
    for copy in copies:
        copy.wait()
    length = x_ref.shape[0] // seqs
    step = 256

    @pl.loop(0, 3 * D // step)
    def _(n):
        j = n // (D // step)
        lane = pl.multiple_of((n - j * (D // step)) * step, step)
        w = w_ref[:, j, :, pl.ds(lane, step)].reshape(D, step)
        qkv_ref[:, pl.ds(pl.multiple_of(n * step, step), step)] = mm(x_ref[...], w).astype(LOW)

    first = lax.broadcasted_iota(jnp.int32, (length, 128), 1) < HEAD_DIM
    row = lax.broadcasted_iota(jnp.int32, (length, length), 0)
    col = lax.broadcasted_iota(jnp.int32, (length, length), 1)
    away = jnp.abs(row - col).astype(F32)

    @pl.loop(0, HEADS // 2)
    def _(t):
        lane = pl.multiple_of(t * 128, 128)
        bias = jnp.concatenate([slope_ref[2 * t] * away, slope_ref[2 * t + 1] * away], axis=0)
        for s in range(seqs):
            rows = slice(s * length, (s + 1) * length)
            q = qkv_ref[rows, pl.ds(lane, 128)]
            k = qkv_ref[rows, pl.ds(D + lane, 128)]
            v = qkv_ref[rows, pl.ds(2 * D + lane, 128)]
            zero = jnp.zeros_like(q)
            both = jnp.concatenate([jnp.where(first, q, zero), jnp.where(first, zero, q)], axis=0)
            score = mm_nt(both, k) * SCALE - bias
            e = jnp.exp(score - jnp.max(score, axis=-1, keepdims=True))
            p = (e * (1.0 / jnp.sum(e, axis=-1, keepdims=True))).astype(LOW)
            mixed = mm(p, v)
            att_ref[rows, pl.ds(lane, 128)] = jnp.where(first, mixed[:length], mixed[length:]).astype(LOW)

    @pl.loop(0, D // step)
    def _(n):
        lane = pl.multiple_of(n * step, step)
        w = w_ref[:, 3, :, pl.ds(lane, step)].reshape(D, step)
        r1_ref[:, pl.ds(lane, step)] = x_ref[:, pl.ds(lane, step)].astype(F32) + mm(att_ref[...], w)

    for s in range(seqs):
        rows = slice(s * length, (s + 1) * length)
        listed = slice(s * most, (s + 1) * most)
        unit, _ = norm_parts(r1_ref[rows, :])
        h1 = unit * norm_ref[0:1, :] + norm_ref[1:2, :]
        h1_ref[rows, :] = h1
        hot = onehot(pos_ref, s, most, length)
        hot_low = hot.astype(LOW)
        r1_m_ref[listed, :] = jnp.dot(hot.astype(F32), r1_ref[rows, :], precision=EXACT, preferred_element_type=F32)
        h1_m_ref[listed, :] = mm(hot_low, h1.astype(LOW)).astype(LOW)
        att_m_ref[listed, :] = mm(hot_low, att_ref[rows, :]).astype(LOW)
        q_m_ref[listed, :] = mm(hot_low, qkv_ref[rows, 0:D]).astype(LOW)


def attention_forward(where, x, lines, norms, pos, slopes, seqs):
    tokens = x.shape[0]
    listed = pos.shape[0]
    return pl.pallas_call(
        functools.partial(attention_kernel, seqs, listed // seqs),
        out_shape=(
            out((tokens, 3 * D), LOW),
            out((tokens, D), F32),
            out((listed, D), LOW),
            out((listed, D), LOW),
            out((listed, D), LOW),
            out((listed, D), F32),
            out((SHARDS, QUARTERS, ROWS, D), LOW),
        ),
        in_specs=[SMEM, SMEM, VMEM, VMEM, VMEM] + [pl.BlockSpec(memory_space=pl.ANY)] * 16,
        out_specs=(VMEM,) * 7,
        scratch_shapes=[pltpu.VMEM((tokens, D), LOW), pltpu.VMEM((tokens, D), F32), pltpu.SemaphoreType.DMA],
        compiler_params=BIG,
        cost_estimate=cost(20),
        name="attention_forward",
    )(where, slopes, x, norms, pos, *lines)


def ffn_kernel(seqs, most, h1_ref, gate_ref, up_ref, down_ref, norm_ref, pos_ref, dy_ref, y_ref, dr2_ref, e2_ref, small_ref, low_ref, act_ref, acc_ref):
    j = pl.program_id(0)
    tokens = h1_ref.shape[0]
    length = tokens // seqs
    step = 256

    @pl.when(j == 0)
    def _():
        low_ref[...] = h1_ref[...].astype(LOW)
        acc_ref[...] = h1_ref[...]

    @pl.loop(0, D // step)
    def _(n):
        lane = pl.multiple_of(n * step, step)
        gate = mm(low_ref[...], gate_ref[:, :, pl.ds(lane, step)].reshape(D, step))
        up = mm(low_ref[...], up_ref[:, :, pl.ds(lane, step)].reshape(D, step))
        cdf = 0.5 * (1.0 + lax.erf(gate * (0.5**0.5)))
        act_ref[:, pl.ds(lane, step)] = (gate * cdf * up).astype(LOW)

    @pl.loop(0, D // step)
    def _(n):
        lane = pl.multiple_of(n * step, step)
        acc_ref[:, pl.ds(lane, step)] += mm(act_ref[...], down_ref[:, :, :, pl.ds(lane, step)].reshape(D, step))

    @pl.when(j == QUARTERS - 1)
    def _():
        gain = norm_ref[2:3, :]
        small = [jnp.zeros((1, D), F32)] * 2
        for s in range(seqs):
            rows = slice(s * length, (s + 1) * length)
            listed = slice(s * most, (s + 1) * most)
            unit, _ = norm_parts(acc_ref[rows, :])
            y_ref[rows, :] = (unit * gain + norm_ref[3:4, :]).astype(LOW)
            hot = onehot(pos_ref, s, most, length).astype(F32)
            picked = jnp.dot(hot, acc_ref[rows, :], precision=EXACT, preferred_element_type=F32)
            unit_m, rstd_m = norm_parts(picked)
            dy = dy_ref[listed, :].astype(F32)
            small = [small[0] + jnp.sum(dy * unit_m, axis=0, keepdims=True), small[1] + jnp.sum(dy, axis=0, keepdims=True)]
            dr2 = norm_back(dy, unit_m, rstd_m, gain)
            dr2_ref[listed, :] = dr2
            e2_ref[listed, :] = dr2.astype(LOW)
        small_ref[...] = jnp.concatenate(small, axis=0)


def ffn_forward(h1, w_ffn, norms, pos, dy, seqs):
    tokens = h1.shape[0]
    listed = pos.shape[0]
    whole = lambda shape: pl.BlockSpec(shape, lambda j: (0,) * len(shape), pipeline_mode=pl.Buffered(1))
    return pl.pallas_call(
        functools.partial(ffn_kernel, seqs, listed // seqs),
        out_shape=(out((tokens, D), LOW), out((listed, D), F32), out((listed, D), LOW), out((2, D), F32)),
        grid=(QUARTERS,),
        in_specs=[
            whole((tokens, D)),
            pl.BlockSpec((SHARDS, None, None, ROWS, D), lambda j: (0, j, 0, 0, 0)),
            pl.BlockSpec((SHARDS, None, None, ROWS, D), lambda j: (0, j, 1, 0, 0)),
            pl.BlockSpec((SHARDS // QUARTERS, QUARTERS, None, ROWS, D), lambda j: (j, 0, 2, 0, 0)),
            whole(norms.shape),
            whole(pos.shape),
            whole(dy.shape),
        ],
        out_specs=(
            pl.BlockSpec((tokens, D), lambda j: (0, 0)),
            pl.BlockSpec((listed, D), lambda j: (0, 0)),
            pl.BlockSpec((listed, D), lambda j: (0, 0)),
            pl.BlockSpec((2, D), lambda j: (0, 0)),
        ),
        scratch_shapes=[pltpu.VMEM((tokens, D), LOW), pltpu.VMEM((tokens, D), LOW), pltpu.VMEM((tokens, D), F32)],
        compiler_params=BIG,
        cost_estimate=cost(16),
        name="ffn_forward",
    )(h1, w_ffn, w_ffn, w_ffn, norms, pos, dy)


def ffn_again_kernel(where_ref, h_ref, gate_ref, up_ref, act_ref, to_gate_ref, to_up_ref):
    step = 256

    @pl.loop(0, D // step)
    def _(n):
        lane = pl.multiple_of(n * step, step)
        rows = block(h_ref)
        gate = mm(rows, gate_ref[:, :, pl.ds(lane, step)].reshape(D, step))
        up = mm(rows, up_ref[:, :, pl.ds(lane, step)].reshape(D, step))
        value, slope = gelu_parts(gate)
        act_ref[:, pl.ds(lane, step)] = (value * up).astype(LOW)
        to_gate_ref[:, pl.ds(lane, step)] = slope * up
        to_up_ref[:, pl.ds(lane, step)] = value


def quarter_specs(which):
    specs = {
        "gate": pl.BlockSpec((SHARDS, None, None, ROWS, D), lambda g, w: (0, w[4], 0, 0, 0)),
        "up": pl.BlockSpec((SHARDS, None, None, ROWS, D), lambda g, w: (0, w[4], 1, 0, 0)),
        "down": pl.BlockSpec((SHARDS // QUARTERS, QUARTERS, None, ROWS, D), lambda g, w: (w[4], 0, 2, 0, 0)),
    }
    return [specs[name] for name in which]


def at_once(shape):
    return pl.BlockSpec(shape, lambda g, w: (0,) * len(shape))


def ffn_again(where, h_all, w_ffn):
    rows = h_all.shape[0] * h_all.shape[1]
    return pl.pallas_call(
        ffn_again_kernel,
        out_shape=(out((rows, D), LOW), out((rows, D), F32), out((rows, D), F32)),
        grid_spec=pltpu.PrefetchScalarGridSpec(
            num_scalar_prefetch=1,
            grid=(1,),
            in_specs=[at_once(h_all.shape), *quarter_specs(["gate", "up"])],
            out_specs=(at_once((rows, D)),) * 3,
        ),
        compiler_params=BIG,
        cost_estimate=cost(6),
        name="ffn_again",
    )(where, h_all, w_ffn, w_ffn)


def ffn_back_kernel(where_ref, e_ref, to_gate_ref, to_up_ref, gate_ref, up_ref, down_ref, dgate_ref, dup_ref, keep_ref, send_ref):
    listed = e_ref.shape[1]
    half = QUARTERS // 2
    for n in range(SHARDS // QUARTERS):
        lanes = slice(n * QUARTERS * ROWS, (n + 1) * QUARTERS * ROWS)
        dact = mm_nt(block(e_ref), block(down_ref, n))
        dgate_ref[:, lanes] = (dact * to_gate_ref[:, lanes]).astype(LOW)
        dup_ref[:, lanes] = (dact * to_up_ref[:, lanes]).astype(LOW)
    for n in range(2):
        shards = slice(n * SHARDS // 2, (n + 1) * SHARDS // 2)
        lanes = slice(n * D // 2, (n + 1) * D // 2)
        part = mm_nt(dgate_ref[...], block(gate_ref, shards)) + mm_nt(dup_ref[...], block(up_ref, shards))
        for r in range(half):
            keep_ref[r, :, lanes] = part[2 * r * listed : (2 * r + 1) * listed]
            send_ref[r, :, lanes] = part[(2 * r + 1) * listed : (2 * r + 2) * listed].astype(LOW)


def ffn_back(where, e_all, to_gate, to_up, w_ffn):
    count, listed, _ = e_all.shape
    rows = count * listed
    return pl.pallas_call(
        ffn_back_kernel,
        out_shape=(out((rows, D), LOW), out((rows, D), LOW), out((count // 2, listed, D), F32), out((count // 2, listed, D), LOW)),
        grid_spec=pltpu.PrefetchScalarGridSpec(
            num_scalar_prefetch=1,
            grid=(1,),
            in_specs=[at_once(e_all.shape), at_once((rows, D)), at_once((rows, D)), *quarter_specs(["gate", "up", "down"])],
            out_specs=(at_once((rows, D)), at_once((rows, D)), at_once((count // 2, listed, D)), at_once((count // 2, listed, D))),
        ),
        compiler_params=BIG,
        cost_estimate=cost(7),
        name="ffn_back",
    )(where, e_all, to_gate, to_up, w_ffn, w_ffn, w_ffn)


def weight_grad_kernel(where_ref, a_ref, b_ref, keep_ref, send_ref, full_ref):
    z, y = where_ref[0], where_ref[1]
    b = block(b_ref)
    step = 256

    @pl.loop(0, D // step)
    def _(n):
        lane = pl.multiple_of(n * step, step)
        a = block(a_ref, *([slice(None)] * (len(a_ref.shape) - 1)), pl.ds(lane, step))
        full_ref[pl.ds(lane, step), :] = mm_tn(a, b)

    for r in range(LINE):
        base = 2 * lax.rem(z + r, LINE)
        for other, ref in ((0, keep_ref), (1, send_ref)):
            start = (base + (y if other == 0 else 1 - y)) * ROWS
            ref[r] = full_ref[pl.ds(pl.multiple_of(start, 8), ROWS), :].astype(LOW)


def weight_grad(where, a, b):
    shape = (LINE, ROWS, D)
    rows = a.size // D
    return pl.pallas_call(
        weight_grad_kernel,
        out_shape=(out(shape, LOW), out(shape, LOW)),
        in_specs=[SMEM, VMEM, VMEM],
        out_specs=(VMEM, VMEM),
        scratch_shapes=[pltpu.VMEM((D, D), F32)],
        compiler_params=BIG,
        cost_estimate=cost(4),
        name="weight_grad",
    )(where, a, b)


def norm_back_kernel(dr2_ref, part_ref, came_ref, r1_ref, w_ref, norm_ref, dr1_ref, low_ref, datt_ref, small_ref):
    dh1 = dr2_ref[...] + part_ref[...] + came_ref[...].astype(F32)
    unit, rstd = norm_parts(r1_ref[...])
    small_ref[0:1, :] = jnp.sum(dh1 * unit, axis=0, keepdims=True)
    small_ref[1:2, :] = jnp.sum(dh1, axis=0, keepdims=True)
    dr1 = norm_back(dh1, unit, rstd, norm_ref[0:1, :])
    dr1_ref[...] = dr1
    low = dr1.astype(LOW)
    low_ref[...] = low
    for n in range(2):
        lanes = slice(n * D // 2, (n + 1) * D // 2)
        datt_ref[:, lanes] = mm_nt(low, block(w_ref, slice(n * SHARDS // 2, (n + 1) * SHARDS // 2))).astype(LOW)


def norm_back_call(dr2, part, came, r1_m, w_attn, norms):
    listed = dr2.shape[0]
    same = lambda shape: pl.BlockSpec(shape, lambda g: (0,) * len(shape))
    rows = same((listed, D))
    return pl.pallas_call(
        norm_back_kernel,
        out_shape=(out((listed, D), F32), out((listed, D), LOW), out((listed, D), LOW), out((2, D), F32)),
        grid=(1,),
        in_specs=[rows, rows, rows, rows, pl.BlockSpec((SHARDS, None, ROWS, D), lambda g: (0, 3, 0, 0)), same((4, D))],
        out_specs=(rows, rows, rows, same((2, D))),
        compiler_params=BIG,
        cost_estimate=cost(4),
        name="norm_back",
    )(dr2, part, came, r1_m, w_attn, norms)


def attention_back_kernel(seqs, most, slope_ref, datt_ref, q_ref, qkv_ref, pos_ref, rhs_ref, away_ref, hot_ref):
    length = qkv_ref.shape[0] // seqs
    listed = seqs * most
    first_m = lax.broadcasted_iota(jnp.int32, (most, 128), 1) < HEAD_DIM
    spots = lax.broadcasted_iota(jnp.int32, (listed, length), 1)
    away_ref[...] = jnp.abs(pos_ref[...] - spots).astype(F32)
    hot_ref[...] = (spots == pos_ref[...]).astype(LOW)

    def both(value):
        zero = jnp.zeros_like(value)
        return jnp.concatenate([jnp.where(first_m, value, zero), jnp.where(first_m, zero, value)], axis=0)

    @pl.loop(0, HEADS // 2)
    def _(t):
        lane = pl.multiple_of(t * 128, 128)
        for s in range(seqs):
            rows = slice(s * length, (s + 1) * length)
            mine = slice(s * most, (s + 1) * most)
            away = away_ref[mine, :]
            q = both(q_ref[mine, pl.ds(lane, 128)])
            da = both(datt_ref[mine, pl.ds(lane, 128)])
            k = qkv_ref[rows, pl.ds(D + lane, 128)]
            v = qkv_ref[rows, pl.ds(2 * D + lane, 128)]
            bias = jnp.concatenate([slope_ref[2 * t] * away, slope_ref[2 * t + 1] * away], axis=0)
            score = mm_nt(q, k) * SCALE - bias
            e = jnp.exp(score - jnp.max(score, axis=-1, keepdims=True))
            p = e * (1.0 / jnp.sum(e, axis=-1, keepdims=True))
            dp = mm_nt(da, v)
            ds = (p * (dp - jnp.sum(dp * p, axis=-1, keepdims=True))).astype(LOW)
            dq = mm(ds, k)
            dq = (jnp.where(first_m, dq[:most], dq[most:]) * SCALE).astype(LOW)
            rhs_ref[rows, pl.ds(lane, 128)] = mm_tn(hot_ref[mine, :], dq).astype(LOW)
            rhs_ref[rows, pl.ds(D + lane, 128)] = (mm_tn(ds, q) * SCALE).astype(LOW)
            rhs_ref[rows, pl.ds(2 * D + lane, 128)] = mm_tn(p.astype(LOW), da).astype(LOW)


def attention_back(datt, q_m, qkv, pos, slopes, seqs):
    tokens = qkv.shape[0]
    listed = pos.shape[0]
    return pl.pallas_call(
        functools.partial(attention_back_kernel, seqs, listed // seqs),
        out_shape=out((tokens, 3 * D), LOW),
        in_specs=[SMEM] + [VMEM] * 4,
        out_specs=VMEM,
        scratch_shapes=[pltpu.VMEM((listed, tokens // seqs), F32), pltpu.VMEM((listed, tokens // seqs), LOW)],
        compiler_params=BIG,
        cost_estimate=cost(15),
        name="attention_back",
    )(slopes, datt, q_m, qkv, pos)


def attention_grads_kernel(rc, where_ref, flip_ref, rhs_ref, att_ref, low_ref, cut_ref, full_ref):
    z, y, mine = where_ref[0], where_ref[1], where_ref[4]
    half = ROWS // 2
    step = 256
    for rx in (0, 1):
        j = jnp.bitwise_xor(mine, 2 * rx + rc)

        @pl.when(j == 3)
        def _():
            for n in range(D // step):
                rows = slice(n * step, (n + 1) * step)
                full_ref[rows, :] = mm_tn(att_ref[:, rows], low_ref[...])

        @pl.when(j != 3)
        def _():
            @pl.loop(0, D // step)
            def _(n):
                lane = pl.multiple_of(n * step, step)
                cols = pl.ds(pl.multiple_of(j * D + n * step, step), step)
                full_ref[:, pl.ds(lane, step)] = mm(flip_ref[...], rhs_ref[:, cols])

        for rz in range(LINE):
            base = 2 * lax.rem(z + rz, LINE)
            for ry in (0, 1):
                start = (base + (y if ry == 0 else 1 - y)) * ROWS
                for part in (0, 1):
                    rows = pl.ds(pl.multiple_of(start + part * half, 8), half)
                    value = full_ref[rows, :].astype(LOW)
                    if part == 0:
                        cut_ref[0, rx, ry, rz] = value
                    else:
                        cut_ref[1, ry, rx, rz] = value


def attention_grads(where, rc, x_flip, rhs, att_m, low):
    return pl.pallas_call(
        functools.partial(attention_grads_kernel, rc),
        out_shape=out((2, 2, 2, LINE, ROWS // 2, D), LOW),
        in_specs=[SMEM] + [VMEM] * 4,
        out_specs=VMEM,
        scratch_shapes=[pltpu.VMEM((D, D), F32)],
        compiler_params=BIG,
        cost_estimate=cost(5),
        name="attention_grads",
    )(where, x_flip, rhs, att_m, low)


def input_grad_kernel(seqs, rhs_ref, w_ref, dr1_ref, pos_ref, out_ref):
    length = out_ref.shape[0] // seqs
    most = dr1_ref.shape[0] // seqs
    for n in range(2):
        lanes = slice(n * D // 2, (n + 1) * D // 2)
        shards = slice(n * SHARDS // 2, (n + 1) * SHARDS // 2)
        total = mm_nt(rhs_ref[:, 0:D], block(w_ref, shards, 0))
        total += mm_nt(rhs_ref[:, D : 2 * D], block(w_ref, shards, 1))
        total += mm_nt(rhs_ref[:, 2 * D : 3 * D], block(w_ref, shards, 2))
        for s in range(seqs):
            rows = slice(s * length, (s + 1) * length)
            hot = (lax.broadcasted_iota(jnp.int32, (length, most), 0) == pos_ref[s : s + 1, :]).astype(F32)
            spread = jnp.dot(hot, dr1_ref[s * most : (s + 1) * most, lanes], precision=EXACT, preferred_element_type=F32)
            out_ref[rows, lanes] = total[rows] + spread


def input_grad(rhs, w_attn, dr1, positions):
    tokens = rhs.shape[0]
    return pl.pallas_call(
        functools.partial(input_grad_kernel, positions.shape[0]),
        out_shape=out((tokens, D), F32),
        in_specs=[VMEM] * 4,
        out_specs=VMEM,
        compiler_params=BIG,
        cost_estimate=cost(8),
        name="input_grad",
    )(rhs, w_attn, dr1, positions)


def place(z, y, x, c):
    return (2 * z + y) * 4 + 2 * x + c


def grid_perm(move):
    return [
        (place(z, y, x, c), place(*move(z, y, x, c)))
        for z in range(4)
        for y in range(2)
        for x in range(2)
        for c in range(2)
    ]


MOVES = {
    "x": grid_perm(lambda z, y, x, c: (z, y, 1 - x, c)),
    "y": grid_perm(lambda z, y, x, c: (z, 1 - y, x, c)),
    "c": grid_perm(lambda z, y, x, c: (z, y, x, 1 - c)),
    1: grid_perm(lambda z, y, x, c: ((z + 1) % 4, y, x, c)),
    2: grid_perm(lambda z, y, x, c: ((z + 2) % 4, y, x, c)),
    3: grid_perm(lambda z, y, x, c: ((z + 3) % 4, y, x, c)),
    "down": [(m * 4 + q, (2 * q + m // 4) * 4 + m % 4) for m in range(8) for q in range(4)],
}


def send(value, move):
    return lax.ppermute(value, AXES, MOVES[move])


def share_dp(value):
    other = send(value, "x")
    return value, send(value, "c"), other, send(other, "c")


def after(value, *earlier):
    return lax.optimization_barrier((value, *earlier))[0]


def add(kept, got):
    return kept.astype(F32) + got.astype(F32)


def line_send(total):
    return [send(total[r].astype(LOW), r) for r in (1, 2, 3)]


def line_add(total, got):
    return (total[0] + got[0].astype(F32) + got[1].astype(F32) + got[2].astype(F32)).astype(LOW)


def finish_ffn_kernel(where_ref, *rest):
    pieces, (down_ref, up_ref) = rest[:QUARTERS], rest[QUARTERS:]
    mine = where_ref[4]
    for n, ref in enumerate(pieces):
        j = jnp.bitwise_xor(mine, n)
        down_ref[pl.ds(pl.multiple_of(j * ROWS, 8), ROWS), :] = ref[0].astype(F32)
        for half in (0, 1):
            up_ref[:, pl.ds(pl.multiple_of((half * QUARTERS + j) * D, D), D)] = ref[1 + half].astype(F32)


def finish_attention_kernel(where_ref, *rest):
    pieces, (qkv_ref, out_ref, held_ref) = rest[:QUARTERS], rest[QUARTERS:]
    mine = where_ref[4]
    for n, ref in enumerate(pieces):
        held_ref[jnp.bitwise_xor(mine, n)] = ref[...].astype(F32)
    for j in range(3):
        qkv_ref[:, j * D : (j + 1) * D] = held_ref[j]
    out_ref[...] = held_ref[3]


def finish_ffn(where, pieces):
    return pl.pallas_call(
        finish_ffn_kernel,
        out_shape=(out((QUARTERS * ROWS, D), F32), out((ROWS, 2 * QUARTERS * D), F32)),
        in_specs=[SMEM] + [VMEM] * QUARTERS,
        out_specs=(VMEM, VMEM),
        compiler_params=BIG,
        cost_estimate=cost(4),
        name="finish_ffn",
    )(where, *pieces)


def finish_attention(where, pieces):
    return pl.pallas_call(
        finish_attention_kernel,
        out_shape=(out((ROWS, 3 * D), F32), out((ROWS, D), F32)),
        in_specs=[SMEM] + [VMEM] * QUARTERS,
        out_specs=(VMEM, VMEM),
        scratch_shapes=[pltpu.VMEM((QUARTERS, ROWS, D), F32)],
        compiler_params=BIG,
        cost_estimate=cost(2),
        name="finish_attention",
    )(where, *pieces)


def spread(piece, order):
    got = {frozenset(): piece}
    for step in (*order, "c"):
        for key in list(got):
            got[key | {step}] = send(got[key], step)
    return [got[frozenset(n for n, b in zip("yxc", key) if b)] for key in KEYS]


def on_block(hidden_in, w_qkv, w_out, w_up, w_down, gain_attn, shift_attn, gain_ffn, shift_ffn, grad_listed, positions, counts):
    seqs, length, width = hidden_in.shape
    tokens = seqs * length
    most = positions.shape[1]
    i, j = lax.axis_index("fsdp"), lax.axis_index("dp")
    where = jnp.stack([i // 2, i % 2, j // 2, j % 2, j]).astype(jnp.int32)
    ff = w_down.shape[0] * SHARDS
    attn_piece = lax.dynamic_slice_in_dim(jnp.concatenate([w_qkv, w_out], axis=1), j * D, D, axis=1)
    norms = jnp.concatenate([gain_attn, shift_attn, gain_ffn, shift_ffn, jnp.zeros((D - 4 * ROWS,), LOW)])
    attn_piece = jnp.concatenate([attn_piece, jnp.broadcast_to(norms, (EXTRA, D))], axis=0)
    line = jnp.stack([attn_piece] + [send(attn_piece, r) for r in (1, 2, 3)])
    x = hidden_in.reshape(tokens, width)
    line, x_flip = lax.optimization_barrier((line, x.T))
    halves = [
        spread(line[:, start : start + size], order)
        for (start, size), order in zip(HALVES, (("y", "x"), ("x", "y")))
    ]
    lines = [half[n] for n in range(len(KEYS)) for half in halves]
    ffn_piece = jnp.stack(
        [
            lax.dynamic_slice_in_dim(w_up, j * D, D, axis=1),
            lax.dynamic_slice_in_dim(w_up, ff + j * D, D, axis=1),
            lax.dynamic_slice_in_dim(w_down, j * ROWS, ROWS, axis=0),
        ]
    )
    w_ffn = lax.all_gather(ffn_piece, AXES, axis=0, tiled=False).reshape(SHARDS, QUARTERS, 3, ROWS, D)
    tails = jnp.stack([halves[1][n][:, 48, : 4 * ROWS] for n in range(2)])
    tails = jnp.where(i % 2 == 0, tails, tails[::-1])
    tails = jnp.roll(tails[:, ::-1], i // 2 + 1, axis=1)
    norms = tails.transpose(1, 0, 2).reshape(SHARDS, 4, ROWS).transpose(1, 0, 2).reshape(4, D).astype(F32)
    slopes = jnp.exp2(-8.0 * (jnp.arange(HEADS, dtype=F32) + 1.0) / HEADS)
    pos = positions.reshape(seqs * most, 1)
    live = jnp.arange(most, dtype=jnp.int32)[None, :] < counts[:, None]
    dy = jnp.where(live[:, :, None], grad_listed, jnp.zeros_like(grad_listed)).reshape(seqs * most, width)

    qkv, h1, att_m, h1_m, q_m, r1_m, w_attn = attention_forward(where, x, lines, norms, pos, slopes, seqs)
    h_all = jnp.stack(share_dp(h1_m))
    h1, h_all = lax.optimization_barrier((h1, h_all))
    layer_out, dr2, e2, small_ffn = ffn_forward(h1, w_ffn, norms, pos, dy, seqs)
    act, to_gate, to_up = ffn_again(where, h_all, w_ffn)
    e_all = jnp.stack(share_dp(e2))
    dgate, dup, keep, away = ffn_back(where, e_all, to_gate, to_up, w_ffn)
    part = add(keep, send(away, "c"))
    keep_d, away_d = weight_grad(where, act, e_all)
    got_d = send(away_d, "y")
    keep_g, away_g = weight_grad(where, after(h_all, away_d), dgate)
    came = send(part[1].astype(LOW), "x")
    got_g = send(away_g, "y")
    keep_u, away_u = weight_grad(where, after(h_all, away_g), dup)
    got_u = send(away_u, "y")
    dr1, low, datt, small_attn = norm_back_call(dr2, part[0], after(came, away_u), r1_m, w_attn, norms)
    small = lax.all_gather(jnp.concatenate([small_attn, small_ffn]), AXES)
    sum_d = add(keep_d, got_d)
    line_d = line_send(sum_d)
    rhs = attention_back(after(datt, sum_d), q_m, qkv, pos, slopes, seqs)
    got_g, got_u, rhs = lax.optimization_barrier((got_g, got_u, rhs))
    sum_gu = jnp.concatenate([add(keep_g, got_g), add(keep_u, got_u)], axis=1)
    line_gu = line_send(sum_gu)
    away = attention_grads(where, 1, x_flip, after(rhs, sum_gu), att_m, low)
    came = send(away, "c")
    g_down = line_add(sum_d, after(line_d, away))
    g_down = send(g_down, "down")
    keep = attention_grads(where, 0, x_flip, after(rhs, away), att_m, low)
    came, keep = lax.optimization_barrier((came, keep))
    total = add(keep, came)
    got0 = send(total[0, 1].astype(LOW), "x")
    got1 = send(total[1, 1].astype(LOW), "y")
    grad_in = input_grad(after(rhs, total), w_attn, dr1, positions)
    g_ffn = jnp.concatenate([g_down, line_add(sum_gu, after(line_gu, grad_in))]).reshape(3, ROWS, D)
    got0, got1 = after((got0, got1), g_ffn)
    shared = share_dp(g_ffn)
    total0 = add(total[0, 0], got0)
    total1 = add(total[1, 0], got1)
    got0 = send(total0[1].astype(LOW), "y")
    got1 = send(total1[1].astype(LOW), "x")
    got0, got1, shared = lax.optimization_barrier((got0, got1, shared))
    total = jnp.concatenate([add(total0[0], got0), add(total1[0], got1)], axis=1)
    line_a = line_send(total)
    grad_down, grad_up = finish_ffn(where, after(shared, total))
    g_attn = line_add(total, after(line_a, grad_down))
    grad_qkv, grad_out = finish_attention(where, share_dp(g_attn))
    small = jnp.sum(lax.dynamic_slice_in_dim(small, i * ROWS, ROWS, axis=2), axis=0)
    return (
        layer_out.reshape(seqs, length, width),
        grad_in.reshape(seqs, length, width),
        grad_qkv,
        grad_out,
        grad_up,
        grad_down,
        small[0],
        small[1],
        small[2],
        small[3],
    )


FF = 3072


def slopes():
    return jnp.exp2(-8.0 * (jnp.arange(HEADS, dtype=F32) + 1.0) / HEADS)


def pick(onehot, rows):
    if rows.dtype == LOW:
        return jnp.einsum("svj,sjd->svd", onehot.astype(LOW), rows, preferred_element_type=F32).astype(LOW)
    return jnp.einsum("svj,sjd->svd", onehot, rows, precision=lax.Precision.HIGHEST)


def gather_weights(w_qkv, w_out, w_up, w_down):
    fsdp = lax.axis_size("fsdp")
    dp = lax.axis_size("dp")
    rows, width = w_out.shape
    if rows % (8 * dp):
        return (
            lax.all_gather(w_qkv, "fsdp", axis=0, tiled=True),
            lax.all_gather(w_out, "fsdp", axis=0, tiled=True),
            lax.all_gather(w_up, "fsdp", axis=0, tiled=True),
            lax.all_gather(w_down, "fsdp", axis=0, tiled=True),
        )
    mine = lax.axis_index("dp")
    part = rows // dp
    group = w_down.shape[0] // rows
    joined = jnp.concatenate([w_qkv, w_out, w_up], axis=1)
    joined = lax.dynamic_slice_in_dim(joined, mine * part, part, axis=0)
    down = lax.dynamic_slice_in_dim(w_down, mine * part * group, part * group, axis=0)
    down = jnp.concatenate([down[k * part : (k + 1) * part] for k in range(group)], axis=1)
    full = lax.all_gather(jnp.concatenate([joined, down], axis=1), AXES, axis=0, tiled=True)
    a, b = w_qkv.shape[1], w_qkv.shape[1] + w_out.shape[1]
    c = b + w_up.shape[1]
    full_down = full[:, c:].reshape(fsdp * dp, part, group, width)
    full_down = full_down.transpose(0, 2, 1, 3).reshape(fsdp * dp * part * group, width)
    return full[:, :a], full[:, a:b], full[:, b:c], full_down


def scatter_grads(g_qkv, g_out, g_up, g_down):
    fsdp = lax.axis_size("fsdp")
    dp = lax.axis_size("dp")
    width = g_out.shape[1]
    rows = g_out.shape[0] // fsdp
    if rows % (8 * dp):
        return tuple(
            lax.psum(lax.psum_scatter(g, "fsdp", scatter_dimension=0, tiled=True), "dp")
            for g in (g_qkv, g_out, g_up, g_down)
        )
    part = rows // dp
    group = g_down.shape[0] // g_out.shape[0]
    down = g_down.reshape(fsdp * dp, group, part, width).transpose(0, 2, 1, 3)
    down = down.reshape(fsdp * rows, group * width)
    joined = jnp.concatenate([g_qkv, g_out, g_up, down], axis=1).astype(LOW)
    mine = lax.psum_scatter(joined, AXES, scatter_dimension=0, tiled=True)
    full = lax.all_gather(mine, "dp", axis=0, tiled=True).astype(F32)
    a, b = g_qkv.shape[1], g_qkv.shape[1] + width
    c = b + g_up.shape[1]
    full_down = full[:, c:].reshape(dp, part, group, width).transpose(0, 2, 1, 3)
    return full[:, :a], full[:, a:b], full[:, b:c], full_down.reshape(rows * group, width)


def on_device(hidden_in, w_qkv, w_out, w_up, w_down, gain_attn, shift_attn, gain_ffn, shift_ffn, grad_listed, positions, counts):
    seqs, length, width = hidden_in.shape
    tokens = seqs * length
    most = positions.shape[1]
    norms = jnp.stack([gain_attn, shift_attn, gain_ffn, shift_ffn])
    norms = lax.all_gather(norms, "fsdp", axis=1, tiled=True).astype(F32)
    w_qkv, w_out, w_up, w_down = gather_weights(w_qkv, w_out, w_up, w_down)
    live = jnp.arange(most, dtype=jnp.int32)[None, :] < counts[:, None]
    onehot = (positions[:, :, None] == jnp.arange(length, dtype=jnp.int32)).astype(F32)
    rows_in = hidden_in.reshape(tokens, width)
    slope = slopes()
    scale = HEAD_DIM**-0.5
    qkv = mm(rows_in, w_qkv).astype(LOW)
    split = qkv.reshape(seqs, length, 3, HEADS, HEAD_DIM)
    q, k, v = split[:, :, 0], split[:, :, 1], split[:, :, 2]
    place = jnp.arange(length, dtype=F32)
    bias = -slope[:, None, None] * jnp.abs(place[:, None] - place[None, :])
    s = jnp.einsum("sqhc,skhc->shqk", q, k, preferred_element_type=F32) * scale + bias
    p = jax.nn.softmax(s, axis=-1).astype(LOW)
    att = jnp.einsum("shqk,skhc->sqhc", p, v, preferred_element_type=F32).astype(LOW)
    att = att.reshape(tokens, width)
    r1 = rows_in.astype(F32) + mm(att, w_out)
    unit1, _ = norm_parts(r1)
    h1 = unit1 * norms[0] + norms[1]
    h1_low = h1.astype(LOW)
    u = mm(h1_low, w_up)
    act = (jax.nn.gelu(u[:, :FF], approximate=False) * u[:, FF:]).astype(LOW)
    r2 = h1 + mm(act, w_down)
    unit2, _ = norm_parts(r2)
    layer_out = (unit2 * norms[2] + norms[3]).astype(LOW).reshape(seqs, length, width)
    def listed(a):
        return pick(onehot, a.reshape(seqs, length, -1)).reshape(seqs * most, -1)

    dy = jnp.where(live[:, :, None], grad_listed, 0).astype(F32).reshape(seqs * most, width)
    unit2_m, rstd2_m = norm_parts(listed(r2))
    g_gain_ffn = jnp.sum(dy * unit2_m, axis=0)
    g_shift_ffn = jnp.sum(dy, axis=0)
    dr2 = norm_back(dy, unit2_m, rstd2_m, norms[2])
    e2 = dr2.astype(LOW)
    h1_m = listed(h1_low)
    u_m = mm(h1_m, w_up)
    gate, up = u_m[:, :FF], u_m[:, FF:]
    cdf = 0.5 * (1.0 + lax.erf(gate * (0.5**0.5)))
    pdf = jnp.exp(-0.5 * gate * gate) * ((2.0 * jnp.pi) ** -0.5)
    gelu = gate * cdf
    act_m = (gelu * up).astype(LOW)
    g_down = jnp.einsum("nf,nd->fd", act_m, e2, preferred_element_type=F32)
    dact = jnp.einsum("nd,fd->nf", e2, w_down, preferred_element_type=F32)
    du = jnp.concatenate([dact * up * (cdf + gate * pdf), dact * gelu], axis=1).astype(LOW)
    g_up = jnp.einsum("nd,nf->df", h1_m, du, preferred_element_type=F32)
    dh1 = dr2 + jnp.einsum("nf,df->nd", du, w_up, preferred_element_type=F32)
    unit1_m, rstd1_m = norm_parts(listed(r1))
    g_gain_attn = jnp.sum(dh1 * unit1_m, axis=0)
    g_shift_attn = jnp.sum(dh1, axis=0)
    dr1 = norm_back(dh1, unit1_m, rstd1_m, norms[0])
    e1 = dr1.astype(LOW)
    g_out = jnp.einsum("nd,ne->de", listed(att), e1, preferred_element_type=F32)
    datt = jnp.einsum("ne,de->nd", e1, w_out, preferred_element_type=F32).astype(LOW)
    datt = datt.reshape(seqs, most, HEADS, HEAD_DIM)
    q_m = listed(qkv[:, :width]).reshape(seqs, most, HEADS, HEAD_DIM)
    away = jnp.abs(positions[:, :, None].astype(F32) - place[None, None, :])
    s_m = jnp.einsum("sqhc,skhc->shqk", q_m, k, preferred_element_type=F32) * scale
    p_m = jax.nn.softmax(s_m - slope[None, :, None, None] * away[:, None], axis=-1)
    dv = jnp.einsum("shqk,sqhc->skhc", p_m.astype(LOW), datt, preferred_element_type=F32)
    dp = jnp.einsum("sqhc,skhc->shqk", datt, v, preferred_element_type=F32)
    ds = (p_m * (dp - jnp.sum(dp * p_m, axis=-1, keepdims=True))).astype(LOW)
    dq_m = (jnp.einsum("shqk,skhc->sqhc", ds, k, preferred_element_type=F32) * scale).astype(LOW)
    dk = (jnp.einsum("shqk,sqhc->skhc", ds, q_m, preferred_element_type=F32) * scale).astype(LOW)
    put = (onehot * live[:, :, None]).astype(LOW)
    dq = jnp.einsum("svj,svd->sjd", put, dq_m.reshape(seqs, most, width), preferred_element_type=F32)
    dqkv = jnp.concatenate(
        [dq.astype(LOW).reshape(tokens, width), dk.reshape(tokens, width), dv.astype(LOW).reshape(tokens, width)], axis=1
    )
    g_qkv = jnp.einsum("nd,ne->de", rows_in, dqkv, preferred_element_type=F32)
    dr1_all = jnp.einsum("svj,svd->sjd", onehot * live[:, :, None], dr1.reshape(seqs, most, width), precision=lax.Precision.HIGHEST)
    grad_in = dr1_all.reshape(tokens, width) + jnp.einsum("ne,de->nd", dqkv, w_qkv, preferred_element_type=F32)
    owned = scatter_grads(g_qkv, g_out, g_up, g_down)
    small = lax.psum(jnp.stack([g_gain_attn, g_shift_attn, g_gain_ffn, g_shift_ffn]), AXES)
    share = width // lax.axis_size("fsdp")
    small = lax.dynamic_slice_in_dim(small, lax.axis_index("fsdp") * share, share, axis=1)
    return (
        layer_out,
        grad_in.reshape(seqs, length, width),
        *owned,
        small[0],
        small[1],
        small[2],
        small[3],
    )


def solution(mesh):
    rows3 = P(("fsdp", "dp"), None, None)
    rows2 = P("fsdp", None)
    rows1 = P("fsdp")
    shape = dict(mesh.shape)
    step = on_block if shape == {"fsdp": SHARDS, "dp": QUARTERS} else on_device
    return jax.shard_map(
        step,
        mesh=mesh,
        in_specs=(rows3, rows2, rows2, rows2, rows2, rows1, rows1, rows1, rows1, rows3, P(("fsdp", "dp"), None), P(("fsdp", "dp"))),
        out_specs=(rows3, rows3, rows2, rows2, rows2, rows2, rows1, rows1, rows1, rows1),
        check_vma=False,
    )
```

```python
import functools

import jax
import jax.numpy as jnp
from jax import lax
from jax.experimental import pallas as pl
from jax.experimental.pallas import tpu as pltpu
from jax.sharding import PartitionSpec as P

HEADS = 12
HEAD_DIM = 64
EPS = 1e-12
F32 = jnp.float32
LOW = jnp.bfloat16
AXES = ("fsdp", "dp")
D = 768
ROWS = 96
LINE = 4
SHARDS = D // ROWS
QUARTERS = 4
EXACT = lax.Precision.HIGHEST
SCALE = HEAD_DIM**-0.5
VMEM = pl.BlockSpec(memory_space=pltpu.VMEM)
SMEM = pl.BlockSpec(memory_space=pltpu.SMEM)
BIG = pltpu.CompilerParams(vmem_limit_bytes=60 * 1024 * 1024)


def out(shape, dtype):
    return jax.ShapeDtypeStruct(shape, dtype)


def cost(us):
    return pl.CostEstimate(flops=0, bytes_accessed=int(us * 3.0e3), transcendentals=0)


def mm(a, b):
    return jnp.dot(a, b, preferred_element_type=F32)


def mm_nt(a, b):
    return lax.dot_general(a, b, (((1,), (1,)), ((), ())), preferred_element_type=F32)


def mm_tn(a, b):
    return lax.dot_general(a, b, (((0,), (0,)), ((), ())), preferred_element_type=F32)


def norm_parts(value):
    center = value - jnp.mean(value, axis=-1, keepdims=True)
    rstd = lax.rsqrt(jnp.mean(center * center, axis=-1, keepdims=True) + EPS)
    return center * rstd, rstd


def norm_back(grad, unit, rstd, gain):
    scaled = grad * gain
    return rstd * (
        scaled
        - jnp.mean(scaled, axis=-1, keepdims=True)
        - unit * jnp.mean(scaled * unit, axis=-1, keepdims=True)
    )


def onehot(pos_ref, seq, most, length):
    spots = lax.broadcasted_iota(jnp.int32, (most, length), 1)
    return spots == pos_ref[pl.ds(seq * most, most), :]


def gelu_parts(gate):
    cdf = 0.5 * (1.0 + lax.erf(gate * (0.5**0.5)))
    pdf = jnp.exp(-0.5 * gate * gate) * ((2.0 * jnp.pi) ** -0.5)
    return gate * cdf, cdf + gate * pdf


def slope_of(head):
    return 2.0 ** (-8.0 * (head + 1.0) / HEADS)


def block(ref, *index):
    value = ref[index] if index else ref[...]
    return value.reshape(-1, value.shape[-1])


EXTRA = 8
TAIL = 16
HALVES = ((0, 48), (48, 56))
KEYS = [(ry, rx, rc) for rc in (0, 1) for rx in (0, 1) for ry in (0, 1)]


def attention_kernel(seqs, most, where_ref, slope_ref, x_ref, norm_ref, pos_ref, *rest):
    lines, rest = rest[:16], rest[16:]
    qkv_ref, h1_ref, att_m_ref, h1_m_ref, q_m_ref, r1_m_ref, w_ref, att_ref, r1_ref, sem = rest
    z, y, c_x = where_ref[0], where_ref[1], where_ref[4]
    copies = []
    for n, (ry, rx, rc) in enumerate(KEYS):
        j = jnp.bitwise_xor(c_x, 2 * rx + rc)
        for r in range(LINE):
            shard = 2 * lax.rem(z + LINE - r, LINE) + jnp.bitwise_xor(y, ry)
            for half, (start, size) in enumerate(HALVES):
                size = min(size, ROWS - start)
                copies.append(
                    pltpu.make_async_copy(
                        lines[2 * n + half].at[r, pl.ds(0, size)], w_ref.at[shard, j, pl.ds(start, size)], sem
                    )
                )
    for copy in copies:
        copy.start()
    for copy in copies:
        copy.wait()
    length = x_ref.shape[0] // seqs
    step = 256

    @pl.loop(0, 3 * D // step)
    def _(n):
        j = n // (D // step)
        lane = pl.multiple_of((n - j * (D // step)) * step, step)
        w = w_ref[:, j, :, pl.ds(lane, step)].reshape(D, step)
        qkv_ref[:, pl.ds(pl.multiple_of(n * step, step), step)] = mm(x_ref[...], w).astype(LOW)

    first = lax.broadcasted_iota(jnp.int32, (length, 128), 1) < HEAD_DIM
    row = lax.broadcasted_iota(jnp.int32, (length, length), 0)
    col = lax.broadcasted_iota(jnp.int32, (length, length), 1)
    away = jnp.abs(row - col).astype(F32)

    @pl.loop(0, HEADS // 2)
    def _(t):
        lane = pl.multiple_of(t * 128, 128)
        bias = jnp.concatenate([slope_ref[2 * t] * away, slope_ref[2 * t + 1] * away], axis=0)
        for s in range(seqs):
            rows = slice(s * length, (s + 1) * length)
            q = qkv_ref[rows, pl.ds(lane, 128)]
            k = qkv_ref[rows, pl.ds(D + lane, 128)]
            v = qkv_ref[rows, pl.ds(2 * D + lane, 128)]
            zero = jnp.zeros_like(q)
            both = jnp.concatenate([jnp.where(first, q, zero), jnp.where(first, zero, q)], axis=0)
            score = mm_nt(both, k) * SCALE - bias
            e = jnp.exp(score - jnp.max(score, axis=-1, keepdims=True))
            p = (e * (1.0 / jnp.sum(e, axis=-1, keepdims=True))).astype(LOW)
            mixed = mm(p, v)
            att_ref[rows, pl.ds(lane, 128)] = jnp.where(first, mixed[:length], mixed[length:]).astype(LOW)

    @pl.loop(0, D // step)
    def _(n):
        lane = pl.multiple_of(n * step, step)
        w = w_ref[:, 3, :, pl.ds(lane, step)].reshape(D, step)
        r1_ref[:, pl.ds(lane, step)] = x_ref[:, pl.ds(lane, step)].astype(F32) + mm(att_ref[...], w)

    for s in range(seqs):
        rows = slice(s * length, (s + 1) * length)
        listed = slice(s * most, (s + 1) * most)
        unit, _ = norm_parts(r1_ref[rows, :])
        h1 = unit * norm_ref[0:1, :] + norm_ref[1:2, :]
        h1_ref[rows, :] = h1
        hot = onehot(pos_ref, s, most, length)
        hot_low = hot.astype(LOW)
        r1_m_ref[listed, :] = jnp.dot(hot.astype(F32), r1_ref[rows, :], precision=EXACT, preferred_element_type=F32)
        h1_m_ref[listed, :] = mm(hot_low, h1.astype(LOW)).astype(LOW)
        att_m_ref[listed, :] = mm(hot_low, att_ref[rows, :]).astype(LOW)
        q_m_ref[listed, :] = mm(hot_low, qkv_ref[rows, 0:D]).astype(LOW)


def attention_forward(where, x, lines, norms, pos, slopes, seqs):
    tokens = x.shape[0]
    listed = pos.shape[0]
    return pl.pallas_call(
        functools.partial(attention_kernel, seqs, listed // seqs),
        out_shape=(
            out((tokens, 3 * D), LOW),
            out((tokens, D), F32),
            out((listed, D), LOW),
            out((listed, D), LOW),
            out((listed, D), LOW),
            out((listed, D), F32),
            out((SHARDS, QUARTERS, ROWS, D), LOW),
        ),
        in_specs=[SMEM, SMEM, VMEM, VMEM, VMEM] + [pl.BlockSpec(memory_space=pl.ANY)] * 16,
        out_specs=(VMEM,) * 7,
        scratch_shapes=[pltpu.VMEM((tokens, D), LOW), pltpu.VMEM((tokens, D), F32), pltpu.SemaphoreType.DMA],
        compiler_params=BIG,
        cost_estimate=cost(20),
        name="attention_forward",
    )(where, slopes, x, norms, pos, *lines)


def ffn_kernel(seqs, most, h1_ref, gate_ref, up_ref, down_ref, norm_ref, pos_ref, dy_ref, y_ref, dr2_ref, e2_ref, small_ref, low_ref, act_ref, acc_ref):
    j = pl.program_id(0)
    tokens = h1_ref.shape[0]
    length = tokens // seqs
    step = 256

    @pl.when(j == 0)
    def _():
        low_ref[...] = h1_ref[...].astype(LOW)
        acc_ref[...] = h1_ref[...]

    @pl.loop(0, D // step)
    def _(n):
        lane = pl.multiple_of(n * step, step)
        gate = mm(low_ref[...], gate_ref[:, :, pl.ds(lane, step)].reshape(D, step))
        up = mm(low_ref[...], up_ref[:, :, pl.ds(lane, step)].reshape(D, step))
        cdf = 0.5 * (1.0 + lax.erf(gate * (0.5**0.5)))
        act_ref[:, pl.ds(lane, step)] = (gate * cdf * up).astype(LOW)

    @pl.loop(0, D // step)
    def _(n):
        lane = pl.multiple_of(n * step, step)
        acc_ref[:, pl.ds(lane, step)] += mm(act_ref[...], down_ref[:, :, :, pl.ds(lane, step)].reshape(D, step))

    @pl.when(j == QUARTERS - 1)
    def _():
        gain = norm_ref[2:3, :]
        small = [jnp.zeros((1, D), F32)] * 2
        for s in range(seqs):
            rows = slice(s * length, (s + 1) * length)
            listed = slice(s * most, (s + 1) * most)
            unit, _ = norm_parts(acc_ref[rows, :])
            y_ref[rows, :] = (unit * gain + norm_ref[3:4, :]).astype(LOW)
            hot = onehot(pos_ref, s, most, length).astype(F32)
            picked = jnp.dot(hot, acc_ref[rows, :], precision=EXACT, preferred_element_type=F32)
            unit_m, rstd_m = norm_parts(picked)
            dy = dy_ref[listed, :].astype(F32)
            small = [small[0] + jnp.sum(dy * unit_m, axis=0, keepdims=True), small[1] + jnp.sum(dy, axis=0, keepdims=True)]
            dr2 = norm_back(dy, unit_m, rstd_m, gain)
            dr2_ref[listed, :] = dr2
            e2_ref[listed, :] = dr2.astype(LOW)
        small_ref[...] = jnp.concatenate(small, axis=0)


def ffn_forward(h1, w_ffn, norms, pos, dy, seqs):
    tokens = h1.shape[0]
    listed = pos.shape[0]
    whole = lambda shape: pl.BlockSpec(shape, lambda j: (0,) * len(shape), pipeline_mode=pl.Buffered(1))
    return pl.pallas_call(
        functools.partial(ffn_kernel, seqs, listed // seqs),
        out_shape=(out((tokens, D), LOW), out((listed, D), F32), out((listed, D), LOW), out((2, D), F32)),
        grid=(QUARTERS,),
        in_specs=[
            whole((tokens, D)),
            pl.BlockSpec((SHARDS, None, None, ROWS, D), lambda j: (0, j, 0, 0, 0)),
            pl.BlockSpec((SHARDS, None, None, ROWS, D), lambda j: (0, j, 1, 0, 0)),
            pl.BlockSpec((SHARDS // QUARTERS, QUARTERS, None, ROWS, D), lambda j: (j, 0, 2, 0, 0)),
            whole(norms.shape),
            whole(pos.shape),
            whole(dy.shape),
        ],
        out_specs=(
            pl.BlockSpec((tokens, D), lambda j: (0, 0)),
            pl.BlockSpec((listed, D), lambda j: (0, 0)),
            pl.BlockSpec((listed, D), lambda j: (0, 0)),
            pl.BlockSpec((2, D), lambda j: (0, 0)),
        ),
        scratch_shapes=[pltpu.VMEM((tokens, D), LOW), pltpu.VMEM((tokens, D), LOW), pltpu.VMEM((tokens, D), F32)],
        compiler_params=BIG,
        cost_estimate=cost(16),
        name="ffn_forward",
    )(h1, w_ffn, w_ffn, w_ffn, norms, pos, dy)


def ffn_again_kernel(where_ref, h_ref, gate_ref, up_ref, act_ref, to_gate_ref, to_up_ref):
    step = 256

    @pl.loop(0, D // step)
    def _(n):
        lane = pl.multiple_of(n * step, step)
        rows = block(h_ref)
        gate = mm(rows, gate_ref[:, :, pl.ds(lane, step)].reshape(D, step))
        up = mm(rows, up_ref[:, :, pl.ds(lane, step)].reshape(D, step))
        value, slope = gelu_parts(gate)
        act_ref[:, pl.ds(lane, step)] = (value * up).astype(LOW)
        to_gate_ref[:, pl.ds(lane, step)] = slope * up
        to_up_ref[:, pl.ds(lane, step)] = value


def quarter_specs(which):
    specs = {
        "gate": pl.BlockSpec((SHARDS, None, None, ROWS, D), lambda g, w: (0, w[4], 0, 0, 0)),
        "up": pl.BlockSpec((SHARDS, None, None, ROWS, D), lambda g, w: (0, w[4], 1, 0, 0)),
        "down": pl.BlockSpec((SHARDS // QUARTERS, QUARTERS, None, ROWS, D), lambda g, w: (w[4], 0, 2, 0, 0)),
    }
    return [specs[name] for name in which]


def at_once(shape):
    return pl.BlockSpec(shape, lambda g, w: (0,) * len(shape))


def ffn_again(where, h_all, w_ffn):
    rows = h_all.shape[0] * h_all.shape[1]
    return pl.pallas_call(
        ffn_again_kernel,
        out_shape=(out((rows, D), LOW), out((rows, D), F32), out((rows, D), F32)),
        grid_spec=pltpu.PrefetchScalarGridSpec(
            num_scalar_prefetch=1,
            grid=(1,),
            in_specs=[at_once(h_all.shape), *quarter_specs(["gate", "up"])],
            out_specs=(at_once((rows, D)),) * 3,
        ),
        compiler_params=BIG,
        cost_estimate=cost(6),
        name="ffn_again",
    )(where, h_all, w_ffn, w_ffn)


def ffn_back_kernel(where_ref, e_ref, to_gate_ref, to_up_ref, gate_ref, up_ref, down_ref, dgate_ref, dup_ref, keep_ref, send_ref):
    listed = e_ref.shape[1]
    half = QUARTERS // 2
    for n in range(SHARDS // QUARTERS):
        lanes = slice(n * QUARTERS * ROWS, (n + 1) * QUARTERS * ROWS)
        dact = mm_nt(block(e_ref), block(down_ref, n))
        dgate_ref[:, lanes] = (dact * to_gate_ref[:, lanes]).astype(LOW)
        dup_ref[:, lanes] = (dact * to_up_ref[:, lanes]).astype(LOW)
    for n in range(2):
        shards = slice(n * SHARDS // 2, (n + 1) * SHARDS // 2)
        lanes = slice(n * D // 2, (n + 1) * D // 2)
        part = mm_nt(dgate_ref[...], block(gate_ref, shards)) + mm_nt(dup_ref[...], block(up_ref, shards))
        for r in range(half):
            keep_ref[r, :, lanes] = part[2 * r * listed : (2 * r + 1) * listed]
            send_ref[r, :, lanes] = part[(2 * r + 1) * listed : (2 * r + 2) * listed].astype(LOW)


def ffn_back(where, e_all, to_gate, to_up, w_ffn):
    count, listed, _ = e_all.shape
    rows = count * listed
    return pl.pallas_call(
        ffn_back_kernel,
        out_shape=(out((rows, D), LOW), out((rows, D), LOW), out((count // 2, listed, D), F32), out((count // 2, listed, D), LOW)),
        grid_spec=pltpu.PrefetchScalarGridSpec(
            num_scalar_prefetch=1,
            grid=(1,),
            in_specs=[at_once(e_all.shape), at_once((rows, D)), at_once((rows, D)), *quarter_specs(["gate", "up", "down"])],
            out_specs=(at_once((rows, D)), at_once((rows, D)), at_once((count // 2, listed, D)), at_once((count // 2, listed, D))),
        ),
        compiler_params=BIG,
        cost_estimate=cost(7),
        name="ffn_back",
    )(where, e_all, to_gate, to_up, w_ffn, w_ffn, w_ffn)


def weight_grad_kernel(where_ref, a_ref, b_ref, keep_ref, send_ref, full_ref):
    z, y = where_ref[0], where_ref[1]
    b = block(b_ref)
    step = 256

    @pl.loop(0, D // step)
    def _(n):
        lane = pl.multiple_of(n * step, step)
        a = block(a_ref, *([slice(None)] * (len(a_ref.shape) - 1)), pl.ds(lane, step))
        full_ref[pl.ds(lane, step), :] = mm_tn(a, b)

    for r in range(LINE):
        base = 2 * lax.rem(z + r, LINE)
        for other, ref in ((0, keep_ref), (1, send_ref)):
            start = (base + (y if other == 0 else 1 - y)) * ROWS
            ref[r] = full_ref[pl.ds(pl.multiple_of(start, 8), ROWS), :].astype(LOW)


def weight_grad(where, a, b):
    shape = (LINE, ROWS, D)
    rows = a.size // D
    return pl.pallas_call(
        weight_grad_kernel,
        out_shape=(out(shape, LOW), out(shape, LOW)),
        in_specs=[SMEM, VMEM, VMEM],
        out_specs=(VMEM, VMEM),
        scratch_shapes=[pltpu.VMEM((D, D), F32)],
        compiler_params=BIG,
        cost_estimate=cost(4),
        name="weight_grad",
    )(where, a, b)


def norm_back_kernel(dr2_ref, part_ref, came_ref, r1_ref, w_ref, norm_ref, dr1_ref, low_ref, datt_ref, small_ref):
    dh1 = dr2_ref[...] + part_ref[...] + came_ref[...].astype(F32)
    unit, rstd = norm_parts(r1_ref[...])
    small_ref[0:1, :] = jnp.sum(dh1 * unit, axis=0, keepdims=True)
    small_ref[1:2, :] = jnp.sum(dh1, axis=0, keepdims=True)
    dr1 = norm_back(dh1, unit, rstd, norm_ref[0:1, :])
    dr1_ref[...] = dr1
    low = dr1.astype(LOW)
    low_ref[...] = low
    for n in range(2):
        lanes = slice(n * D // 2, (n + 1) * D // 2)
        datt_ref[:, lanes] = mm_nt(low, block(w_ref, slice(n * SHARDS // 2, (n + 1) * SHARDS // 2))).astype(LOW)


def norm_back_call(dr2, part, came, r1_m, w_attn, norms):
    listed = dr2.shape[0]
    same = lambda shape: pl.BlockSpec(shape, lambda g: (0,) * len(shape))
    rows = same((listed, D))
    return pl.pallas_call(
        norm_back_kernel,
        out_shape=(out((listed, D), F32), out((listed, D), LOW), out((listed, D), LOW), out((2, D), F32)),
        grid=(1,),
        in_specs=[rows, rows, rows, rows, pl.BlockSpec((SHARDS, None, ROWS, D), lambda g: (0, 3, 0, 0)), same((4, D))],
        out_specs=(rows, rows, rows, same((2, D))),
        compiler_params=BIG,
        cost_estimate=cost(4),
        name="norm_back",
    )(dr2, part, came, r1_m, w_attn, norms)


def attention_back_kernel(seqs, most, slope_ref, datt_ref, q_ref, qkv_ref, pos_ref, rhs_ref, away_ref, hot_ref):
    length = qkv_ref.shape[0] // seqs
    listed = seqs * most
    first_m = lax.broadcasted_iota(jnp.int32, (most, 128), 1) < HEAD_DIM
    spots = lax.broadcasted_iota(jnp.int32, (listed, length), 1)
    away_ref[...] = jnp.abs(pos_ref[...] - spots).astype(F32)
    hot_ref[...] = (spots == pos_ref[...]).astype(LOW)

    def both(value):
        zero = jnp.zeros_like(value)
        return jnp.concatenate([jnp.where(first_m, value, zero), jnp.where(first_m, zero, value)], axis=0)

    @pl.loop(0, HEADS // 2)
    def _(t):
        lane = pl.multiple_of(t * 128, 128)
        for s in range(seqs):
            rows = slice(s * length, (s + 1) * length)
            mine = slice(s * most, (s + 1) * most)
            away = away_ref[mine, :]
            q = both(q_ref[mine, pl.ds(lane, 128)])
            da = both(datt_ref[mine, pl.ds(lane, 128)])
            k = qkv_ref[rows, pl.ds(D + lane, 128)]
            v = qkv_ref[rows, pl.ds(2 * D + lane, 128)]
            bias = jnp.concatenate([slope_ref[2 * t] * away, slope_ref[2 * t + 1] * away], axis=0)
            score = mm_nt(q, k) * SCALE - bias
            e = jnp.exp(score - jnp.max(score, axis=-1, keepdims=True))
            p = e * (1.0 / jnp.sum(e, axis=-1, keepdims=True))
            dp = mm_nt(da, v)
            ds = (p * (dp - jnp.sum(dp * p, axis=-1, keepdims=True))).astype(LOW)
            dq = mm(ds, k)
            dq = (jnp.where(first_m, dq[:most], dq[most:]) * SCALE).astype(LOW)
            rhs_ref[rows, pl.ds(lane, 128)] = mm_tn(hot_ref[mine, :], dq).astype(LOW)
            rhs_ref[rows, pl.ds(D + lane, 128)] = (mm_tn(ds, q) * SCALE).astype(LOW)
            rhs_ref[rows, pl.ds(2 * D + lane, 128)] = mm_tn(p.astype(LOW), da).astype(LOW)


def attention_back(datt, q_m, qkv, pos, slopes, seqs):
    tokens = qkv.shape[0]
    listed = pos.shape[0]
    return pl.pallas_call(
        functools.partial(attention_back_kernel, seqs, listed // seqs),
        out_shape=out((tokens, 3 * D), LOW),
        in_specs=[SMEM] + [VMEM] * 4,
        out_specs=VMEM,
        scratch_shapes=[pltpu.VMEM((listed, tokens // seqs), F32), pltpu.VMEM((listed, tokens // seqs), LOW)],
        compiler_params=BIG,
        cost_estimate=cost(15),
        name="attention_back",
    )(slopes, datt, q_m, qkv, pos)


def attention_grads_kernel(rc, where_ref, flip_ref, rhs_ref, att_ref, low_ref, small_attn_ref, small_ffn_ref, cut0_ref, cut1_ref, full_ref, tail_ref):
    z, y, mine = where_ref[0], where_ref[1], where_ref[4]
    half = ROWS // 2
    step = 256
    tail_ref[...] = jnp.zeros(tail_ref.shape, LOW)
    small = jnp.concatenate([small_attn_ref[...], small_ffn_ref[...]], axis=0).astype(LOW)
    for n in range(SHARDS):
        tail_ref[n, 0:4, 0:ROWS] = small[:, n * ROWS : (n + 1) * ROWS]
    for rx in (0, 1):
        j = jnp.bitwise_xor(mine, 2 * rx + rc)

        @pl.when(j == 3)
        def _():
            for n in range(D // step):
                rows = slice(n * step, (n + 1) * step)
                full_ref[rows, :] = mm_tn(att_ref[:, rows], low_ref[...])

        @pl.when(j != 3)
        def _():
            @pl.loop(0, D // step)
            def _(n):
                lane = pl.multiple_of(n * step, step)
                cols = pl.ds(pl.multiple_of(j * D + n * step, step), step)
                full_ref[:, pl.ds(lane, step)] = mm(flip_ref[...], rhs_ref[:, cols])

        for rz in range(LINE):
            base = 2 * lax.rem(z + rz, LINE)
            for ry in (0, 1):
                shard = base + (y if ry == 0 else 1 - y)
                start = shard * ROWS
                cut0_ref[rx, ry, rz] = full_ref[pl.ds(pl.multiple_of(start, 8), half), :].astype(LOW)
                cut1_ref[ry, rx, rz, 0:half] = full_ref[pl.ds(pl.multiple_of(start + half, 8), half), :].astype(LOW)
                cut1_ref[ry, rx, rz, half:] = tail_ref[shard]


def attention_grads(where, rc, x_flip, rhs, att_m, low, small_attn, small_ffn):
    half = ROWS // 2
    return pl.pallas_call(
        functools.partial(attention_grads_kernel, rc),
        out_shape=(out((2, 2, LINE, half, D), LOW), out((2, 2, LINE, half + TAIL, D), LOW)),
        in_specs=[SMEM] + [VMEM] * 6,
        out_specs=(VMEM, VMEM),
        scratch_shapes=[pltpu.VMEM((D, D), F32), pltpu.VMEM((SHARDS, TAIL, D), LOW)],
        compiler_params=BIG,
        cost_estimate=cost(5),
        name="attention_grads",
    )(where, x_flip, rhs, att_m, low, small_attn, small_ffn)


def input_grad_kernel(seqs, rhs_ref, w_ref, dr1_ref, pos_ref, out_ref):
    length = out_ref.shape[0] // seqs
    most = dr1_ref.shape[0] // seqs
    for n in range(2):
        lanes = slice(n * D // 2, (n + 1) * D // 2)
        shards = slice(n * SHARDS // 2, (n + 1) * SHARDS // 2)
        total = mm_nt(rhs_ref[:, 0:D], block(w_ref, shards, 0))
        total += mm_nt(rhs_ref[:, D : 2 * D], block(w_ref, shards, 1))
        total += mm_nt(rhs_ref[:, 2 * D : 3 * D], block(w_ref, shards, 2))
        for s in range(seqs):
            rows = slice(s * length, (s + 1) * length)
            hot = (lax.broadcasted_iota(jnp.int32, (length, most), 0) == pos_ref[s : s + 1, :]).astype(F32)
            spread = jnp.dot(hot, dr1_ref[s * most : (s + 1) * most, lanes], precision=EXACT, preferred_element_type=F32)
            out_ref[rows, lanes] = total[rows] + spread


def input_grad(rhs, w_attn, dr1, positions):
    tokens = rhs.shape[0]
    return pl.pallas_call(
        functools.partial(input_grad_kernel, positions.shape[0]),
        out_shape=out((tokens, D), F32),
        in_specs=[VMEM] * 4,
        out_specs=VMEM,
        compiler_params=BIG,
        cost_estimate=cost(8),
        name="input_grad",
    )(rhs, w_attn, dr1, positions)


def place(z, y, x, c):
    return (2 * z + y) * 4 + 2 * x + c


def grid_perm(move):
    return [
        (place(z, y, x, c), place(*move(z, y, x, c)))
        for z in range(4)
        for y in range(2)
        for x in range(2)
        for c in range(2)
    ]


MOVES = {
    "x": grid_perm(lambda z, y, x, c: (z, y, 1 - x, c)),
    "y": grid_perm(lambda z, y, x, c: (z, 1 - y, x, c)),
    "c": grid_perm(lambda z, y, x, c: (z, y, x, 1 - c)),
    1: grid_perm(lambda z, y, x, c: ((z + 1) % 4, y, x, c)),
    2: grid_perm(lambda z, y, x, c: ((z + 2) % 4, y, x, c)),
    3: grid_perm(lambda z, y, x, c: ((z + 3) % 4, y, x, c)),
    "down": [(m * 4 + q, (2 * q + m // 4) * 4 + m % 4) for m in range(8) for q in range(4)],
}


def send(value, move):
    return lax.ppermute(value, AXES, MOVES[move])


def share_dp(value):
    other = send(value, "x")
    return value, send(value, "c"), other, send(other, "c")


def after(value, *earlier):
    return lax.optimization_barrier((value, *earlier))[0]


def add(kept, got):
    return kept.astype(F32) + got.astype(F32)


def line_parts(keep, got):
    return [add(keep[r], got[r]).astype(LOW) for r in (1, 2, 3)]


def line_send(parts):
    return [send(value, r) for r, value in zip((1, 2, 3), parts)]


def line_add(keep, got, came):
    return (add(keep[0], got[0]) + came[0].astype(F32) + came[1].astype(F32) + came[2].astype(F32)).astype(LOW)


def finish_ffn_kernel(where_ref, *rest):
    pieces, (down_ref, up_ref) = rest[:QUARTERS], rest[QUARTERS:]
    mine = where_ref[4]
    for n, ref in enumerate(pieces):
        j = jnp.bitwise_xor(mine, n)
        down_ref[pl.ds(pl.multiple_of(j * ROWS, 8), ROWS), :] = ref[0].astype(F32)
        for half in (0, 1):
            up_ref[:, pl.ds(pl.multiple_of((half * QUARTERS + j) * D, D), D)] = ref[1 + half].astype(F32)


def finish_attention_kernel(where_ref, *rest):
    pieces, (qkv_ref, out_ref, held_ref) = rest[:QUARTERS], rest[QUARTERS:]
    mine = where_ref[4]
    for n, ref in enumerate(pieces):
        held_ref[jnp.bitwise_xor(mine, n)] = ref[...].astype(F32)
    for j in range(3):
        qkv_ref[:, j * D : (j + 1) * D] = held_ref[j]
    out_ref[...] = held_ref[3]


def finish_ffn(where, pieces):
    return pl.pallas_call(
        finish_ffn_kernel,
        out_shape=(out((QUARTERS * ROWS, D), F32), out((ROWS, 2 * QUARTERS * D), F32)),
        in_specs=[SMEM] + [VMEM] * QUARTERS,
        out_specs=(VMEM, VMEM),
        compiler_params=BIG,
        cost_estimate=cost(4),
        name="finish_ffn",
    )(where, *pieces)


def finish_attention(where, pieces):
    return pl.pallas_call(
        finish_attention_kernel,
        out_shape=(out((ROWS, 3 * D), F32), out((ROWS, D), F32)),
        in_specs=[SMEM] + [VMEM] * QUARTERS,
        out_specs=(VMEM, VMEM),
        scratch_shapes=[pltpu.VMEM((QUARTERS, ROWS, D), F32)],
        compiler_params=BIG,
        cost_estimate=cost(2),
        name="finish_attention",
    )(where, *pieces)


def spread(piece, order):
    got = {frozenset(): piece}
    for step in (*order, "c"):
        for key in list(got):
            got[key | {step}] = send(got[key], step)
    return [got[frozenset(n for n, b in zip("yxc", key) if b)] for key in KEYS]


def on_block(hidden_in, w_qkv, w_out, w_up, w_down, gain_attn, shift_attn, gain_ffn, shift_ffn, grad_listed, positions, counts):
    seqs, length, width = hidden_in.shape
    tokens = seqs * length
    most = positions.shape[1]
    i, j = lax.axis_index("fsdp"), lax.axis_index("dp")
    where = jnp.stack([i // 2, i % 2, j // 2, j % 2, j]).astype(jnp.int32)
    ff = w_down.shape[0] * SHARDS
    attn_piece = lax.dynamic_slice_in_dim(jnp.concatenate([w_qkv, w_out], axis=1), j * D, D, axis=1)
    norms = jnp.concatenate([gain_attn, shift_attn, gain_ffn, shift_ffn, jnp.zeros((D - 4 * ROWS,), LOW)])
    attn_piece = jnp.concatenate([attn_piece, jnp.broadcast_to(norms, (EXTRA, D))], axis=0)
    line = jnp.stack([attn_piece] + [send(attn_piece, r) for r in (1, 2, 3)])
    x = hidden_in.reshape(tokens, width)
    line, x_flip = lax.optimization_barrier((line, x.T))
    halves = [
        spread(line[:, start : start + size], order)
        for (start, size), order in zip(HALVES, (("y", "x"), ("x", "y")))
    ]
    lines = [half[n] for n in range(len(KEYS)) for half in halves]
    ffn_piece = jnp.stack(
        [
            lax.dynamic_slice_in_dim(w_up, j * D, D, axis=1),
            lax.dynamic_slice_in_dim(w_up, ff + j * D, D, axis=1),
            lax.dynamic_slice_in_dim(w_down, j * ROWS, ROWS, axis=0),
        ]
    )
    w_ffn = lax.all_gather(ffn_piece, AXES, axis=0, tiled=False).reshape(SHARDS, QUARTERS, 3, ROWS, D)
    tails = jnp.stack([halves[1][n][:, 48, : 4 * ROWS] for n in range(2)])
    tails = jnp.where(i % 2 == 0, tails, tails[::-1])
    tails = jnp.roll(tails[:, ::-1], i // 2 + 1, axis=1)
    norms = tails.transpose(1, 0, 2).reshape(SHARDS, 4, ROWS).transpose(1, 0, 2).reshape(4, D).astype(F32)
    slopes = jnp.exp2(-8.0 * (jnp.arange(HEADS, dtype=F32) + 1.0) / HEADS)
    pos = positions.reshape(seqs * most, 1)
    live = jnp.arange(most, dtype=jnp.int32)[None, :] < counts[:, None]
    dy = jnp.where(live[:, :, None], grad_listed, jnp.zeros_like(grad_listed)).reshape(seqs * most, width)

    qkv, h1, att_m, h1_m, q_m, r1_m, w_attn = attention_forward(where, x, lines, norms, pos, slopes, seqs)
    h_all = jnp.stack(share_dp(h1_m))
    h1, h_all = lax.optimization_barrier((h1, h_all))
    layer_out, dr2, e2, small_ffn = ffn_forward(h1, w_ffn, norms, pos, dy, seqs)
    act, to_gate, to_up = ffn_again(where, h_all, w_ffn)
    e_all = jnp.stack(share_dp(e2))
    dgate, dup, keep, away = ffn_back(where, e_all, to_gate, to_up, w_ffn)
    part = add(keep, send(away, "c"))
    keep_d, away_d = weight_grad(where, act, e_all)
    got_d = send(away_d, "y")
    keep_g, away_g = weight_grad(where, after(h_all, away_d), dgate)
    came = send(part[1].astype(LOW), "x")
    got_g = send(away_g, "y")
    keep_u, away_u = weight_grad(where, after(h_all, away_g), dup)
    got_u = send(away_u, "y")
    dr1, low, datt, small_attn = norm_back_call(dr2, part[0], after(came, away_u), r1_m, w_attn, norms)
    parts_d = line_parts(keep_d, got_d)
    rhs = attention_back(after(datt, parts_d), q_m, qkv, pos, slopes, seqs)
    got_d, got_g, got_u, rhs = lax.optimization_barrier((got_d, got_g, got_u, rhs))
    keep_gu, got_gu = jnp.concatenate([keep_g, keep_u], axis=1), jnp.concatenate([got_g, got_u], axis=1)
    parts_gu = line_parts(keep_gu, got_gu)
    away0, away1 = attention_grads(where, 1, x_flip, after(rhs, parts_gu), att_m, low, small_attn, small_ffn)
    came0, came1 = send(away0, "c"), send(away1, "c")
    g_down = line_add(keep_d, got_d, after(line_send(parts_d), away0))
    g_down = send(g_down, "down")
    keep0, keep1 = attention_grads(where, 0, x_flip, after(rhs, away0), att_m, low, small_attn, small_ffn)
    came0, came1, keep0, keep1 = lax.optimization_barrier((came0, came1, keep0, keep1))
    away0, away1 = add(keep0[1], came0[1]).astype(LOW), add(keep1[1], came1[1]).astype(LOW)
    got0, got1 = send(away0, "x"), send(away1, "y")
    grad_in = input_grad(after(rhs, (away0, away1)), w_attn, dr1, positions)
    g_gu = line_add(keep_gu, got_gu, after(line_send(parts_gu), grad_in))
    g_ffn = jnp.concatenate([g_down, g_gu]).reshape(3, ROWS, D)
    got0, got1 = after((got0, got1), g_ffn)
    shared = share_dp(g_ffn)
    total0 = add(keep0[0], came0[0]) + got0.astype(F32)
    total1 = add(keep1[0], came1[0]) + got1.astype(F32)
    got0 = send(total0[1].astype(LOW), "y")
    got1 = send(total1[1].astype(LOW), "x")
    got0, got1, shared = lax.optimization_barrier((got0, got1, shared))
    total = jnp.concatenate([add(total0[0], got0), add(total1[0], got1)], axis=1)
    parts = [total[r].astype(LOW) for r in (1, 2, 3)]
    line_a = line_send(parts)
    grad_down, grad_up = finish_ffn(where, after(shared, parts))
    line_a = after(line_a, grad_down)
    g_attn = (total[0] + line_a[0].astype(F32) + line_a[1].astype(F32) + line_a[2].astype(F32))
    small = g_attn[ROWS : ROWS + 4, :ROWS]
    grad_qkv, grad_out = finish_attention(where, share_dp(g_attn[:ROWS].astype(LOW)))
    return (
        layer_out.reshape(seqs, length, width),
        grad_in.reshape(seqs, length, width),
        grad_qkv,
        grad_out,
        grad_up,
        grad_down,
        small[0],
        small[1],
        small[2],
        small[3],
    )


FF = 3072


def slopes():
    return jnp.exp2(-8.0 * (jnp.arange(HEADS, dtype=F32) + 1.0) / HEADS)


def pick(onehot, rows):
    if rows.dtype == LOW:
        return jnp.einsum("svj,sjd->svd", onehot.astype(LOW), rows, preferred_element_type=F32).astype(LOW)
    return jnp.einsum("svj,sjd->svd", onehot, rows, precision=lax.Precision.HIGHEST)


def gather_weights(w_qkv, w_out, w_up, w_down):
    fsdp = lax.axis_size("fsdp")
    dp = lax.axis_size("dp")
    rows, width = w_out.shape
    if rows % (8 * dp):
        return (
            lax.all_gather(w_qkv, "fsdp", axis=0, tiled=True),
            lax.all_gather(w_out, "fsdp", axis=0, tiled=True),
            lax.all_gather(w_up, "fsdp", axis=0, tiled=True),
            lax.all_gather(w_down, "fsdp", axis=0, tiled=True),
        )
    mine = lax.axis_index("dp")
    part = rows // dp
    group = w_down.shape[0] // rows
    joined = jnp.concatenate([w_qkv, w_out, w_up], axis=1)
    joined = lax.dynamic_slice_in_dim(joined, mine * part, part, axis=0)
    down = lax.dynamic_slice_in_dim(w_down, mine * part * group, part * group, axis=0)
    down = jnp.concatenate([down[k * part : (k + 1) * part] for k in range(group)], axis=1)
    full = lax.all_gather(jnp.concatenate([joined, down], axis=1), AXES, axis=0, tiled=True)
    a, b = w_qkv.shape[1], w_qkv.shape[1] + w_out.shape[1]
    c = b + w_up.shape[1]
    full_down = full[:, c:].reshape(fsdp * dp, part, group, width)
    full_down = full_down.transpose(0, 2, 1, 3).reshape(fsdp * dp * part * group, width)
    return full[:, :a], full[:, a:b], full[:, b:c], full_down


def scatter_grads(g_qkv, g_out, g_up, g_down):
    fsdp = lax.axis_size("fsdp")
    dp = lax.axis_size("dp")
    width = g_out.shape[1]
    rows = g_out.shape[0] // fsdp
    if rows % (8 * dp):
        return tuple(
            lax.psum(lax.psum_scatter(g, "fsdp", scatter_dimension=0, tiled=True), "dp")
            for g in (g_qkv, g_out, g_up, g_down)
        )
    part = rows // dp
    group = g_down.shape[0] // g_out.shape[0]
    down = g_down.reshape(fsdp * dp, group, part, width).transpose(0, 2, 1, 3)
    down = down.reshape(fsdp * rows, group * width)
    joined = jnp.concatenate([g_qkv, g_out, g_up, down], axis=1).astype(LOW)
    mine = lax.psum_scatter(joined, AXES, scatter_dimension=0, tiled=True)
    full = lax.all_gather(mine, "dp", axis=0, tiled=True).astype(F32)
    a, b = g_qkv.shape[1], g_qkv.shape[1] + width
    c = b + g_up.shape[1]
    full_down = full[:, c:].reshape(dp, part, group, width).transpose(0, 2, 1, 3)
    return full[:, :a], full[:, a:b], full[:, b:c], full_down.reshape(rows * group, width)


def on_device(hidden_in, w_qkv, w_out, w_up, w_down, gain_attn, shift_attn, gain_ffn, shift_ffn, grad_listed, positions, counts):
    seqs, length, width = hidden_in.shape
    tokens = seqs * length
    most = positions.shape[1]
    norms = jnp.stack([gain_attn, shift_attn, gain_ffn, shift_ffn])
    norms = lax.all_gather(norms, "fsdp", axis=1, tiled=True).astype(F32)
    w_qkv, w_out, w_up, w_down = gather_weights(w_qkv, w_out, w_up, w_down)
    live = jnp.arange(most, dtype=jnp.int32)[None, :] < counts[:, None]
    onehot = (positions[:, :, None] == jnp.arange(length, dtype=jnp.int32)).astype(F32)
    rows_in = hidden_in.reshape(tokens, width)
    slope = slopes()
    scale = HEAD_DIM**-0.5
    qkv = mm(rows_in, w_qkv).astype(LOW)
    split = qkv.reshape(seqs, length, 3, HEADS, HEAD_DIM)
    q, k, v = split[:, :, 0], split[:, :, 1], split[:, :, 2]
    place = jnp.arange(length, dtype=F32)
    bias = -slope[:, None, None] * jnp.abs(place[:, None] - place[None, :])
    s = jnp.einsum("sqhc,skhc->shqk", q, k, preferred_element_type=F32) * scale + bias
    p = jax.nn.softmax(s, axis=-1).astype(LOW)
    att = jnp.einsum("shqk,skhc->sqhc", p, v, preferred_element_type=F32).astype(LOW)
    att = att.reshape(tokens, width)
    r1 = rows_in.astype(F32) + mm(att, w_out)
    unit1, _ = norm_parts(r1)
    h1 = unit1 * norms[0] + norms[1]
    h1_low = h1.astype(LOW)
    u = mm(h1_low, w_up)
    act = (jax.nn.gelu(u[:, :FF], approximate=False) * u[:, FF:]).astype(LOW)
    r2 = h1 + mm(act, w_down)
    unit2, _ = norm_parts(r2)
    layer_out = (unit2 * norms[2] + norms[3]).astype(LOW).reshape(seqs, length, width)
    def listed(a):
        return pick(onehot, a.reshape(seqs, length, -1)).reshape(seqs * most, -1)

    dy = jnp.where(live[:, :, None], grad_listed, 0).astype(F32).reshape(seqs * most, width)
    unit2_m, rstd2_m = norm_parts(listed(r2))
    g_gain_ffn = jnp.sum(dy * unit2_m, axis=0)
    g_shift_ffn = jnp.sum(dy, axis=0)
    dr2 = norm_back(dy, unit2_m, rstd2_m, norms[2])
    e2 = dr2.astype(LOW)
    h1_m = listed(h1_low)
    u_m = mm(h1_m, w_up)
    gate, up = u_m[:, :FF], u_m[:, FF:]
    cdf = 0.5 * (1.0 + lax.erf(gate * (0.5**0.5)))
    pdf = jnp.exp(-0.5 * gate * gate) * ((2.0 * jnp.pi) ** -0.5)
    gelu = gate * cdf
    act_m = (gelu * up).astype(LOW)
    g_down = jnp.einsum("nf,nd->fd", act_m, e2, preferred_element_type=F32)
    dact = jnp.einsum("nd,fd->nf", e2, w_down, preferred_element_type=F32)
    du = jnp.concatenate([dact * up * (cdf + gate * pdf), dact * gelu], axis=1).astype(LOW)
    g_up = jnp.einsum("nd,nf->df", h1_m, du, preferred_element_type=F32)
    dh1 = dr2 + jnp.einsum("nf,df->nd", du, w_up, preferred_element_type=F32)
    unit1_m, rstd1_m = norm_parts(listed(r1))
    g_gain_attn = jnp.sum(dh1 * unit1_m, axis=0)
    g_shift_attn = jnp.sum(dh1, axis=0)
    dr1 = norm_back(dh1, unit1_m, rstd1_m, norms[0])
    e1 = dr1.astype(LOW)
    g_out = jnp.einsum("nd,ne->de", listed(att), e1, preferred_element_type=F32)
    datt = jnp.einsum("ne,de->nd", e1, w_out, preferred_element_type=F32).astype(LOW)
    datt = datt.reshape(seqs, most, HEADS, HEAD_DIM)
    q_m = listed(qkv[:, :width]).reshape(seqs, most, HEADS, HEAD_DIM)
    away = jnp.abs(positions[:, :, None].astype(F32) - place[None, None, :])
    s_m = jnp.einsum("sqhc,skhc->shqk", q_m, k, preferred_element_type=F32) * scale
    p_m = jax.nn.softmax(s_m - slope[None, :, None, None] * away[:, None], axis=-1)
    dv = jnp.einsum("shqk,sqhc->skhc", p_m.astype(LOW), datt, preferred_element_type=F32)
    dp = jnp.einsum("sqhc,skhc->shqk", datt, v, preferred_element_type=F32)
    ds = (p_m * (dp - jnp.sum(dp * p_m, axis=-1, keepdims=True))).astype(LOW)
    dq_m = (jnp.einsum("shqk,skhc->sqhc", ds, k, preferred_element_type=F32) * scale).astype(LOW)
    dk = (jnp.einsum("shqk,sqhc->skhc", ds, q_m, preferred_element_type=F32) * scale).astype(LOW)
    put = (onehot * live[:, :, None]).astype(LOW)
    dq = jnp.einsum("svj,svd->sjd", put, dq_m.reshape(seqs, most, width), preferred_element_type=F32)
    dqkv = jnp.concatenate(
        [dq.astype(LOW).reshape(tokens, width), dk.reshape(tokens, width), dv.astype(LOW).reshape(tokens, width)], axis=1
    )
    g_qkv = jnp.einsum("nd,ne->de", rows_in, dqkv, preferred_element_type=F32)
    dr1_all = jnp.einsum("svj,svd->sjd", onehot * live[:, :, None], dr1.reshape(seqs, most, width), precision=lax.Precision.HIGHEST)
    grad_in = dr1_all.reshape(tokens, width) + jnp.einsum("ne,de->nd", dqkv, w_qkv, preferred_element_type=F32)
    owned = scatter_grads(g_qkv, g_out, g_up, g_down)
    small = lax.psum(jnp.stack([g_gain_attn, g_shift_attn, g_gain_ffn, g_shift_ffn]), AXES)
    share = width // lax.axis_size("fsdp")
    small = lax.dynamic_slice_in_dim(small, lax.axis_index("fsdp") * share, share, axis=1)
    return (
        layer_out,
        grad_in.reshape(seqs, length, width),
        *owned,
        small[0],
        small[1],
        small[2],
        small[3],
    )


def solution(mesh):
    rows3 = P(("fsdp", "dp"), None, None)
    rows2 = P("fsdp", None)
    rows1 = P("fsdp")
    shape = dict(mesh.shape)
    step = on_block if shape == {"fsdp": SHARDS, "dp": QUARTERS} else on_device
    return jax.shard_map(
        step,
        mesh=mesh,
        in_specs=(rows3, rows2, rows2, rows2, rows2, rows1, rows1, rows1, rows1, rows3, P(("fsdp", "dp"), None), P(("fsdp", "dp"))),
        out_specs=(rows3, rows3, rows2, rows2, rows2, rows2, rows1, rows1, rows1, rows1),
        check_vma=False,
    )
```

```python
import functools

import jax
import jax.numpy as jnp
from jax import lax
from jax.experimental import pallas as pl
from jax.experimental.pallas import tpu as pltpu
from jax.sharding import PartitionSpec as P

HEADS = 12
HEAD_DIM = 64
EPS = 1e-12
F32 = jnp.float32
LOW = jnp.bfloat16
AXES = ("fsdp", "dp")
D = 768
ROWS = 96
LINE = 4
SHARDS = D // ROWS
QUARTERS = 4
EXACT = lax.Precision.HIGHEST
SCALE = HEAD_DIM**-0.5
VMEM = pl.BlockSpec(memory_space=pltpu.VMEM)
SMEM = pl.BlockSpec(memory_space=pltpu.SMEM)
BIG = pltpu.CompilerParams(vmem_limit_bytes=60 * 1024 * 1024)


def out(shape, dtype):
    return jax.ShapeDtypeStruct(shape, dtype)


def cost(us):
    return pl.CostEstimate(flops=0, bytes_accessed=int(us * 3.0e6), transcendentals=0)


def mm(a, b):
    return jnp.dot(a, b, preferred_element_type=F32)


def mm_nt(a, b):
    return lax.dot_general(a, b, (((1,), (1,)), ((), ())), preferred_element_type=F32)


def mm_tn(a, b):
    return lax.dot_general(a, b, (((0,), (0,)), ((), ())), preferred_element_type=F32)


def norm_parts(value):
    center = value - jnp.mean(value, axis=-1, keepdims=True)
    rstd = lax.rsqrt(jnp.mean(center * center, axis=-1, keepdims=True) + EPS)
    return center * rstd, rstd


def norm_back(grad, unit, rstd, gain):
    scaled = grad * gain
    return rstd * (
        scaled
        - jnp.mean(scaled, axis=-1, keepdims=True)
        - unit * jnp.mean(scaled * unit, axis=-1, keepdims=True)
    )


def onehot(pos_ref, seq, most, length):
    spots = lax.broadcasted_iota(jnp.int32, (most, length), 1)
    return spots == pos_ref[pl.ds(seq * most, most), :]


def gelu_parts(gate):
    cdf = 0.5 * (1.0 + lax.erf(gate * (0.5**0.5)))
    pdf = jnp.exp(-0.5 * gate * gate) * ((2.0 * jnp.pi) ** -0.5)
    return gate * cdf, cdf + gate * pdf


def slope_of(head):
    return 2.0 ** (-8.0 * (head + 1.0) / HEADS)


def block(ref, *index):
    value = ref[index] if index else ref[...]
    return value.reshape(-1, value.shape[-1])


EXTRA = 8
TAIL = 16
HALVES = ((0, 48), (48, 56))
KEYS = [(ry, rx, rc) for rc in (0, 1) for rx in (0, 1) for ry in (0, 1)]


def attention_kernel(seqs, most, where_ref, slope_ref, x_ref, norm_ref, pos_ref, *rest):
    lines, rest = rest[:16], rest[16:]
    qkv_ref, h1_ref, att_m_ref, h1_m_ref, q_m_ref, r1_m_ref, w_ref, att_ref, r1_ref, sem = rest
    z, y, c_x = where_ref[0], where_ref[1], where_ref[4]
    copies = []
    for n, (ry, rx, rc) in enumerate(KEYS):
        j = jnp.bitwise_xor(c_x, 2 * rx + rc)
        for r in range(LINE):
            shard = 2 * lax.rem(z + LINE - r, LINE) + jnp.bitwise_xor(y, ry)
            for half, (start, size) in enumerate(HALVES):
                size = min(size, ROWS - start)
                copies.append(
                    pltpu.make_async_copy(
                        lines[2 * n + half].at[r, pl.ds(0, size)], w_ref.at[shard, j, pl.ds(start, size)], sem
                    )
                )
    for copy in copies:
        copy.start()
    for copy in copies:
        copy.wait()
    length = x_ref.shape[0] // seqs
    step = 256

    @pl.loop(0, 3 * D // step)
    def _(n):
        j = n // (D // step)
        lane = pl.multiple_of((n - j * (D // step)) * step, step)
        w = w_ref[:, j, :, pl.ds(lane, step)].reshape(D, step)
        qkv_ref[:, pl.ds(pl.multiple_of(n * step, step), step)] = mm(x_ref[...], w).astype(LOW)

    first = lax.broadcasted_iota(jnp.int32, (length, 128), 1) < HEAD_DIM
    row = lax.broadcasted_iota(jnp.int32, (length, length), 0)
    col = lax.broadcasted_iota(jnp.int32, (length, length), 1)
    away = jnp.abs(row - col).astype(F32)

    @pl.loop(0, HEADS // 2)
    def _(t):
        lane = pl.multiple_of(t * 128, 128)
        bias = jnp.concatenate([slope_ref[2 * t] * away, slope_ref[2 * t + 1] * away], axis=0)
        for s in range(seqs):
            rows = slice(s * length, (s + 1) * length)
            q = qkv_ref[rows, pl.ds(lane, 128)]
            k = qkv_ref[rows, pl.ds(D + lane, 128)]
            v = qkv_ref[rows, pl.ds(2 * D + lane, 128)]
            zero = jnp.zeros_like(q)
            both = jnp.concatenate([jnp.where(first, q, zero), jnp.where(first, zero, q)], axis=0)
            score = mm_nt(both, k) * SCALE - bias
            e = jnp.exp(score - jnp.max(score, axis=-1, keepdims=True))
            p = (e * (1.0 / jnp.sum(e, axis=-1, keepdims=True))).astype(LOW)
            mixed = mm(p, v)
            att_ref[rows, pl.ds(lane, 128)] = jnp.where(first, mixed[:length], mixed[length:]).astype(LOW)

    @pl.loop(0, D // step)
    def _(n):
        lane = pl.multiple_of(n * step, step)
        w = w_ref[:, 3, :, pl.ds(lane, step)].reshape(D, step)
        r1_ref[:, pl.ds(lane, step)] = x_ref[:, pl.ds(lane, step)].astype(F32) + mm(att_ref[...], w)

    for s in range(seqs):
        rows = slice(s * length, (s + 1) * length)
        listed = slice(s * most, (s + 1) * most)
        unit, _ = norm_parts(r1_ref[rows, :])
        h1 = unit * norm_ref[0:1, :] + norm_ref[1:2, :]
        h1_ref[rows, :] = h1
        hot = onehot(pos_ref, s, most, length)
        hot_low = hot.astype(LOW)
        r1_m_ref[listed, :] = jnp.dot(hot.astype(F32), r1_ref[rows, :], precision=EXACT, preferred_element_type=F32)
        h1_m_ref[listed, :] = mm(hot_low, h1.astype(LOW)).astype(LOW)
        att_m_ref[listed, :] = mm(hot_low, att_ref[rows, :]).astype(LOW)
        q_m_ref[listed, :] = mm(hot_low, qkv_ref[rows, 0:D]).astype(LOW)


def attention_forward(where, x, lines, norms, pos, slopes, seqs):
    tokens = x.shape[0]
    listed = pos.shape[0]
    return pl.pallas_call(
        functools.partial(attention_kernel, seqs, listed // seqs),
        out_shape=(
            out((tokens, 3 * D), LOW),
            out((tokens, D), F32),
            out((listed, D), LOW),
            out((listed, D), LOW),
            out((listed, D), LOW),
            out((listed, D), F32),
            out((SHARDS, QUARTERS, ROWS, D), LOW),
        ),
        in_specs=[SMEM, SMEM, VMEM, VMEM, VMEM] + [pl.BlockSpec(memory_space=pl.ANY)] * 16,
        out_specs=(VMEM,) * 7,
        scratch_shapes=[pltpu.VMEM((tokens, D), LOW), pltpu.VMEM((tokens, D), F32), pltpu.SemaphoreType.DMA],
        compiler_params=BIG,
        cost_estimate=cost(20),
        name="attention_forward",
    )(where, slopes, x, norms, pos, *lines)


def ffn_kernel(seqs, most, h1_ref, gate_ref, up_ref, down_ref, norm_ref, pos_ref, dy_ref, y_ref, dr2_ref, e2_ref, small_ref, low_ref, act_ref, acc_ref):
    j = pl.program_id(0)
    tokens = h1_ref.shape[0]
    length = tokens // seqs
    step = 256

    @pl.when(j == 0)
    def _():
        low_ref[...] = h1_ref[...].astype(LOW)
        acc_ref[...] = h1_ref[...]

    @pl.loop(0, D // step)
    def _(n):
        lane = pl.multiple_of(n * step, step)
        gate = mm(low_ref[...], gate_ref[:, :, pl.ds(lane, step)].reshape(D, step))
        up = mm(low_ref[...], up_ref[:, :, pl.ds(lane, step)].reshape(D, step))
        cdf = 0.5 * (1.0 + lax.erf(gate * (0.5**0.5)))
        act_ref[:, pl.ds(lane, step)] = (gate * cdf * up).astype(LOW)

    @pl.loop(0, D // step)
    def _(n):
        lane = pl.multiple_of(n * step, step)
        acc_ref[:, pl.ds(lane, step)] += mm(act_ref[...], down_ref[:, :, :, pl.ds(lane, step)].reshape(D, step))

    @pl.when(j == QUARTERS - 1)
    def _():
        gain = norm_ref[2:3, :]
        small = [jnp.zeros((1, D), F32)] * 2
        for s in range(seqs):
            rows = slice(s * length, (s + 1) * length)
            listed = slice(s * most, (s + 1) * most)
            unit, _ = norm_parts(acc_ref[rows, :])
            y_ref[rows, :] = (unit * gain + norm_ref[3:4, :]).astype(LOW)
            hot = onehot(pos_ref, s, most, length).astype(F32)
            picked = jnp.dot(hot, acc_ref[rows, :], precision=EXACT, preferred_element_type=F32)
            unit_m, rstd_m = norm_parts(picked)
            dy = dy_ref[listed, :].astype(F32)
            small = [small[0] + jnp.sum(dy * unit_m, axis=0, keepdims=True), small[1] + jnp.sum(dy, axis=0, keepdims=True)]
            dr2 = norm_back(dy, unit_m, rstd_m, gain)
            dr2_ref[listed, :] = dr2
            e2_ref[listed, :] = dr2.astype(LOW)
        small_ref[...] = jnp.concatenate(small, axis=0)


def ffn_forward(h1, w_ffn, norms, pos, dy, seqs):
    tokens = h1.shape[0]
    listed = pos.shape[0]
    whole = lambda shape: pl.BlockSpec(shape, lambda j: (0,) * len(shape), pipeline_mode=pl.Buffered(1))
    return pl.pallas_call(
        functools.partial(ffn_kernel, seqs, listed // seqs),
        out_shape=(out((tokens, D), LOW), out((listed, D), F32), out((listed, D), LOW), out((2, D), F32)),
        grid=(QUARTERS,),
        in_specs=[
            whole((tokens, D)),
            pl.BlockSpec((SHARDS, None, None, ROWS, D), lambda j: (0, j, 0, 0, 0)),
            pl.BlockSpec((SHARDS, None, None, ROWS, D), lambda j: (0, j, 1, 0, 0)),
            pl.BlockSpec((SHARDS // QUARTERS, QUARTERS, None, ROWS, D), lambda j: (j, 0, 2, 0, 0)),
            whole(norms.shape),
            whole(pos.shape),
            whole(dy.shape),
        ],
        out_specs=(
            pl.BlockSpec((tokens, D), lambda j: (0, 0)),
            pl.BlockSpec((listed, D), lambda j: (0, 0)),
            pl.BlockSpec((listed, D), lambda j: (0, 0)),
            pl.BlockSpec((2, D), lambda j: (0, 0)),
        ),
        scratch_shapes=[pltpu.VMEM((tokens, D), LOW), pltpu.VMEM((tokens, D), LOW), pltpu.VMEM((tokens, D), F32)],
        compiler_params=BIG,
        cost_estimate=cost(16),
        name="ffn_forward",
    )(h1, w_ffn, w_ffn, w_ffn, norms, pos, dy)


def ffn_again_kernel(where_ref, h_ref, gate_ref, up_ref, act_ref, to_gate_ref, to_up_ref):
    step = 256

    @pl.loop(0, D // step)
    def _(n):
        lane = pl.multiple_of(n * step, step)
        rows = block(h_ref)
        gate = mm(rows, gate_ref[:, :, pl.ds(lane, step)].reshape(D, step))
        up = mm(rows, up_ref[:, :, pl.ds(lane, step)].reshape(D, step))
        value, slope = gelu_parts(gate)
        act_ref[:, pl.ds(lane, step)] = (value * up).astype(LOW)
        to_gate_ref[:, pl.ds(lane, step)] = slope * up
        to_up_ref[:, pl.ds(lane, step)] = value


def quarter_specs(which):
    specs = {
        "gate": pl.BlockSpec((SHARDS, None, None, ROWS, D), lambda g, w: (0, w[4], 0, 0, 0)),
        "up": pl.BlockSpec((SHARDS, None, None, ROWS, D), lambda g, w: (0, w[4], 1, 0, 0)),
        "down": pl.BlockSpec((SHARDS // QUARTERS, QUARTERS, None, ROWS, D), lambda g, w: (w[4], 0, 2, 0, 0)),
    }
    return [specs[name] for name in which]


def at_once(shape):
    return pl.BlockSpec(shape, lambda g, w: (0,) * len(shape))


def ffn_again(where, h_all, w_ffn):
    rows = h_all.shape[0] * h_all.shape[1]
    return pl.pallas_call(
        ffn_again_kernel,
        out_shape=(out((rows, D), LOW), out((rows, D), F32), out((rows, D), F32)),
        grid_spec=pltpu.PrefetchScalarGridSpec(
            num_scalar_prefetch=1,
            grid=(1,),
            in_specs=[at_once(h_all.shape), *quarter_specs(["gate", "up"])],
            out_specs=(at_once((rows, D)),) * 3,
        ),
        compiler_params=BIG,
        cost_estimate=cost(6),
        name="ffn_again",
    )(where, h_all, w_ffn, w_ffn)


def ffn_back_kernel(where_ref, e_ref, to_gate_ref, to_up_ref, gate_ref, up_ref, down_ref, dgate_ref, dup_ref, keep_ref, send_ref):
    listed = e_ref.shape[1]
    half = QUARTERS // 2
    for n in range(SHARDS // QUARTERS):
        lanes = slice(n * QUARTERS * ROWS, (n + 1) * QUARTERS * ROWS)
        dact = mm_nt(block(e_ref), block(down_ref, n))
        dgate_ref[:, lanes] = (dact * to_gate_ref[:, lanes]).astype(LOW)
        dup_ref[:, lanes] = (dact * to_up_ref[:, lanes]).astype(LOW)
    for n in range(2):
        shards = slice(n * SHARDS // 2, (n + 1) * SHARDS // 2)
        lanes = slice(n * D // 2, (n + 1) * D // 2)
        part = mm_nt(dgate_ref[...], block(gate_ref, shards)) + mm_nt(dup_ref[...], block(up_ref, shards))
        for r in range(half):
            keep_ref[r, :, lanes] = part[2 * r * listed : (2 * r + 1) * listed]
            send_ref[r, :, lanes] = part[(2 * r + 1) * listed : (2 * r + 2) * listed].astype(LOW)


def ffn_back(where, e_all, to_gate, to_up, w_ffn):
    count, listed, _ = e_all.shape
    rows = count * listed
    return pl.pallas_call(
        ffn_back_kernel,
        out_shape=(out((rows, D), LOW), out((rows, D), LOW), out((count // 2, listed, D), F32), out((count // 2, listed, D), LOW)),
        grid_spec=pltpu.PrefetchScalarGridSpec(
            num_scalar_prefetch=1,
            grid=(1,),
            in_specs=[at_once(e_all.shape), at_once((rows, D)), at_once((rows, D)), *quarter_specs(["gate", "up", "down"])],
            out_specs=(at_once((rows, D)), at_once((rows, D)), at_once((count // 2, listed, D)), at_once((count // 2, listed, D))),
        ),
        compiler_params=BIG,
        cost_estimate=cost(7),
        name="ffn_back",
    )(where, e_all, to_gate, to_up, w_ffn, w_ffn, w_ffn)


def weight_grad_kernel(where_ref, a_ref, b_ref, keep_ref, send_ref, full_ref):
    z, y = where_ref[0], where_ref[1]
    b = block(b_ref)
    step = 256

    @pl.loop(0, D // step)
    def _(n):
        lane = pl.multiple_of(n * step, step)
        a = block(a_ref, *([slice(None)] * (len(a_ref.shape) - 1)), pl.ds(lane, step))
        full_ref[pl.ds(lane, step), :] = mm_tn(a, b)

    for r in range(LINE):
        base = 2 * lax.rem(z + r, LINE)
        for other, ref in ((0, keep_ref), (1, send_ref)):
            start = (base + (y if other == 0 else 1 - y)) * ROWS
            ref[r] = full_ref[pl.ds(pl.multiple_of(start, 8), ROWS), :].astype(LOW)


def weight_grad(where, a, b):
    shape = (LINE, ROWS, D)
    rows = a.size // D
    return pl.pallas_call(
        weight_grad_kernel,
        out_shape=(out(shape, LOW), out(shape, LOW)),
        in_specs=[SMEM, VMEM, VMEM],
        out_specs=(VMEM, VMEM),
        scratch_shapes=[pltpu.VMEM((D, D), F32)],
        compiler_params=BIG,
        cost_estimate=cost(4),
        name="weight_grad",
    )(where, a, b)


def norm_back_kernel(dr2_ref, part_ref, came_ref, r1_ref, w_ref, norm_ref, dr1_ref, low_ref, datt_ref, small_ref):
    dh1 = dr2_ref[...] + part_ref[...] + came_ref[...].astype(F32)
    unit, rstd = norm_parts(r1_ref[...])
    small_ref[0:1, :] = jnp.sum(dh1 * unit, axis=0, keepdims=True)
    small_ref[1:2, :] = jnp.sum(dh1, axis=0, keepdims=True)
    dr1 = norm_back(dh1, unit, rstd, norm_ref[0:1, :])
    dr1_ref[...] = dr1
    low = dr1.astype(LOW)
    low_ref[...] = low
    for n in range(2):
        lanes = slice(n * D // 2, (n + 1) * D // 2)
        datt_ref[:, lanes] = mm_nt(low, block(w_ref, slice(n * SHARDS // 2, (n + 1) * SHARDS // 2))).astype(LOW)


def norm_back_call(dr2, part, came, r1_m, w_attn, norms):
    listed = dr2.shape[0]
    same = lambda shape: pl.BlockSpec(shape, lambda g: (0,) * len(shape))
    rows = same((listed, D))
    return pl.pallas_call(
        norm_back_kernel,
        out_shape=(out((listed, D), F32), out((listed, D), LOW), out((listed, D), LOW), out((2, D), F32)),
        grid=(1,),
        in_specs=[rows, rows, rows, rows, pl.BlockSpec((SHARDS, None, ROWS, D), lambda g: (0, 3, 0, 0)), same((4, D))],
        out_specs=(rows, rows, rows, same((2, D))),
        compiler_params=BIG,
        cost_estimate=cost(4),
        name="norm_back",
    )(dr2, part, came, r1_m, w_attn, norms)


def attention_back_kernel(seqs, most, slope_ref, datt_ref, q_ref, qkv_ref, pos_ref, rhs_ref, away_ref, hot_ref):
    length = qkv_ref.shape[0] // seqs
    listed = seqs * most
    first_m = lax.broadcasted_iota(jnp.int32, (most, 128), 1) < HEAD_DIM
    spots = lax.broadcasted_iota(jnp.int32, (listed, length), 1)
    away_ref[...] = jnp.abs(pos_ref[...] - spots).astype(F32)
    hot_ref[...] = (spots == pos_ref[...]).astype(LOW)

    def both(value):
        zero = jnp.zeros_like(value)
        return jnp.concatenate([jnp.where(first_m, value, zero), jnp.where(first_m, zero, value)], axis=0)

    @pl.loop(0, HEADS // 2)
    def _(t):
        lane = pl.multiple_of(t * 128, 128)
        for s in range(seqs):
            rows = slice(s * length, (s + 1) * length)
            mine = slice(s * most, (s + 1) * most)
            away = away_ref[mine, :]
            q = both(q_ref[mine, pl.ds(lane, 128)])
            da = both(datt_ref[mine, pl.ds(lane, 128)])
            k = qkv_ref[rows, pl.ds(D + lane, 128)]
            v = qkv_ref[rows, pl.ds(2 * D + lane, 128)]
            bias = jnp.concatenate([slope_ref[2 * t] * away, slope_ref[2 * t + 1] * away], axis=0)
            score = mm_nt(q, k) * SCALE - bias
            e = jnp.exp(score - jnp.max(score, axis=-1, keepdims=True))
            p = e * (1.0 / jnp.sum(e, axis=-1, keepdims=True))
            dp = mm_nt(da, v)
            ds = (p * (dp - jnp.sum(dp * p, axis=-1, keepdims=True))).astype(LOW)
            dq = mm(ds, k)
            dq = (jnp.where(first_m, dq[:most], dq[most:]) * SCALE).astype(LOW)
            rhs_ref[rows, pl.ds(lane, 128)] = mm_tn(hot_ref[mine, :], dq).astype(LOW)
            rhs_ref[rows, pl.ds(D + lane, 128)] = (mm_tn(ds, q) * SCALE).astype(LOW)
            rhs_ref[rows, pl.ds(2 * D + lane, 128)] = mm_tn(p.astype(LOW), da).astype(LOW)


def attention_back(datt, q_m, qkv, pos, slopes, seqs):
    tokens = qkv.shape[0]
    listed = pos.shape[0]
    return pl.pallas_call(
        functools.partial(attention_back_kernel, seqs, listed // seqs),
        out_shape=out((tokens, 3 * D), LOW),
        in_specs=[SMEM] + [VMEM] * 4,
        out_specs=VMEM,
        scratch_shapes=[pltpu.VMEM((listed, tokens // seqs), F32), pltpu.VMEM((listed, tokens // seqs), LOW)],
        compiler_params=BIG,
        cost_estimate=cost(15),
        name="attention_back",
    )(slopes, datt, q_m, qkv, pos)


def attention_grads_kernel(where_ref, flip_ref, rhs_ref, att_ref, low_ref, small_attn_ref, small_ffn_ref, keep0_ref, keep1_ref, away0_ref, away1_ref, full_ref, tail_ref):
    z, y, mine = where_ref[0], where_ref[1], where_ref[4]
    half = ROWS // 2
    step = 256
    tail_ref[...] = jnp.zeros(tail_ref.shape, LOW)
    small = jnp.concatenate([small_attn_ref[...], small_ffn_ref[...]], axis=0).astype(LOW)
    for n in range(SHARDS):
        tail_ref[n, 0:4, 0:ROWS] = small[:, n * ROWS : (n + 1) * ROWS]
    for rc in (1, 0):
        cut0_ref, cut1_ref = (keep0_ref, keep1_ref) if rc == 0 else (away0_ref, away1_ref)
        for rx in (0, 1):
            j = jnp.bitwise_xor(mine, 2 * rx + rc)

            @pl.when(j == 3)
            def _():
                for n in range(D // step):
                    rows = slice(n * step, (n + 1) * step)
                    full_ref[rows, :] = mm_tn(att_ref[:, rows], low_ref[...])

            @pl.when(j != 3)
            def _():
                @pl.loop(0, D // step)
                def _(n):
                    lane = pl.multiple_of(n * step, step)
                    cols = pl.ds(pl.multiple_of(j * D + n * step, step), step)
                    full_ref[:, pl.ds(lane, step)] = mm(flip_ref[...], rhs_ref[:, cols])

            for rz in range(LINE):
                base = 2 * lax.rem(z + rz, LINE)
                for ry in (0, 1):
                    shard = base + (y if ry == 0 else 1 - y)
                    start = shard * ROWS
                    cut0_ref[rx, ry, rz] = full_ref[pl.ds(pl.multiple_of(start, 8), half), :].astype(LOW)
                    cut1_ref[ry, rx, rz, 0:half] = full_ref[pl.ds(pl.multiple_of(start + half, 8), half), :].astype(LOW)
                    cut1_ref[ry, rx, rz, half:] = tail_ref[shard]


def attention_grads(where, x_flip, rhs, att_m, low, small_attn, small_ffn):
    half = ROWS // 2
    return pl.pallas_call(
        attention_grads_kernel,
        out_shape=(out((2, 2, LINE, half, D), LOW), out((2, 2, LINE, half + TAIL, D), LOW)) * 2,
        in_specs=[SMEM] + [VMEM] * 6,
        out_specs=(VMEM,) * 4,
        scratch_shapes=[pltpu.VMEM((D, D), F32), pltpu.VMEM((SHARDS, TAIL, D), LOW)],
        compiler_params=BIG,
        cost_estimate=cost(10),
        name="attention_grads",
    )(where, x_flip, rhs, att_m, low, small_attn, small_ffn)


def input_grad_kernel(seqs, rhs_ref, w_ref, dr1_ref, pos_ref, out_ref):
    length = out_ref.shape[0] // seqs
    most = dr1_ref.shape[0] // seqs
    for n in range(2):
        lanes = slice(n * D // 2, (n + 1) * D // 2)
        shards = slice(n * SHARDS // 2, (n + 1) * SHARDS // 2)
        total = mm_nt(rhs_ref[:, 0:D], block(w_ref, shards, 0))
        total += mm_nt(rhs_ref[:, D : 2 * D], block(w_ref, shards, 1))
        total += mm_nt(rhs_ref[:, 2 * D : 3 * D], block(w_ref, shards, 2))
        for s in range(seqs):
            rows = slice(s * length, (s + 1) * length)
            hot = (lax.broadcasted_iota(jnp.int32, (length, most), 0) == pos_ref[s : s + 1, :]).astype(F32)
            spread = jnp.dot(hot, dr1_ref[s * most : (s + 1) * most, lanes], precision=EXACT, preferred_element_type=F32)
            out_ref[rows, lanes] = total[rows] + spread


def input_grad(rhs, w_attn, dr1, positions):
    tokens = rhs.shape[0]
    return pl.pallas_call(
        functools.partial(input_grad_kernel, positions.shape[0]),
        out_shape=out((tokens, D), F32),
        in_specs=[VMEM] * 4,
        out_specs=VMEM,
        compiler_params=BIG,
        cost_estimate=cost(8),
        name="input_grad",
    )(rhs, w_attn, dr1, positions)


def place(z, y, x, c):
    return (2 * z + y) * 4 + 2 * x + c


def grid_perm(move):
    return [
        (place(z, y, x, c), place(*move(z, y, x, c)))
        for z in range(4)
        for y in range(2)
        for x in range(2)
        for c in range(2)
    ]


MOVES = {
    "x": grid_perm(lambda z, y, x, c: (z, y, 1 - x, c)),
    "y": grid_perm(lambda z, y, x, c: (z, 1 - y, x, c)),
    "c": grid_perm(lambda z, y, x, c: (z, y, x, 1 - c)),
    1: grid_perm(lambda z, y, x, c: ((z + 1) % 4, y, x, c)),
    2: grid_perm(lambda z, y, x, c: ((z + 2) % 4, y, x, c)),
    3: grid_perm(lambda z, y, x, c: ((z + 3) % 4, y, x, c)),
    "down": [(m * 4 + q, (2 * q + m // 4) * 4 + m % 4) for m in range(8) for q in range(4)],
}


def send(value, move):
    return lax.ppermute(value, AXES, MOVES[move])


def share_dp(value):
    other = send(value, "x")
    return value, send(value, "c"), other, send(other, "c")


def after(value, *earlier):
    return lax.optimization_barrier((value, *earlier))[0]


def add(kept, got):
    return kept.astype(F32) + got.astype(F32)


def line_parts(keep, got):
    return [add(keep[r], got[r]).astype(LOW) for r in (1, 2, 3)]


def line_send(parts):
    return [send(value, r) for r, value in zip((1, 2, 3), parts)]


def line_add(keep, got, came):
    return (add(keep[0], got[0]) + came[0].astype(F32) + came[1].astype(F32) + came[2].astype(F32)).astype(LOW)


def finish_ffn_kernel(where_ref, *rest):
    pieces, (down_ref, up_ref) = rest[:QUARTERS], rest[QUARTERS:]
    mine = where_ref[4]
    for n, ref in enumerate(pieces):
        j = jnp.bitwise_xor(mine, n)
        down_ref[pl.ds(pl.multiple_of(j * ROWS, 8), ROWS), :] = ref[0].astype(F32)
        for half in (0, 1):
            up_ref[:, pl.ds(pl.multiple_of((half * QUARTERS + j) * D, D), D)] = ref[1 + half].astype(F32)


def finish_attention_kernel(where_ref, *rest):
    pieces, (qkv_ref, out_ref, held_ref) = rest[:QUARTERS], rest[QUARTERS:]
    mine = where_ref[4]
    for n, ref in enumerate(pieces):
        held_ref[jnp.bitwise_xor(mine, n)] = ref[...].astype(F32)
    for j in range(3):
        qkv_ref[:, j * D : (j + 1) * D] = held_ref[j]
    out_ref[...] = held_ref[3]


def finish_ffn(where, pieces):
    return pl.pallas_call(
        finish_ffn_kernel,
        out_shape=(out((QUARTERS * ROWS, D), F32), out((ROWS, 2 * QUARTERS * D), F32)),
        in_specs=[SMEM] + [VMEM] * QUARTERS,
        out_specs=(VMEM, VMEM),
        compiler_params=BIG,
        cost_estimate=cost(4),
        name="finish_ffn",
    )(where, *pieces)


def finish_attention(where, pieces):
    return pl.pallas_call(
        finish_attention_kernel,
        out_shape=(out((ROWS, 3 * D), F32), out((ROWS, D), F32)),
        in_specs=[SMEM] + [VMEM] * QUARTERS,
        out_specs=(VMEM, VMEM),
        scratch_shapes=[pltpu.VMEM((QUARTERS, ROWS, D), F32)],
        compiler_params=BIG,
        cost_estimate=cost(2),
        name="finish_attention",
    )(where, *pieces)


def spread(piece, order):
    got = {frozenset(): piece}
    for step in (*order, "c"):
        for key in list(got):
            got[key | {step}] = send(got[key], step)
    return [got[frozenset(n for n, b in zip("yxc", key) if b)] for key in KEYS]


def on_block(hidden_in, w_qkv, w_out, w_up, w_down, gain_attn, shift_attn, gain_ffn, shift_ffn, grad_listed, positions, counts):
    seqs, length, width = hidden_in.shape
    tokens = seqs * length
    most = positions.shape[1]
    i, j = lax.axis_index("fsdp"), lax.axis_index("dp")
    where = jnp.stack([i // 2, i % 2, j // 2, j % 2, j]).astype(jnp.int32)
    ff = w_down.shape[0] * SHARDS
    attn_piece = lax.dynamic_slice_in_dim(jnp.concatenate([w_qkv, w_out], axis=1), j * D, D, axis=1)
    norms = jnp.concatenate([gain_attn, shift_attn, gain_ffn, shift_ffn, jnp.zeros((D - 4 * ROWS,), LOW)])
    attn_piece = jnp.concatenate([attn_piece, jnp.broadcast_to(norms, (EXTRA, D))], axis=0)
    line = jnp.stack([attn_piece] + [send(attn_piece, r) for r in (1, 2, 3)])
    x = hidden_in.reshape(tokens, width)
    line, x_flip = lax.optimization_barrier((line, x.T))
    halves = [
        spread(line[:, start : start + size], order)
        for (start, size), order in zip(HALVES, (("y", "x"), ("x", "y")))
    ]
    lines = [half[n] for n in range(len(KEYS)) for half in halves]
    ffn_piece = jnp.stack(
        [
            lax.dynamic_slice_in_dim(w_up, j * D, D, axis=1),
            lax.dynamic_slice_in_dim(w_up, ff + j * D, D, axis=1),
            lax.dynamic_slice_in_dim(w_down, j * ROWS, ROWS, axis=0),
        ]
    )
    w_ffn = lax.all_gather(ffn_piece, AXES, axis=0, tiled=False).reshape(SHARDS, QUARTERS, 3, ROWS, D)
    tails = jnp.stack([halves[1][n][:, 48, : 4 * ROWS] for n in range(2)])
    tails = jnp.where(i % 2 == 0, tails, tails[::-1])
    tails = jnp.roll(tails[:, ::-1], i // 2 + 1, axis=1)
    norms = tails.transpose(1, 0, 2).reshape(SHARDS, 4, ROWS).transpose(1, 0, 2).reshape(4, D).astype(F32)
    slopes = jnp.exp2(-8.0 * (jnp.arange(HEADS, dtype=F32) + 1.0) / HEADS)
    pos = positions.reshape(seqs * most, 1)
    live = jnp.arange(most, dtype=jnp.int32)[None, :] < counts[:, None]
    dy = jnp.where(live[:, :, None], grad_listed, jnp.zeros_like(grad_listed)).reshape(seqs * most, width)

    qkv, h1, att_m, h1_m, q_m, r1_m, w_attn = attention_forward(where, x, lines, norms, pos, slopes, seqs)
    h_all = jnp.stack(share_dp(h1_m))
    h1, h_all = lax.optimization_barrier((h1, h_all))
    layer_out, dr2, e2, small_ffn = ffn_forward(h1, w_ffn, norms, pos, dy, seqs)
    act, to_gate, to_up = ffn_again(where, h_all, w_ffn)
    other = after(send(e2, "x"), act)
    e_all = jnp.stack([e2, send(e2, "c"), other, send(other, "c")])
    dgate, dup, keep, away = ffn_back(where, e_all, to_gate, to_up, w_ffn)
    part = add(keep, send(away, "c"))
    part, part_away = part[0], part[1].astype(LOW)
    keep_d, away_d = weight_grad(where, act, e_all)
    came = send(part_away, "x")
    got_d = send(away_d, "y")
    keep_g, away_g = weight_grad(where, after(h_all, (away_d, part_away)), dgate)
    got_g = send(away_g, "y")
    keep_u, away_u = weight_grad(where, after(h_all, (away_g, came)), dup)
    got_u = send(away_u, "y")
    dr1, low, datt, small_attn = norm_back_call(dr2, part, after(came, away_u), r1_m, w_attn, norms)
    rhs = attention_back(datt, q_m, qkv, pos, slopes, seqs)
    got_d, got_g, got_u, rhs = lax.optimization_barrier((got_d, got_g, got_u, rhs))
    parts_d = line_parts(keep_d, got_d)
    line_d = line_send(parts_d)
    keep0, keep1, away0, away1 = attention_grads(where, x_flip, after(rhs, parts_d), att_m, low, small_attn, small_ffn)
    away0, away1, line_d = lax.optimization_barrier((away0, away1, line_d))
    came0, came1 = send(away0, "c"), send(away1, "c")
    keep_gu, got_gu = jnp.concatenate([keep_g, keep_u], axis=1), jnp.concatenate([got_g, got_u], axis=1)
    parts_gu = line_parts(keep_gu, after(got_gu, away0))
    line_gu = line_send(parts_gu)
    g_down = send(line_add(keep_d, got_d, line_d), "down")
    away0, away1 = add(keep0[1], came0[1]).astype(LOW), add(keep1[1], came1[1]).astype(LOW)
    got0, got1 = send(away0, "x"), send(away1, "y")
    grad_in = input_grad(after(rhs, (away0, away1)), w_attn, dr1, positions)
    g_down, line_gu, grad_in = lax.optimization_barrier((g_down, line_gu, grad_in))
    g_ffn = jnp.concatenate([g_down, line_add(keep_gu, got_gu, line_gu)]).reshape(3, ROWS, D)
    got0, got1 = after((got0, got1), g_ffn)
    shared = share_dp(g_ffn)
    total0 = add(keep0[0], came0[0]) + got0.astype(F32)
    total1 = add(keep1[0], came1[0]) + got1.astype(F32)
    got0 = send(total0[1].astype(LOW), "y")
    got1 = send(total1[1].astype(LOW), "x")
    got0, got1, shared = lax.optimization_barrier((got0, got1, shared))
    total = jnp.concatenate([add(total0[0], got0), add(total1[0], got1)], axis=1)
    parts = [total[r].astype(LOW) for r in (1, 2, 3)]
    line_a = line_send(parts)
    grad_down, grad_up = finish_ffn(where, after(shared, parts))
    line_a = after(line_a, grad_down)
    g_attn = (total[0] + line_a[0].astype(F32) + line_a[1].astype(F32) + line_a[2].astype(F32))
    small = g_attn[ROWS : ROWS + 4, :ROWS]
    grad_qkv, grad_out = finish_attention(where, share_dp(g_attn[:ROWS].astype(LOW)))
    return (
        layer_out.reshape(seqs, length, width),
        grad_in.reshape(seqs, length, width),
        grad_qkv,
        grad_out,
        grad_up,
        grad_down,
        small[0],
        small[1],
        small[2],
        small[3],
    )


FF = 3072


def slopes():
    return jnp.exp2(-8.0 * (jnp.arange(HEADS, dtype=F32) + 1.0) / HEADS)


def pick(onehot, rows):
    if rows.dtype == LOW:
        return jnp.einsum("svj,sjd->svd", onehot.astype(LOW), rows, preferred_element_type=F32).astype(LOW)
    return jnp.einsum("svj,sjd->svd", onehot, rows, precision=lax.Precision.HIGHEST)


def gather_weights(w_qkv, w_out, w_up, w_down):
    fsdp = lax.axis_size("fsdp")
    dp = lax.axis_size("dp")
    rows, width = w_out.shape
    if rows % (8 * dp):
        return (
            lax.all_gather(w_qkv, "fsdp", axis=0, tiled=True),
            lax.all_gather(w_out, "fsdp", axis=0, tiled=True),
            lax.all_gather(w_up, "fsdp", axis=0, tiled=True),
            lax.all_gather(w_down, "fsdp", axis=0, tiled=True),
        )
    mine = lax.axis_index("dp")
    part = rows // dp
    group = w_down.shape[0] // rows
    joined = jnp.concatenate([w_qkv, w_out, w_up], axis=1)
    joined = lax.dynamic_slice_in_dim(joined, mine * part, part, axis=0)
    down = lax.dynamic_slice_in_dim(w_down, mine * part * group, part * group, axis=0)
    down = jnp.concatenate([down[k * part : (k + 1) * part] for k in range(group)], axis=1)
    full = lax.all_gather(jnp.concatenate([joined, down], axis=1), AXES, axis=0, tiled=True)
    a, b = w_qkv.shape[1], w_qkv.shape[1] + w_out.shape[1]
    c = b + w_up.shape[1]
    full_down = full[:, c:].reshape(fsdp * dp, part, group, width)
    full_down = full_down.transpose(0, 2, 1, 3).reshape(fsdp * dp * part * group, width)
    return full[:, :a], full[:, a:b], full[:, b:c], full_down


def scatter_grads(g_qkv, g_out, g_up, g_down):
    fsdp = lax.axis_size("fsdp")
    dp = lax.axis_size("dp")
    width = g_out.shape[1]
    rows = g_out.shape[0] // fsdp
    if rows % (8 * dp):
        return tuple(
            lax.psum(lax.psum_scatter(g, "fsdp", scatter_dimension=0, tiled=True), "dp")
            for g in (g_qkv, g_out, g_up, g_down)
        )
    part = rows // dp
    group = g_down.shape[0] // g_out.shape[0]
    down = g_down.reshape(fsdp * dp, group, part, width).transpose(0, 2, 1, 3)
    down = down.reshape(fsdp * rows, group * width)
    joined = jnp.concatenate([g_qkv, g_out, g_up, down], axis=1).astype(LOW)
    mine = lax.psum_scatter(joined, AXES, scatter_dimension=0, tiled=True)
    full = lax.all_gather(mine, "dp", axis=0, tiled=True).astype(F32)
    a, b = g_qkv.shape[1], g_qkv.shape[1] + width
    c = b + g_up.shape[1]
    full_down = full[:, c:].reshape(dp, part, group, width).transpose(0, 2, 1, 3)
    return full[:, :a], full[:, a:b], full[:, b:c], full_down.reshape(rows * group, width)


def on_device(hidden_in, w_qkv, w_out, w_up, w_down, gain_attn, shift_attn, gain_ffn, shift_ffn, grad_listed, positions, counts):
    seqs, length, width = hidden_in.shape
    tokens = seqs * length
    most = positions.shape[1]
    norms = jnp.stack([gain_attn, shift_attn, gain_ffn, shift_ffn])
    norms = lax.all_gather(norms, "fsdp", axis=1, tiled=True).astype(F32)
    w_qkv, w_out, w_up, w_down = gather_weights(w_qkv, w_out, w_up, w_down)
    live = jnp.arange(most, dtype=jnp.int32)[None, :] < counts[:, None]
    onehot = (positions[:, :, None] == jnp.arange(length, dtype=jnp.int32)).astype(F32)
    rows_in = hidden_in.reshape(tokens, width)
    slope = slopes()
    scale = HEAD_DIM**-0.5
    qkv = mm(rows_in, w_qkv).astype(LOW)
    split = qkv.reshape(seqs, length, 3, HEADS, HEAD_DIM)
    q, k, v = split[:, :, 0], split[:, :, 1], split[:, :, 2]
    place = jnp.arange(length, dtype=F32)
    bias = -slope[:, None, None] * jnp.abs(place[:, None] - place[None, :])
    s = jnp.einsum("sqhc,skhc->shqk", q, k, preferred_element_type=F32) * scale + bias
    p = jax.nn.softmax(s, axis=-1).astype(LOW)
    att = jnp.einsum("shqk,skhc->sqhc", p, v, preferred_element_type=F32).astype(LOW)
    att = att.reshape(tokens, width)
    r1 = rows_in.astype(F32) + mm(att, w_out)
    unit1, _ = norm_parts(r1)
    h1 = unit1 * norms[0] + norms[1]
    h1_low = h1.astype(LOW)
    u = mm(h1_low, w_up)
    act = (jax.nn.gelu(u[:, :FF], approximate=False) * u[:, FF:]).astype(LOW)
    r2 = h1 + mm(act, w_down)
    unit2, _ = norm_parts(r2)
    layer_out = (unit2 * norms[2] + norms[3]).astype(LOW).reshape(seqs, length, width)
    def listed(a):
        return pick(onehot, a.reshape(seqs, length, -1)).reshape(seqs * most, -1)

    dy = jnp.where(live[:, :, None], grad_listed, 0).astype(F32).reshape(seqs * most, width)
    unit2_m, rstd2_m = norm_parts(listed(r2))
    g_gain_ffn = jnp.sum(dy * unit2_m, axis=0)
    g_shift_ffn = jnp.sum(dy, axis=0)
    dr2 = norm_back(dy, unit2_m, rstd2_m, norms[2])
    e2 = dr2.astype(LOW)
    h1_m = listed(h1_low)
    u_m = mm(h1_m, w_up)
    gate, up = u_m[:, :FF], u_m[:, FF:]
    cdf = 0.5 * (1.0 + lax.erf(gate * (0.5**0.5)))
    pdf = jnp.exp(-0.5 * gate * gate) * ((2.0 * jnp.pi) ** -0.5)
    gelu = gate * cdf
    act_m = (gelu * up).astype(LOW)
    g_down = jnp.einsum("nf,nd->fd", act_m, e2, preferred_element_type=F32)
    dact = jnp.einsum("nd,fd->nf", e2, w_down, preferred_element_type=F32)
    du = jnp.concatenate([dact * up * (cdf + gate * pdf), dact * gelu], axis=1).astype(LOW)
    g_up = jnp.einsum("nd,nf->df", h1_m, du, preferred_element_type=F32)
    dh1 = dr2 + jnp.einsum("nf,df->nd", du, w_up, preferred_element_type=F32)
    unit1_m, rstd1_m = norm_parts(listed(r1))
    g_gain_attn = jnp.sum(dh1 * unit1_m, axis=0)
    g_shift_attn = jnp.sum(dh1, axis=0)
    dr1 = norm_back(dh1, unit1_m, rstd1_m, norms[0])
    e1 = dr1.astype(LOW)
    g_out = jnp.einsum("nd,ne->de", listed(att), e1, preferred_element_type=F32)
    datt = jnp.einsum("ne,de->nd", e1, w_out, preferred_element_type=F32).astype(LOW)
    datt = datt.reshape(seqs, most, HEADS, HEAD_DIM)
    q_m = listed(qkv[:, :width]).reshape(seqs, most, HEADS, HEAD_DIM)
    away = jnp.abs(positions[:, :, None].astype(F32) - place[None, None, :])
    s_m = jnp.einsum("sqhc,skhc->shqk", q_m, k, preferred_element_type=F32) * scale
    p_m = jax.nn.softmax(s_m - slope[None, :, None, None] * away[:, None], axis=-1)
    dv = jnp.einsum("shqk,sqhc->skhc", p_m.astype(LOW), datt, preferred_element_type=F32)
    dp = jnp.einsum("sqhc,skhc->shqk", datt, v, preferred_element_type=F32)
    ds = (p_m * (dp - jnp.sum(dp * p_m, axis=-1, keepdims=True))).astype(LOW)
    dq_m = (jnp.einsum("shqk,skhc->sqhc", ds, k, preferred_element_type=F32) * scale).astype(LOW)
    dk = (jnp.einsum("shqk,sqhc->skhc", ds, q_m, preferred_element_type=F32) * scale).astype(LOW)
    put = (onehot * live[:, :, None]).astype(LOW)
    dq = jnp.einsum("svj,svd->sjd", put, dq_m.reshape(seqs, most, width), preferred_element_type=F32)
    dqkv = jnp.concatenate(
        [dq.astype(LOW).reshape(tokens, width), dk.reshape(tokens, width), dv.astype(LOW).reshape(tokens, width)], axis=1
    )
    g_qkv = jnp.einsum("nd,ne->de", rows_in, dqkv, preferred_element_type=F32)
    dr1_all = jnp.einsum("svj,svd->sjd", onehot * live[:, :, None], dr1.reshape(seqs, most, width), precision=lax.Precision.HIGHEST)
    grad_in = dr1_all.reshape(tokens, width) + jnp.einsum("ne,de->nd", dqkv, w_qkv, preferred_element_type=F32)
    owned = scatter_grads(g_qkv, g_out, g_up, g_down)
    small = lax.psum(jnp.stack([g_gain_attn, g_shift_attn, g_gain_ffn, g_shift_ffn]), AXES)
    share = width // lax.axis_size("fsdp")
    small = lax.dynamic_slice_in_dim(small, lax.axis_index("fsdp") * share, share, axis=1)
    return (
        layer_out,
        grad_in.reshape(seqs, length, width),
        *owned,
        small[0],
        small[1],
        small[2],
        small[3],
    )


def solution(mesh):
    rows3 = P(("fsdp", "dp"), None, None)
    rows2 = P("fsdp", None)
    rows1 = P("fsdp")
    shape = dict(mesh.shape)
    step = on_block if shape == {"fsdp": SHARDS, "dp": QUARTERS} else on_device
    return jax.shard_map(
        step,
        mesh=mesh,
        in_specs=(rows3, rows2, rows2, rows2, rows2, rows1, rows1, rows1, rows1, rows3, P(("fsdp", "dp"), None), P(("fsdp", "dp"))),
        out_specs=(rows3, rows3, rows2, rows2, rows2, rows2, rows1, rows1, rows1, rows1),
        check_vma=False,
    )
```

```python
import functools

import jax
import jax.numpy as jnp
from jax import lax
from jax.experimental import pallas as pl
from jax.experimental.pallas import tpu as pltpu
from jax.sharding import PartitionSpec as P

HEADS = 12
HEAD_DIM = 64
EPS = 1e-12
F32 = jnp.float32
LOW = jnp.bfloat16
AXES = ("fsdp", "dp")
D = 768
ROWS = 96
LINE = 4
SHARDS = D // ROWS
QUARTERS = 4
EXACT = lax.Precision.HIGHEST
SCALE = HEAD_DIM**-0.5
VMEM = pl.BlockSpec(memory_space=pltpu.VMEM)
SMEM = pl.BlockSpec(memory_space=pltpu.SMEM)
BIG = pltpu.CompilerParams(vmem_limit_bytes=60 * 1024 * 1024)


def out(shape, dtype):
    return jax.ShapeDtypeStruct(shape, dtype)


def cost(us):
    return pl.CostEstimate(flops=0, bytes_accessed=int(us * 3.0e6), transcendentals=0)


def mm(a, b):
    return jnp.dot(a, b, preferred_element_type=F32)


def mm_nt(a, b):
    return lax.dot_general(a, b, (((1,), (1,)), ((), ())), preferred_element_type=F32)


def mm_tn(a, b):
    return lax.dot_general(a, b, (((0,), (0,)), ((), ())), preferred_element_type=F32)


def norm_parts(value):
    center = value - jnp.mean(value, axis=-1, keepdims=True)
    rstd = lax.rsqrt(jnp.mean(center * center, axis=-1, keepdims=True) + EPS)
    return center * rstd, rstd


def norm_back(grad, unit, rstd, gain):
    scaled = grad * gain
    return rstd * (
        scaled
        - jnp.mean(scaled, axis=-1, keepdims=True)
        - unit * jnp.mean(scaled * unit, axis=-1, keepdims=True)
    )


def onehot(pos_ref, seq, most, length):
    spots = lax.broadcasted_iota(jnp.int32, (most, length), 1)
    return spots == pos_ref[pl.ds(seq * most, most), :]


def gelu_parts(gate):
    cdf = 0.5 * (1.0 + lax.erf(gate * (0.5**0.5)))
    pdf = jnp.exp(-0.5 * gate * gate) * ((2.0 * jnp.pi) ** -0.5)
    return gate * cdf, cdf + gate * pdf


def slope_of(head):
    return 2.0 ** (-8.0 * (head + 1.0) / HEADS)


def block(ref, *index):
    value = ref[index] if index else ref[...]
    return value.reshape(-1, value.shape[-1])


EXTRA = 8
TAIL = 16
HALVES = ((0, 48), (48, 56))
KEYS = [(ry, rx, rc) for rc in (0, 1) for rx in (0, 1) for ry in (0, 1)]


def attention_kernel(seqs, most, where_ref, slope_ref, x_ref, norm_ref, pos_ref, *rest):
    lines, rest = rest[:16], rest[16:]
    qkv_ref, h1_ref, att_m_ref, h1_m_ref, q_m_ref, r1_m_ref, w_ref, att_ref, r1_ref, sem = rest
    z, y, c_x = where_ref[0], where_ref[1], where_ref[4]
    copies = []
    for n, (ry, rx, rc) in enumerate(KEYS):
        j = jnp.bitwise_xor(c_x, 2 * rx + rc)
        for r in range(LINE):
            shard = 2 * lax.rem(z + LINE - r, LINE) + jnp.bitwise_xor(y, ry)
            for half, (start, size) in enumerate(HALVES):
                size = min(size, ROWS - start)
                copies.append(
                    pltpu.make_async_copy(
                        lines[2 * n + half].at[r, pl.ds(0, size)], w_ref.at[shard, j, pl.ds(start, size)], sem
                    )
                )
    for copy in copies:
        copy.start()
    for copy in copies:
        copy.wait()
    length = x_ref.shape[0] // seqs
    step = 256

    @pl.loop(0, 3 * D // step)
    def _(n):
        j = n // (D // step)
        lane = pl.multiple_of((n - j * (D // step)) * step, step)
        w = w_ref[:, j, :, pl.ds(lane, step)].reshape(D, step)
        qkv_ref[:, pl.ds(pl.multiple_of(n * step, step), step)] = mm(x_ref[...], w).astype(LOW)

    first = lax.broadcasted_iota(jnp.int32, (length, 128), 1) < HEAD_DIM
    row = lax.broadcasted_iota(jnp.int32, (length, length), 0)
    col = lax.broadcasted_iota(jnp.int32, (length, length), 1)
    away = jnp.abs(row - col).astype(F32)

    @pl.loop(0, HEADS // 2)
    def _(t):
        lane = pl.multiple_of(t * 128, 128)
        bias = jnp.concatenate([slope_ref[2 * t] * away, slope_ref[2 * t + 1] * away], axis=0)
        for s in range(seqs):
            rows = slice(s * length, (s + 1) * length)
            q = qkv_ref[rows, pl.ds(lane, 128)]
            k = qkv_ref[rows, pl.ds(D + lane, 128)]
            v = qkv_ref[rows, pl.ds(2 * D + lane, 128)]
            zero = jnp.zeros_like(q)
            both = jnp.concatenate([jnp.where(first, q, zero), jnp.where(first, zero, q)], axis=0)
            score = mm_nt(both, k) * SCALE - bias
            e = jnp.exp(score - jnp.max(score, axis=-1, keepdims=True))
            p = (e * (1.0 / jnp.sum(e, axis=-1, keepdims=True))).astype(LOW)
            mixed = mm(p, v)
            att_ref[rows, pl.ds(lane, 128)] = jnp.where(first, mixed[:length], mixed[length:]).astype(LOW)

    @pl.loop(0, D // step)
    def _(n):
        lane = pl.multiple_of(n * step, step)
        w = w_ref[:, 3, :, pl.ds(lane, step)].reshape(D, step)
        r1_ref[:, pl.ds(lane, step)] = x_ref[:, pl.ds(lane, step)].astype(F32) + mm(att_ref[...], w)

    for s in range(seqs):
        rows = slice(s * length, (s + 1) * length)
        listed = slice(s * most, (s + 1) * most)
        unit, _ = norm_parts(r1_ref[rows, :])
        h1 = unit * norm_ref[0:1, :] + norm_ref[1:2, :]
        h1_ref[rows, :] = h1
        hot = onehot(pos_ref, s, most, length)
        hot_low = hot.astype(LOW)
        r1_m_ref[listed, :] = jnp.dot(hot.astype(F32), r1_ref[rows, :], precision=EXACT, preferred_element_type=F32)
        h1_m_ref[listed, :] = mm(hot_low, h1.astype(LOW)).astype(LOW)
        att_m_ref[listed, :] = mm(hot_low, att_ref[rows, :]).astype(LOW)
        q_m_ref[listed, :] = mm(hot_low, qkv_ref[rows, 0:D]).astype(LOW)


def attention_forward(where, x, lines, norms, pos, slopes, seqs):
    tokens = x.shape[0]
    listed = pos.shape[0]
    return pl.pallas_call(
        functools.partial(attention_kernel, seqs, listed // seqs),
        out_shape=(
            out((tokens, 3 * D), LOW),
            out((tokens, D), F32),
            out((listed, D), LOW),
            out((listed, D), LOW),
            out((listed, D), LOW),
            out((listed, D), F32),
            out((SHARDS, QUARTERS, ROWS, D), LOW),
        ),
        in_specs=[SMEM, SMEM, VMEM, VMEM, VMEM] + [pl.BlockSpec(memory_space=pl.ANY)] * 16,
        out_specs=(VMEM,) * 7,
        scratch_shapes=[pltpu.VMEM((tokens, D), LOW), pltpu.VMEM((tokens, D), F32), pltpu.SemaphoreType.DMA],
        compiler_params=BIG,
        cost_estimate=cost(20),
        name="attention_forward",
    )(where, slopes, x, norms, pos, *lines)


def ffn_kernel(seqs, most, h1_ref, gate_ref, up_ref, down_ref, norm_ref, pos_ref, dy_ref, y_ref, dr2_ref, e2_ref, small_ref, low_ref, act_ref, acc_ref):
    j = pl.program_id(0)
    tokens = h1_ref.shape[0]
    length = tokens // seqs
    step = 256

    @pl.when(j == 0)
    def _():
        low_ref[...] = h1_ref[...].astype(LOW)
        acc_ref[...] = h1_ref[...]

    @pl.loop(0, D // step)
    def _(n):
        lane = pl.multiple_of(n * step, step)
        gate = mm(low_ref[...], gate_ref[:, :, pl.ds(lane, step)].reshape(D, step))
        up = mm(low_ref[...], up_ref[:, :, pl.ds(lane, step)].reshape(D, step))
        cdf = 0.5 * (1.0 + lax.erf(gate * (0.5**0.5)))
        act_ref[:, pl.ds(lane, step)] = (gate * cdf * up).astype(LOW)

    @pl.loop(0, D // step)
    def _(n):
        lane = pl.multiple_of(n * step, step)
        acc_ref[:, pl.ds(lane, step)] += mm(act_ref[...], down_ref[:, :, :, pl.ds(lane, step)].reshape(D, step))

    @pl.when(j == QUARTERS - 1)
    def _():
        gain = norm_ref[2:3, :]
        small = [jnp.zeros((1, D), F32)] * 2
        for s in range(seqs):
            rows = slice(s * length, (s + 1) * length)
            listed = slice(s * most, (s + 1) * most)
            unit, _ = norm_parts(acc_ref[rows, :])
            y_ref[rows, :] = (unit * gain + norm_ref[3:4, :]).astype(LOW)
            hot = onehot(pos_ref, s, most, length).astype(F32)
            picked = jnp.dot(hot, acc_ref[rows, :], precision=EXACT, preferred_element_type=F32)
            unit_m, rstd_m = norm_parts(picked)
            dy = dy_ref[listed, :].astype(F32)
            small = [small[0] + jnp.sum(dy * unit_m, axis=0, keepdims=True), small[1] + jnp.sum(dy, axis=0, keepdims=True)]
            dr2 = norm_back(dy, unit_m, rstd_m, gain)
            dr2_ref[listed, :] = dr2
            e2_ref[listed, :] = dr2.astype(LOW)
        small_ref[...] = jnp.concatenate(small, axis=0)


def ffn_forward(h1, w_ffn, norms, pos, dy, seqs):
    tokens = h1.shape[0]
    listed = pos.shape[0]
    whole = lambda shape: pl.BlockSpec(shape, lambda j: (0,) * len(shape), pipeline_mode=pl.Buffered(1))
    return pl.pallas_call(
        functools.partial(ffn_kernel, seqs, listed // seqs),
        out_shape=(out((tokens, D), LOW), out((listed, D), F32), out((listed, D), LOW), out((2, D), F32)),
        grid=(QUARTERS,),
        in_specs=[
            whole((tokens, D)),
            pl.BlockSpec((SHARDS, None, None, ROWS, D), lambda j: (0, j, 0, 0, 0)),
            pl.BlockSpec((SHARDS, None, None, ROWS, D), lambda j: (0, j, 1, 0, 0)),
            pl.BlockSpec((SHARDS // QUARTERS, QUARTERS, None, ROWS, D), lambda j: (j, 0, 2, 0, 0)),
            whole(norms.shape),
            whole(pos.shape),
            whole(dy.shape),
        ],
        out_specs=(
            pl.BlockSpec((tokens, D), lambda j: (0, 0)),
            pl.BlockSpec((listed, D), lambda j: (0, 0)),
            pl.BlockSpec((listed, D), lambda j: (0, 0)),
            pl.BlockSpec((2, D), lambda j: (0, 0)),
        ),
        scratch_shapes=[pltpu.VMEM((tokens, D), LOW), pltpu.VMEM((tokens, D), LOW), pltpu.VMEM((tokens, D), F32)],
        compiler_params=BIG,
        cost_estimate=cost(16),
        name="ffn_forward",
    )(h1, w_ffn, w_ffn, w_ffn, norms, pos, dy)


def ffn_again_kernel(where_ref, h_ref, gate_ref, up_ref, act_ref, to_gate_ref, to_up_ref):
    step = 256

    @pl.loop(0, D // step)
    def _(n):
        lane = pl.multiple_of(n * step, step)
        rows = block(h_ref)
        gate = mm(rows, gate_ref[:, :, pl.ds(lane, step)].reshape(D, step))
        up = mm(rows, up_ref[:, :, pl.ds(lane, step)].reshape(D, step))
        value, slope = gelu_parts(gate)
        act_ref[:, pl.ds(lane, step)] = (value * up).astype(LOW)
        to_gate_ref[:, pl.ds(lane, step)] = slope * up
        to_up_ref[:, pl.ds(lane, step)] = value


def quarter_specs(which):
    specs = {
        "gate": pl.BlockSpec((SHARDS, None, None, ROWS, D), lambda g, w: (0, w[4], 0, 0, 0)),
        "up": pl.BlockSpec((SHARDS, None, None, ROWS, D), lambda g, w: (0, w[4], 1, 0, 0)),
        "down": pl.BlockSpec((SHARDS // QUARTERS, QUARTERS, None, ROWS, D), lambda g, w: (w[4], 0, 2, 0, 0)),
    }
    return [specs[name] for name in which]


def at_once(shape):
    return pl.BlockSpec(shape, lambda g, w: (0,) * len(shape))


def ffn_again(where, h_all, w_ffn):
    rows = h_all.shape[0] * h_all.shape[1]
    return pl.pallas_call(
        ffn_again_kernel,
        out_shape=(out((rows, D), LOW), out((rows, D), F32), out((rows, D), F32)),
        grid_spec=pltpu.PrefetchScalarGridSpec(
            num_scalar_prefetch=1,
            grid=(1,),
            in_specs=[at_once(h_all.shape), *quarter_specs(["gate", "up"])],
            out_specs=(at_once((rows, D)),) * 3,
        ),
        compiler_params=BIG,
        cost_estimate=cost(6),
        name="ffn_again",
    )(where, h_all, w_ffn, w_ffn)


def ffn_back_kernel(where_ref, e_ref, to_gate_ref, to_up_ref, gate_ref, up_ref, down_ref, dgate_ref, dup_ref, keep_ref, send_ref):
    listed = e_ref.shape[1]
    half = QUARTERS // 2
    for n in range(SHARDS // QUARTERS):
        lanes = slice(n * QUARTERS * ROWS, (n + 1) * QUARTERS * ROWS)
        dact = mm_nt(block(e_ref), block(down_ref, n))
        dgate_ref[:, lanes] = (dact * to_gate_ref[:, lanes]).astype(LOW)
        dup_ref[:, lanes] = (dact * to_up_ref[:, lanes]).astype(LOW)
    for n in range(2):
        shards = slice(n * SHARDS // 2, (n + 1) * SHARDS // 2)
        lanes = slice(n * D // 2, (n + 1) * D // 2)
        part = mm_nt(dgate_ref[...], block(gate_ref, shards)) + mm_nt(dup_ref[...], block(up_ref, shards))
        for r in range(half):
            keep_ref[r, :, lanes] = part[2 * r * listed : (2 * r + 1) * listed]
            send_ref[r, :, lanes] = part[(2 * r + 1) * listed : (2 * r + 2) * listed].astype(LOW)


def ffn_back(where, e_all, to_gate, to_up, w_ffn):
    count, listed, _ = e_all.shape
    rows = count * listed
    return pl.pallas_call(
        ffn_back_kernel,
        out_shape=(out((rows, D), LOW), out((rows, D), LOW), out((count // 2, listed, D), F32), out((count // 2, listed, D), LOW)),
        grid_spec=pltpu.PrefetchScalarGridSpec(
            num_scalar_prefetch=1,
            grid=(1,),
            in_specs=[at_once(e_all.shape), at_once((rows, D)), at_once((rows, D)), *quarter_specs(["gate", "up", "down"])],
            out_specs=(at_once((rows, D)), at_once((rows, D)), at_once((count // 2, listed, D)), at_once((count // 2, listed, D))),
        ),
        compiler_params=BIG,
        cost_estimate=cost(7),
        name="ffn_back",
    )(where, e_all, to_gate, to_up, w_ffn, w_ffn, w_ffn)


def weight_grad_kernel(where_ref, a_ref, b_ref, keep_ref, send_ref, full_ref):
    z, y = where_ref[0], where_ref[1]
    b = block(b_ref)
    step = 256

    @pl.loop(0, D // step)
    def _(n):
        lane = pl.multiple_of(n * step, step)
        a = block(a_ref, *([slice(None)] * (len(a_ref.shape) - 1)), pl.ds(lane, step))
        full_ref[pl.ds(lane, step), :] = mm_tn(a, b)

    for r in range(LINE):
        base = 2 * lax.rem(z + r, LINE)
        for other, ref in ((0, keep_ref), (1, send_ref)):
            start = (base + (y if other == 0 else 1 - y)) * ROWS
            ref[r] = full_ref[pl.ds(pl.multiple_of(start, 8), ROWS), :].astype(LOW)


def weight_grad(where, a, b):
    shape = (LINE, ROWS, D)
    rows = a.size // D
    return pl.pallas_call(
        weight_grad_kernel,
        out_shape=(out(shape, LOW), out(shape, LOW)),
        in_specs=[SMEM, VMEM, VMEM],
        out_specs=(VMEM, VMEM),
        scratch_shapes=[pltpu.VMEM((D, D), F32)],
        compiler_params=BIG,
        cost_estimate=cost(4),
        name="weight_grad",
    )(where, a, b)


def norm_back_kernel(dr2_ref, part_ref, came_ref, r1_ref, w_ref, norm_ref, dr1_ref, low_ref, datt_ref, small_ref):
    dh1 = dr2_ref[...] + part_ref[...] + came_ref[...].astype(F32)
    unit, rstd = norm_parts(r1_ref[...])
    small_ref[0:1, :] = jnp.sum(dh1 * unit, axis=0, keepdims=True)
    small_ref[1:2, :] = jnp.sum(dh1, axis=0, keepdims=True)
    dr1 = norm_back(dh1, unit, rstd, norm_ref[0:1, :])
    dr1_ref[...] = dr1
    low = dr1.astype(LOW)
    low_ref[...] = low
    for n in range(2):
        lanes = slice(n * D // 2, (n + 1) * D // 2)
        datt_ref[:, lanes] = mm_nt(low, block(w_ref, slice(n * SHARDS // 2, (n + 1) * SHARDS // 2))).astype(LOW)


def norm_back_call(dr2, part, came, r1_m, w_attn, norms):
    listed = dr2.shape[0]
    same = lambda shape: pl.BlockSpec(shape, lambda g: (0,) * len(shape))
    rows = same((listed, D))
    return pl.pallas_call(
        norm_back_kernel,
        out_shape=(out((listed, D), F32), out((listed, D), LOW), out((listed, D), LOW), out((2, D), F32)),
        grid=(1,),
        in_specs=[rows, rows, rows, rows, pl.BlockSpec((SHARDS, None, ROWS, D), lambda g: (0, 3, 0, 0)), same((4, D))],
        out_specs=(rows, rows, rows, same((2, D))),
        compiler_params=BIG,
        cost_estimate=cost(4),
        name="norm_back",
    )(dr2, part, came, r1_m, w_attn, norms)


def attention_back_kernel(seqs, most, slope_ref, datt_ref, q_ref, qkv_ref, pos_ref, rhs_ref, away_ref, hot_ref):
    length = qkv_ref.shape[0] // seqs
    listed = seqs * most
    first_m = lax.broadcasted_iota(jnp.int32, (most, 128), 1) < HEAD_DIM
    spots = lax.broadcasted_iota(jnp.int32, (listed, length), 1)
    away_ref[...] = jnp.abs(pos_ref[...] - spots).astype(F32)
    hot_ref[...] = (spots == pos_ref[...]).astype(LOW)

    def both(value):
        zero = jnp.zeros_like(value)
        return jnp.concatenate([jnp.where(first_m, value, zero), jnp.where(first_m, zero, value)], axis=0)

    @pl.loop(0, HEADS // 2)
    def _(t):
        lane = pl.multiple_of(t * 128, 128)
        for s in range(seqs):
            rows = slice(s * length, (s + 1) * length)
            mine = slice(s * most, (s + 1) * most)
            away = away_ref[mine, :]
            q = both(q_ref[mine, pl.ds(lane, 128)])
            da = both(datt_ref[mine, pl.ds(lane, 128)])
            k = qkv_ref[rows, pl.ds(D + lane, 128)]
            v = qkv_ref[rows, pl.ds(2 * D + lane, 128)]
            bias = jnp.concatenate([slope_ref[2 * t] * away, slope_ref[2 * t + 1] * away], axis=0)
            score = mm_nt(q, k) * SCALE - bias
            e = jnp.exp(score - jnp.max(score, axis=-1, keepdims=True))
            p = e * (1.0 / jnp.sum(e, axis=-1, keepdims=True))
            dp = mm_nt(da, v)
            ds = (p * (dp - jnp.sum(dp * p, axis=-1, keepdims=True))).astype(LOW)
            dq = mm(ds, k)
            dq = (jnp.where(first_m, dq[:most], dq[most:]) * SCALE).astype(LOW)
            rhs_ref[rows, pl.ds(lane, 128)] = mm_tn(hot_ref[mine, :], dq).astype(LOW)
            rhs_ref[rows, pl.ds(D + lane, 128)] = (mm_tn(ds, q) * SCALE).astype(LOW)
            rhs_ref[rows, pl.ds(2 * D + lane, 128)] = mm_tn(p.astype(LOW), da).astype(LOW)


def attention_back(datt, q_m, qkv, pos, slopes, seqs):
    tokens = qkv.shape[0]
    listed = pos.shape[0]
    return pl.pallas_call(
        functools.partial(attention_back_kernel, seqs, listed // seqs),
        out_shape=out((tokens, 3 * D), LOW),
        in_specs=[SMEM] + [VMEM] * 4,
        out_specs=VMEM,
        scratch_shapes=[pltpu.VMEM((listed, tokens // seqs), F32), pltpu.VMEM((listed, tokens // seqs), LOW)],
        compiler_params=BIG,
        cost_estimate=cost(15),
        name="attention_back",
    )(slopes, datt, q_m, qkv, pos)


def attention_grads_kernel(where_ref, flip_ref, rhs_ref, att_ref, low_ref, small_attn_ref, small_ffn_ref, keep0_ref, keep1_ref, away0_ref, away1_ref, full_ref, tail_ref):
    z, y, mine = where_ref[0], where_ref[1], where_ref[4]
    half = ROWS // 2
    step = 256
    tail_ref[...] = jnp.zeros(tail_ref.shape, LOW)
    small = jnp.concatenate([small_attn_ref[...], small_ffn_ref[...]], axis=0).astype(LOW)
    for n in range(SHARDS):
        tail_ref[n, 0:4, 0:ROWS] = small[:, n * ROWS : (n + 1) * ROWS]
    for rc in (1, 0):
        cut0_ref, cut1_ref = (keep0_ref, keep1_ref) if rc == 0 else (away0_ref, away1_ref)
        for rx in (0, 1):
            j = jnp.bitwise_xor(mine, 2 * rx + rc)

            @pl.when(j == 3)
            def _():
                for n in range(D // step):
                    rows = slice(n * step, (n + 1) * step)
                    full_ref[rows, :] = mm_tn(att_ref[:, rows], low_ref[...])

            @pl.when(j != 3)
            def _():
                @pl.loop(0, D // step)
                def _(n):
                    lane = pl.multiple_of(n * step, step)
                    cols = pl.ds(pl.multiple_of(j * D + n * step, step), step)
                    full_ref[:, pl.ds(lane, step)] = mm(flip_ref[...], rhs_ref[:, cols])

            for rz in range(LINE):
                base = 2 * lax.rem(z + rz, LINE)
                for ry in (0, 1):
                    shard = base + (y if ry == 0 else 1 - y)
                    start = shard * ROWS
                    cut0_ref[rx, ry, rz] = full_ref[pl.ds(pl.multiple_of(start, 8), half), :].astype(LOW)
                    cut1_ref[ry, rx, rz, 0:half] = full_ref[pl.ds(pl.multiple_of(start + half, 8), half), :].astype(LOW)
                    cut1_ref[ry, rx, rz, half:] = tail_ref[shard]


def attention_grads(where, x_flip, rhs, att_m, low, small_attn, small_ffn):
    half = ROWS // 2
    return pl.pallas_call(
        attention_grads_kernel,
        out_shape=(out((2, 2, LINE, half, D), LOW), out((2, 2, LINE, half + TAIL, D), LOW)) * 2,
        in_specs=[SMEM] + [VMEM] * 6,
        out_specs=(VMEM,) * 4,
        scratch_shapes=[pltpu.VMEM((D, D), F32), pltpu.VMEM((SHARDS, TAIL, D), LOW)],
        compiler_params=BIG,
        cost_estimate=cost(10),
        name="attention_grads",
    )(where, x_flip, rhs, att_m, low, small_attn, small_ffn)


def input_grad_kernel(seqs, rhs_ref, w_ref, dr1_ref, pos_ref, out_ref):
    length = out_ref.shape[0] // seqs
    most = dr1_ref.shape[0] // seqs
    for n in range(2):
        lanes = slice(n * D // 2, (n + 1) * D // 2)
        shards = slice(n * SHARDS // 2, (n + 1) * SHARDS // 2)
        total = mm_nt(rhs_ref[:, 0:D], block(w_ref, shards, 0))
        total += mm_nt(rhs_ref[:, D : 2 * D], block(w_ref, shards, 1))
        total += mm_nt(rhs_ref[:, 2 * D : 3 * D], block(w_ref, shards, 2))
        for s in range(seqs):
            rows = slice(s * length, (s + 1) * length)
            hot = (lax.broadcasted_iota(jnp.int32, (length, most), 0) == pos_ref[s : s + 1, :]).astype(F32)
            spread = jnp.dot(hot, dr1_ref[s * most : (s + 1) * most, lanes], precision=EXACT, preferred_element_type=F32)
            out_ref[rows, lanes] = total[rows] + spread


def input_grad(rhs, w_attn, dr1, positions):
    tokens = rhs.shape[0]
    return pl.pallas_call(
        functools.partial(input_grad_kernel, positions.shape[0]),
        out_shape=out((tokens, D), F32),
        in_specs=[VMEM] * 4,
        out_specs=VMEM,
        compiler_params=BIG,
        cost_estimate=cost(8),
        name="input_grad",
    )(rhs, w_attn, dr1, positions)


def place(z, y, x, c):
    return (2 * z + y) * 4 + 2 * x + c


def grid_perm(move):
    return [
        (place(z, y, x, c), place(*move(z, y, x, c)))
        for z in range(4)
        for y in range(2)
        for x in range(2)
        for c in range(2)
    ]


MOVES = {
    "x": grid_perm(lambda z, y, x, c: (z, y, 1 - x, c)),
    "y": grid_perm(lambda z, y, x, c: (z, 1 - y, x, c)),
    "c": grid_perm(lambda z, y, x, c: (z, y, x, 1 - c)),
    1: grid_perm(lambda z, y, x, c: ((z + 1) % 4, y, x, c)),
    2: grid_perm(lambda z, y, x, c: ((z + 2) % 4, y, x, c)),
    3: grid_perm(lambda z, y, x, c: ((z + 3) % 4, y, x, c)),
    "down": [(m * 4 + q, (2 * q + m // 4) * 4 + m % 4) for m in range(8) for q in range(4)],
}


def send(value, move):
    return lax.ppermute(value, AXES, MOVES[move])


def share_dp(value):
    other = send(value, "x")
    return value, send(value, "c"), other, send(other, "c")


def after(value, *earlier):
    return lax.optimization_barrier((value, *earlier))[0]


def add(kept, got):
    return kept.astype(F32) + got.astype(F32)


def line_parts(keep, got):
    return [add(keep[r], got[r]).astype(LOW) for r in (1, 2, 3)]


def line_send(parts):
    return [send(value, r) for r, value in zip((1, 2, 3), parts)]


def line_add(keep, got, came):
    return (add(keep[0], got[0]) + came[0].astype(F32) + came[1].astype(F32) + came[2].astype(F32)).astype(LOW)


def finish_ffn_kernel(where_ref, *rest):
    pieces, (down_ref, up_ref) = rest[:QUARTERS], rest[QUARTERS:]
    mine = where_ref[4]
    for n, ref in enumerate(pieces):
        j = jnp.bitwise_xor(mine, n)
        down_ref[pl.ds(pl.multiple_of(j * ROWS, 8), ROWS), :] = ref[0].astype(F32)
        for half in (0, 1):
            up_ref[:, pl.ds(pl.multiple_of((half * QUARTERS + j) * D, D), D)] = ref[1 + half].astype(F32)


def finish_attention_kernel(where_ref, *rest):
    pieces, (qkv_ref, out_ref, held_ref) = rest[:QUARTERS], rest[QUARTERS:]
    mine = where_ref[4]
    for n, ref in enumerate(pieces):
        held_ref[jnp.bitwise_xor(mine, n)] = ref[...].astype(F32)
    for j in range(3):
        qkv_ref[:, j * D : (j + 1) * D] = held_ref[j]
    out_ref[...] = held_ref[3]


def finish_ffn(where, pieces):
    return pl.pallas_call(
        finish_ffn_kernel,
        out_shape=(out((QUARTERS * ROWS, D), F32), out((ROWS, 2 * QUARTERS * D), F32)),
        in_specs=[SMEM] + [VMEM] * QUARTERS,
        out_specs=(VMEM, VMEM),
        compiler_params=BIG,
        cost_estimate=cost(4),
        name="finish_ffn",
    )(where, *pieces)


def finish_attention(where, pieces):
    return pl.pallas_call(
        finish_attention_kernel,
        out_shape=(out((ROWS, 3 * D), F32), out((ROWS, D), F32)),
        in_specs=[SMEM] + [VMEM] * QUARTERS,
        out_specs=(VMEM, VMEM),
        scratch_shapes=[pltpu.VMEM((QUARTERS, ROWS, D), F32)],
        compiler_params=BIG,
        cost_estimate=cost(2),
        name="finish_attention",
    )(where, *pieces)


def spread(piece, order):
    got = {frozenset(): piece}
    for step in (*order, "c"):
        for key in list(got):
            got[key | {step}] = send(got[key], step)
    return [got[frozenset(n for n, b in zip("yxc", key) if b)] for key in KEYS]


def on_block(hidden_in, w_qkv, w_out, w_up, w_down, gain_attn, shift_attn, gain_ffn, shift_ffn, grad_listed, positions, counts):
    seqs, length, width = hidden_in.shape
    tokens = seqs * length
    most = positions.shape[1]
    i, j = lax.axis_index("fsdp"), lax.axis_index("dp")
    where = jnp.stack([i // 2, i % 2, j // 2, j % 2, j]).astype(jnp.int32)
    ff = w_down.shape[0] * SHARDS
    attn_piece = lax.dynamic_slice_in_dim(jnp.concatenate([w_qkv, w_out], axis=1), j * D, D, axis=1)
    norms = jnp.concatenate([gain_attn, shift_attn, gain_ffn, shift_ffn, jnp.zeros((D - 4 * ROWS,), LOW)])
    attn_piece = jnp.concatenate([attn_piece, jnp.broadcast_to(norms, (EXTRA, D))], axis=0)
    line = jnp.stack([attn_piece] + [send(attn_piece, r) for r in (1, 2, 3)])
    x = hidden_in.reshape(tokens, width)
    line, x_flip = lax.optimization_barrier((line, x.T))
    halves = [
        spread(line[:, start : start + size], order)
        for (start, size), order in zip(HALVES, (("y", "x"), ("x", "y")))
    ]
    lines = [half[n] for n in range(len(KEYS)) for half in halves]
    ffn_piece = jnp.stack(
        [
            lax.dynamic_slice_in_dim(w_up, j * D, D, axis=1),
            lax.dynamic_slice_in_dim(w_up, ff + j * D, D, axis=1),
            lax.dynamic_slice_in_dim(w_down, j * ROWS, ROWS, axis=0),
        ]
    )
    w_ffn = lax.all_gather(ffn_piece, AXES, axis=0, tiled=False).reshape(SHARDS, QUARTERS, 3, ROWS, D)
    tails = jnp.stack([halves[1][n][:, 48, : 4 * ROWS] for n in range(2)])
    tails = jnp.where(i % 2 == 0, tails, tails[::-1])
    tails = jnp.roll(tails[:, ::-1], i // 2 + 1, axis=1)
    norms = tails.transpose(1, 0, 2).reshape(SHARDS, 4, ROWS).transpose(1, 0, 2).reshape(4, D).astype(F32)
    slopes = jnp.exp2(-8.0 * (jnp.arange(HEADS, dtype=F32) + 1.0) / HEADS)
    pos = positions.reshape(seqs * most, 1)
    live = jnp.arange(most, dtype=jnp.int32)[None, :] < counts[:, None]
    dy = jnp.where(live[:, :, None], grad_listed, jnp.zeros_like(grad_listed)).reshape(seqs * most, width)

    qkv, h1, att_m, h1_m, q_m, r1_m, w_attn = attention_forward(where, x, lines, norms, pos, slopes, seqs)
    h_all = jnp.stack(share_dp(h1_m))
    h1, h_all = lax.optimization_barrier((h1, h_all))
    layer_out, dr2, e2, small_ffn = ffn_forward(h1, w_ffn, norms, pos, dy, seqs)
    act, to_gate, to_up = ffn_again(where, h_all, w_ffn)
    other = after(send(e2, "x"), act)
    e_all = jnp.stack([e2, send(e2, "c"), other, send(other, "c")])
    dgate, dup, keep, away = ffn_back(where, e_all, to_gate, to_up, w_ffn)
    part = add(keep, send(away, "c"))
    part, part_away = part[0], part[1].astype(LOW)
    keep_d, away_d = weight_grad(where, act, e_all)
    came = send(part_away, "x")
    got_d = send(away_d, "y")
    keep_g, away_g = weight_grad(where, after(h_all, (away_d, part_away)), dgate)
    got_g = send(away_g, "y")
    keep_u, away_u = weight_grad(where, after(h_all, (away_g, came)), dup)
    got_u = send(away_u, "y")
    dr1, low, datt, small_attn = norm_back_call(dr2, part, after(came, away_u), r1_m, w_attn, norms)
    rhs = attention_back(datt, q_m, qkv, pos, slopes, seqs)
    got_d, rhs = lax.optimization_barrier((got_d, rhs))
    parts_d = line_parts(keep_d, got_d)
    line_d = line_send(parts_d)
    keep0, keep1, away0, away1 = attention_grads(where, x_flip, after(rhs, parts_d), att_m, low, small_attn, small_ffn)
    away0, away1, line_d, got_g, got_u = lax.optimization_barrier((away0, away1, line_d, got_g, got_u))
    came0, came1 = send(away0, "c"), send(away1, "c")
    keep_gu, got_gu = jnp.concatenate([keep_g, keep_u], axis=1), jnp.concatenate([got_g, got_u], axis=1)
    parts_gu = line_parts(keep_gu, got_gu)
    line_gu = line_send(parts_gu)
    g_down = send(line_add(keep_d, got_d, line_d), "down")
    away0, away1 = add(keep0[1], came0[1]).astype(LOW), add(keep1[1], came1[1]).astype(LOW)
    got0, got1 = send(away0, "x"), send(away1, "y")
    grad_in = input_grad(after(rhs, (away0, away1)), w_attn, dr1, positions)
    got0, got1, grad_in = lax.optimization_barrier((got0, got1, grad_in))
    total0 = add(keep0[0], came0[0]) + got0.astype(F32)
    total1 = add(keep1[0], came1[0]) + got1.astype(F32)
    away0, away1 = total0[1].astype(LOW), total1[1].astype(LOW)
    got0, got1 = send(away0, "y"), send(away1, "x")
    g_down, line_gu = after((g_down, line_gu), (away0, away1))
    g_ffn = jnp.concatenate([g_down, line_add(keep_gu, got_gu, line_gu)]).reshape(3, ROWS, D)
    shared = share_dp(g_ffn)
    got0, got1 = after((got0, got1), g_ffn)
    total = jnp.concatenate([add(total0[0], got0), add(total1[0], got1)], axis=1)
    parts = [total[r].astype(LOW) for r in (1, 2, 3)]
    line_a = line_send(parts)
    grad_down, grad_up = finish_ffn(where, after(shared, parts))
    line_a = after(line_a, grad_down)
    g_attn = (total[0] + line_a[0].astype(F32) + line_a[1].astype(F32) + line_a[2].astype(F32))
    small = g_attn[ROWS : ROWS + 4, :ROWS]
    grad_qkv, grad_out = finish_attention(where, share_dp(g_attn[:ROWS].astype(LOW)))
    return (
        layer_out.reshape(seqs, length, width),
        grad_in.reshape(seqs, length, width),
        grad_qkv,
        grad_out,
        grad_up,
        grad_down,
        small[0],
        small[1],
        small[2],
        small[3],
    )


FF = 3072


def slopes():
    return jnp.exp2(-8.0 * (jnp.arange(HEADS, dtype=F32) + 1.0) / HEADS)


def pick(onehot, rows):
    if rows.dtype == LOW:
        return jnp.einsum("svj,sjd->svd", onehot.astype(LOW), rows, preferred_element_type=F32).astype(LOW)
    return jnp.einsum("svj,sjd->svd", onehot, rows, precision=lax.Precision.HIGHEST)


def gather_weights(w_qkv, w_out, w_up, w_down):
    fsdp = lax.axis_size("fsdp")
    dp = lax.axis_size("dp")
    rows, width = w_out.shape
    if rows % (8 * dp):
        return (
            lax.all_gather(w_qkv, "fsdp", axis=0, tiled=True),
            lax.all_gather(w_out, "fsdp", axis=0, tiled=True),
            lax.all_gather(w_up, "fsdp", axis=0, tiled=True),
            lax.all_gather(w_down, "fsdp", axis=0, tiled=True),
        )
    mine = lax.axis_index("dp")
    part = rows // dp
    group = w_down.shape[0] // rows
    joined = jnp.concatenate([w_qkv, w_out, w_up], axis=1)
    joined = lax.dynamic_slice_in_dim(joined, mine * part, part, axis=0)
    down = lax.dynamic_slice_in_dim(w_down, mine * part * group, part * group, axis=0)
    down = jnp.concatenate([down[k * part : (k + 1) * part] for k in range(group)], axis=1)
    full = lax.all_gather(jnp.concatenate([joined, down], axis=1), AXES, axis=0, tiled=True)
    a, b = w_qkv.shape[1], w_qkv.shape[1] + w_out.shape[1]
    c = b + w_up.shape[1]
    full_down = full[:, c:].reshape(fsdp * dp, part, group, width)
    full_down = full_down.transpose(0, 2, 1, 3).reshape(fsdp * dp * part * group, width)
    return full[:, :a], full[:, a:b], full[:, b:c], full_down


def scatter_grads(g_qkv, g_out, g_up, g_down):
    fsdp = lax.axis_size("fsdp")
    dp = lax.axis_size("dp")
    width = g_out.shape[1]
    rows = g_out.shape[0] // fsdp
    if rows % (8 * dp):
        return tuple(
            lax.psum(lax.psum_scatter(g, "fsdp", scatter_dimension=0, tiled=True), "dp")
            for g in (g_qkv, g_out, g_up, g_down)
        )
    part = rows // dp
    group = g_down.shape[0] // g_out.shape[0]
    down = g_down.reshape(fsdp * dp, group, part, width).transpose(0, 2, 1, 3)
    down = down.reshape(fsdp * rows, group * width)
    joined = jnp.concatenate([g_qkv, g_out, g_up, down], axis=1).astype(LOW)
    mine = lax.psum_scatter(joined, AXES, scatter_dimension=0, tiled=True)
    full = lax.all_gather(mine, "dp", axis=0, tiled=True).astype(F32)
    a, b = g_qkv.shape[1], g_qkv.shape[1] + width
    c = b + g_up.shape[1]
    full_down = full[:, c:].reshape(dp, part, group, width).transpose(0, 2, 1, 3)
    return full[:, :a], full[:, a:b], full[:, b:c], full_down.reshape(rows * group, width)


def on_device(hidden_in, w_qkv, w_out, w_up, w_down, gain_attn, shift_attn, gain_ffn, shift_ffn, grad_listed, positions, counts):
    seqs, length, width = hidden_in.shape
    tokens = seqs * length
    most = positions.shape[1]
    norms = jnp.stack([gain_attn, shift_attn, gain_ffn, shift_ffn])
    norms = lax.all_gather(norms, "fsdp", axis=1, tiled=True).astype(F32)
    w_qkv, w_out, w_up, w_down = gather_weights(w_qkv, w_out, w_up, w_down)
    live = jnp.arange(most, dtype=jnp.int32)[None, :] < counts[:, None]
    onehot = (positions[:, :, None] == jnp.arange(length, dtype=jnp.int32)).astype(F32)
    rows_in = hidden_in.reshape(tokens, width)
    slope = slopes()
    scale = HEAD_DIM**-0.5
    qkv = mm(rows_in, w_qkv).astype(LOW)
    split = qkv.reshape(seqs, length, 3, HEADS, HEAD_DIM)
    q, k, v = split[:, :, 0], split[:, :, 1], split[:, :, 2]
    place = jnp.arange(length, dtype=F32)
    bias = -slope[:, None, None] * jnp.abs(place[:, None] - place[None, :])
    s = jnp.einsum("sqhc,skhc->shqk", q, k, preferred_element_type=F32) * scale + bias
    p = jax.nn.softmax(s, axis=-1).astype(LOW)
    att = jnp.einsum("shqk,skhc->sqhc", p, v, preferred_element_type=F32).astype(LOW)
    att = att.reshape(tokens, width)
    r1 = rows_in.astype(F32) + mm(att, w_out)
    unit1, _ = norm_parts(r1)
    h1 = unit1 * norms[0] + norms[1]
    h1_low = h1.astype(LOW)
    u = mm(h1_low, w_up)
    act = (jax.nn.gelu(u[:, :FF], approximate=False) * u[:, FF:]).astype(LOW)
    r2 = h1 + mm(act, w_down)
    unit2, _ = norm_parts(r2)
    layer_out = (unit2 * norms[2] + norms[3]).astype(LOW).reshape(seqs, length, width)
    def listed(a):
        return pick(onehot, a.reshape(seqs, length, -1)).reshape(seqs * most, -1)

    dy = jnp.where(live[:, :, None], grad_listed, 0).astype(F32).reshape(seqs * most, width)
    unit2_m, rstd2_m = norm_parts(listed(r2))
    g_gain_ffn = jnp.sum(dy * unit2_m, axis=0)
    g_shift_ffn = jnp.sum(dy, axis=0)
    dr2 = norm_back(dy, unit2_m, rstd2_m, norms[2])
    e2 = dr2.astype(LOW)
    h1_m = listed(h1_low)
    u_m = mm(h1_m, w_up)
    gate, up = u_m[:, :FF], u_m[:, FF:]
    cdf = 0.5 * (1.0 + lax.erf(gate * (0.5**0.5)))
    pdf = jnp.exp(-0.5 * gate * gate) * ((2.0 * jnp.pi) ** -0.5)
    gelu = gate * cdf
    act_m = (gelu * up).astype(LOW)
    g_down = jnp.einsum("nf,nd->fd", act_m, e2, preferred_element_type=F32)
    dact = jnp.einsum("nd,fd->nf", e2, w_down, preferred_element_type=F32)
    du = jnp.concatenate([dact * up * (cdf + gate * pdf), dact * gelu], axis=1).astype(LOW)
    g_up = jnp.einsum("nd,nf->df", h1_m, du, preferred_element_type=F32)
    dh1 = dr2 + jnp.einsum("nf,df->nd", du, w_up, preferred_element_type=F32)
    unit1_m, rstd1_m = norm_parts(listed(r1))
    g_gain_attn = jnp.sum(dh1 * unit1_m, axis=0)
    g_shift_attn = jnp.sum(dh1, axis=0)
    dr1 = norm_back(dh1, unit1_m, rstd1_m, norms[0])
    e1 = dr1.astype(LOW)
    g_out = jnp.einsum("nd,ne->de", listed(att), e1, preferred_element_type=F32)
    datt = jnp.einsum("ne,de->nd", e1, w_out, preferred_element_type=F32).astype(LOW)
    datt = datt.reshape(seqs, most, HEADS, HEAD_DIM)
    q_m = listed(qkv[:, :width]).reshape(seqs, most, HEADS, HEAD_DIM)
    away = jnp.abs(positions[:, :, None].astype(F32) - place[None, None, :])
    s_m = jnp.einsum("sqhc,skhc->shqk", q_m, k, preferred_element_type=F32) * scale
    p_m = jax.nn.softmax(s_m - slope[None, :, None, None] * away[:, None], axis=-1)
    dv = jnp.einsum("shqk,sqhc->skhc", p_m.astype(LOW), datt, preferred_element_type=F32)
    dp = jnp.einsum("sqhc,skhc->shqk", datt, v, preferred_element_type=F32)
    ds = (p_m * (dp - jnp.sum(dp * p_m, axis=-1, keepdims=True))).astype(LOW)
    dq_m = (jnp.einsum("shqk,skhc->sqhc", ds, k, preferred_element_type=F32) * scale).astype(LOW)
    dk = (jnp.einsum("shqk,sqhc->skhc", ds, q_m, preferred_element_type=F32) * scale).astype(LOW)
    put = (onehot * live[:, :, None]).astype(LOW)
    dq = jnp.einsum("svj,svd->sjd", put, dq_m.reshape(seqs, most, width), preferred_element_type=F32)
    dqkv = jnp.concatenate(
        [dq.astype(LOW).reshape(tokens, width), dk.reshape(tokens, width), dv.astype(LOW).reshape(tokens, width)], axis=1
    )
    g_qkv = jnp.einsum("nd,ne->de", rows_in, dqkv, preferred_element_type=F32)
    dr1_all = jnp.einsum("svj,svd->sjd", onehot * live[:, :, None], dr1.reshape(seqs, most, width), precision=lax.Precision.HIGHEST)
    grad_in = dr1_all.reshape(tokens, width) + jnp.einsum("ne,de->nd", dqkv, w_qkv, preferred_element_type=F32)
    owned = scatter_grads(g_qkv, g_out, g_up, g_down)
    small = lax.psum(jnp.stack([g_gain_attn, g_shift_attn, g_gain_ffn, g_shift_ffn]), AXES)
    share = width // lax.axis_size("fsdp")
    small = lax.dynamic_slice_in_dim(small, lax.axis_index("fsdp") * share, share, axis=1)
    return (
        layer_out,
        grad_in.reshape(seqs, length, width),
        *owned,
        small[0],
        small[1],
        small[2],
        small[3],
    )


def solution(mesh):
    rows3 = P(("fsdp", "dp"), None, None)
    rows2 = P("fsdp", None)
    rows1 = P("fsdp")
    shape = dict(mesh.shape)
    step = on_block if shape == {"fsdp": SHARDS, "dp": QUARTERS} else on_device
    return jax.shard_map(
        step,
        mesh=mesh,
        in_specs=(rows3, rows2, rows2, rows2, rows2, rows1, rows1, rows1, rows1, rows3, P(("fsdp", "dp"), None), P(("fsdp", "dp"))),
        out_specs=(rows3, rows3, rows2, rows2, rows2, rows2, rows1, rows1, rows1, rows1),
        check_vma=False,
    )
```

```python
import functools

import jax
import jax.numpy as jnp
from jax import lax
from jax.experimental import pallas as pl
from jax.experimental.pallas import tpu as pltpu
from jax.sharding import PartitionSpec as P

HEADS = 12
HEAD_DIM = 64
EPS = 1e-12
F32 = jnp.float32
LOW = jnp.bfloat16
AXES = ("fsdp", "dp")
D = 768
ROWS = 96
LINE = 4
SHARDS = D // ROWS
QUARTERS = 4
EXACT = lax.Precision.HIGHEST
SCALE = HEAD_DIM**-0.5
VMEM = pl.BlockSpec(memory_space=pltpu.VMEM)
SMEM = pl.BlockSpec(memory_space=pltpu.SMEM)
BIG = pltpu.CompilerParams(vmem_limit_bytes=60 * 1024 * 1024)


def out(shape, dtype):
    return jax.ShapeDtypeStruct(shape, dtype)


def cost(us):
    return pl.CostEstimate(flops=0, bytes_accessed=int(us * 3.0e6), transcendentals=0)


def mm(a, b):
    return jnp.dot(a, b, preferred_element_type=F32)


def mm_nt(a, b):
    return lax.dot_general(a, b, (((1,), (1,)), ((), ())), preferred_element_type=F32)


def mm_tn(a, b):
    return lax.dot_general(a, b, (((0,), (0,)), ((), ())), preferred_element_type=F32)


def norm_parts(value):
    center = value - jnp.mean(value, axis=-1, keepdims=True)
    rstd = lax.rsqrt(jnp.mean(center * center, axis=-1, keepdims=True) + EPS)
    return center * rstd, rstd


def norm_back(grad, unit, rstd, gain):
    scaled = grad * gain
    return rstd * (
        scaled
        - jnp.mean(scaled, axis=-1, keepdims=True)
        - unit * jnp.mean(scaled * unit, axis=-1, keepdims=True)
    )


def onehot(pos_ref, seq, most, length):
    spots = lax.broadcasted_iota(jnp.int32, (most, length), 1)
    return spots == pos_ref[pl.ds(seq * most, most), :]


def gelu_parts(gate):
    cdf = 0.5 * (1.0 + lax.erf(gate * (0.5**0.5)))
    pdf = jnp.exp(-0.5 * gate * gate) * ((2.0 * jnp.pi) ** -0.5)
    return gate * cdf, cdf + gate * pdf


def slope_of(head):
    return 2.0 ** (-8.0 * (head + 1.0) / HEADS)


def block(ref, *index):
    value = ref[index] if index else ref[...]
    return value.reshape(-1, value.shape[-1])


EXTRA = 8
TAIL = 16
HALVES = ((0, 48), (48, 56))
KEYS = [(ry, rx, rc) for rc in (0, 1) for rx in (0, 1) for ry in (0, 1)]


def attention_kernel(seqs, most, where_ref, slope_ref, x_ref, norm_ref, pos_ref, *rest):
    lines, rest = rest[:16], rest[16:]
    qkv_ref, h1_ref, att_m_ref, h1_m_ref, q_m_ref, r1_m_ref, w_ref, att_ref, r1_ref, sem = rest
    z, y, c_x = where_ref[0], where_ref[1], where_ref[4]
    copies = []
    for n, (ry, rx, rc) in enumerate(KEYS):
        j = jnp.bitwise_xor(c_x, 2 * rx + rc)
        for r in range(LINE):
            shard = 2 * lax.rem(z + LINE - r, LINE) + jnp.bitwise_xor(y, ry)
            for half, (start, size) in enumerate(HALVES):
                size = min(size, ROWS - start)
                copies.append(
                    pltpu.make_async_copy(
                        lines[2 * n + half].at[r, pl.ds(0, size)], w_ref.at[shard, j, pl.ds(start, size)], sem
                    )
                )
    for copy in copies:
        copy.start()
    for copy in copies:
        copy.wait()
    length = x_ref.shape[0] // seqs
    step = 256

    @pl.loop(0, 3 * D // step)
    def _(n):
        j = n // (D // step)
        lane = pl.multiple_of((n - j * (D // step)) * step, step)
        w = w_ref[:, j, :, pl.ds(lane, step)].reshape(D, step)
        qkv_ref[:, pl.ds(pl.multiple_of(n * step, step), step)] = mm(x_ref[...], w).astype(LOW)

    first = lax.broadcasted_iota(jnp.int32, (length, 128), 1) < HEAD_DIM
    row = lax.broadcasted_iota(jnp.int32, (length, length), 0)
    col = lax.broadcasted_iota(jnp.int32, (length, length), 1)
    away = jnp.abs(row - col).astype(F32)

    @pl.loop(0, HEADS // 2)
    def _(t):
        lane = pl.multiple_of(t * 128, 128)
        bias = jnp.concatenate([slope_ref[2 * t] * away, slope_ref[2 * t + 1] * away], axis=0)
        for s in range(seqs):
            rows = slice(s * length, (s + 1) * length)
            q = qkv_ref[rows, pl.ds(lane, 128)]
            k = qkv_ref[rows, pl.ds(D + lane, 128)]
            v = qkv_ref[rows, pl.ds(2 * D + lane, 128)]
            zero = jnp.zeros_like(q)
            both = jnp.concatenate([jnp.where(first, q, zero), jnp.where(first, zero, q)], axis=0)
            score = mm_nt(both, k) * SCALE - bias
            e = jnp.exp(score - jnp.max(score, axis=-1, keepdims=True))
            p = (e * (1.0 / jnp.sum(e, axis=-1, keepdims=True))).astype(LOW)
            mixed = mm(p, v)
            att_ref[rows, pl.ds(lane, 128)] = jnp.where(first, mixed[:length], mixed[length:]).astype(LOW)

    @pl.loop(0, D // step)
    def _(n):
        lane = pl.multiple_of(n * step, step)
        w = w_ref[:, 3, :, pl.ds(lane, step)].reshape(D, step)
        r1_ref[:, pl.ds(lane, step)] = x_ref[:, pl.ds(lane, step)].astype(F32) + mm(att_ref[...], w)

    for s in range(seqs):
        rows = slice(s * length, (s + 1) * length)
        listed = slice(s * most, (s + 1) * most)
        unit, _ = norm_parts(r1_ref[rows, :])
        h1 = unit * norm_ref[0:1, :] + norm_ref[1:2, :]
        h1_ref[rows, :] = h1
        hot = onehot(pos_ref, s, most, length)
        hot_low = hot.astype(LOW)
        r1_m_ref[listed, :] = jnp.dot(hot.astype(F32), r1_ref[rows, :], precision=EXACT, preferred_element_type=F32)
        h1_m_ref[listed, :] = mm(hot_low, h1.astype(LOW)).astype(LOW)
        att_m_ref[listed, :] = mm(hot_low, att_ref[rows, :]).astype(LOW)
        q_m_ref[listed, :] = mm(hot_low, qkv_ref[rows, 0:D]).astype(LOW)


def attention_forward(where, x, lines, norms, pos, slopes, seqs):
    tokens = x.shape[0]
    listed = pos.shape[0]
    return pl.pallas_call(
        functools.partial(attention_kernel, seqs, listed // seqs),
        out_shape=(
            out((tokens, 3 * D), LOW),
            out((tokens, D), F32),
            out((listed, D), LOW),
            out((listed, D), LOW),
            out((listed, D), LOW),
            out((listed, D), F32),
            out((SHARDS, QUARTERS, ROWS, D), LOW),
        ),
        in_specs=[SMEM, SMEM, VMEM, VMEM, VMEM] + [pl.BlockSpec(memory_space=pl.ANY)] * 16,
        out_specs=(VMEM,) * 7,
        scratch_shapes=[pltpu.VMEM((tokens, D), LOW), pltpu.VMEM((tokens, D), F32), pltpu.SemaphoreType.DMA],
        compiler_params=BIG,
        cost_estimate=cost(20),
        name="attention_forward",
    )(where, slopes, x, norms, pos, *lines)


def ffn_kernel(seqs, most, h1_ref, gate_ref, up_ref, down_ref, norm_ref, pos_ref, dy_ref, y_ref, dr2_ref, e2_ref, small_ref, low_ref, act_ref, acc_ref):
    j = pl.program_id(0)
    tokens = h1_ref.shape[0]
    length = tokens // seqs
    step = 256

    @pl.when(j == 0)
    def _():
        low_ref[...] = h1_ref[...].astype(LOW)
        acc_ref[...] = h1_ref[...]

    @pl.loop(0, D // step)
    def _(n):
        lane = pl.multiple_of(n * step, step)
        gate = mm(low_ref[...], gate_ref[:, :, pl.ds(lane, step)].reshape(D, step))
        up = mm(low_ref[...], up_ref[:, :, pl.ds(lane, step)].reshape(D, step))
        cdf = 0.5 * (1.0 + lax.erf(gate * (0.5**0.5)))
        act_ref[:, pl.ds(lane, step)] = (gate * cdf * up).astype(LOW)

    @pl.loop(0, D // step)
    def _(n):
        lane = pl.multiple_of(n * step, step)
        acc_ref[:, pl.ds(lane, step)] += mm(act_ref[...], down_ref[:, :, :, pl.ds(lane, step)].reshape(D, step))

    @pl.when(j == QUARTERS - 1)
    def _():
        gain = norm_ref[2:3, :]
        small = [jnp.zeros((1, D), F32)] * 2
        for s in range(seqs):
            rows = slice(s * length, (s + 1) * length)
            listed = slice(s * most, (s + 1) * most)
            unit, _ = norm_parts(acc_ref[rows, :])
            y_ref[rows, :] = (unit * gain + norm_ref[3:4, :]).astype(LOW)
            hot = onehot(pos_ref, s, most, length).astype(F32)
            picked = jnp.dot(hot, acc_ref[rows, :], precision=EXACT, preferred_element_type=F32)
            unit_m, rstd_m = norm_parts(picked)
            dy = dy_ref[listed, :].astype(F32)
            small = [small[0] + jnp.sum(dy * unit_m, axis=0, keepdims=True), small[1] + jnp.sum(dy, axis=0, keepdims=True)]
            dr2 = norm_back(dy, unit_m, rstd_m, gain)
            dr2_ref[listed, :] = dr2
            e2_ref[listed, :] = dr2.astype(LOW)
        small_ref[...] = jnp.concatenate(small, axis=0)


def ffn_forward(h1, w_ffn, norms, pos, dy, seqs):
    tokens = h1.shape[0]
    listed = pos.shape[0]
    whole = lambda shape: pl.BlockSpec(shape, lambda j: (0,) * len(shape), pipeline_mode=pl.Buffered(1))
    return pl.pallas_call(
        functools.partial(ffn_kernel, seqs, listed // seqs),
        out_shape=(out((tokens, D), LOW), out((listed, D), F32), out((listed, D), LOW), out((2, D), F32)),
        grid=(QUARTERS,),
        in_specs=[
            whole((tokens, D)),
            pl.BlockSpec((SHARDS, None, None, ROWS, D), lambda j: (0, j, 0, 0, 0)),
            pl.BlockSpec((SHARDS, None, None, ROWS, D), lambda j: (0, j, 1, 0, 0)),
            pl.BlockSpec((SHARDS // QUARTERS, QUARTERS, None, ROWS, D), lambda j: (j, 0, 2, 0, 0)),
            whole(norms.shape),
            whole(pos.shape),
            whole(dy.shape),
        ],
        out_specs=(
            pl.BlockSpec((tokens, D), lambda j: (0, 0)),
            pl.BlockSpec((listed, D), lambda j: (0, 0)),
            pl.BlockSpec((listed, D), lambda j: (0, 0)),
            pl.BlockSpec((2, D), lambda j: (0, 0)),
        ),
        scratch_shapes=[pltpu.VMEM((tokens, D), LOW), pltpu.VMEM((tokens, D), LOW), pltpu.VMEM((tokens, D), F32)],
        compiler_params=BIG,
        cost_estimate=cost(16),
        name="ffn_forward",
    )(h1, w_ffn, w_ffn, w_ffn, norms, pos, dy)


def ffn_again_kernel(where_ref, h_ref, gate_ref, up_ref, act_ref, to_gate_ref, to_up_ref):
    step = 256

    @pl.loop(0, D // step)
    def _(n):
        lane = pl.multiple_of(n * step, step)
        rows = block(h_ref)
        gate = mm(rows, gate_ref[:, :, pl.ds(lane, step)].reshape(D, step))
        up = mm(rows, up_ref[:, :, pl.ds(lane, step)].reshape(D, step))
        value, slope = gelu_parts(gate)
        act_ref[:, pl.ds(lane, step)] = (value * up).astype(LOW)
        to_gate_ref[:, pl.ds(lane, step)] = slope * up
        to_up_ref[:, pl.ds(lane, step)] = value


def quarter_specs(which):
    specs = {
        "gate": pl.BlockSpec((SHARDS, None, None, ROWS, D), lambda g, w: (0, w[4], 0, 0, 0)),
        "up": pl.BlockSpec((SHARDS, None, None, ROWS, D), lambda g, w: (0, w[4], 1, 0, 0)),
        "down": pl.BlockSpec((SHARDS // QUARTERS, QUARTERS, None, ROWS, D), lambda g, w: (w[4], 0, 2, 0, 0)),
    }
    return [specs[name] for name in which]


def at_once(shape):
    return pl.BlockSpec(shape, lambda g, w: (0,) * len(shape))


def ffn_again(where, h_all, w_ffn):
    rows = h_all.shape[0] * h_all.shape[1]
    return pl.pallas_call(
        ffn_again_kernel,
        out_shape=(out((rows, D), LOW), out((rows, D), F32), out((rows, D), F32)),
        grid_spec=pltpu.PrefetchScalarGridSpec(
            num_scalar_prefetch=1,
            grid=(1,),
            in_specs=[at_once(h_all.shape), *quarter_specs(["gate", "up"])],
            out_specs=(at_once((rows, D)),) * 3,
        ),
        compiler_params=BIG,
        cost_estimate=cost(6),
        name="ffn_again",
    )(where, h_all, w_ffn, w_ffn)


def ffn_back_kernel(where_ref, e_ref, to_gate_ref, to_up_ref, gate_ref, up_ref, down_ref, dgate_ref, dup_ref, keep_ref, send_ref):
    listed = e_ref.shape[1]
    half = QUARTERS // 2
    for n in range(SHARDS // QUARTERS):
        lanes = slice(n * QUARTERS * ROWS, (n + 1) * QUARTERS * ROWS)
        dact = mm_nt(block(e_ref), block(down_ref, n))
        dgate_ref[:, lanes] = (dact * to_gate_ref[:, lanes]).astype(LOW)
        dup_ref[:, lanes] = (dact * to_up_ref[:, lanes]).astype(LOW)
    for n in range(2):
        shards = slice(n * SHARDS // 2, (n + 1) * SHARDS // 2)
        lanes = slice(n * D // 2, (n + 1) * D // 2)
        part = mm_nt(dgate_ref[...], block(gate_ref, shards)) + mm_nt(dup_ref[...], block(up_ref, shards))
        for r in range(half):
            keep_ref[r, :, lanes] = part[2 * r * listed : (2 * r + 1) * listed]
            send_ref[r, :, lanes] = part[(2 * r + 1) * listed : (2 * r + 2) * listed].astype(LOW)


def ffn_back(where, e_all, to_gate, to_up, w_ffn):
    count, listed, _ = e_all.shape
    rows = count * listed
    return pl.pallas_call(
        ffn_back_kernel,
        out_shape=(out((rows, D), LOW), out((rows, D), LOW), out((count // 2, listed, D), F32), out((count // 2, listed, D), LOW)),
        grid_spec=pltpu.PrefetchScalarGridSpec(
            num_scalar_prefetch=1,
            grid=(1,),
            in_specs=[at_once(e_all.shape), at_once((rows, D)), at_once((rows, D)), *quarter_specs(["gate", "up", "down"])],
            out_specs=(at_once((rows, D)), at_once((rows, D)), at_once((count // 2, listed, D)), at_once((count // 2, listed, D))),
        ),
        compiler_params=BIG,
        cost_estimate=cost(7),
        name="ffn_back",
    )(where, e_all, to_gate, to_up, w_ffn, w_ffn, w_ffn)


def weight_grad_kernel(where_ref, a_ref, b_ref, keep_ref, send_ref, full_ref):
    z, y = where_ref[0], where_ref[1]
    b = block(b_ref)
    step = 256

    @pl.loop(0, D // step)
    def _(n):
        lane = pl.multiple_of(n * step, step)
        a = block(a_ref, *([slice(None)] * (len(a_ref.shape) - 1)), pl.ds(lane, step))
        full_ref[pl.ds(lane, step), :] = mm_tn(a, b)

    for r in range(LINE):
        base = 2 * lax.rem(z + r, LINE)
        for other, ref in ((0, keep_ref), (1, send_ref)):
            start = (base + (y if other == 0 else 1 - y)) * ROWS
            ref[r] = full_ref[pl.ds(pl.multiple_of(start, 8), ROWS), :].astype(LOW)


def weight_grad(where, a, b):
    shape = (LINE, ROWS, D)
    rows = a.size // D
    return pl.pallas_call(
        weight_grad_kernel,
        out_shape=(out(shape, LOW), out(shape, LOW)),
        in_specs=[SMEM, VMEM, VMEM],
        out_specs=(VMEM, VMEM),
        scratch_shapes=[pltpu.VMEM((D, D), F32)],
        compiler_params=BIG,
        cost_estimate=cost(4),
        name="weight_grad",
    )(where, a, b)


def norm_back_kernel(dr2_ref, part_ref, came_ref, r1_ref, w_ref, norm_ref, dr1_ref, low_ref, datt_ref, small_ref):
    dh1 = dr2_ref[...] + part_ref[...] + came_ref[...].astype(F32)
    unit, rstd = norm_parts(r1_ref[...])
    small_ref[0:1, :] = jnp.sum(dh1 * unit, axis=0, keepdims=True)
    small_ref[1:2, :] = jnp.sum(dh1, axis=0, keepdims=True)
    dr1 = norm_back(dh1, unit, rstd, norm_ref[0:1, :])
    dr1_ref[...] = dr1
    low = dr1.astype(LOW)
    low_ref[...] = low
    for n in range(2):
        lanes = slice(n * D // 2, (n + 1) * D // 2)
        datt_ref[:, lanes] = mm_nt(low, block(w_ref, slice(n * SHARDS // 2, (n + 1) * SHARDS // 2))).astype(LOW)


def norm_back_call(dr2, part, came, r1_m, w_attn, norms):
    listed = dr2.shape[0]
    same = lambda shape: pl.BlockSpec(shape, lambda g: (0,) * len(shape))
    rows = same((listed, D))
    return pl.pallas_call(
        norm_back_kernel,
        out_shape=(out((listed, D), F32), out((listed, D), LOW), out((listed, D), LOW), out((2, D), F32)),
        grid=(1,),
        in_specs=[rows, rows, rows, rows, pl.BlockSpec((SHARDS, None, ROWS, D), lambda g: (0, 3, 0, 0)), same((4, D))],
        out_specs=(rows, rows, rows, same((2, D))),
        compiler_params=BIG,
        cost_estimate=cost(4),
        name="norm_back",
    )(dr2, part, came, r1_m, w_attn, norms)


def attention_back_kernel(seqs, most, chosen, slope_ref, datt_ref, q_ref, qkv_ref, pos_ref, rhs_ref, away_ref, hot_ref):
    length = qkv_ref.shape[0] // seqs
    listed = seqs * most
    first_m = lax.broadcasted_iota(jnp.int32, (most, 128), 1) < HEAD_DIM
    spots = lax.broadcasted_iota(jnp.int32, (listed, length), 1)
    away_ref[...] = jnp.abs(pos_ref[...] - spots).astype(F32)
    hot_ref[...] = (spots == pos_ref[...]).astype(LOW)

    def both(value):
        zero = jnp.zeros_like(value)
        return jnp.concatenate([jnp.where(first_m, value, zero), jnp.where(first_m, zero, value)], axis=0)

    @pl.loop(0, HEADS // 2)
    def _(t):
        lane = pl.multiple_of(t * 128, 128)
        for n, s in enumerate(chosen):
            rows = slice(s * length, (s + 1) * length)
            placed = slice(n * length, (n + 1) * length)
            mine = slice(s * most, (s + 1) * most)
            away = away_ref[mine, :]
            q = both(q_ref[mine, pl.ds(lane, 128)])
            da = both(datt_ref[mine, pl.ds(lane, 128)])
            k = qkv_ref[rows, pl.ds(D + lane, 128)]
            v = qkv_ref[rows, pl.ds(2 * D + lane, 128)]
            bias = jnp.concatenate([slope_ref[2 * t] * away, slope_ref[2 * t + 1] * away], axis=0)
            score = mm_nt(q, k) * SCALE - bias
            e = jnp.exp(score - jnp.max(score, axis=-1, keepdims=True))
            p = e * (1.0 / jnp.sum(e, axis=-1, keepdims=True))
            dp = mm_nt(da, v)
            ds = (p * (dp - jnp.sum(dp * p, axis=-1, keepdims=True))).astype(LOW)
            dq = mm(ds, k)
            dq = (jnp.where(first_m, dq[:most], dq[most:]) * SCALE).astype(LOW)
            rhs_ref[placed, pl.ds(lane, 128)] = mm_tn(hot_ref[mine, :], dq).astype(LOW)
            rhs_ref[placed, pl.ds(D + lane, 128)] = (mm_tn(ds, q) * SCALE).astype(LOW)
            rhs_ref[placed, pl.ds(2 * D + lane, 128)] = mm_tn(p.astype(LOW), da).astype(LOW)


def attention_back(datt, q_m, qkv, pos, slopes, seqs, chosen):
    tokens = qkv.shape[0]
    listed = pos.shape[0]
    return pl.pallas_call(
        functools.partial(attention_back_kernel, seqs, listed // seqs, chosen),
        out_shape=out((tokens // seqs * len(chosen), 3 * D), LOW),
        in_specs=[SMEM] + [VMEM] * 4,
        out_specs=VMEM,
        scratch_shapes=[pltpu.VMEM((listed, tokens // seqs), F32), pltpu.VMEM((listed, tokens // seqs), LOW)],
        compiler_params=BIG,
        cost_estimate=cost(8),
        name="attention_back",
    )(slopes, datt, q_m, qkv, pos)


def attention_grads_kernel(where_ref, flip_ref, rhs0_ref, rhs1_ref, att_ref, low_ref, small_attn_ref, small_ffn_ref, keep0_ref, keep1_ref, away0_ref, away1_ref, full_ref, tail_ref):
    z, y, mine = where_ref[0], where_ref[1], where_ref[4]
    half = ROWS // 2
    step = 256
    tail_ref[...] = jnp.zeros(tail_ref.shape, LOW)
    small = jnp.concatenate([small_attn_ref[...], small_ffn_ref[...]], axis=0).astype(LOW)
    for n in range(SHARDS):
        tail_ref[n, 0:4, 0:ROWS] = small[:, n * ROWS : (n + 1) * ROWS]
    for rc in (1, 0):
        cut0_ref, cut1_ref = (keep0_ref, keep1_ref) if rc == 0 else (away0_ref, away1_ref)
        for rx in (0, 1):
            j = jnp.bitwise_xor(mine, 2 * rx + rc)

            @pl.when(j == 3)
            def _():
                for n in range(D // step):
                    rows = slice(n * step, (n + 1) * step)
                    full_ref[rows, :] = mm_tn(att_ref[:, rows], low_ref[...])

            @pl.when(j != 3)
            def _():
                @pl.loop(0, D // step)
                def _(n):
                    lane = pl.multiple_of(n * step, step)
                    cols = pl.ds(pl.multiple_of(j * D + n * step, step), step)
                    first = rhs0_ref.shape[0]
                    full_ref[:, pl.ds(lane, step)] = mm(flip_ref[:, :first], rhs0_ref[:, cols]) + mm(flip_ref[:, first:], rhs1_ref[:, cols])

            for rz in range(LINE):
                base = 2 * lax.rem(z + rz, LINE)
                for ry in (0, 1):
                    shard = base + (y if ry == 0 else 1 - y)
                    start = shard * ROWS
                    cut0_ref[rx, ry, rz] = full_ref[pl.ds(pl.multiple_of(start, 8), half), :].astype(LOW)
                    cut1_ref[ry, rx, rz, 0:half] = full_ref[pl.ds(pl.multiple_of(start + half, 8), half), :].astype(LOW)
                    cut1_ref[ry, rx, rz, half:] = tail_ref[shard]


def attention_grads(where, x_flip, rhs0, rhs1, att_m, low, small_attn, small_ffn):
    half = ROWS // 2
    return pl.pallas_call(
        attention_grads_kernel,
        out_shape=(out((2, 2, LINE, half, D), LOW), out((2, 2, LINE, half + TAIL, D), LOW)) * 2,
        in_specs=[SMEM] + [VMEM] * 7,
        out_specs=(VMEM,) * 4,
        scratch_shapes=[pltpu.VMEM((D, D), F32), pltpu.VMEM((SHARDS, TAIL, D), LOW)],
        compiler_params=BIG,
        cost_estimate=cost(10),
        name="attention_grads",
    )(where, x_flip, rhs0, rhs1, att_m, low, small_attn, small_ffn)


def input_grad_kernel(seqs, rhs0_ref, rhs1_ref, w_ref, dr1_ref, pos_ref, out_ref):
    length = out_ref.shape[0] // seqs
    most = dr1_ref.shape[0] // seqs
    for n in range(2):
        lanes = slice(n * D // 2, (n + 1) * D // 2)
        shards = slice(n * SHARDS // 2, (n + 1) * SHARDS // 2)
        s = 0
        for rhs_ref in (rhs0_ref, rhs1_ref):
            total = mm_nt(rhs_ref[:, 0:D], block(w_ref, shards, 0))
            total += mm_nt(rhs_ref[:, D : 2 * D], block(w_ref, shards, 1))
            total += mm_nt(rhs_ref[:, 2 * D : 3 * D], block(w_ref, shards, 2))
            for m in range(rhs_ref.shape[0] // length):
                hot = (lax.broadcasted_iota(jnp.int32, (length, most), 0) == pos_ref[s : s + 1, :]).astype(F32)
                spread = jnp.dot(hot, dr1_ref[s * most : (s + 1) * most, lanes], precision=EXACT, preferred_element_type=F32)
                out_ref[s * length : (s + 1) * length, lanes] = total[m * length : (m + 1) * length] + spread
                s += 1


def input_grad(rhs0, rhs1, w_attn, dr1, positions):
    tokens = rhs0.shape[0] + rhs1.shape[0]
    return pl.pallas_call(
        functools.partial(input_grad_kernel, positions.shape[0]),
        out_shape=out((tokens, D), F32),
        in_specs=[VMEM] * 5,
        out_specs=VMEM,
        compiler_params=BIG,
        cost_estimate=cost(8),
        name="input_grad",
    )(rhs0, rhs1, w_attn, dr1, positions)


def place(z, y, x, c):
    return (2 * z + y) * 4 + 2 * x + c


def grid_perm(move):
    return [
        (place(z, y, x, c), place(*move(z, y, x, c)))
        for z in range(4)
        for y in range(2)
        for x in range(2)
        for c in range(2)
    ]


MOVES = {
    "x": grid_perm(lambda z, y, x, c: (z, y, 1 - x, c)),
    "y": grid_perm(lambda z, y, x, c: (z, 1 - y, x, c)),
    "c": grid_perm(lambda z, y, x, c: (z, y, x, 1 - c)),
    1: grid_perm(lambda z, y, x, c: ((z + 1) % 4, y, x, c)),
    2: grid_perm(lambda z, y, x, c: ((z + 2) % 4, y, x, c)),
    3: grid_perm(lambda z, y, x, c: ((z + 3) % 4, y, x, c)),
    "down": [(m * 4 + q, (2 * q + m // 4) * 4 + m % 4) for m in range(8) for q in range(4)],
}


def send(value, move):
    return lax.ppermute(value, AXES, MOVES[move])


def share_dp(value):
    other = send(value, "x")
    return value, send(value, "c"), other, send(other, "c")


def after(value, *earlier):
    return lax.optimization_barrier((value, *earlier))[0]


def add(kept, got):
    return kept.astype(F32) + got.astype(F32)


def line_parts(keep, got):
    return [add(keep[r], got[r]).astype(LOW) for r in (1, 2, 3)]


def line_send(parts):
    return [send(value, r) for r, value in zip((1, 2, 3), parts)]


def line_add(keep, got, came):
    return (add(keep[0], got[0]) + came[0].astype(F32) + came[1].astype(F32) + came[2].astype(F32)).astype(LOW)


def finish_ffn_kernel(where_ref, *rest):
    pieces, (down_ref, up_ref) = rest[:QUARTERS], rest[QUARTERS:]
    mine = where_ref[4]
    for n, ref in enumerate(pieces):
        j = jnp.bitwise_xor(mine, n)
        down_ref[pl.ds(pl.multiple_of(j * ROWS, 8), ROWS), :] = ref[0].astype(F32)
        for half in (0, 1):
            up_ref[:, pl.ds(pl.multiple_of((half * QUARTERS + j) * D, D), D)] = ref[1 + half].astype(F32)


def finish_attention_kernel(where_ref, *rest):
    pieces, (qkv_ref, out_ref, held_ref) = rest[:QUARTERS], rest[QUARTERS:]
    mine = where_ref[4]
    for n, ref in enumerate(pieces):
        held_ref[jnp.bitwise_xor(mine, n)] = ref[...].astype(F32)
    for j in range(3):
        qkv_ref[:, j * D : (j + 1) * D] = held_ref[j]
    out_ref[...] = held_ref[3]


def finish_ffn(where, pieces):
    return pl.pallas_call(
        finish_ffn_kernel,
        out_shape=(out((QUARTERS * ROWS, D), F32), out((ROWS, 2 * QUARTERS * D), F32)),
        in_specs=[SMEM] + [VMEM] * QUARTERS,
        out_specs=(VMEM, VMEM),
        compiler_params=BIG,
        cost_estimate=cost(4),
        name="finish_ffn",
    )(where, *pieces)


def finish_attention(where, pieces):
    return pl.pallas_call(
        finish_attention_kernel,
        out_shape=(out((ROWS, 3 * D), F32), out((ROWS, D), F32)),
        in_specs=[SMEM] + [VMEM] * QUARTERS,
        out_specs=(VMEM, VMEM),
        scratch_shapes=[pltpu.VMEM((QUARTERS, ROWS, D), F32)],
        compiler_params=BIG,
        cost_estimate=cost(2),
        name="finish_attention",
    )(where, *pieces)


def spread(piece, order):
    got = {frozenset(): piece}
    for step in (*order, "c"):
        for key in list(got):
            got[key | {step}] = send(got[key], step)
    return [got[frozenset(n for n, b in zip("yxc", key) if b)] for key in KEYS]


def on_block(hidden_in, w_qkv, w_out, w_up, w_down, gain_attn, shift_attn, gain_ffn, shift_ffn, grad_listed, positions, counts):
    seqs, length, width = hidden_in.shape
    tokens = seqs * length
    most = positions.shape[1]
    i, j = lax.axis_index("fsdp"), lax.axis_index("dp")
    where = jnp.stack([i // 2, i % 2, j // 2, j % 2, j]).astype(jnp.int32)
    ff = w_down.shape[0] * SHARDS
    attn_piece = lax.dynamic_slice_in_dim(jnp.concatenate([w_qkv, w_out], axis=1), j * D, D, axis=1)
    norms = jnp.concatenate([gain_attn, shift_attn, gain_ffn, shift_ffn, jnp.zeros((D - 4 * ROWS,), LOW)])
    attn_piece = jnp.concatenate([attn_piece, jnp.broadcast_to(norms, (EXTRA, D))], axis=0)
    line = jnp.stack([attn_piece] + [send(attn_piece, r) for r in (1, 2, 3)])
    x = hidden_in.reshape(tokens, width)
    line, x_flip = lax.optimization_barrier((line, x.T))
    halves = [
        spread(line[:, start : start + size], order)
        for (start, size), order in zip(HALVES, (("y", "x"), ("x", "y")))
    ]
    lines = [half[n] for n in range(len(KEYS)) for half in halves]
    ffn_piece = jnp.stack(
        [
            lax.dynamic_slice_in_dim(w_up, j * D, D, axis=1),
            lax.dynamic_slice_in_dim(w_up, ff + j * D, D, axis=1),
            lax.dynamic_slice_in_dim(w_down, j * ROWS, ROWS, axis=0),
        ]
    )
    w_ffn = lax.all_gather(ffn_piece, AXES, axis=0, tiled=False).reshape(SHARDS, QUARTERS, 3, ROWS, D)
    tails = jnp.stack([halves[1][n][:, 48, : 4 * ROWS] for n in range(2)])
    tails = jnp.where(i % 2 == 0, tails, tails[::-1])
    tails = jnp.roll(tails[:, ::-1], i // 2 + 1, axis=1)
    norms = tails.transpose(1, 0, 2).reshape(SHARDS, 4, ROWS).transpose(1, 0, 2).reshape(4, D).astype(F32)
    slopes = jnp.exp2(-8.0 * (jnp.arange(HEADS, dtype=F32) + 1.0) / HEADS)
    pos = positions.reshape(seqs * most, 1)
    live = jnp.arange(most, dtype=jnp.int32)[None, :] < counts[:, None]
    dy = jnp.where(live[:, :, None], grad_listed, jnp.zeros_like(grad_listed)).reshape(seqs * most, width)

    qkv, h1, att_m, h1_m, q_m, r1_m, w_attn = attention_forward(where, x, lines, norms, pos, slopes, seqs)
    h_all = jnp.stack(share_dp(h1_m))
    h1, h_all = lax.optimization_barrier((h1, h_all))
    layer_out, dr2, e2, small_ffn = ffn_forward(h1, w_ffn, norms, pos, dy, seqs)
    act, to_gate, to_up = ffn_again(where, h_all, w_ffn)
    other = after(send(e2, "x"), act)
    e_all = jnp.stack([e2, send(e2, "c"), other, send(other, "c")])
    dgate, dup, keep, away = ffn_back(where, e_all, to_gate, to_up, w_ffn)
    part = add(keep, send(away, "c"))
    part, part_away = part[0], part[1].astype(LOW)
    keep_d, away_d = weight_grad(where, act, e_all)
    came = send(part_away, "x")
    got_d = send(away_d, "y")
    keep_g, away_g = weight_grad(where, after(h_all, (away_d, part_away)), dgate)
    got_g = send(away_g, "y")
    keep_u, away_u = weight_grad(where, after(h_all, (away_g, came)), dup)
    got_u = send(away_u, "y")
    dr1, low, datt, small_attn = norm_back_call(dr2, part, after(came, away_u), r1_m, w_attn, norms)
    half = seqs // 2
    rhs0 = attention_back(datt, q_m, qkv, pos, slopes, seqs, tuple(range(half)))
    got_d, rhs0 = lax.optimization_barrier((got_d, rhs0))
    parts_d = line_parts(keep_d, got_d)
    line_d = line_send(parts_d)
    rhs1 = attention_back(after(datt, (rhs0, parts_d)), q_m, qkv, pos, slopes, seqs, tuple(range(half, seqs)))
    line_d, got_g, rhs1 = lax.optimization_barrier((line_d, got_g, rhs1))
    parts_g = line_parts(keep_g, got_g)
    line_g = line_send(parts_g)
    keep0, keep1, away0, away1 = attention_grads(where, x_flip, rhs0, after(rhs1, parts_g), att_m, low, small_attn, small_ffn)
    away0, away1, line_g, got_u = lax.optimization_barrier((away0, away1, line_g, got_u))
    came0, came1 = send(away0, "c"), send(away1, "c")
    parts_u = line_parts(keep_u, got_u)
    line_u = line_send(parts_u)
    g_down = send(line_add(keep_d, got_d, line_d), "down")
    away0, away1 = add(keep0[1], came0[1]).astype(LOW), add(keep1[1], came1[1]).astype(LOW)
    got0, got1 = send(away0, "x"), send(away1, "y")
    grad_in = input_grad(rhs0, after(rhs1, (away0, away1)), w_attn, dr1, positions)
    got0, got1, grad_in = lax.optimization_barrier((got0, got1, grad_in))
    total0 = add(keep0[0], came0[0]) + got0.astype(F32)
    total1 = add(keep1[0], came1[0]) + got1.astype(F32)
    away0, away1 = total0[1].astype(LOW), total1[1].astype(LOW)
    got0, got1 = send(away0, "y"), send(away1, "x")
    g_down, line_u = after((g_down, line_u), (away0, away1))
    g_ffn = jnp.stack([g_down, line_add(keep_g, got_g, line_g), line_add(keep_u, got_u, line_u)])
    got0, got1 = after((got0, got1), g_ffn)
    total = jnp.concatenate([add(total0[0], got0), add(total1[0], got1)], axis=1)
    parts = [total[r].astype(LOW) for r in (1, 2, 3)]
    line_a = line_send(parts)
    other = send(g_ffn, "x")
    line_a, other = lax.optimization_barrier((line_a, other))
    g_attn = total[0] + line_a[0].astype(F32) + line_a[1].astype(F32) + line_a[2].astype(F32)
    small = g_attn[ROWS : ROWS + 4, :ROWS]
    g_attn = g_attn[:ROWS].astype(LOW)
    shared = (g_ffn, send(g_ffn, "c"), other, send(other, "c"))
    grad_down, grad_up = finish_ffn(where, after(shared, g_attn))
    other = after(send(g_attn, "x"), grad_down)
    grad_qkv, grad_out = finish_attention(where, (g_attn, send(g_attn, "c"), other, send(other, "c")))
    return (
        layer_out.reshape(seqs, length, width),
        grad_in.reshape(seqs, length, width),
        grad_qkv,
        grad_out,
        grad_up,
        grad_down,
        small[0],
        small[1],
        small[2],
        small[3],
    )


FF = 3072


def slopes():
    return jnp.exp2(-8.0 * (jnp.arange(HEADS, dtype=F32) + 1.0) / HEADS)


def pick(onehot, rows):
    if rows.dtype == LOW:
        return jnp.einsum("svj,sjd->svd", onehot.astype(LOW), rows, preferred_element_type=F32).astype(LOW)
    return jnp.einsum("svj,sjd->svd", onehot, rows, precision=lax.Precision.HIGHEST)


def gather_weights(w_qkv, w_out, w_up, w_down):
    fsdp = lax.axis_size("fsdp")
    dp = lax.axis_size("dp")
    rows, width = w_out.shape
    if rows % (8 * dp):
        return (
            lax.all_gather(w_qkv, "fsdp", axis=0, tiled=True),
            lax.all_gather(w_out, "fsdp", axis=0, tiled=True),
            lax.all_gather(w_up, "fsdp", axis=0, tiled=True),
            lax.all_gather(w_down, "fsdp", axis=0, tiled=True),
        )
    mine = lax.axis_index("dp")
    part = rows // dp
    group = w_down.shape[0] // rows
    joined = jnp.concatenate([w_qkv, w_out, w_up], axis=1)
    joined = lax.dynamic_slice_in_dim(joined, mine * part, part, axis=0)
    down = lax.dynamic_slice_in_dim(w_down, mine * part * group, part * group, axis=0)
    down = jnp.concatenate([down[k * part : (k + 1) * part] for k in range(group)], axis=1)
    full = lax.all_gather(jnp.concatenate([joined, down], axis=1), AXES, axis=0, tiled=True)
    a, b = w_qkv.shape[1], w_qkv.shape[1] + w_out.shape[1]
    c = b + w_up.shape[1]
    full_down = full[:, c:].reshape(fsdp * dp, part, group, width)
    full_down = full_down.transpose(0, 2, 1, 3).reshape(fsdp * dp * part * group, width)
    return full[:, :a], full[:, a:b], full[:, b:c], full_down


def scatter_grads(g_qkv, g_out, g_up, g_down):
    fsdp = lax.axis_size("fsdp")
    dp = lax.axis_size("dp")
    width = g_out.shape[1]
    rows = g_out.shape[0] // fsdp
    if rows % (8 * dp):
        return tuple(
            lax.psum(lax.psum_scatter(g, "fsdp", scatter_dimension=0, tiled=True), "dp")
            for g in (g_qkv, g_out, g_up, g_down)
        )
    part = rows // dp
    group = g_down.shape[0] // g_out.shape[0]
    down = g_down.reshape(fsdp * dp, group, part, width).transpose(0, 2, 1, 3)
    down = down.reshape(fsdp * rows, group * width)
    joined = jnp.concatenate([g_qkv, g_out, g_up, down], axis=1).astype(LOW)
    mine = lax.psum_scatter(joined, AXES, scatter_dimension=0, tiled=True)
    full = lax.all_gather(mine, "dp", axis=0, tiled=True).astype(F32)
    a, b = g_qkv.shape[1], g_qkv.shape[1] + width
    c = b + g_up.shape[1]
    full_down = full[:, c:].reshape(dp, part, group, width).transpose(0, 2, 1, 3)
    return full[:, :a], full[:, a:b], full[:, b:c], full_down.reshape(rows * group, width)


def on_device(hidden_in, w_qkv, w_out, w_up, w_down, gain_attn, shift_attn, gain_ffn, shift_ffn, grad_listed, positions, counts):
    seqs, length, width = hidden_in.shape
    tokens = seqs * length
    most = positions.shape[1]
    norms = jnp.stack([gain_attn, shift_attn, gain_ffn, shift_ffn])
    norms = lax.all_gather(norms, "fsdp", axis=1, tiled=True).astype(F32)
    w_qkv, w_out, w_up, w_down = gather_weights(w_qkv, w_out, w_up, w_down)
    live = jnp.arange(most, dtype=jnp.int32)[None, :] < counts[:, None]
    onehot = (positions[:, :, None] == jnp.arange(length, dtype=jnp.int32)).astype(F32)
    rows_in = hidden_in.reshape(tokens, width)
    slope = slopes()
    scale = HEAD_DIM**-0.5
    qkv = mm(rows_in, w_qkv).astype(LOW)
    split = qkv.reshape(seqs, length, 3, HEADS, HEAD_DIM)
    q, k, v = split[:, :, 0], split[:, :, 1], split[:, :, 2]
    place = jnp.arange(length, dtype=F32)
    bias = -slope[:, None, None] * jnp.abs(place[:, None] - place[None, :])
    s = jnp.einsum("sqhc,skhc->shqk", q, k, preferred_element_type=F32) * scale + bias
    p = jax.nn.softmax(s, axis=-1).astype(LOW)
    att = jnp.einsum("shqk,skhc->sqhc", p, v, preferred_element_type=F32).astype(LOW)
    att = att.reshape(tokens, width)
    r1 = rows_in.astype(F32) + mm(att, w_out)
    unit1, _ = norm_parts(r1)
    h1 = unit1 * norms[0] + norms[1]
    h1_low = h1.astype(LOW)
    u = mm(h1_low, w_up)
    act = (jax.nn.gelu(u[:, :FF], approximate=False) * u[:, FF:]).astype(LOW)
    r2 = h1 + mm(act, w_down)
    unit2, _ = norm_parts(r2)
    layer_out = (unit2 * norms[2] + norms[3]).astype(LOW).reshape(seqs, length, width)
    def listed(a):
        return pick(onehot, a.reshape(seqs, length, -1)).reshape(seqs * most, -1)

    dy = jnp.where(live[:, :, None], grad_listed, 0).astype(F32).reshape(seqs * most, width)
    unit2_m, rstd2_m = norm_parts(listed(r2))
    g_gain_ffn = jnp.sum(dy * unit2_m, axis=0)
    g_shift_ffn = jnp.sum(dy, axis=0)
    dr2 = norm_back(dy, unit2_m, rstd2_m, norms[2])
    e2 = dr2.astype(LOW)
    h1_m = listed(h1_low)
    u_m = mm(h1_m, w_up)
    gate, up = u_m[:, :FF], u_m[:, FF:]
    cdf = 0.5 * (1.0 + lax.erf(gate * (0.5**0.5)))
    pdf = jnp.exp(-0.5 * gate * gate) * ((2.0 * jnp.pi) ** -0.5)
    gelu = gate * cdf
    act_m = (gelu * up).astype(LOW)
    g_down = jnp.einsum("nf,nd->fd", act_m, e2, preferred_element_type=F32)
    dact = jnp.einsum("nd,fd->nf", e2, w_down, preferred_element_type=F32)
    du = jnp.concatenate([dact * up * (cdf + gate * pdf), dact * gelu], axis=1).astype(LOW)
    g_up = jnp.einsum("nd,nf->df", h1_m, du, preferred_element_type=F32)
    dh1 = dr2 + jnp.einsum("nf,df->nd", du, w_up, preferred_element_type=F32)
    unit1_m, rstd1_m = norm_parts(listed(r1))
    g_gain_attn = jnp.sum(dh1 * unit1_m, axis=0)
    g_shift_attn = jnp.sum(dh1, axis=0)
    dr1 = norm_back(dh1, unit1_m, rstd1_m, norms[0])
    e1 = dr1.astype(LOW)
    g_out = jnp.einsum("nd,ne->de", listed(att), e1, preferred_element_type=F32)
    datt = jnp.einsum("ne,de->nd", e1, w_out, preferred_element_type=F32).astype(LOW)
    datt = datt.reshape(seqs, most, HEADS, HEAD_DIM)
    q_m = listed(qkv[:, :width]).reshape(seqs, most, HEADS, HEAD_DIM)
    away = jnp.abs(positions[:, :, None].astype(F32) - place[None, None, :])
    s_m = jnp.einsum("sqhc,skhc->shqk", q_m, k, preferred_element_type=F32) * scale
    p_m = jax.nn.softmax(s_m - slope[None, :, None, None] * away[:, None], axis=-1)
    dv = jnp.einsum("shqk,sqhc->skhc", p_m.astype(LOW), datt, preferred_element_type=F32)
    dp = jnp.einsum("sqhc,skhc->shqk", datt, v, preferred_element_type=F32)
    ds = (p_m * (dp - jnp.sum(dp * p_m, axis=-1, keepdims=True))).astype(LOW)
    dq_m = (jnp.einsum("shqk,skhc->sqhc", ds, k, preferred_element_type=F32) * scale).astype(LOW)
    dk = (jnp.einsum("shqk,sqhc->skhc", ds, q_m, preferred_element_type=F32) * scale).astype(LOW)
    put = (onehot * live[:, :, None]).astype(LOW)
    dq = jnp.einsum("svj,svd->sjd", put, dq_m.reshape(seqs, most, width), preferred_element_type=F32)
    dqkv = jnp.concatenate(
        [dq.astype(LOW).reshape(tokens, width), dk.reshape(tokens, width), dv.astype(LOW).reshape(tokens, width)], axis=1
    )
    g_qkv = jnp.einsum("nd,ne->de", rows_in, dqkv, preferred_element_type=F32)
    dr1_all = jnp.einsum("svj,svd->sjd", onehot * live[:, :, None], dr1.reshape(seqs, most, width), precision=lax.Precision.HIGHEST)
    grad_in = dr1_all.reshape(tokens, width) + jnp.einsum("ne,de->nd", dqkv, w_qkv, preferred_element_type=F32)
    owned = scatter_grads(g_qkv, g_out, g_up, g_down)
    small = lax.psum(jnp.stack([g_gain_attn, g_shift_attn, g_gain_ffn, g_shift_ffn]), AXES)
    share = width // lax.axis_size("fsdp")
    small = lax.dynamic_slice_in_dim(small, lax.axis_index("fsdp") * share, share, axis=1)
    return (
        layer_out,
        grad_in.reshape(seqs, length, width),
        *owned,
        small[0],
        small[1],
        small[2],
        small[3],
    )


def solution(mesh):
    rows3 = P(("fsdp", "dp"), None, None)
    rows2 = P("fsdp", None)
    rows1 = P("fsdp")
    shape = dict(mesh.shape)
    step = on_block if shape == {"fsdp": SHARDS, "dp": QUARTERS} else on_device
    return jax.shard_map(
        step,
        mesh=mesh,
        in_specs=(rows3, rows2, rows2, rows2, rows2, rows1, rows1, rows1, rows1, rows3, P(("fsdp", "dp"), None), P(("fsdp", "dp"))),
        out_specs=(rows3, rows3, rows2, rows2, rows2, rows2, rows1, rows1, rows1, rows1),
        check_vma=False,
    )
```

```python
import functools

import jax
import jax.numpy as jnp
from jax import lax
from jax.experimental import pallas as pl
from jax.experimental.pallas import tpu as pltpu
from jax.sharding import PartitionSpec as P

HEADS = 12
HEAD_DIM = 64
EPS = 1e-12
F32 = jnp.float32
LOW = jnp.bfloat16
AXES = ("fsdp", "dp")
D = 768
ROWS = 96
LINE = 4
SHARDS = D // ROWS
QUARTERS = 4
EXACT = lax.Precision.HIGHEST
SCALE = HEAD_DIM**-0.5
VMEM = pl.BlockSpec(memory_space=pltpu.VMEM)
SMEM = pl.BlockSpec(memory_space=pltpu.SMEM)
BIG = pltpu.CompilerParams(vmem_limit_bytes=60 * 1024 * 1024)


def out(shape, dtype):
    return jax.ShapeDtypeStruct(shape, dtype)


def cost(us):
    return pl.CostEstimate(flops=0, bytes_accessed=int(us * 3.0e6), transcendentals=0)


def mm(a, b):
    return jnp.dot(a, b, preferred_element_type=F32)


def mm_nt(a, b):
    return lax.dot_general(a, b, (((1,), (1,)), ((), ())), preferred_element_type=F32)


def mm_tn(a, b):
    return lax.dot_general(a, b, (((0,), (0,)), ((), ())), preferred_element_type=F32)


def norm_parts(value):
    center = value - jnp.mean(value, axis=-1, keepdims=True)
    rstd = lax.rsqrt(jnp.mean(center * center, axis=-1, keepdims=True) + EPS)
    return center * rstd, rstd


def norm_back(grad, unit, rstd, gain):
    scaled = grad * gain
    return rstd * (
        scaled
        - jnp.mean(scaled, axis=-1, keepdims=True)
        - unit * jnp.mean(scaled * unit, axis=-1, keepdims=True)
    )


def onehot(pos_ref, seq, most, length):
    spots = lax.broadcasted_iota(jnp.int32, (most, length), 1)
    return spots == pos_ref[pl.ds(seq * most, most), :]


def gelu_parts(gate):
    cdf = 0.5 * (1.0 + lax.erf(gate * (0.5**0.5)))
    pdf = jnp.exp(-0.5 * gate * gate) * ((2.0 * jnp.pi) ** -0.5)
    return gate * cdf, cdf + gate * pdf


def slope_of(head):
    return 2.0 ** (-8.0 * (head + 1.0) / HEADS)


def block(ref, *index):
    value = ref[index] if index else ref[...]
    return value.reshape(-1, value.shape[-1])


EXTRA = 8
TAIL = 16
HALVES = ((0, 48), (48, 56))
KEYS = [(ry, rx, rc) for rc in (0, 1) for rx in (0, 1) for ry in (0, 1)]


def attention_kernel(seqs, most, where_ref, slope_ref, x_ref, norm_ref, pos_ref, *rest):
    lines, rest = rest[:16], rest[16:]
    qkv_ref, h1_ref, att_m_ref, h1_m_ref, q_m_ref, r1_m_ref, w_ref, att_ref, r1_ref, sem = rest
    z, y, c_x = where_ref[0], where_ref[1], where_ref[4]
    copies = []
    for n, (ry, rx, rc) in enumerate(KEYS):
        j = jnp.bitwise_xor(c_x, 2 * rx + rc)
        for r in range(LINE):
            shard = 2 * lax.rem(z + LINE - r, LINE) + jnp.bitwise_xor(y, ry)
            for half, (start, size) in enumerate(HALVES):
                size = min(size, ROWS - start)
                copies.append(
                    pltpu.make_async_copy(
                        lines[2 * n + half].at[r, pl.ds(0, size)], w_ref.at[shard, j, pl.ds(start, size)], sem
                    )
                )
    for copy in copies:
        copy.start()
    for copy in copies:
        copy.wait()
    length = x_ref.shape[0] // seqs
    step = 256

    @pl.loop(0, 3 * D // step)
    def _(n):
        j = n // (D // step)
        lane = pl.multiple_of((n - j * (D // step)) * step, step)
        w = w_ref[:, j, :, pl.ds(lane, step)].reshape(D, step)
        qkv_ref[:, pl.ds(pl.multiple_of(n * step, step), step)] = mm(x_ref[...], w).astype(LOW)

    first = lax.broadcasted_iota(jnp.int32, (length, 128), 1) < HEAD_DIM
    row = lax.broadcasted_iota(jnp.int32, (length, length), 0)
    col = lax.broadcasted_iota(jnp.int32, (length, length), 1)
    away = jnp.abs(row - col).astype(F32)

    @pl.loop(0, HEADS // 2)
    def _(t):
        lane = pl.multiple_of(t * 128, 128)
        bias = jnp.concatenate([slope_ref[2 * t] * away, slope_ref[2 * t + 1] * away], axis=0)
        for s in range(seqs):
            rows = slice(s * length, (s + 1) * length)
            q = qkv_ref[rows, pl.ds(lane, 128)]
            k = qkv_ref[rows, pl.ds(D + lane, 128)]
            v = qkv_ref[rows, pl.ds(2 * D + lane, 128)]
            zero = jnp.zeros_like(q)
            both = jnp.concatenate([jnp.where(first, q, zero), jnp.where(first, zero, q)], axis=0)
            score = mm_nt(both, k) * SCALE - bias
            e = jnp.exp(score - jnp.max(score, axis=-1, keepdims=True))
            p = (e * (1.0 / jnp.sum(e, axis=-1, keepdims=True))).astype(LOW)
            mixed = mm(p, v)
            att_ref[rows, pl.ds(lane, 128)] = jnp.where(first, mixed[:length], mixed[length:]).astype(LOW)

    @pl.loop(0, D // step)
    def _(n):
        lane = pl.multiple_of(n * step, step)
        w = w_ref[:, 3, :, pl.ds(lane, step)].reshape(D, step)
        r1_ref[:, pl.ds(lane, step)] = x_ref[:, pl.ds(lane, step)].astype(F32) + mm(att_ref[...], w)

    for s in range(seqs):
        rows = slice(s * length, (s + 1) * length)
        listed = slice(s * most, (s + 1) * most)
        unit, _ = norm_parts(r1_ref[rows, :])
        h1 = unit * norm_ref[0:1, :] + norm_ref[1:2, :]
        h1_ref[rows, :] = h1
        hot = onehot(pos_ref, s, most, length)
        hot_low = hot.astype(LOW)
        r1_m_ref[listed, :] = jnp.dot(hot.astype(F32), r1_ref[rows, :], precision=EXACT, preferred_element_type=F32)
        h1_m_ref[listed, :] = mm(hot_low, h1.astype(LOW)).astype(LOW)
        att_m_ref[listed, :] = mm(hot_low, att_ref[rows, :]).astype(LOW)
        q_m_ref[listed, :] = mm(hot_low, qkv_ref[rows, 0:D]).astype(LOW)


def attention_forward(where, x, lines, norms, pos, slopes, seqs):
    tokens = x.shape[0]
    listed = pos.shape[0]
    return pl.pallas_call(
        functools.partial(attention_kernel, seqs, listed // seqs),
        out_shape=(
            out((tokens, 3 * D), LOW),
            out((tokens, D), F32),
            out((listed, D), LOW),
            out((listed, D), LOW),
            out((listed, D), LOW),
            out((listed, D), F32),
            out((SHARDS, QUARTERS, ROWS, D), LOW),
        ),
        in_specs=[SMEM, SMEM, VMEM, VMEM, VMEM] + [pl.BlockSpec(memory_space=pl.ANY)] * 16,
        out_specs=(VMEM,) * 7,
        scratch_shapes=[pltpu.VMEM((tokens, D), LOW), pltpu.VMEM((tokens, D), F32), pltpu.SemaphoreType.DMA],
        compiler_params=BIG,
        cost_estimate=cost(20),
        name="attention_forward",
    )(where, slopes, x, norms, pos, *lines)


def assemble_kernel(where_ref, *rest):
    pieces, (full_ref, sem) = rest[:4], rest[4:]
    z, y, mine = where_ref[0], where_ref[1], where_ref[4]
    size = ROWS // 2
    copies = []
    for n, piece in enumerate(pieces):
        half, rc = n % 2, n // 2
        for second in (0, 1):
            for first in (0, 1):
                ry, rx = (first, second) if half == 0 else (second, first)
                j = jnp.bitwise_xor(mine, 2 * rx + rc)
                for r in range(LINE):
                    shard = 2 * lax.rem(z + LINE - r, LINE) + jnp.bitwise_xor(y, ry)
                    copies.append(
                        pltpu.make_async_copy(piece.at[second, first, r], full_ref.at[shard, j, pl.ds(half * size, size)], sem)
                    )
    for copy in copies:
        copy.start()
    for copy in copies:
        copy.wait()


def assemble(where, pieces):
    anywhere = pl.BlockSpec(memory_space=pl.ANY)
    return pl.pallas_call(
        assemble_kernel,
        out_shape=out((SHARDS, QUARTERS, ROWS, D), LOW),
        in_specs=[SMEM] + [anywhere] * 4,
        out_specs=anywhere,
        scratch_shapes=[pltpu.SemaphoreType.DMA],
        compiler_params=BIG,
        cost_estimate=cost(3),
        name="assemble",
    )(where, *pieces)


def ffn_kernel(seqs, most, h1_ref, gate_ref, up_ref, down_ref, norm_ref, pos_ref, dy_ref, y_ref, dr2_ref, e2_ref, small_ref, low_ref, act_ref, acc_ref):
    j = pl.program_id(0)
    tokens = h1_ref.shape[0]
    length = tokens // seqs
    step = 256

    @pl.when(j == 0)
    def _():
        low_ref[...] = h1_ref[...].astype(LOW)
        acc_ref[...] = h1_ref[...]

    @pl.loop(0, D // step)
    def _(n):
        lane = pl.multiple_of(n * step, step)
        gate = mm(low_ref[...], gate_ref[:, :, pl.ds(lane, step)].reshape(D, step))
        up = mm(low_ref[...], up_ref[:, :, pl.ds(lane, step)].reshape(D, step))
        cdf = 0.5 * (1.0 + lax.erf(gate * (0.5**0.5)))
        act_ref[:, pl.ds(lane, step)] = (gate * cdf * up).astype(LOW)

    @pl.loop(0, D // step)
    def _(n):
        lane = pl.multiple_of(n * step, step)
        acc_ref[:, pl.ds(lane, step)] += mm(act_ref[...], down_ref[:, :, :, pl.ds(lane, step)].reshape(D, step))

    @pl.when(j == QUARTERS - 1)
    def _():
        gain = norm_ref[2:3, :]
        small = [jnp.zeros((1, D), F32)] * 2
        for s in range(seqs):
            rows = slice(s * length, (s + 1) * length)
            listed = slice(s * most, (s + 1) * most)
            unit, _ = norm_parts(acc_ref[rows, :])
            y_ref[rows, :] = (unit * gain + norm_ref[3:4, :]).astype(LOW)
            hot = onehot(pos_ref, s, most, length).astype(F32)
            picked = jnp.dot(hot, acc_ref[rows, :], precision=EXACT, preferred_element_type=F32)
            unit_m, rstd_m = norm_parts(picked)
            dy = dy_ref[listed, :].astype(F32)
            small = [small[0] + jnp.sum(dy * unit_m, axis=0, keepdims=True), small[1] + jnp.sum(dy, axis=0, keepdims=True)]
            dr2 = norm_back(dy, unit_m, rstd_m, gain)
            dr2_ref[listed, :] = dr2
            e2_ref[listed, :] = dr2.astype(LOW)
        small_ref[...] = jnp.concatenate(small, axis=0)


def ffn_forward(h1, w_gu, w_down, norms, pos, dy, seqs):
    tokens = h1.shape[0]
    listed = pos.shape[0]
    whole = lambda shape: pl.BlockSpec(shape, lambda j: (0,) * len(shape), pipeline_mode=pl.Buffered(1))
    return pl.pallas_call(
        functools.partial(ffn_kernel, seqs, listed // seqs),
        out_shape=(out((tokens, D), LOW), out((listed, D), F32), out((listed, D), LOW), out((2, D), F32)),
        grid=(QUARTERS,),
        in_specs=[
            whole((tokens, D)),
            pl.BlockSpec((SHARDS, None, None, ROWS, D), lambda j: (0, j, 0, 0, 0)),
            pl.BlockSpec((SHARDS, None, None, ROWS, D), lambda j: (0, j, 1, 0, 0)),
            pl.BlockSpec((SHARDS // QUARTERS, QUARTERS, ROWS, D), lambda j: (j, 0, 0, 0)),
            whole(norms.shape),
            whole(pos.shape),
            whole(dy.shape),
        ],
        out_specs=(
            pl.BlockSpec((tokens, D), lambda j: (0, 0)),
            pl.BlockSpec((listed, D), lambda j: (0, 0)),
            pl.BlockSpec((listed, D), lambda j: (0, 0)),
            pl.BlockSpec((2, D), lambda j: (0, 0)),
        ),
        scratch_shapes=[pltpu.VMEM((tokens, D), LOW), pltpu.VMEM((tokens, D), LOW), pltpu.VMEM((tokens, D), F32)],
        compiler_params=BIG,
        cost_estimate=cost(16),
        name="ffn_forward",
    )(h1, w_gu, w_gu, w_down, norms, pos, dy)


def ffn_again_kernel(where_ref, h_ref, gate_ref, up_ref, act_ref, to_gate_ref, to_up_ref):
    step = 256

    @pl.loop(0, D // step)
    def _(n):
        lane = pl.multiple_of(n * step, step)
        rows = block(h_ref)
        gate = mm(rows, gate_ref[:, :, pl.ds(lane, step)].reshape(D, step))
        up = mm(rows, up_ref[:, :, pl.ds(lane, step)].reshape(D, step))
        value, slope = gelu_parts(gate)
        act_ref[:, pl.ds(lane, step)] = (value * up).astype(LOW)
        to_gate_ref[:, pl.ds(lane, step)] = slope * up
        to_up_ref[:, pl.ds(lane, step)] = value


def quarter_specs(which):
    specs = {
        "gate": pl.BlockSpec((SHARDS, None, None, ROWS, D), lambda g, w: (0, w[4], 0, 0, 0)),
        "up": pl.BlockSpec((SHARDS, None, None, ROWS, D), lambda g, w: (0, w[4], 1, 0, 0)),
        "down": pl.BlockSpec((SHARDS // QUARTERS, QUARTERS, ROWS, D), lambda g, w: (w[4], 0, 0, 0)),
    }
    return [specs[name] for name in which]


def at_once(shape):
    return pl.BlockSpec(shape, lambda g, w: (0,) * len(shape))


def ffn_again(where, h_all, w_gu):
    rows = h_all.shape[0] * h_all.shape[1]
    return pl.pallas_call(
        ffn_again_kernel,
        out_shape=(out((rows, D), LOW), out((rows, D), F32), out((rows, D), F32)),
        grid_spec=pltpu.PrefetchScalarGridSpec(
            num_scalar_prefetch=1,
            grid=(1,),
            in_specs=[at_once(h_all.shape), *quarter_specs(["gate", "up"])],
            out_specs=(at_once((rows, D)),) * 3,
        ),
        compiler_params=BIG,
        cost_estimate=cost(6),
        name="ffn_again",
    )(where, h_all, w_gu, w_gu)


def ffn_back_kernel(where_ref, e_ref, to_gate_ref, to_up_ref, gate_ref, up_ref, down_ref, dgate_ref, dup_ref, keep_ref, send_ref):
    listed = e_ref.shape[1]
    half = QUARTERS // 2
    for n in range(SHARDS // QUARTERS):
        lanes = slice(n * QUARTERS * ROWS, (n + 1) * QUARTERS * ROWS)
        dact = mm_nt(block(e_ref), block(down_ref, n))
        dgate_ref[:, lanes] = (dact * to_gate_ref[:, lanes]).astype(LOW)
        dup_ref[:, lanes] = (dact * to_up_ref[:, lanes]).astype(LOW)
    for n in range(2):
        shards = slice(n * SHARDS // 2, (n + 1) * SHARDS // 2)
        lanes = slice(n * D // 2, (n + 1) * D // 2)
        part = mm_nt(dgate_ref[...], block(gate_ref, shards)) + mm_nt(dup_ref[...], block(up_ref, shards))
        for r in range(half):
            keep_ref[r, :, lanes] = part[2 * r * listed : (2 * r + 1) * listed]
            send_ref[r, :, lanes] = part[(2 * r + 1) * listed : (2 * r + 2) * listed].astype(LOW)


def ffn_back(where, e_all, to_gate, to_up, w_gu, w_down):
    count, listed, _ = e_all.shape
    rows = count * listed
    return pl.pallas_call(
        ffn_back_kernel,
        out_shape=(out((rows, D), LOW), out((rows, D), LOW), out((count // 2, listed, D), F32), out((count // 2, listed, D), LOW)),
        grid_spec=pltpu.PrefetchScalarGridSpec(
            num_scalar_prefetch=1,
            grid=(1,),
            in_specs=[at_once(e_all.shape), at_once((rows, D)), at_once((rows, D)), *quarter_specs(["gate", "up", "down"])],
            out_specs=(at_once((rows, D)), at_once((rows, D)), at_once((count // 2, listed, D)), at_once((count // 2, listed, D))),
        ),
        compiler_params=BIG,
        cost_estimate=cost(7),
        name="ffn_back",
    )(where, e_all, to_gate, to_up, w_gu, w_gu, w_down)


def weight_grad_kernel(where_ref, a_ref, b_ref, keep_ref, send_ref, full_ref):
    z, y = where_ref[0], where_ref[1]
    b = block(b_ref)
    step = 256

    @pl.loop(0, D // step)
    def _(n):
        lane = pl.multiple_of(n * step, step)
        a = block(a_ref, *([slice(None)] * (len(a_ref.shape) - 1)), pl.ds(lane, step))
        full_ref[pl.ds(lane, step), :] = mm_tn(a, b)

    for r in range(LINE):
        base = 2 * lax.rem(z + r, LINE)
        for other, ref in ((0, keep_ref), (1, send_ref)):
            start = (base + (y if other == 0 else 1 - y)) * ROWS
            ref[r] = full_ref[pl.ds(pl.multiple_of(start, 8), ROWS), :].astype(LOW)


def weight_grad(where, a, b):
    shape = (LINE, ROWS, D)
    rows = a.size // D
    return pl.pallas_call(
        weight_grad_kernel,
        out_shape=(out(shape, LOW), out(shape, LOW)),
        in_specs=[SMEM, VMEM, VMEM],
        out_specs=(VMEM, VMEM),
        scratch_shapes=[pltpu.VMEM((D, D), F32)],
        compiler_params=BIG,
        cost_estimate=cost(4),
        name="weight_grad",
    )(where, a, b)


def norm_back_kernel(dr2_ref, part_ref, came_ref, r1_ref, w_ref, norm_ref, dr1_ref, low_ref, datt_ref, small_ref):
    dh1 = dr2_ref[...] + part_ref[...] + came_ref[...].astype(F32)
    unit, rstd = norm_parts(r1_ref[...])
    small_ref[0:1, :] = jnp.sum(dh1 * unit, axis=0, keepdims=True)
    small_ref[1:2, :] = jnp.sum(dh1, axis=0, keepdims=True)
    dr1 = norm_back(dh1, unit, rstd, norm_ref[0:1, :])
    dr1_ref[...] = dr1
    low = dr1.astype(LOW)
    low_ref[...] = low
    for n in range(2):
        lanes = slice(n * D // 2, (n + 1) * D // 2)
        datt_ref[:, lanes] = mm_nt(low, block(w_ref, slice(n * SHARDS // 2, (n + 1) * SHARDS // 2))).astype(LOW)


def norm_back_call(dr2, part, came, r1_m, w_attn, norms):
    listed = dr2.shape[0]
    same = lambda shape: pl.BlockSpec(shape, lambda g: (0,) * len(shape))
    rows = same((listed, D))
    return pl.pallas_call(
        norm_back_kernel,
        out_shape=(out((listed, D), F32), out((listed, D), LOW), out((listed, D), LOW), out((2, D), F32)),
        grid=(1,),
        in_specs=[rows, rows, rows, rows, pl.BlockSpec((SHARDS, None, ROWS, D), lambda g: (0, 3, 0, 0)), same((4, D))],
        out_specs=(rows, rows, rows, same((2, D))),
        compiler_params=BIG,
        cost_estimate=cost(4),
        name="norm_back",
    )(dr2, part, came, r1_m, w_attn, norms)


def attention_back_kernel(seqs, most, slope_ref, datt_ref, q_ref, qkv_ref, pos_ref, rhs_ref, away_ref, hot_ref):
    length = qkv_ref.shape[0] // seqs
    listed = seqs * most
    first_m = lax.broadcasted_iota(jnp.int32, (most, 128), 1) < HEAD_DIM
    spots = lax.broadcasted_iota(jnp.int32, (listed, length), 1)
    away_ref[...] = jnp.abs(pos_ref[...] - spots).astype(F32)
    hot_ref[...] = (spots == pos_ref[...]).astype(LOW)

    def both(value):
        zero = jnp.zeros_like(value)
        return jnp.concatenate([jnp.where(first_m, value, zero), jnp.where(first_m, zero, value)], axis=0)

    @pl.loop(0, HEADS // 2)
    def _(t):
        lane = pl.multiple_of(t * 128, 128)
        for s in range(seqs):
            rows = slice(s * length, (s + 1) * length)
            mine = slice(s * most, (s + 1) * most)
            away = away_ref[mine, :]
            q = both(q_ref[mine, pl.ds(lane, 128)])
            da = both(datt_ref[mine, pl.ds(lane, 128)])
            k = qkv_ref[rows, pl.ds(D + lane, 128)]
            v = qkv_ref[rows, pl.ds(2 * D + lane, 128)]
            bias = jnp.concatenate([slope_ref[2 * t] * away, slope_ref[2 * t + 1] * away], axis=0)
            score = mm_nt(q, k) * SCALE - bias
            e = jnp.exp(score - jnp.max(score, axis=-1, keepdims=True))
            p = e * (1.0 / jnp.sum(e, axis=-1, keepdims=True))
            dp = mm_nt(da, v)
            ds = (p * (dp - jnp.sum(dp * p, axis=-1, keepdims=True))).astype(LOW)
            dq = mm(ds, k)
            dq = (jnp.where(first_m, dq[:most], dq[most:]) * SCALE).astype(LOW)
            rhs_ref[rows, pl.ds(lane, 128)] = mm_tn(hot_ref[mine, :], dq).astype(LOW)
            rhs_ref[rows, pl.ds(D + lane, 128)] = (mm_tn(ds, q) * SCALE).astype(LOW)
            rhs_ref[rows, pl.ds(2 * D + lane, 128)] = mm_tn(p.astype(LOW), da).astype(LOW)


def attention_back(datt, q_m, qkv, pos, slopes, seqs, part):
    tokens, listed = qkv.shape[0] // 2, pos.shape[0] // 2
    length = tokens * 2 // seqs
    mine = lambda shape: pl.BlockSpec(shape, lambda g: (part, 0))
    return pl.pallas_call(
        functools.partial(attention_back_kernel, seqs // 2, listed * 2 // seqs),
        out_shape=out((tokens, 3 * D), LOW),
        grid=(1,),
        in_specs=[SMEM, mine((listed, D)), mine((listed, D)), mine((tokens, 3 * D)), mine((listed, 1))],
        out_specs=pl.BlockSpec((tokens, 3 * D), lambda g: (0, 0)),
        scratch_shapes=[pltpu.VMEM((listed, length), F32), pltpu.VMEM((listed, length), LOW)],
        compiler_params=BIG,
        cost_estimate=cost(8),
        name="attention_back",
    )(slopes, datt, q_m, qkv, pos)


def attention_grads_kernel(where_ref, flip_ref, rhs0_ref, rhs1_ref, att_ref, low_ref, small_attn_ref, small_ffn_ref, keep0_ref, keep1_ref, away0_ref, away1_ref, full_ref, tail_ref):
    z, y, mine = where_ref[0], where_ref[1], where_ref[4]
    half = ROWS // 2
    step = 256
    tail_ref[...] = jnp.zeros(tail_ref.shape, LOW)
    small = jnp.concatenate([small_attn_ref[...], small_ffn_ref[...]], axis=0).astype(LOW)
    for n in range(SHARDS):
        tail_ref[n, 0:4, 0:ROWS] = small[:, n * ROWS : (n + 1) * ROWS]
    for rc in (1, 0):
        cut0_ref, cut1_ref = (keep0_ref, keep1_ref) if rc == 0 else (away0_ref, away1_ref)
        for rx in (0, 1):
            j = jnp.bitwise_xor(mine, 2 * rx + rc)

            @pl.when(j == 3)
            def _():
                for n in range(D // step):
                    rows = slice(n * step, (n + 1) * step)
                    full_ref[rows, :] = mm_tn(att_ref[:, rows], low_ref[...])

            @pl.when(j != 3)
            def _():
                @pl.loop(0, D // step)
                def _(n):
                    lane = pl.multiple_of(n * step, step)
                    cols = pl.ds(pl.multiple_of(j * D + n * step, step), step)
                    first = rhs0_ref.shape[0]
                    full_ref[:, pl.ds(lane, step)] = mm(flip_ref[:, :first], rhs0_ref[:, cols]) + mm(flip_ref[:, first:], rhs1_ref[:, cols])

            for rz in range(LINE):
                base = 2 * lax.rem(z + rz, LINE)
                for ry in (0, 1):
                    shard = base + (y if ry == 0 else 1 - y)
                    start = shard * ROWS
                    cut0_ref[rx, ry, rz] = full_ref[pl.ds(pl.multiple_of(start, 8), half), :].astype(LOW)
                    cut1_ref[ry, rx, rz, 0:half] = full_ref[pl.ds(pl.multiple_of(start + half, 8), half), :].astype(LOW)
                    cut1_ref[ry, rx, rz, half:] = tail_ref[shard]


def attention_grads(where, x_flip, rhs0, rhs1, att_m, low, small_attn, small_ffn):
    half = ROWS // 2
    return pl.pallas_call(
        attention_grads_kernel,
        out_shape=(out((2, 2, LINE, half, D), LOW), out((2, 2, LINE, half + TAIL, D), LOW)) * 2,
        in_specs=[SMEM] + [VMEM] * 7,
        out_specs=(VMEM,) * 4,
        scratch_shapes=[pltpu.VMEM((D, D), F32), pltpu.VMEM((SHARDS, TAIL, D), LOW)],
        compiler_params=BIG,
        cost_estimate=cost(10),
        name="attention_grads",
    )(where, x_flip, rhs0, rhs1, att_m, low, small_attn, small_ffn)


def input_grad_kernel(seqs, rhs0_ref, rhs1_ref, w_ref, dr1_ref, pos_ref, out_ref):
    length = out_ref.shape[0] // seqs
    most = dr1_ref.shape[0] // seqs
    for n in range(2):
        lanes = slice(n * D // 2, (n + 1) * D // 2)
        shards = slice(n * SHARDS // 2, (n + 1) * SHARDS // 2)
        s = 0
        for rhs_ref in (rhs0_ref, rhs1_ref):
            total = mm_nt(rhs_ref[:, 0:D], block(w_ref, shards, 0))
            total += mm_nt(rhs_ref[:, D : 2 * D], block(w_ref, shards, 1))
            total += mm_nt(rhs_ref[:, 2 * D : 3 * D], block(w_ref, shards, 2))
            for m in range(rhs_ref.shape[0] // length):
                hot = (lax.broadcasted_iota(jnp.int32, (length, most), 0) == pos_ref[s : s + 1, :]).astype(F32)
                spread = jnp.dot(hot, dr1_ref[s * most : (s + 1) * most, lanes], precision=EXACT, preferred_element_type=F32)
                out_ref[s * length : (s + 1) * length, lanes] = total[m * length : (m + 1) * length] + spread
                s += 1


def input_grad(rhs0, rhs1, w_attn, dr1, positions):
    tokens = rhs0.shape[0] + rhs1.shape[0]
    return pl.pallas_call(
        functools.partial(input_grad_kernel, positions.shape[0]),
        out_shape=out((tokens, D), F32),
        in_specs=[VMEM] * 5,
        out_specs=VMEM,
        compiler_params=BIG,
        cost_estimate=cost(8),
        name="input_grad",
    )(rhs0, rhs1, w_attn, dr1, positions)


def place(z, y, x, c):
    return (2 * z + y) * 4 + 2 * x + c


def grid_perm(move):
    return [
        (place(z, y, x, c), place(*move(z, y, x, c)))
        for z in range(4)
        for y in range(2)
        for x in range(2)
        for c in range(2)
    ]


MOVES = {
    "x": grid_perm(lambda z, y, x, c: (z, y, 1 - x, c)),
    "y": grid_perm(lambda z, y, x, c: (z, 1 - y, x, c)),
    "c": grid_perm(lambda z, y, x, c: (z, y, x, 1 - c)),
    1: grid_perm(lambda z, y, x, c: ((z + 1) % 4, y, x, c)),
    2: grid_perm(lambda z, y, x, c: ((z + 2) % 4, y, x, c)),
    3: grid_perm(lambda z, y, x, c: ((z + 3) % 4, y, x, c)),
    "down": [(m * 4 + q, (2 * q + m // 4) * 4 + m % 4) for m in range(8) for q in range(4)],
}


def send(value, move):
    return lax.ppermute(value, AXES, MOVES[move])


def share_dp(value):
    other = send(value, "x")
    return value, send(value, "c"), other, send(other, "c")


def after(value, *earlier):
    return lax.optimization_barrier((value, *earlier))[0]


def add(kept, got):
    return kept.astype(F32) + got.astype(F32)


def line_parts(keep, got):
    return [add(keep[r], got[r]).astype(LOW) for r in (1, 2, 3)]


def line_send(parts):
    return [send(value, r) for r, value in zip((1, 2, 3), parts)]


def line_add(keep, got, came):
    return (add(keep[0], got[0]) + came[0].astype(F32) + came[1].astype(F32) + came[2].astype(F32)).astype(LOW)


def finish_ffn_kernel(where_ref, *rest):
    pieces, (down_ref, up_ref) = rest[:QUARTERS], rest[QUARTERS:]
    mine = where_ref[4]
    for n, ref in enumerate(pieces):
        j = jnp.bitwise_xor(mine, n)
        down_ref[pl.ds(pl.multiple_of(j * ROWS, 8), ROWS), :] = ref[0].astype(F32)
        for half in (0, 1):
            up_ref[:, pl.ds(pl.multiple_of((half * QUARTERS + j) * D, D), D)] = ref[1 + half].astype(F32)


def finish_attention_kernel(where_ref, *rest):
    pieces, (qkv_ref, out_ref, held_ref) = rest[:QUARTERS], rest[QUARTERS:]
    mine = where_ref[4]
    for n, ref in enumerate(pieces):
        held_ref[jnp.bitwise_xor(mine, n)] = ref[...].astype(F32)
    for j in range(3):
        qkv_ref[:, j * D : (j + 1) * D] = held_ref[j]
    out_ref[...] = held_ref[3]


def finish_ffn(where, pieces):
    return pl.pallas_call(
        finish_ffn_kernel,
        out_shape=(out((QUARTERS * ROWS, D), F32), out((ROWS, 2 * QUARTERS * D), F32)),
        in_specs=[SMEM] + [VMEM] * QUARTERS,
        out_specs=(VMEM, VMEM),
        compiler_params=BIG,
        cost_estimate=cost(4),
        name="finish_ffn",
    )(where, *pieces)


def finish_attention(where, pieces):
    return pl.pallas_call(
        finish_attention_kernel,
        out_shape=(out((ROWS, 3 * D), F32), out((ROWS, D), F32)),
        in_specs=[SMEM] + [VMEM] * QUARTERS,
        out_specs=(VMEM, VMEM),
        scratch_shapes=[pltpu.VMEM((QUARTERS, ROWS, D), F32)],
        compiler_params=BIG,
        cost_estimate=cost(2),
        name="finish_attention",
    )(where, *pieces)


def on_block(hidden_in, w_qkv, w_out, w_up, w_down, gain_attn, shift_attn, gain_ffn, shift_ffn, grad_listed, positions, counts):
    seqs, length, width = hidden_in.shape
    tokens = seqs * length
    most = positions.shape[1]
    i, j = lax.axis_index("fsdp"), lax.axis_index("dp")
    where = jnp.stack([i // 2, i % 2, j // 2, j % 2, j]).astype(jnp.int32)
    ff = w_down.shape[0] * SHARDS
    attn_piece = lax.dynamic_slice_in_dim(jnp.concatenate([w_qkv, w_out], axis=1), j * D, D, axis=1)
    norms = jnp.concatenate([gain_attn, shift_attn, gain_ffn, shift_ffn, jnp.zeros((D - 4 * ROWS,), LOW)])
    attn_piece = jnp.concatenate([attn_piece, jnp.broadcast_to(norms, (EXTRA, D))], axis=0)
    line = jnp.stack([attn_piece] + [send(attn_piece, r) for r in (1, 2, 3)])
    x = hidden_in.reshape(tokens, width)
    line, x_flip = lax.optimization_barrier((line, x.T))
    down_piece = after(lax.dynamic_slice_in_dim(w_down, j * ROWS, ROWS, axis=0), line)
    down_line = jnp.stack([down_piece] + [send(down_piece, r) for r in (1, 2, 3)])
    cuts = [line[:, start : start + size] for start, size in HALVES]
    orders = (("y", "x"), ("x", "y"))
    got = [{(): cut, (order[0],): send(cut, order[0])} for cut, order in zip(cuts, orders)]
    got, down_line = lax.optimization_barrier((got, down_line))
    for have, order in zip(got, orders):
        for key in list(have):
            have[(*key, order[1])] = send(have[key], order[1])
    got, down_line = lax.optimization_barrier((got, down_line))
    downs = [down_line[:, : ROWS // 2], down_line[:, ROWS // 2 :]]
    downs = [jnp.stack([cut, send(cut, order[0])]) for cut, order in zip(downs, orders)]
    for have in got:
        for key in list(have):
            have[(*key, "c")] = send(have[key], "c")
    halves = []
    for have, order in zip(got, orders):
        flags = [dict(zip("yxc", key)) for key in KEYS]
        halves.append([have[tuple(step for step in (*order, "c") if flag[step])] for flag in flags])
    lines = [half[n] for n in range(len(KEYS)) for half in halves]
    gu_piece = jnp.stack([lax.dynamic_slice_in_dim(w_up, start + j * D, D, axis=1) for start in (0, ff)])
    w_gu = lax.all_gather(gu_piece, AXES, axis=0, tiled=False).reshape(SHARDS, QUARTERS, 2, ROWS, D)
    tails = jnp.stack([halves[1][n][:, 48, : 4 * ROWS] for n in range(2)])
    tails = jnp.where(i % 2 == 0, tails, tails[::-1])
    tails = jnp.roll(tails[:, ::-1], i // 2 + 1, axis=1)
    norms = tails.transpose(1, 0, 2).reshape(SHARDS, 4, ROWS).transpose(1, 0, 2).reshape(4, D).astype(F32)
    slopes = jnp.exp2(-8.0 * (jnp.arange(HEADS, dtype=F32) + 1.0) / HEADS)
    pos = positions.reshape(seqs * most, 1)
    live = jnp.arange(most, dtype=jnp.int32)[None, :] < counts[:, None]
    dy = jnp.where(live[:, :, None], grad_listed, jnp.zeros_like(grad_listed)).reshape(seqs * most, width)

    qkv, h1, att_m, h1_m, q_m, r1_m, w_attn = attention_forward(where, after(x, downs), lines, norms, pos, slopes, seqs)
    downs_far, h1 = lax.optimization_barrier(([send(cut, order[1]) for cut, order in zip(downs, orders)], h1))
    downs = [jnp.stack(pair) for pair in zip(downs, downs_far)]
    down_all = assemble(where, (*downs, *[send(cut, "c") for cut in downs]))
    h_all = jnp.stack(share_dp(h1_m))
    h1, h_all = lax.optimization_barrier((h1, h_all))
    layer_out, dr2, e2, small_ffn = ffn_forward(h1, w_gu, down_all, norms, pos, dy, seqs)
    act, to_gate, to_up = ffn_again(where, h_all, w_gu)
    other = after(send(e2, "x"), act)
    e_all = jnp.stack([e2, send(e2, "c"), other, send(other, "c")])
    dgate, dup, keep, away = ffn_back(where, e_all, to_gate, to_up, w_gu, down_all)
    part = add(keep, send(away, "c"))
    part, part_away = part[0], part[1].astype(LOW)
    keep_d, away_d = weight_grad(where, act, e_all)
    came = send(part_away, "x")
    got_d = send(away_d, "y")
    keep_g, away_g = weight_grad(where, after(h_all, (away_d, part_away)), dgate)
    got_g = send(away_g, "y")
    keep_u, away_u = weight_grad(where, after(h_all, (away_g, came)), dup)
    got_u = send(away_u, "y")
    dr1, low, datt, small_attn = norm_back_call(dr2, part, after(came, away_u), r1_m, w_attn, norms)
    rhs0 = attention_back(datt, q_m, qkv, pos, slopes, seqs, 0)
    got_d, rhs0 = lax.optimization_barrier((got_d, rhs0))
    parts_d = line_parts(keep_d, got_d)
    line_d = line_send(parts_d)
    rhs1 = attention_back(after(datt, (rhs0, parts_d)), q_m, qkv, pos, slopes, seqs, 1)
    line_d, got_g, rhs1 = lax.optimization_barrier((line_d, got_g, rhs1))
    parts_g = line_parts(keep_g, got_g)
    line_g = line_send(parts_g)
    keep0, keep1, away0, away1 = attention_grads(where, x_flip, rhs0, after(rhs1, parts_g), att_m, low, small_attn, small_ffn)
    away0, away1, line_g, got_u = lax.optimization_barrier((away0, away1, line_g, got_u))
    came0, came1 = send(away0, "c"), send(away1, "c")
    parts_u = line_parts(keep_u, got_u)
    line_u = line_send(parts_u)
    g_down = send(line_add(keep_d, got_d, line_d), "down")
    away0, away1 = add(keep0[1], came0[1]).astype(LOW), add(keep1[1], came1[1]).astype(LOW)
    got0, got1 = send(away0, "x"), send(away1, "y")
    grad_in = input_grad(rhs0, after(rhs1, (away0, away1)), w_attn, dr1, positions)
    got0, got1, grad_in = lax.optimization_barrier((got0, got1, grad_in))
    total0 = add(keep0[0], came0[0]) + got0.astype(F32)
    total1 = add(keep1[0], came1[0]) + got1.astype(F32)
    away0, away1 = total0[1].astype(LOW), total1[1].astype(LOW)
    got0, got1 = send(away0, "y"), send(away1, "x")
    g_down, line_u = after((g_down, line_u), (away0, away1))
    g_ffn = jnp.stack([g_down, line_add(keep_g, got_g, line_g), line_add(keep_u, got_u, line_u)])
    got0, got1 = after((got0, got1), g_ffn)
    total = jnp.concatenate([add(total0[0], got0), add(total1[0], got1)], axis=1)
    parts = [total[r].astype(LOW) for r in (1, 2, 3)]
    line_a = line_send(parts)
    other = send(g_ffn, "x")
    line_a, other = lax.optimization_barrier((line_a, other))
    g_attn = total[0] + line_a[0].astype(F32) + line_a[1].astype(F32) + line_a[2].astype(F32)
    small = g_attn[ROWS : ROWS + 4, :ROWS]
    g_attn = g_attn[:ROWS].astype(LOW)
    shared = (g_ffn, send(g_ffn, "c"), other, send(other, "c"))
    grad_down, grad_up = finish_ffn(where, after(shared, g_attn))
    other = after(send(g_attn, "x"), grad_down)
    grad_qkv, grad_out = finish_attention(where, (g_attn, send(g_attn, "c"), other, send(other, "c")))
    return (
        layer_out.reshape(seqs, length, width),
        grad_in.reshape(seqs, length, width),
        grad_qkv,
        grad_out,
        grad_up,
        grad_down,
        small[0],
        small[1],
        small[2],
        small[3],
    )


FF = 3072


def slopes():
    return jnp.exp2(-8.0 * (jnp.arange(HEADS, dtype=F32) + 1.0) / HEADS)


def pick(onehot, rows):
    if rows.dtype == LOW:
        return jnp.einsum("svj,sjd->svd", onehot.astype(LOW), rows, preferred_element_type=F32).astype(LOW)
    return jnp.einsum("svj,sjd->svd", onehot, rows, precision=lax.Precision.HIGHEST)


def gather_weights(w_qkv, w_out, w_up, w_down):
    fsdp = lax.axis_size("fsdp")
    dp = lax.axis_size("dp")
    rows, width = w_out.shape
    if rows % (8 * dp):
        return (
            lax.all_gather(w_qkv, "fsdp", axis=0, tiled=True),
            lax.all_gather(w_out, "fsdp", axis=0, tiled=True),
            lax.all_gather(w_up, "fsdp", axis=0, tiled=True),
            lax.all_gather(w_down, "fsdp", axis=0, tiled=True),
        )
    mine = lax.axis_index("dp")
    part = rows // dp
    group = w_down.shape[0] // rows
    joined = jnp.concatenate([w_qkv, w_out, w_up], axis=1)
    joined = lax.dynamic_slice_in_dim(joined, mine * part, part, axis=0)
    down = lax.dynamic_slice_in_dim(w_down, mine * part * group, part * group, axis=0)
    down = jnp.concatenate([down[k * part : (k + 1) * part] for k in range(group)], axis=1)
    full = lax.all_gather(jnp.concatenate([joined, down], axis=1), AXES, axis=0, tiled=True)
    a, b = w_qkv.shape[1], w_qkv.shape[1] + w_out.shape[1]
    c = b + w_up.shape[1]
    full_down = full[:, c:].reshape(fsdp * dp, part, group, width)
    full_down = full_down.transpose(0, 2, 1, 3).reshape(fsdp * dp * part * group, width)
    return full[:, :a], full[:, a:b], full[:, b:c], full_down


def scatter_grads(g_qkv, g_out, g_up, g_down):
    fsdp = lax.axis_size("fsdp")
    dp = lax.axis_size("dp")
    width = g_out.shape[1]
    rows = g_out.shape[0] // fsdp
    if rows % (8 * dp):
        return tuple(
            lax.psum(lax.psum_scatter(g, "fsdp", scatter_dimension=0, tiled=True), "dp")
            for g in (g_qkv, g_out, g_up, g_down)
        )
    part = rows // dp
    group = g_down.shape[0] // g_out.shape[0]
    down = g_down.reshape(fsdp * dp, group, part, width).transpose(0, 2, 1, 3)
    down = down.reshape(fsdp * rows, group * width)
    joined = jnp.concatenate([g_qkv, g_out, g_up, down], axis=1).astype(LOW)
    mine = lax.psum_scatter(joined, AXES, scatter_dimension=0, tiled=True)
    full = lax.all_gather(mine, "dp", axis=0, tiled=True).astype(F32)
    a, b = g_qkv.shape[1], g_qkv.shape[1] + width
    c = b + g_up.shape[1]
    full_down = full[:, c:].reshape(dp, part, group, width).transpose(0, 2, 1, 3)
    return full[:, :a], full[:, a:b], full[:, b:c], full_down.reshape(rows * group, width)


def on_device(hidden_in, w_qkv, w_out, w_up, w_down, gain_attn, shift_attn, gain_ffn, shift_ffn, grad_listed, positions, counts):
    seqs, length, width = hidden_in.shape
    tokens = seqs * length
    most = positions.shape[1]
    norms = jnp.stack([gain_attn, shift_attn, gain_ffn, shift_ffn])
    norms = lax.all_gather(norms, "fsdp", axis=1, tiled=True).astype(F32)
    w_qkv, w_out, w_up, w_down = gather_weights(w_qkv, w_out, w_up, w_down)
    live = jnp.arange(most, dtype=jnp.int32)[None, :] < counts[:, None]
    onehot = (positions[:, :, None] == jnp.arange(length, dtype=jnp.int32)).astype(F32)
    rows_in = hidden_in.reshape(tokens, width)
    slope = slopes()
    scale = HEAD_DIM**-0.5
    qkv = mm(rows_in, w_qkv).astype(LOW)
    split = qkv.reshape(seqs, length, 3, HEADS, HEAD_DIM)
    q, k, v = split[:, :, 0], split[:, :, 1], split[:, :, 2]
    place = jnp.arange(length, dtype=F32)
    bias = -slope[:, None, None] * jnp.abs(place[:, None] - place[None, :])
    s = jnp.einsum("sqhc,skhc->shqk", q, k, preferred_element_type=F32) * scale + bias
    p = jax.nn.softmax(s, axis=-1).astype(LOW)
    att = jnp.einsum("shqk,skhc->sqhc", p, v, preferred_element_type=F32).astype(LOW)
    att = att.reshape(tokens, width)
    r1 = rows_in.astype(F32) + mm(att, w_out)
    unit1, _ = norm_parts(r1)
    h1 = unit1 * norms[0] + norms[1]
    h1_low = h1.astype(LOW)
    u = mm(h1_low, w_up)
    act = (jax.nn.gelu(u[:, :FF], approximate=False) * u[:, FF:]).astype(LOW)
    r2 = h1 + mm(act, w_down)
    unit2, _ = norm_parts(r2)
    layer_out = (unit2 * norms[2] + norms[3]).astype(LOW).reshape(seqs, length, width)
    def listed(a):
        return pick(onehot, a.reshape(seqs, length, -1)).reshape(seqs * most, -1)

    dy = jnp.where(live[:, :, None], grad_listed, 0).astype(F32).reshape(seqs * most, width)
    unit2_m, rstd2_m = norm_parts(listed(r2))
    g_gain_ffn = jnp.sum(dy * unit2_m, axis=0)
    g_shift_ffn = jnp.sum(dy, axis=0)
    dr2 = norm_back(dy, unit2_m, rstd2_m, norms[2])
    e2 = dr2.astype(LOW)
    h1_m = listed(h1_low)
    u_m = mm(h1_m, w_up)
    gate, up = u_m[:, :FF], u_m[:, FF:]
    cdf = 0.5 * (1.0 + lax.erf(gate * (0.5**0.5)))
    pdf = jnp.exp(-0.5 * gate * gate) * ((2.0 * jnp.pi) ** -0.5)
    gelu = gate * cdf
    act_m = (gelu * up).astype(LOW)
    g_down = jnp.einsum("nf,nd->fd", act_m, e2, preferred_element_type=F32)
    dact = jnp.einsum("nd,fd->nf", e2, w_down, preferred_element_type=F32)
    du = jnp.concatenate([dact * up * (cdf + gate * pdf), dact * gelu], axis=1).astype(LOW)
    g_up = jnp.einsum("nd,nf->df", h1_m, du, preferred_element_type=F32)
    dh1 = dr2 + jnp.einsum("nf,df->nd", du, w_up, preferred_element_type=F32)
    unit1_m, rstd1_m = norm_parts(listed(r1))
    g_gain_attn = jnp.sum(dh1 * unit1_m, axis=0)
    g_shift_attn = jnp.sum(dh1, axis=0)
    dr1 = norm_back(dh1, unit1_m, rstd1_m, norms[0])
    e1 = dr1.astype(LOW)
    g_out = jnp.einsum("nd,ne->de", listed(att), e1, preferred_element_type=F32)
    datt = jnp.einsum("ne,de->nd", e1, w_out, preferred_element_type=F32).astype(LOW)
    datt = datt.reshape(seqs, most, HEADS, HEAD_DIM)
    q_m = listed(qkv[:, :width]).reshape(seqs, most, HEADS, HEAD_DIM)
    away = jnp.abs(positions[:, :, None].astype(F32) - place[None, None, :])
    s_m = jnp.einsum("sqhc,skhc->shqk", q_m, k, preferred_element_type=F32) * scale
    p_m = jax.nn.softmax(s_m - slope[None, :, None, None] * away[:, None], axis=-1)
    dv = jnp.einsum("shqk,sqhc->skhc", p_m.astype(LOW), datt, preferred_element_type=F32)
    dp = jnp.einsum("sqhc,skhc->shqk", datt, v, preferred_element_type=F32)
    ds = (p_m * (dp - jnp.sum(dp * p_m, axis=-1, keepdims=True))).astype(LOW)
    dq_m = (jnp.einsum("shqk,skhc->sqhc", ds, k, preferred_element_type=F32) * scale).astype(LOW)
    dk = (jnp.einsum("shqk,sqhc->skhc", ds, q_m, preferred_element_type=F32) * scale).astype(LOW)
    put = (onehot * live[:, :, None]).astype(LOW)
    dq = jnp.einsum("svj,svd->sjd", put, dq_m.reshape(seqs, most, width), preferred_element_type=F32)
    dqkv = jnp.concatenate(
        [dq.astype(LOW).reshape(tokens, width), dk.reshape(tokens, width), dv.astype(LOW).reshape(tokens, width)], axis=1
    )
    g_qkv = jnp.einsum("nd,ne->de", rows_in, dqkv, preferred_element_type=F32)
    dr1_all = jnp.einsum("svj,svd->sjd", onehot * live[:, :, None], dr1.reshape(seqs, most, width), precision=lax.Precision.HIGHEST)
    grad_in = dr1_all.reshape(tokens, width) + jnp.einsum("ne,de->nd", dqkv, w_qkv, preferred_element_type=F32)
    owned = scatter_grads(g_qkv, g_out, g_up, g_down)
    small = lax.psum(jnp.stack([g_gain_attn, g_shift_attn, g_gain_ffn, g_shift_ffn]), AXES)
    share = width // lax.axis_size("fsdp")
    small = lax.dynamic_slice_in_dim(small, lax.axis_index("fsdp") * share, share, axis=1)
    return (
        layer_out,
        grad_in.reshape(seqs, length, width),
        *owned,
        small[0],
        small[1],
        small[2],
        small[3],
    )


def solution(mesh):
    rows3 = P(("fsdp", "dp"), None, None)
    rows2 = P("fsdp", None)
    rows1 = P("fsdp")
    shape = dict(mesh.shape)
    step = on_block if shape == {"fsdp": SHARDS, "dp": QUARTERS} else on_device
    return jax.shard_map(
        step,
        mesh=mesh,
        in_specs=(rows3, rows2, rows2, rows2, rows2, rows1, rows1, rows1, rows1, rows3, P(("fsdp", "dp"), None), P(("fsdp", "dp"))),
        out_specs=(rows3, rows3, rows2, rows2, rows2, rows2, rows1, rows1, rows1, rows1),
        check_vma=False,
    )
```

```python
import functools

import jax
import jax.numpy as jnp
from jax import lax
from jax.experimental import pallas as pl
from jax.experimental.pallas import tpu as pltpu
from jax.sharding import PartitionSpec as P

HEADS = 12
HEAD_DIM = 64
EPS = 1e-12
F32 = jnp.float32
LOW = jnp.bfloat16
AXES = ("fsdp", "dp")
D = 768
ROWS = 96
LINE = 4
SHARDS = D // ROWS
QUARTERS = 4
EXACT = lax.Precision.HIGHEST
SCALE = HEAD_DIM**-0.5
VMEM = pl.BlockSpec(memory_space=pltpu.VMEM)
SMEM = pl.BlockSpec(memory_space=pltpu.SMEM)
BIG = pltpu.CompilerParams(vmem_limit_bytes=60 * 1024 * 1024)


def out(shape, dtype):
    return jax.ShapeDtypeStruct(shape, dtype)


def cost(us):
    return pl.CostEstimate(flops=0, bytes_accessed=int(us * 3.0e6), transcendentals=0)


def mm(a, b):
    return jnp.dot(a, b, preferred_element_type=F32)


def mm_nt(a, b):
    return lax.dot_general(a, b, (((1,), (1,)), ((), ())), preferred_element_type=F32)


def mm_tn(a, b):
    return lax.dot_general(a, b, (((0,), (0,)), ((), ())), preferred_element_type=F32)


def norm_parts(value):
    center = value - jnp.mean(value, axis=-1, keepdims=True)
    rstd = lax.rsqrt(jnp.mean(center * center, axis=-1, keepdims=True) + EPS)
    return center * rstd, rstd


def norm_back(grad, unit, rstd, gain):
    scaled = grad * gain
    return rstd * (
        scaled
        - jnp.mean(scaled, axis=-1, keepdims=True)
        - unit * jnp.mean(scaled * unit, axis=-1, keepdims=True)
    )


def onehot(pos_ref, seq, most, length):
    spots = lax.broadcasted_iota(jnp.int32, (most, length), 1)
    return spots == pos_ref[pl.ds(seq * most, most), :]


def gelu_parts(gate):
    cdf = 0.5 * (1.0 + lax.erf(gate * (0.5**0.5)))
    pdf = jnp.exp(-0.5 * gate * gate) * ((2.0 * jnp.pi) ** -0.5)
    return gate * cdf, cdf + gate * pdf


def slope_of(head):
    return 2.0 ** (-8.0 * (head + 1.0) / HEADS)


def block(ref, *index):
    value = ref[index] if index else ref[...]
    return value.reshape(-1, value.shape[-1])


EXTRA = 8
TAIL = 8
HALVES = ((0, 48), (48, 56))
KEYS = [(ry, rx, rc) for rc in (0, 1) for rx in (0, 1) for ry in (0, 1)]


def attention_kernel(seqs, most, where_ref, slope_ref, x_ref, norm_ref, pos_ref, *rest):
    lines, rest = rest[:16], rest[16:]
    qkv_ref, h1_ref, att_m_ref, h1_m_ref, q_m_ref, r1_m_ref, w_ref, att_ref, r1_ref, sem = rest
    z, y, c_x = where_ref[0], where_ref[1], where_ref[4]
    copies = []
    for n, (ry, rx, rc) in enumerate(KEYS):
        j = jnp.bitwise_xor(c_x, 2 * rx + rc)
        for r in range(LINE):
            shard = 2 * lax.rem(z + LINE - r, LINE) + jnp.bitwise_xor(y, ry)
            for half, (start, size) in enumerate(HALVES):
                size = min(size, ROWS - start)
                copies.append(
                    pltpu.make_async_copy(
                        lines[2 * n + half].at[r, pl.ds(0, size)], w_ref.at[shard, j, pl.ds(start, size)], sem
                    )
                )
    for copy in copies:
        copy.start()
    for copy in copies:
        copy.wait()
    length = x_ref.shape[0] // seqs
    step = 256

    @pl.loop(0, 3 * D // step)
    def _(n):
        j = n // (D // step)
        lane = pl.multiple_of((n - j * (D // step)) * step, step)
        w = w_ref[:, j, :, pl.ds(lane, step)].reshape(D, step)
        qkv_ref[:, pl.ds(pl.multiple_of(n * step, step), step)] = mm(x_ref[...], w).astype(LOW)

    first = lax.broadcasted_iota(jnp.int32, (length, 128), 1) < HEAD_DIM
    row = lax.broadcasted_iota(jnp.int32, (length, length), 0)
    col = lax.broadcasted_iota(jnp.int32, (length, length), 1)
    away = jnp.abs(row - col).astype(F32)

    @pl.loop(0, HEADS // 2)
    def _(t):
        lane = pl.multiple_of(t * 128, 128)
        bias = jnp.concatenate([slope_ref[2 * t] * away, slope_ref[2 * t + 1] * away], axis=0)
        for s in range(seqs):
            rows = slice(s * length, (s + 1) * length)
            q = qkv_ref[rows, pl.ds(lane, 128)]
            k = qkv_ref[rows, pl.ds(D + lane, 128)]
            v = qkv_ref[rows, pl.ds(2 * D + lane, 128)]
            zero = jnp.zeros_like(q)
            both = jnp.concatenate([jnp.where(first, q, zero), jnp.where(first, zero, q)], axis=0)
            score = mm_nt(both, k) * SCALE - bias
            e = jnp.exp(score - jnp.max(score, axis=-1, keepdims=True))
            p = (e * (1.0 / jnp.sum(e, axis=-1, keepdims=True))).astype(LOW)
            mixed = mm(p, v)
            att_ref[rows, pl.ds(lane, 128)] = jnp.where(first, mixed[:length], mixed[length:]).astype(LOW)

    @pl.loop(0, D // step)
    def _(n):
        lane = pl.multiple_of(n * step, step)
        w = w_ref[:, 3, :, pl.ds(lane, step)].reshape(D, step)
        r1_ref[:, pl.ds(lane, step)] = x_ref[:, pl.ds(lane, step)].astype(F32) + mm(att_ref[...], w)

    for s in range(seqs):
        rows = slice(s * length, (s + 1) * length)
        listed = slice(s * most, (s + 1) * most)
        unit, _ = norm_parts(r1_ref[rows, :])
        h1 = unit * norm_ref[0:1, :] + norm_ref[1:2, :]
        h1_ref[rows, :] = h1
        hot = onehot(pos_ref, s, most, length)
        hot_low = hot.astype(LOW)
        r1_m_ref[listed, :] = jnp.dot(hot.astype(F32), r1_ref[rows, :], precision=EXACT, preferred_element_type=F32)
        h1_m_ref[listed, :] = mm(hot_low, h1.astype(LOW)).astype(LOW)
        att_m_ref[listed, :] = mm(hot_low, att_ref[rows, :]).astype(LOW)
        q_m_ref[listed, :] = mm(hot_low, qkv_ref[rows, 0:D]).astype(LOW)


def attention_forward(where, x, lines, norms, pos, slopes, seqs):
    tokens = x.shape[0]
    listed = pos.shape[0]
    return pl.pallas_call(
        functools.partial(attention_kernel, seqs, listed // seqs),
        out_shape=(
            out((tokens, 3 * D), LOW),
            out((tokens, D), F32),
            out((listed, D), LOW),
            out((listed, D), LOW),
            out((listed, D), LOW),
            out((listed, D), F32),
            out((SHARDS, QUARTERS, ROWS, D), LOW),
        ),
        in_specs=[SMEM, SMEM, VMEM, VMEM, VMEM] + [pl.BlockSpec(memory_space=pl.ANY)] * 16,
        out_specs=(VMEM,) * 7,
        scratch_shapes=[pltpu.VMEM((tokens, D), LOW), pltpu.VMEM((tokens, D), F32), pltpu.SemaphoreType.DMA],
        compiler_params=BIG,
        cost_estimate=cost(20),
        name="attention_forward",
    )(where, slopes, x, norms, pos, *lines)


def ffn_kernel(seqs, most, h1_ref, gate_ref, up_ref, down_ref, norm_ref, pos_ref, dy_ref, y_ref, dr2_ref, e2_ref, small_ref, low_ref, act_ref, acc_ref):
    j = pl.program_id(0)
    tokens = h1_ref.shape[0]
    length = tokens // seqs
    step = 256

    @pl.when(j == 0)
    def _():
        low_ref[...] = h1_ref[...].astype(LOW)
        acc_ref[...] = h1_ref[...]

    @pl.loop(0, D // step)
    def _(n):
        lane = pl.multiple_of(n * step, step)
        gate = mm(low_ref[...], gate_ref[:, :, pl.ds(lane, step)].reshape(D, step))
        up = mm(low_ref[...], up_ref[:, :, pl.ds(lane, step)].reshape(D, step))
        cdf = 0.5 * (1.0 + lax.erf(gate * (0.5**0.5)))
        act_ref[:, pl.ds(lane, step)] = (gate * cdf * up).astype(LOW)

    @pl.loop(0, D // step)
    def _(n):
        lane = pl.multiple_of(n * step, step)
        acc_ref[:, pl.ds(lane, step)] += mm(act_ref[...], down_ref[:, :, :, pl.ds(lane, step)].reshape(D, step))

    @pl.when(j == QUARTERS - 1)
    def _():
        gain = norm_ref[2:3, :]
        small = [jnp.zeros((1, D), F32)] * 2
        for s in range(seqs):
            rows = slice(s * length, (s + 1) * length)
            listed = slice(s * most, (s + 1) * most)
            unit, _ = norm_parts(acc_ref[rows, :])
            y_ref[rows, :] = (unit * gain + norm_ref[3:4, :]).astype(LOW)
            hot = onehot(pos_ref, s, most, length).astype(F32)
            picked = jnp.dot(hot, acc_ref[rows, :], precision=EXACT, preferred_element_type=F32)
            unit_m, rstd_m = norm_parts(picked)
            dy = dy_ref[listed, :].astype(F32)
            small = [small[0] + jnp.sum(dy * unit_m, axis=0, keepdims=True), small[1] + jnp.sum(dy, axis=0, keepdims=True)]
            dr2 = norm_back(dy, unit_m, rstd_m, gain)
            dr2_ref[listed, :] = dr2
            e2_ref[listed, :] = dr2.astype(LOW)
        small_ref[...] = jnp.concatenate(small, axis=0)


def ffn_forward(h1, w_ffn, norms, pos, dy, seqs):
    tokens = h1.shape[0]
    listed = pos.shape[0]
    whole = lambda shape: pl.BlockSpec(shape, lambda j: (0,) * len(shape), pipeline_mode=pl.Buffered(1))
    return pl.pallas_call(
        functools.partial(ffn_kernel, seqs, listed // seqs),
        out_shape=(out((tokens, D), LOW), out((listed, D), F32), out((listed, D), LOW), out((2, D), F32)),
        grid=(QUARTERS,),
        in_specs=[
            whole((tokens, D)),
            pl.BlockSpec((SHARDS, None, None, ROWS, D), lambda j: (0, j, 0, 0, 0)),
            pl.BlockSpec((SHARDS, None, None, ROWS, D), lambda j: (0, j, 1, 0, 0)),
            pl.BlockSpec((SHARDS // QUARTERS, QUARTERS, None, ROWS, D), lambda j: (j, 0, 2, 0, 0)),
            whole(norms.shape),
            whole(pos.shape),
            whole(dy.shape),
        ],
        out_specs=(
            pl.BlockSpec((tokens, D), lambda j: (0, 0)),
            pl.BlockSpec((listed, D), lambda j: (0, 0)),
            pl.BlockSpec((listed, D), lambda j: (0, 0)),
            pl.BlockSpec((2, D), lambda j: (0, 0)),
        ),
        scratch_shapes=[pltpu.VMEM((tokens, D), LOW), pltpu.VMEM((tokens, D), LOW), pltpu.VMEM((tokens, D), F32)],
        compiler_params=BIG,
        cost_estimate=cost(16),
        name="ffn_forward",
    )(h1, w_ffn, w_ffn, w_ffn, norms, pos, dy)


def ffn_again_kernel(where_ref, h_ref, gate_ref, up_ref, act_ref, to_gate_ref, to_up_ref):
    step = 256

    @pl.loop(0, D // step)
    def _(n):
        lane = pl.multiple_of(n * step, step)
        rows = block(h_ref)
        gate = mm(rows, gate_ref[:, :, pl.ds(lane, step)].reshape(D, step))
        up = mm(rows, up_ref[:, :, pl.ds(lane, step)].reshape(D, step))
        value, slope = gelu_parts(gate)
        act_ref[:, pl.ds(lane, step)] = (value * up).astype(LOW)
        to_gate_ref[:, pl.ds(lane, step)] = slope * up
        to_up_ref[:, pl.ds(lane, step)] = value


def quarter_specs(which):
    specs = {
        "gate": pl.BlockSpec((SHARDS, None, None, ROWS, D), lambda g, w: (0, w[4], 0, 0, 0)),
        "up": pl.BlockSpec((SHARDS, None, None, ROWS, D), lambda g, w: (0, w[4], 1, 0, 0)),
        "down": pl.BlockSpec((SHARDS // QUARTERS, QUARTERS, None, ROWS, D), lambda g, w: (w[4], 0, 2, 0, 0)),
    }
    return [specs[name] for name in which]


def at_once(shape):
    return pl.BlockSpec(shape, lambda g, w: (0,) * len(shape))


def ffn_again(where, h_all, w_ffn):
    rows = h_all.shape[0] * h_all.shape[1]
    return pl.pallas_call(
        ffn_again_kernel,
        out_shape=(out((rows, D), LOW), out((rows, D), F32), out((rows, D), F32)),
        grid_spec=pltpu.PrefetchScalarGridSpec(
            num_scalar_prefetch=1,
            grid=(1,),
            in_specs=[at_once(h_all.shape), *quarter_specs(["gate", "up"])],
            out_specs=(at_once((rows, D)),) * 3,
        ),
        compiler_params=BIG,
        cost_estimate=cost(6),
        name="ffn_again",
    )(where, h_all, w_ffn, w_ffn)


def ffn_back_kernel(where_ref, e_ref, to_gate_ref, to_up_ref, gate_ref, up_ref, down_ref, dgate_ref, dup_ref, keep_ref, send_ref):
    listed = e_ref.shape[1]
    half = QUARTERS // 2
    for n in range(SHARDS // QUARTERS):
        lanes = slice(n * QUARTERS * ROWS, (n + 1) * QUARTERS * ROWS)
        dact = mm_nt(block(e_ref), block(down_ref, n))
        dgate_ref[:, lanes] = (dact * to_gate_ref[:, lanes]).astype(LOW)
        dup_ref[:, lanes] = (dact * to_up_ref[:, lanes]).astype(LOW)
    for n in range(2):
        shards = slice(n * SHARDS // 2, (n + 1) * SHARDS // 2)
        lanes = slice(n * D // 2, (n + 1) * D // 2)
        part = mm_nt(dgate_ref[...], block(gate_ref, shards)) + mm_nt(dup_ref[...], block(up_ref, shards))
        for r in range(half):
            keep_ref[r, :, lanes] = part[2 * r * listed : (2 * r + 1) * listed]
            send_ref[r, :, lanes] = part[(2 * r + 1) * listed : (2 * r + 2) * listed].astype(LOW)


def ffn_back(where, e_all, to_gate, to_up, w_ffn):
    count, listed, _ = e_all.shape
    rows = count * listed
    return pl.pallas_call(
        ffn_back_kernel,
        out_shape=(out((rows, D), LOW), out((rows, D), LOW), out((count // 2, listed, D), F32), out((count // 2, listed, D), LOW)),
        grid_spec=pltpu.PrefetchScalarGridSpec(
            num_scalar_prefetch=1,
            grid=(1,),
            in_specs=[at_once(e_all.shape), at_once((rows, D)), at_once((rows, D)), *quarter_specs(["gate", "up", "down"])],
            out_specs=(at_once((rows, D)), at_once((rows, D)), at_once((count // 2, listed, D)), at_once((count // 2, listed, D))),
        ),
        compiler_params=BIG,
        cost_estimate=cost(7),
        name="ffn_back",
    )(where, e_all, to_gate, to_up, w_ffn, w_ffn, w_ffn)


def weight_grad_kernel(where_ref, a_ref, b_ref, keep_ref, send_ref, full_ref):
    z, y = where_ref[0], where_ref[1]
    b = block(b_ref)
    step = 256

    @pl.loop(0, D // step)
    def _(n):
        lane = pl.multiple_of(n * step, step)
        a = block(a_ref, *([slice(None)] * (len(a_ref.shape) - 1)), pl.ds(lane, step))
        full_ref[pl.ds(lane, step), :] = mm_tn(a, b)

    for r in range(LINE):
        base = 2 * lax.rem(z + r, LINE)
        for other, ref in ((0, keep_ref), (1, send_ref)):
            start = (base + (y if other == 0 else 1 - y)) * ROWS
            ref[r] = full_ref[pl.ds(pl.multiple_of(start, 8), ROWS), :].astype(LOW)


def weight_grad(where, a, b):
    shape = (LINE, ROWS, D)
    rows = a.size // D
    return pl.pallas_call(
        weight_grad_kernel,
        out_shape=(out(shape, LOW), out(shape, LOW)),
        in_specs=[SMEM, VMEM, VMEM],
        out_specs=(VMEM, VMEM),
        scratch_shapes=[pltpu.VMEM((D, D), F32)],
        compiler_params=BIG,
        cost_estimate=cost(4),
        name="weight_grad",
    )(where, a, b)


def norm_back_kernel(dr2_ref, part_ref, came_ref, r1_ref, w_ref, norm_ref, dr1_ref, low_ref, datt_ref, small_ref):
    dh1 = dr2_ref[...] + part_ref[...] + came_ref[...].astype(F32)
    unit, rstd = norm_parts(r1_ref[...])
    small_ref[0:1, :] = jnp.sum(dh1 * unit, axis=0, keepdims=True)
    small_ref[1:2, :] = jnp.sum(dh1, axis=0, keepdims=True)
    dr1 = norm_back(dh1, unit, rstd, norm_ref[0:1, :])
    dr1_ref[...] = dr1
    low = dr1.astype(LOW)
    low_ref[...] = low
    for n in range(2):
        lanes = slice(n * D // 2, (n + 1) * D // 2)
        datt_ref[:, lanes] = mm_nt(low, block(w_ref, slice(n * SHARDS // 2, (n + 1) * SHARDS // 2))).astype(LOW)


def norm_back_call(dr2, part, came, r1_m, w_attn, norms):
    listed = dr2.shape[0]
    same = lambda shape: pl.BlockSpec(shape, lambda g: (0,) * len(shape))
    rows = same((listed, D))
    return pl.pallas_call(
        norm_back_kernel,
        out_shape=(out((listed, D), F32), out((listed, D), LOW), out((listed, D), LOW), out((2, D), F32)),
        grid=(1,),
        in_specs=[rows, rows, rows, rows, pl.BlockSpec((SHARDS, None, ROWS, D), lambda g: (0, 3, 0, 0)), same((4, D))],
        out_specs=(rows, rows, rows, same((2, D))),
        compiler_params=BIG,
        cost_estimate=cost(4),
        name="norm_back",
    )(dr2, part, came, r1_m, w_attn, norms)


def attention_back_kernel(seqs, most, slope_ref, datt_ref, q_ref, qkv_ref, pos_ref, rhs_ref, away_ref, hot_ref):
    length = qkv_ref.shape[0] // seqs
    listed = seqs * most
    first_m = lax.broadcasted_iota(jnp.int32, (most, 128), 1) < HEAD_DIM
    spots = lax.broadcasted_iota(jnp.int32, (listed, length), 1)
    away_ref[...] = jnp.abs(pos_ref[...] - spots).astype(F32)
    hot_ref[...] = (spots == pos_ref[...]).astype(LOW)

    def both(value):
        zero = jnp.zeros_like(value)
        return jnp.concatenate([jnp.where(first_m, value, zero), jnp.where(first_m, zero, value)], axis=0)

    @pl.loop(0, HEADS // 2)
    def _(t):
        lane = pl.multiple_of(t * 128, 128)
        for s in range(seqs):
            rows = slice(s * length, (s + 1) * length)
            mine = slice(s * most, (s + 1) * most)
            away = away_ref[mine, :]
            q = both(q_ref[mine, pl.ds(lane, 128)])
            da = both(datt_ref[mine, pl.ds(lane, 128)])
            k = qkv_ref[rows, pl.ds(D + lane, 128)]
            v = qkv_ref[rows, pl.ds(2 * D + lane, 128)]
            bias = jnp.concatenate([slope_ref[2 * t] * away, slope_ref[2 * t + 1] * away], axis=0)
            score = mm_nt(q, k) * SCALE - bias
            e = jnp.exp(score - jnp.max(score, axis=-1, keepdims=True))
            p = e * (1.0 / jnp.sum(e, axis=-1, keepdims=True))
            dp = mm_nt(da, v)
            ds = (p * (dp - jnp.sum(dp * p, axis=-1, keepdims=True))).astype(LOW)
            dq = mm(ds, k)
            dq = (jnp.where(first_m, dq[:most], dq[most:]) * SCALE).astype(LOW)
            rhs_ref[rows, pl.ds(lane, 128)] = mm_tn(hot_ref[mine, :], dq).astype(LOW)
            rhs_ref[rows, pl.ds(D + lane, 128)] = (mm_tn(ds, q) * SCALE).astype(LOW)
            rhs_ref[rows, pl.ds(2 * D + lane, 128)] = mm_tn(p.astype(LOW), da).astype(LOW)


def attention_back(datt, q_m, qkv, pos, slopes, seqs, part):
    tokens, listed = qkv.shape[0] // 2, pos.shape[0] // 2
    length = tokens * 2 // seqs
    mine = lambda shape: pl.BlockSpec(shape, lambda g: (part, 0))
    return pl.pallas_call(
        functools.partial(attention_back_kernel, seqs // 2, listed * 2 // seqs),
        out_shape=out((tokens, 3 * D), LOW),
        grid=(1,),
        in_specs=[SMEM, mine((listed, D)), mine((listed, D)), mine((tokens, 3 * D)), mine((listed, 1))],
        out_specs=pl.BlockSpec((tokens, 3 * D), lambda g: (0, 0)),
        scratch_shapes=[pltpu.VMEM((listed, length), F32), pltpu.VMEM((listed, length), LOW)],
        compiler_params=BIG,
        cost_estimate=cost(8),
        name="attention_back",
    )(slopes, datt, q_m, qkv, pos)


def attention_grads_kernel(where_ref, flip_ref, rhs0_ref, rhs1_ref, att_ref, low_ref, small_attn_ref, small_ffn_ref, keep0_ref, keep1_ref, away0_ref, away1_ref, full_ref, tail_ref):
    z, y, mine = where_ref[0], where_ref[1], where_ref[4]
    half = ROWS // 2
    step = 256
    tail_ref[...] = jnp.zeros(tail_ref.shape, LOW)
    small = jnp.concatenate([small_attn_ref[...], small_ffn_ref[...]], axis=0).astype(LOW)
    for n in range(SHARDS):
        tail_ref[n, 0:4, 0:ROWS] = small[:, n * ROWS : (n + 1) * ROWS]
    for rc in (1, 0):
        cut0_ref, cut1_ref = (keep0_ref, keep1_ref) if rc == 0 else (away0_ref, away1_ref)
        for rx in (0, 1):
            j = jnp.bitwise_xor(mine, 2 * rx + rc)

            @pl.when(j == 3)
            def _():
                for n in range(D // step):
                    rows = slice(n * step, (n + 1) * step)
                    full_ref[rows, :] = mm_tn(att_ref[:, rows], low_ref[...])

            @pl.when(j != 3)
            def _():
                @pl.loop(0, D // step)
                def _(n):
                    lane = pl.multiple_of(n * step, step)
                    cols = pl.ds(pl.multiple_of(j * D + n * step, step), step)
                    first = rhs0_ref.shape[0]
                    full_ref[:, pl.ds(lane, step)] = mm(flip_ref[:, :first], rhs0_ref[:, cols]) + mm(flip_ref[:, first:], rhs1_ref[:, cols])

            for rz in range(LINE):
                base = 2 * lax.rem(z + rz, LINE)
                for ry in (0, 1):
                    shard = base + (y if ry == 0 else 1 - y)
                    start = shard * ROWS
                    cut0_ref[rx, ry, rz] = full_ref[pl.ds(pl.multiple_of(start, 8), half), :].astype(LOW)
                    cut1_ref[ry, rx, rz, 0:half] = full_ref[pl.ds(pl.multiple_of(start + half, 8), half), :].astype(LOW)
                    cut1_ref[ry, rx, rz, half:] = tail_ref[shard]


def attention_grads(where, x_flip, rhs0, rhs1, att_m, low, small_attn, small_ffn):
    half = ROWS // 2
    return pl.pallas_call(
        attention_grads_kernel,
        out_shape=(out((2, 2, LINE, half, D), LOW), out((2, 2, LINE, half + TAIL, D), LOW)) * 2,
        in_specs=[SMEM] + [VMEM] * 7,
        out_specs=(VMEM,) * 4,
        scratch_shapes=[pltpu.VMEM((D, D), F32), pltpu.VMEM((SHARDS, TAIL, D), LOW)],
        compiler_params=BIG,
        cost_estimate=cost(10),
        name="attention_grads",
    )(where, x_flip, rhs0, rhs1, att_m, low, small_attn, small_ffn)


def input_grad_kernel(seqs, rhs0_ref, rhs1_ref, w_ref, dr1_ref, pos_ref, out_ref):
    length = out_ref.shape[0] // seqs
    most = dr1_ref.shape[0] // seqs
    for n in range(2):
        lanes = slice(n * D // 2, (n + 1) * D // 2)
        shards = slice(n * SHARDS // 2, (n + 1) * SHARDS // 2)
        s = 0
        for rhs_ref in (rhs0_ref, rhs1_ref):
            total = mm_nt(rhs_ref[:, 0:D], block(w_ref, shards, 0))
            total += mm_nt(rhs_ref[:, D : 2 * D], block(w_ref, shards, 1))
            total += mm_nt(rhs_ref[:, 2 * D : 3 * D], block(w_ref, shards, 2))
            for m in range(rhs_ref.shape[0] // length):
                hot = (lax.broadcasted_iota(jnp.int32, (length, most), 0) == pos_ref[s : s + 1, :]).astype(F32)
                spread = jnp.dot(hot, dr1_ref[s * most : (s + 1) * most, lanes], precision=EXACT, preferred_element_type=F32)
                out_ref[s * length : (s + 1) * length, lanes] = total[m * length : (m + 1) * length] + spread
                s += 1


def input_grad(rhs0, rhs1, w_attn, dr1, positions):
    tokens = rhs0.shape[0] + rhs1.shape[0]
    return pl.pallas_call(
        functools.partial(input_grad_kernel, positions.shape[0]),
        out_shape=out((tokens, D), F32),
        in_specs=[VMEM] * 5,
        out_specs=VMEM,
        compiler_params=BIG,
        cost_estimate=cost(8),
        name="input_grad",
    )(rhs0, rhs1, w_attn, dr1, positions)


def place(z, y, x, c):
    return (2 * z + y) * 4 + 2 * x + c


def grid_perm(move):
    return [
        (place(z, y, x, c), place(*move(z, y, x, c)))
        for z in range(4)
        for y in range(2)
        for x in range(2)
        for c in range(2)
    ]


MOVES = {
    "x": grid_perm(lambda z, y, x, c: (z, y, 1 - x, c)),
    "y": grid_perm(lambda z, y, x, c: (z, 1 - y, x, c)),
    "c": grid_perm(lambda z, y, x, c: (z, y, x, 1 - c)),
    1: grid_perm(lambda z, y, x, c: ((z + 1) % 4, y, x, c)),
    2: grid_perm(lambda z, y, x, c: ((z + 2) % 4, y, x, c)),
    3: grid_perm(lambda z, y, x, c: ((z + 3) % 4, y, x, c)),
    "down": [(m * 4 + q, (2 * q + m // 4) * 4 + m % 4) for m in range(8) for q in range(4)],
}


def send(value, move):
    return lax.ppermute(value, AXES, MOVES[move])


def share_dp(value):
    other = send(value, "x")
    return value, send(value, "c"), other, send(other, "c")


def after(value, *earlier):
    return lax.optimization_barrier((value, *earlier))[0]


def add(kept, got):
    return kept.astype(F32) + got.astype(F32)


def line_parts(keep, got):
    return [add(keep[r], got[r]).astype(LOW) for r in (1, 2, 3)]


def line_send(parts):
    return [send(value, r) for r, value in zip((1, 2, 3), parts)]


def line_add(keep, got, came):
    return (add(keep[0], got[0]) + came[0].astype(F32) + came[1].astype(F32) + came[2].astype(F32)).astype(LOW)


def finish_ffn_kernel(where_ref, *rest):
    pieces, (down_ref, up_ref) = rest[:QUARTERS], rest[QUARTERS:]
    mine = where_ref[4]
    for n, ref in enumerate(pieces):
        j = jnp.bitwise_xor(mine, n)
        down_ref[pl.ds(pl.multiple_of(j * ROWS, 8), ROWS), :] = ref[0].astype(F32)
        for half in (0, 1):
            up_ref[:, pl.ds(pl.multiple_of((half * QUARTERS + j) * D, D), D)] = ref[1 + half].astype(F32)


def finish_attention_kernel(where_ref, *rest):
    pieces, (qkv_ref, out_ref, held_ref) = rest[:QUARTERS], rest[QUARTERS:]
    mine = where_ref[4]
    for n, ref in enumerate(pieces):
        held_ref[jnp.bitwise_xor(mine, n)] = ref[...].astype(F32)
    for j in range(3):
        qkv_ref[:, j * D : (j + 1) * D] = held_ref[j]
    out_ref[...] = held_ref[3]


def finish_ffn(where, pieces):
    return pl.pallas_call(
        finish_ffn_kernel,
        out_shape=(out((QUARTERS * ROWS, D), F32), out((ROWS, 2 * QUARTERS * D), F32)),
        in_specs=[SMEM] + [VMEM] * QUARTERS,
        out_specs=(VMEM, VMEM),
        compiler_params=BIG,
        cost_estimate=cost(4),
        name="finish_ffn",
    )(where, *pieces)


def finish_attention(where, pieces):
    return pl.pallas_call(
        finish_attention_kernel,
        out_shape=(out((ROWS, 3 * D), F32), out((ROWS, D), F32)),
        in_specs=[SMEM] + [VMEM] * QUARTERS,
        out_specs=(VMEM, VMEM),
        scratch_shapes=[pltpu.VMEM((QUARTERS, ROWS, D), F32)],
        compiler_params=BIG,
        cost_estimate=cost(2),
        name="finish_attention",
    )(where, *pieces)


def spread(piece, order):
    got = {frozenset(): piece}
    for step in (*order, "c"):
        for key in list(got):
            got[key | {step}] = send(got[key], step)
    return [got[frozenset(n for n, b in zip("yxc", key) if b)] for key in KEYS]


def on_block(hidden_in, w_qkv, w_out, w_up, w_down, gain_attn, shift_attn, gain_ffn, shift_ffn, grad_listed, positions, counts):
    seqs, length, width = hidden_in.shape
    tokens = seqs * length
    most = positions.shape[1]
    i, j = lax.axis_index("fsdp"), lax.axis_index("dp")
    where = jnp.stack([i // 2, i % 2, j // 2, j % 2, j]).astype(jnp.int32)
    ff = w_down.shape[0] * SHARDS
    attn_piece = lax.dynamic_slice_in_dim(jnp.concatenate([w_qkv, w_out], axis=1), j * D, D, axis=1)
    norms = jnp.concatenate([gain_attn, shift_attn, gain_ffn, shift_ffn, jnp.zeros((D - 4 * ROWS,), LOW)])
    attn_piece = jnp.concatenate([attn_piece, jnp.broadcast_to(norms, (EXTRA, D))], axis=0)
    line = jnp.stack([attn_piece] + [send(attn_piece, r) for r in (1, 2, 3)])
    x = hidden_in.reshape(tokens, width)
    line, x_flip = lax.optimization_barrier((line, x.T))
    halves = [
        spread(line[:, start : start + size], order)
        for (start, size), order in zip(HALVES, (("y", "x"), ("x", "y")))
    ]
    lines = [half[n] for n in range(len(KEYS)) for half in halves]
    ffn_piece = jnp.stack(
        [
            lax.dynamic_slice_in_dim(w_up, j * D, D, axis=1),
            lax.dynamic_slice_in_dim(w_up, ff + j * D, D, axis=1),
            lax.dynamic_slice_in_dim(w_down, j * ROWS, ROWS, axis=0),
        ]
    )
    w_ffn = lax.all_gather(ffn_piece, AXES, axis=0, tiled=False).reshape(SHARDS, QUARTERS, 3, ROWS, D)
    tails = jnp.stack([halves[1][n][:, 48, : 4 * ROWS] for n in range(2)])
    tails = jnp.where(i % 2 == 0, tails, tails[::-1])
    tails = jnp.roll(tails[:, ::-1], i // 2 + 1, axis=1)
    norms = tails.transpose(1, 0, 2).reshape(SHARDS, 4, ROWS).transpose(1, 0, 2).reshape(4, D).astype(F32)
    slopes = jnp.exp2(-8.0 * (jnp.arange(HEADS, dtype=F32) + 1.0) / HEADS)
    pos = positions.reshape(seqs * most, 1)
    live = jnp.arange(most, dtype=jnp.int32)[None, :] < counts[:, None]
    dy = jnp.where(live[:, :, None], grad_listed, jnp.zeros_like(grad_listed)).reshape(seqs * most, width)

    qkv, h1, att_m, h1_m, q_m, r1_m, w_attn = attention_forward(where, x, lines, norms, pos, slopes, seqs)
    h_all = jnp.stack(share_dp(h1_m))
    h1, h_all = lax.optimization_barrier((h1, h_all))
    layer_out, dr2, e2, small_ffn = ffn_forward(h1, w_ffn, norms, pos, dy, seqs)
    act, to_gate, to_up = ffn_again(where, h_all, w_ffn)
    other = after(send(e2, "x"), act)
    e_all = jnp.stack([e2, send(e2, "c"), other, send(other, "c")])
    dgate, dup, keep, away = ffn_back(where, e_all, to_gate, to_up, w_ffn)
    part = add(keep, send(away, "c"))
    part, part_away = part[0], part[1].astype(LOW)
    keep_d, away_d = weight_grad(where, act, e_all)
    came = send(part_away, "x")
    got_d = send(away_d, "y")
    keep_g, away_g = weight_grad(where, after(h_all, (away_d, part_away)), dgate)
    got_g = send(away_g, "y")
    keep_u, away_u = weight_grad(where, after(h_all, (away_g, came)), dup)
    got_u = send(away_u, "y")
    dr1, low, datt, small_attn = norm_back_call(dr2, part, after(came, away_u), r1_m, w_attn, norms)
    rhs0 = attention_back(datt, q_m, qkv, pos, slopes, seqs, 0)
    got_d, rhs0 = lax.optimization_barrier((got_d, rhs0))
    parts_d = line_parts(keep_d, got_d)
    line_d = line_send(parts_d)
    rhs1 = attention_back(after(datt, (rhs0, parts_d)), q_m, qkv, pos, slopes, seqs, 1)
    line_d, got_g, rhs1 = lax.optimization_barrier((line_d, got_g, rhs1))
    parts_g = line_parts(keep_g, got_g)
    line_g = line_send(parts_g)
    keep0, keep1, away0, away1 = attention_grads(where, x_flip, rhs0, after(rhs1, parts_g), att_m, low, small_attn, small_ffn)
    away0, away1, line_g, got_u = lax.optimization_barrier((away0, away1, line_g, got_u))
    came0, came1 = send(away0, "c"), send(away1, "c")
    parts_u = line_parts(keep_u, got_u)
    line_u = line_send(parts_u)
    g_down = send(line_add(keep_d, got_d, line_d), "down")
    away0, away1 = add(keep0[1], came0[1]).astype(LOW), add(keep1[1], came1[1]).astype(LOW)
    got0, got1 = send(away0, "x"), send(away1, "y")
    total0 = add(keep0[0], came0[0]) + got0.astype(F32)
    total1 = add(keep1[0], came1[0]) + got1.astype(F32)
    away0, away1 = total0[1].astype(LOW), total1[1].astype(LOW)
    got0, got1 = send(away0, "y"), send(away1, "x")
    g_down, line_u = after((g_down, line_u), (away0, away1))
    g_ffn = jnp.stack([g_down, line_add(keep_g, got_g, line_g), line_add(keep_u, got_u, line_u)])
    got0, got1 = after((got0, got1), g_ffn)
    total = jnp.concatenate([add(total0[0], got0), add(total1[0], got1)], axis=1)
    parts = [total[r].astype(LOW) for r in (1, 2, 3)]
    line_a = line_send(parts)
    other = send(g_ffn, "x")
    grad_in = input_grad(rhs0, after(rhs1, parts), w_attn, dr1, positions)
    line_a, other, grad_in = lax.optimization_barrier((line_a, other, grad_in))
    g_attn = total[0] + line_a[0].astype(F32) + line_a[1].astype(F32) + line_a[2].astype(F32)
    small = g_attn[ROWS : ROWS + 4, :ROWS]
    g_attn = g_attn[:ROWS].astype(LOW)
    shared = (g_ffn, send(g_ffn, "c"), other, send(other, "c"))
    grad_down, grad_up = finish_ffn(where, after(shared, g_attn))
    other = after(send(g_attn, "x"), grad_down)
    grad_qkv, grad_out = finish_attention(where, (g_attn, send(g_attn, "c"), other, send(other, "c")))
    return (
        layer_out.reshape(seqs, length, width),
        grad_in.reshape(seqs, length, width),
        grad_qkv,
        grad_out,
        grad_up,
        grad_down,
        small[0],
        small[1],
        small[2],
        small[3],
    )


FF = 3072


def slopes():
    return jnp.exp2(-8.0 * (jnp.arange(HEADS, dtype=F32) + 1.0) / HEADS)


def pick(onehot, rows):
    if rows.dtype == LOW:
        return jnp.einsum("svj,sjd->svd", onehot.astype(LOW), rows, preferred_element_type=F32).astype(LOW)
    return jnp.einsum("svj,sjd->svd", onehot, rows, precision=lax.Precision.HIGHEST)


def gather_weights(w_qkv, w_out, w_up, w_down):
    fsdp = lax.axis_size("fsdp")
    dp = lax.axis_size("dp")
    rows, width = w_out.shape
    if rows % (8 * dp):
        return (
            lax.all_gather(w_qkv, "fsdp", axis=0, tiled=True),
            lax.all_gather(w_out, "fsdp", axis=0, tiled=True),
            lax.all_gather(w_up, "fsdp", axis=0, tiled=True),
            lax.all_gather(w_down, "fsdp", axis=0, tiled=True),
        )
    mine = lax.axis_index("dp")
    part = rows // dp
    group = w_down.shape[0] // rows
    joined = jnp.concatenate([w_qkv, w_out, w_up], axis=1)
    joined = lax.dynamic_slice_in_dim(joined, mine * part, part, axis=0)
    down = lax.dynamic_slice_in_dim(w_down, mine * part * group, part * group, axis=0)
    down = jnp.concatenate([down[k * part : (k + 1) * part] for k in range(group)], axis=1)
    full = lax.all_gather(jnp.concatenate([joined, down], axis=1), AXES, axis=0, tiled=True)
    a, b = w_qkv.shape[1], w_qkv.shape[1] + w_out.shape[1]
    c = b + w_up.shape[1]
    full_down = full[:, c:].reshape(fsdp * dp, part, group, width)
    full_down = full_down.transpose(0, 2, 1, 3).reshape(fsdp * dp * part * group, width)
    return full[:, :a], full[:, a:b], full[:, b:c], full_down


def scatter_grads(g_qkv, g_out, g_up, g_down):
    fsdp = lax.axis_size("fsdp")
    dp = lax.axis_size("dp")
    width = g_out.shape[1]
    rows = g_out.shape[0] // fsdp
    if rows % (8 * dp):
        return tuple(
            lax.psum(lax.psum_scatter(g, "fsdp", scatter_dimension=0, tiled=True), "dp")
            for g in (g_qkv, g_out, g_up, g_down)
        )
    part = rows // dp
    group = g_down.shape[0] // g_out.shape[0]
    down = g_down.reshape(fsdp * dp, group, part, width).transpose(0, 2, 1, 3)
    down = down.reshape(fsdp * rows, group * width)
    joined = jnp.concatenate([g_qkv, g_out, g_up, down], axis=1).astype(LOW)
    mine = lax.psum_scatter(joined, AXES, scatter_dimension=0, tiled=True)
    full = lax.all_gather(mine, "dp", axis=0, tiled=True).astype(F32)
    a, b = g_qkv.shape[1], g_qkv.shape[1] + width
    c = b + g_up.shape[1]
    full_down = full[:, c:].reshape(dp, part, group, width).transpose(0, 2, 1, 3)
    return full[:, :a], full[:, a:b], full[:, b:c], full_down.reshape(rows * group, width)


def on_device(hidden_in, w_qkv, w_out, w_up, w_down, gain_attn, shift_attn, gain_ffn, shift_ffn, grad_listed, positions, counts):
    seqs, length, width = hidden_in.shape
    tokens = seqs * length
    most = positions.shape[1]
    norms = jnp.stack([gain_attn, shift_attn, gain_ffn, shift_ffn])
    norms = lax.all_gather(norms, "fsdp", axis=1, tiled=True).astype(F32)
    w_qkv, w_out, w_up, w_down = gather_weights(w_qkv, w_out, w_up, w_down)
    live = jnp.arange(most, dtype=jnp.int32)[None, :] < counts[:, None]
    onehot = (positions[:, :, None] == jnp.arange(length, dtype=jnp.int32)).astype(F32)
    rows_in = hidden_in.reshape(tokens, width)
    slope = slopes()
    scale = HEAD_DIM**-0.5
    qkv = mm(rows_in, w_qkv).astype(LOW)
    split = qkv.reshape(seqs, length, 3, HEADS, HEAD_DIM)
    q, k, v = split[:, :, 0], split[:, :, 1], split[:, :, 2]
    place = jnp.arange(length, dtype=F32)
    bias = -slope[:, None, None] * jnp.abs(place[:, None] - place[None, :])
    s = jnp.einsum("sqhc,skhc->shqk", q, k, preferred_element_type=F32) * scale + bias
    p = jax.nn.softmax(s, axis=-1).astype(LOW)
    att = jnp.einsum("shqk,skhc->sqhc", p, v, preferred_element_type=F32).astype(LOW)
    att = att.reshape(tokens, width)
    r1 = rows_in.astype(F32) + mm(att, w_out)
    unit1, _ = norm_parts(r1)
    h1 = unit1 * norms[0] + norms[1]
    h1_low = h1.astype(LOW)
    u = mm(h1_low, w_up)
    act = (jax.nn.gelu(u[:, :FF], approximate=False) * u[:, FF:]).astype(LOW)
    r2 = h1 + mm(act, w_down)
    unit2, _ = norm_parts(r2)
    layer_out = (unit2 * norms[2] + norms[3]).astype(LOW).reshape(seqs, length, width)
    def listed(a):
        return pick(onehot, a.reshape(seqs, length, -1)).reshape(seqs * most, -1)

    dy = jnp.where(live[:, :, None], grad_listed, 0).astype(F32).reshape(seqs * most, width)
    unit2_m, rstd2_m = norm_parts(listed(r2))
    g_gain_ffn = jnp.sum(dy * unit2_m, axis=0)
    g_shift_ffn = jnp.sum(dy, axis=0)
    dr2 = norm_back(dy, unit2_m, rstd2_m, norms[2])
    e2 = dr2.astype(LOW)
    h1_m = listed(h1_low)
    u_m = mm(h1_m, w_up)
    gate, up = u_m[:, :FF], u_m[:, FF:]
    cdf = 0.5 * (1.0 + lax.erf(gate * (0.5**0.5)))
    pdf = jnp.exp(-0.5 * gate * gate) * ((2.0 * jnp.pi) ** -0.5)
    gelu = gate * cdf
    act_m = (gelu * up).astype(LOW)
    g_down = jnp.einsum("nf,nd->fd", act_m, e2, preferred_element_type=F32)
    dact = jnp.einsum("nd,fd->nf", e2, w_down, preferred_element_type=F32)
    du = jnp.concatenate([dact * up * (cdf + gate * pdf), dact * gelu], axis=1).astype(LOW)
    g_up = jnp.einsum("nd,nf->df", h1_m, du, preferred_element_type=F32)
    dh1 = dr2 + jnp.einsum("nf,df->nd", du, w_up, preferred_element_type=F32)
    unit1_m, rstd1_m = norm_parts(listed(r1))
    g_gain_attn = jnp.sum(dh1 * unit1_m, axis=0)
    g_shift_attn = jnp.sum(dh1, axis=0)
    dr1 = norm_back(dh1, unit1_m, rstd1_m, norms[0])
    e1 = dr1.astype(LOW)
    g_out = jnp.einsum("nd,ne->de", listed(att), e1, preferred_element_type=F32)
    datt = jnp.einsum("ne,de->nd", e1, w_out, preferred_element_type=F32).astype(LOW)
    datt = datt.reshape(seqs, most, HEADS, HEAD_DIM)
    q_m = listed(qkv[:, :width]).reshape(seqs, most, HEADS, HEAD_DIM)
    away = jnp.abs(positions[:, :, None].astype(F32) - place[None, None, :])
    s_m = jnp.einsum("sqhc,skhc->shqk", q_m, k, preferred_element_type=F32) * scale
    p_m = jax.nn.softmax(s_m - slope[None, :, None, None] * away[:, None], axis=-1)
    dv = jnp.einsum("shqk,sqhc->skhc", p_m.astype(LOW), datt, preferred_element_type=F32)
    dp = jnp.einsum("sqhc,skhc->shqk", datt, v, preferred_element_type=F32)
    ds = (p_m * (dp - jnp.sum(dp * p_m, axis=-1, keepdims=True))).astype(LOW)
    dq_m = (jnp.einsum("shqk,skhc->sqhc", ds, k, preferred_element_type=F32) * scale).astype(LOW)
    dk = (jnp.einsum("shqk,sqhc->skhc", ds, q_m, preferred_element_type=F32) * scale).astype(LOW)
    put = (onehot * live[:, :, None]).astype(LOW)
    dq = jnp.einsum("svj,svd->sjd", put, dq_m.reshape(seqs, most, width), preferred_element_type=F32)
    dqkv = jnp.concatenate(
        [dq.astype(LOW).reshape(tokens, width), dk.reshape(tokens, width), dv.astype(LOW).reshape(tokens, width)], axis=1
    )
    g_qkv = jnp.einsum("nd,ne->de", rows_in, dqkv, preferred_element_type=F32)
    dr1_all = jnp.einsum("svj,svd->sjd", onehot * live[:, :, None], dr1.reshape(seqs, most, width), precision=lax.Precision.HIGHEST)
    grad_in = dr1_all.reshape(tokens, width) + jnp.einsum("ne,de->nd", dqkv, w_qkv, preferred_element_type=F32)
    owned = scatter_grads(g_qkv, g_out, g_up, g_down)
    small = lax.psum(jnp.stack([g_gain_attn, g_shift_attn, g_gain_ffn, g_shift_ffn]), AXES)
    share = width // lax.axis_size("fsdp")
    small = lax.dynamic_slice_in_dim(small, lax.axis_index("fsdp") * share, share, axis=1)
    return (
        layer_out,
        grad_in.reshape(seqs, length, width),
        *owned,
        small[0],
        small[1],
        small[2],
        small[3],
    )


def solution(mesh):
    rows3 = P(("fsdp", "dp"), None, None)
    rows2 = P("fsdp", None)
    rows1 = P("fsdp")
    shape = dict(mesh.shape)
    step = on_block if shape == {"fsdp": SHARDS, "dp": QUARTERS} else on_device
    return jax.shard_map(
        step,
        mesh=mesh,
        in_specs=(rows3, rows2, rows2, rows2, rows2, rows1, rows1, rows1, rows1, rows3, P(("fsdp", "dp"), None), P(("fsdp", "dp"))),
        out_specs=(rows3, rows3, rows2, rows2, rows2, rows2, rows1, rows1, rows1, rows1),
        check_vma=False,
    )
```

```python
import functools

import jax
import jax.numpy as jnp
from jax import lax
from jax.experimental import pallas as pl
from jax.experimental.pallas import tpu as pltpu
from jax.sharding import PartitionSpec as P

HEADS = 12
HEAD_DIM = 64
EPS = 1e-12
F32 = jnp.float32
LOW = jnp.bfloat16
AXES = ("fsdp", "dp")
D = 768
ROWS = 96
LINE = 4
SHARDS = D // ROWS
QUARTERS = 4
EXACT = lax.Precision.HIGHEST
SCALE = HEAD_DIM**-0.5
VMEM = pl.BlockSpec(memory_space=pltpu.VMEM)
SMEM = pl.BlockSpec(memory_space=pltpu.SMEM)
BIG = pltpu.CompilerParams(vmem_limit_bytes=60 * 1024 * 1024)


def out(shape, dtype):
    return jax.ShapeDtypeStruct(shape, dtype)


def cost(us):
    return pl.CostEstimate(flops=0, bytes_accessed=int(us * 3.0e6), transcendentals=0)


def mm(a, b):
    return jnp.dot(a, b, preferred_element_type=F32)


def mm_nt(a, b):
    return lax.dot_general(a, b, (((1,), (1,)), ((), ())), preferred_element_type=F32)


def mm_tn(a, b):
    return lax.dot_general(a, b, (((0,), (0,)), ((), ())), preferred_element_type=F32)


def norm_parts(value):
    center = value - jnp.mean(value, axis=-1, keepdims=True)
    rstd = lax.rsqrt(jnp.mean(center * center, axis=-1, keepdims=True) + EPS)
    return center * rstd, rstd


def norm_back(grad, unit, rstd, gain):
    scaled = grad * gain
    return rstd * (
        scaled
        - jnp.mean(scaled, axis=-1, keepdims=True)
        - unit * jnp.mean(scaled * unit, axis=-1, keepdims=True)
    )


def onehot(pos_ref, seq, most, length):
    spots = lax.broadcasted_iota(jnp.int32, (most, length), 1)
    return spots == pos_ref[pl.ds(seq * most, most), :]


def gelu_parts(gate):
    cdf = 0.5 * (1.0 + lax.erf(gate * (0.5**0.5)))
    pdf = jnp.exp(-0.5 * gate * gate) * ((2.0 * jnp.pi) ** -0.5)
    return gate * cdf, cdf + gate * pdf


def slope_of(head):
    return 2.0 ** (-8.0 * (head + 1.0) / HEADS)


def block(ref, *index):
    value = ref[index] if index else ref[...]
    return value.reshape(-1, value.shape[-1])


EXTRA = 8
TAIL = 8
HALVES = ((0, 48), (48, 56))
KEYS = [(ry, rx, rc) for rc in (0, 1) for rx in (0, 1) for ry in (0, 1)]


def attention_kernel(seqs, most, where_ref, slope_ref, x_ref, norm_ref, pos_ref, *rest):
    lines, rest = rest[:16], rest[16:]
    qkv_ref, h1_ref, att_m_ref, h1_m_ref, q_m_ref, r1_m_ref, w_ref, att_ref, r1_ref, sem = rest
    z, y, c_x = where_ref[0], where_ref[1], where_ref[4]
    copies = []
    for n, (ry, rx, rc) in enumerate(KEYS):
        j = jnp.bitwise_xor(c_x, 2 * rx + rc)
        for r in range(LINE):
            shard = 2 * lax.rem(z + LINE - r, LINE) + jnp.bitwise_xor(y, ry)
            for half, (start, size) in enumerate(HALVES):
                size = min(size, ROWS - start)
                copies.append(
                    pltpu.make_async_copy(
                        lines[2 * n + half].at[r, pl.ds(0, size)], w_ref.at[shard, j, pl.ds(start, size)], sem
                    )
                )
    for copy in copies:
        copy.start()
    for copy in copies:
        copy.wait()
    length = x_ref.shape[0] // seqs
    step = 256

    @pl.loop(0, 3 * D // step)
    def _(n):
        j = n // (D // step)
        lane = pl.multiple_of((n - j * (D // step)) * step, step)
        w = w_ref[:, j, :, pl.ds(lane, step)].reshape(D, step)
        qkv_ref[:, pl.ds(pl.multiple_of(n * step, step), step)] = mm(x_ref[...], w).astype(LOW)

    first = lax.broadcasted_iota(jnp.int32, (length, 128), 1) < HEAD_DIM
    row = lax.broadcasted_iota(jnp.int32, (length, length), 0)
    col = lax.broadcasted_iota(jnp.int32, (length, length), 1)
    away = jnp.abs(row - col).astype(F32)

    @pl.loop(0, HEADS // 2)
    def _(t):
        lane = pl.multiple_of(t * 128, 128)
        bias = jnp.concatenate([slope_ref[2 * t] * away, slope_ref[2 * t + 1] * away], axis=0)
        for s in range(seqs):
            rows = slice(s * length, (s + 1) * length)
            q = qkv_ref[rows, pl.ds(lane, 128)]
            k = qkv_ref[rows, pl.ds(D + lane, 128)]
            v = qkv_ref[rows, pl.ds(2 * D + lane, 128)]
            zero = jnp.zeros_like(q)
            both = jnp.concatenate([jnp.where(first, q, zero), jnp.where(first, zero, q)], axis=0)
            score = mm_nt(both, k) * SCALE - bias
            e = jnp.exp(score - jnp.max(score, axis=-1, keepdims=True))
            p = (e * (1.0 / jnp.sum(e, axis=-1, keepdims=True))).astype(LOW)
            mixed = mm(p, v)
            att_ref[rows, pl.ds(lane, 128)] = jnp.where(first, mixed[:length], mixed[length:]).astype(LOW)

    @pl.loop(0, D // step)
    def _(n):
        lane = pl.multiple_of(n * step, step)
        w = w_ref[:, 3, :, pl.ds(lane, step)].reshape(D, step)
        r1_ref[:, pl.ds(lane, step)] = x_ref[:, pl.ds(lane, step)].astype(F32) + mm(att_ref[...], w)

    for s in range(seqs):
        rows = slice(s * length, (s + 1) * length)
        listed = slice(s * most, (s + 1) * most)
        unit, _ = norm_parts(r1_ref[rows, :])
        h1 = unit * norm_ref[0:1, :] + norm_ref[1:2, :]
        h1_ref[rows, :] = h1
        hot = onehot(pos_ref, s, most, length)
        hot_low = hot.astype(LOW)
        r1_m_ref[listed, :] = jnp.dot(hot.astype(F32), r1_ref[rows, :], precision=EXACT, preferred_element_type=F32)
        h1_m_ref[listed, :] = mm(hot_low, h1.astype(LOW)).astype(LOW)
        att_m_ref[listed, :] = mm(hot_low, att_ref[rows, :]).astype(LOW)
        q_m_ref[listed, :] = mm(hot_low, qkv_ref[rows, 0:D]).astype(LOW)


def attention_forward(where, x, lines, norms, pos, slopes, seqs):
    tokens = x.shape[0]
    listed = pos.shape[0]
    return pl.pallas_call(
        functools.partial(attention_kernel, seqs, listed // seqs),
        out_shape=(
            out((tokens, 3 * D), LOW),
            out((tokens, D), F32),
            out((listed, D), LOW),
            out((listed, D), LOW),
            out((listed, D), LOW),
            out((listed, D), F32),
            out((SHARDS, QUARTERS, ROWS, D), LOW),
        ),
        in_specs=[SMEM, SMEM, VMEM, VMEM, VMEM] + [pl.BlockSpec(memory_space=pl.ANY)] * 16,
        out_specs=(VMEM,) * 7,
        scratch_shapes=[pltpu.VMEM((tokens, D), LOW), pltpu.VMEM((tokens, D), F32), pltpu.SemaphoreType.DMA],
        compiler_params=BIG,
        cost_estimate=cost(20),
        name="attention_forward",
    )(where, slopes, x, norms, pos, *lines)


def ffn_kernel(seqs, most, h1_ref, gate_ref, up_ref, down_ref, norm_ref, pos_ref, dy_ref, y_ref, dr2_ref, e2_ref, small_ref, low_ref, act_ref, acc_ref):
    j = pl.program_id(0)
    tokens = h1_ref.shape[0]
    length = tokens // seqs
    step = 256

    @pl.when(j == 0)
    def _():
        low_ref[...] = h1_ref[...].astype(LOW)
        acc_ref[...] = h1_ref[...]

    def products(n):
        lanes = slice(n * step, (n + 1) * step)
        return mm(low_ref[...], gate_ref[:, :, lanes].reshape(D, step)), mm(low_ref[...], up_ref[:, :, lanes].reshape(D, step))

    gate, up = products(0)
    for n in range(D // step):
        following = products(n + 1) if (n + 1) * step < D else (None, None)
        cdf = 0.5 * (1.0 + lax.erf(gate * (0.5**0.5)))
        act_ref[:, n * step : (n + 1) * step] = (gate * cdf * up).astype(LOW)
        gate, up = following
    for n in range(D // step):
        lanes = slice(n * step, (n + 1) * step)
        acc_ref[:, lanes] += mm(act_ref[...], down_ref[:, :, :, lanes].reshape(D, step))

    @pl.when(j == QUARTERS - 1)
    def _():
        gain = norm_ref[2:3, :]
        small = [jnp.zeros((1, D), F32)] * 2
        for s in range(seqs):
            rows = slice(s * length, (s + 1) * length)
            listed = slice(s * most, (s + 1) * most)
            unit, _ = norm_parts(acc_ref[rows, :])
            y_ref[rows, :] = (unit * gain + norm_ref[3:4, :]).astype(LOW)
            hot = onehot(pos_ref, s, most, length).astype(F32)
            picked = jnp.dot(hot, acc_ref[rows, :], precision=EXACT, preferred_element_type=F32)
            unit_m, rstd_m = norm_parts(picked)
            dy = dy_ref[listed, :].astype(F32)
            small = [small[0] + jnp.sum(dy * unit_m, axis=0, keepdims=True), small[1] + jnp.sum(dy, axis=0, keepdims=True)]
            dr2 = norm_back(dy, unit_m, rstd_m, gain)
            dr2_ref[listed, :] = dr2
            e2_ref[listed, :] = dr2.astype(LOW)
        small_ref[...] = jnp.concatenate(small, axis=0)


def ffn_forward(h1, w_ffn, norms, pos, dy, seqs):
    tokens = h1.shape[0]
    listed = pos.shape[0]
    whole = lambda shape: pl.BlockSpec(shape, lambda j: (0,) * len(shape), pipeline_mode=pl.Buffered(1))
    return pl.pallas_call(
        functools.partial(ffn_kernel, seqs, listed // seqs),
        out_shape=(out((tokens, D), LOW), out((listed, D), F32), out((listed, D), LOW), out((2, D), F32)),
        grid=(QUARTERS,),
        in_specs=[
            whole((tokens, D)),
            pl.BlockSpec((SHARDS, None, None, ROWS, D), lambda j: (0, j, 0, 0, 0)),
            pl.BlockSpec((SHARDS, None, None, ROWS, D), lambda j: (0, j, 1, 0, 0)),
            pl.BlockSpec((SHARDS // QUARTERS, QUARTERS, None, ROWS, D), lambda j: (j, 0, 2, 0, 0)),
            whole(norms.shape),
            whole(pos.shape),
            whole(dy.shape),
        ],
        out_specs=(
            pl.BlockSpec((tokens, D), lambda j: (0, 0)),
            pl.BlockSpec((listed, D), lambda j: (0, 0)),
            pl.BlockSpec((listed, D), lambda j: (0, 0)),
            pl.BlockSpec((2, D), lambda j: (0, 0)),
        ),
        scratch_shapes=[pltpu.VMEM((tokens, D), LOW), pltpu.VMEM((tokens, D), LOW), pltpu.VMEM((tokens, D), F32)],
        compiler_params=BIG,
        cost_estimate=cost(16),
        name="ffn_forward",
    )(h1, w_ffn, w_ffn, w_ffn, norms, pos, dy)


def ffn_again_kernel(where_ref, h_ref, gate_ref, up_ref, act_ref, to_gate_ref, to_up_ref):
    step = 256

    rows = block(h_ref)

    def products(n):
        lanes = slice(n * step, (n + 1) * step)
        return mm(rows, gate_ref[:, :, lanes].reshape(D, step)), mm(rows, up_ref[:, :, lanes].reshape(D, step))

    gate, up = products(0)
    for n in range(D // step):
        following = products(n + 1) if (n + 1) * step < D else (None, None)
        lanes = slice(n * step, (n + 1) * step)
        value, slope = gelu_parts(gate)
        act_ref[:, lanes] = (value * up).astype(LOW)
        to_gate_ref[:, lanes] = slope * up
        to_up_ref[:, lanes] = value
        gate, up = following


def quarter_specs(which):
    specs = {
        "gate": pl.BlockSpec((SHARDS, None, None, ROWS, D), lambda g, w: (0, w[4], 0, 0, 0)),
        "up": pl.BlockSpec((SHARDS, None, None, ROWS, D), lambda g, w: (0, w[4], 1, 0, 0)),
        "down": pl.BlockSpec((SHARDS // QUARTERS, QUARTERS, None, ROWS, D), lambda g, w: (w[4], 0, 2, 0, 0)),
    }
    return [specs[name] for name in which]


def at_once(shape):
    return pl.BlockSpec(shape, lambda g, w: (0,) * len(shape))


def ffn_again(where, h_all, w_ffn):
    rows = h_all.shape[0] * h_all.shape[1]
    return pl.pallas_call(
        ffn_again_kernel,
        out_shape=(out((rows, D), LOW), out((rows, D), F32), out((rows, D), F32)),
        grid_spec=pltpu.PrefetchScalarGridSpec(
            num_scalar_prefetch=1,
            grid=(1,),
            in_specs=[at_once(h_all.shape), *quarter_specs(["gate", "up"])],
            out_specs=(at_once((rows, D)),) * 3,
        ),
        compiler_params=BIG,
        cost_estimate=cost(6),
        name="ffn_again",
    )(where, h_all, w_ffn, w_ffn)


def ffn_back_kernel(where_ref, e_ref, to_gate_ref, to_up_ref, gate_ref, up_ref, down_ref, dgate_ref, dup_ref, keep_ref, send_ref):
    listed = e_ref.shape[1]
    half = QUARTERS // 2
    for n in range(SHARDS // QUARTERS):
        lanes = slice(n * QUARTERS * ROWS, (n + 1) * QUARTERS * ROWS)
        dact = mm_nt(block(e_ref), block(down_ref, n))
        dgate_ref[:, lanes] = (dact * to_gate_ref[:, lanes]).astype(LOW)
        dup_ref[:, lanes] = (dact * to_up_ref[:, lanes]).astype(LOW)
    for n in range(2):
        shards = slice(n * SHARDS // 2, (n + 1) * SHARDS // 2)
        lanes = slice(n * D // 2, (n + 1) * D // 2)
        part = mm_nt(dgate_ref[...], block(gate_ref, shards)) + mm_nt(dup_ref[...], block(up_ref, shards))
        for r in range(half):
            keep_ref[r, :, lanes] = part[2 * r * listed : (2 * r + 1) * listed]
            send_ref[r, :, lanes] = part[(2 * r + 1) * listed : (2 * r + 2) * listed].astype(LOW)


def ffn_back(where, e_all, to_gate, to_up, w_ffn):
    count, listed, _ = e_all.shape
    rows = count * listed
    return pl.pallas_call(
        ffn_back_kernel,
        out_shape=(out((rows, D), LOW), out((rows, D), LOW), out((count // 2, listed, D), F32), out((count // 2, listed, D), LOW)),
        grid_spec=pltpu.PrefetchScalarGridSpec(
            num_scalar_prefetch=1,
            grid=(1,),
            in_specs=[at_once(e_all.shape), at_once((rows, D)), at_once((rows, D)), *quarter_specs(["gate", "up", "down"])],
            out_specs=(at_once((rows, D)), at_once((rows, D)), at_once((count // 2, listed, D)), at_once((count // 2, listed, D))),
        ),
        compiler_params=BIG,
        cost_estimate=cost(7),
        name="ffn_back",
    )(where, e_all, to_gate, to_up, w_ffn, w_ffn, w_ffn)


def weight_grad_kernel(where_ref, a_ref, b_ref, keep_ref, send_ref, full_ref):
    z, y = where_ref[0], where_ref[1]
    b = block(b_ref)
    step = 256

    for n in range(D // step):
        rows = slice(n * step, (n + 1) * step)
        full_ref[rows, :] = mm_tn(block(a_ref, *([slice(None)] * (len(a_ref.shape) - 1)), rows), b)

    for r in range(LINE):
        base = 2 * lax.rem(z + r, LINE)
        for other, ref in ((0, keep_ref), (1, send_ref)):
            start = (base + (y if other == 0 else 1 - y)) * ROWS
            ref[r] = full_ref[pl.ds(pl.multiple_of(start, 8), ROWS), :].astype(LOW)


def weight_grad(where, a, b):
    shape = (LINE, ROWS, D)
    rows = a.size // D
    return pl.pallas_call(
        weight_grad_kernel,
        out_shape=(out(shape, LOW), out(shape, LOW)),
        in_specs=[SMEM, VMEM, VMEM],
        out_specs=(VMEM, VMEM),
        scratch_shapes=[pltpu.VMEM((D, D), F32)],
        compiler_params=BIG,
        cost_estimate=cost(4),
        name="weight_grad",
    )(where, a, b)


def norm_back_kernel(dr2_ref, part_ref, came_ref, r1_ref, w_ref, norm_ref, dr1_ref, low_ref, datt_ref, small_ref):
    dh1 = dr2_ref[...] + part_ref[...] + came_ref[...].astype(F32)
    unit, rstd = norm_parts(r1_ref[...])
    small_ref[0:1, :] = jnp.sum(dh1 * unit, axis=0, keepdims=True)
    small_ref[1:2, :] = jnp.sum(dh1, axis=0, keepdims=True)
    dr1 = norm_back(dh1, unit, rstd, norm_ref[0:1, :])
    dr1_ref[...] = dr1
    low = dr1.astype(LOW)
    low_ref[...] = low
    for n in range(2):
        lanes = slice(n * D // 2, (n + 1) * D // 2)
        datt_ref[:, lanes] = mm_nt(low, block(w_ref, slice(n * SHARDS // 2, (n + 1) * SHARDS // 2))).astype(LOW)


def norm_back_call(dr2, part, came, r1_m, w_attn, norms):
    listed = dr2.shape[0]
    same = lambda shape: pl.BlockSpec(shape, lambda g: (0,) * len(shape))
    rows = same((listed, D))
    return pl.pallas_call(
        norm_back_kernel,
        out_shape=(out((listed, D), F32), out((listed, D), LOW), out((listed, D), LOW), out((2, D), F32)),
        grid=(1,),
        in_specs=[rows, rows, rows, rows, pl.BlockSpec((SHARDS, None, ROWS, D), lambda g: (0, 3, 0, 0)), same((4, D))],
        out_specs=(rows, rows, rows, same((2, D))),
        compiler_params=BIG,
        cost_estimate=cost(4),
        name="norm_back",
    )(dr2, part, came, r1_m, w_attn, norms)


def attention_back_kernel(seqs, most, slope_ref, datt_ref, q_ref, qkv_ref, pos_ref, rhs_ref, away_ref, hot_ref):
    length = qkv_ref.shape[0] // seqs
    listed = seqs * most
    first_m = lax.broadcasted_iota(jnp.int32, (most, 128), 1) < HEAD_DIM
    spots = lax.broadcasted_iota(jnp.int32, (listed, length), 1)
    away_ref[...] = jnp.abs(pos_ref[...] - spots).astype(F32)
    hot_ref[...] = (spots == pos_ref[...]).astype(LOW)

    def both(value):
        zero = jnp.zeros_like(value)
        return jnp.concatenate([jnp.where(first_m, value, zero), jnp.where(first_m, zero, value)], axis=0)

    @pl.loop(0, HEADS // 4)
    def _(step):
        for n, s in ((n, s) for n in (0, 1) for s in range(seqs)):
            t = 2 * step + n
            lane = pl.multiple_of(t * 128, 128)
            rows = slice(s * length, (s + 1) * length)
            mine = slice(s * most, (s + 1) * most)
            away = away_ref[mine, :]
            q = both(q_ref[mine, pl.ds(lane, 128)])
            da = both(datt_ref[mine, pl.ds(lane, 128)])
            k = qkv_ref[rows, pl.ds(D + lane, 128)]
            v = qkv_ref[rows, pl.ds(2 * D + lane, 128)]
            bias = jnp.concatenate([slope_ref[2 * t] * away, slope_ref[2 * t + 1] * away], axis=0)
            score = mm_nt(q, k) * SCALE - bias
            e = jnp.exp(score - jnp.max(score, axis=-1, keepdims=True))
            p = e * (1.0 / jnp.sum(e, axis=-1, keepdims=True))
            dp = mm_nt(da, v)
            ds = (p * (dp - jnp.sum(dp * p, axis=-1, keepdims=True))).astype(LOW)
            dq = mm(ds, k)
            dq = (jnp.where(first_m, dq[:most], dq[most:]) * SCALE).astype(LOW)
            rhs_ref[rows, pl.ds(lane, 128)] = mm_tn(hot_ref[mine, :], dq).astype(LOW)
            rhs_ref[rows, pl.ds(D + lane, 128)] = (mm_tn(ds, q) * SCALE).astype(LOW)
            rhs_ref[rows, pl.ds(2 * D + lane, 128)] = mm_tn(p.astype(LOW), da).astype(LOW)


def attention_back(datt, q_m, qkv, pos, slopes, seqs, part):
    tokens, listed = qkv.shape[0] // 2, pos.shape[0] // 2
    length = tokens * 2 // seqs
    mine = lambda shape: pl.BlockSpec(shape, lambda g: (part, 0))
    return pl.pallas_call(
        functools.partial(attention_back_kernel, seqs // 2, listed * 2 // seqs),
        out_shape=out((tokens, 3 * D), LOW),
        grid=(1,),
        in_specs=[SMEM, mine((listed, D)), mine((listed, D)), mine((tokens, 3 * D)), mine((listed, 1))],
        out_specs=pl.BlockSpec((tokens, 3 * D), lambda g: (0, 0)),
        scratch_shapes=[pltpu.VMEM((listed, length), F32), pltpu.VMEM((listed, length), LOW)],
        compiler_params=BIG,
        cost_estimate=cost(8),
        name="attention_back",
    )(slopes, datt, q_m, qkv, pos)


def attention_grads_kernel(where_ref, flip_ref, rhs0_ref, rhs1_ref, att_ref, low_ref, small_attn_ref, small_ffn_ref, keep0_ref, keep1_ref, away0_ref, away1_ref, full_ref, tail_ref):
    z, y, mine = where_ref[0], where_ref[1], where_ref[4]
    half = ROWS // 2
    step = 256
    tail_ref[...] = jnp.zeros(tail_ref.shape, LOW)
    small = jnp.concatenate([small_attn_ref[...], small_ffn_ref[...]], axis=0).astype(LOW)
    for n in range(SHARDS):
        tail_ref[n, 0:4, 0:ROWS] = small[:, n * ROWS : (n + 1) * ROWS]
    for rc in (1, 0):
        cut0_ref, cut1_ref = (keep0_ref, keep1_ref) if rc == 0 else (away0_ref, away1_ref)
        for rx in (0, 1):
            j = jnp.bitwise_xor(mine, 2 * rx + rc)

            @pl.when(j == 3)
            def _():
                for n in range(D // step):
                    rows = slice(n * step, (n + 1) * step)
                    full_ref[rows, :] = mm_tn(att_ref[:, rows], low_ref[...])

            @pl.when(j != 3)
            def _():
                @pl.loop(0, D // step)
                def _(n):
                    lane = pl.multiple_of(n * step, step)
                    cols = pl.ds(pl.multiple_of(j * D + n * step, step), step)
                    first = rhs0_ref.shape[0]
                    full_ref[:, pl.ds(lane, step)] = mm(flip_ref[:, :first], rhs0_ref[:, cols]) + mm(flip_ref[:, first:], rhs1_ref[:, cols])

            for rz in range(LINE):
                base = 2 * lax.rem(z + rz, LINE)
                for ry in (0, 1):
                    shard = base + (y if ry == 0 else 1 - y)
                    start = shard * ROWS
                    cut0_ref[rx, ry, rz] = full_ref[pl.ds(pl.multiple_of(start, 8), half), :].astype(LOW)
                    cut1_ref[ry, rx, rz, 0:half] = full_ref[pl.ds(pl.multiple_of(start + half, 8), half), :].astype(LOW)
                    cut1_ref[ry, rx, rz, half:] = tail_ref[shard]


def attention_grads(where, x_flip, rhs0, rhs1, att_m, low, small_attn, small_ffn):
    half = ROWS // 2
    return pl.pallas_call(
        attention_grads_kernel,
        out_shape=(out((2, 2, LINE, half, D), LOW), out((2, 2, LINE, half + TAIL, D), LOW)) * 2,
        in_specs=[SMEM] + [VMEM] * 7,
        out_specs=(VMEM,) * 4,
        scratch_shapes=[pltpu.VMEM((D, D), F32), pltpu.VMEM((SHARDS, TAIL, D), LOW)],
        compiler_params=BIG,
        cost_estimate=cost(10),
        name="attention_grads",
    )(where, x_flip, rhs0, rhs1, att_m, low, small_attn, small_ffn)


def input_grad_kernel(seqs, rhs0_ref, rhs1_ref, w_ref, dr1_ref, pos_ref, out_ref):
    length = out_ref.shape[0] // seqs
    most = dr1_ref.shape[0] // seqs
    for n in range(2):
        lanes = slice(n * D // 2, (n + 1) * D // 2)
        shards = slice(n * SHARDS // 2, (n + 1) * SHARDS // 2)
        s = 0
        for rhs_ref in (rhs0_ref, rhs1_ref):
            total = mm_nt(rhs_ref[:, 0:D], block(w_ref, shards, 0))
            total += mm_nt(rhs_ref[:, D : 2 * D], block(w_ref, shards, 1))
            total += mm_nt(rhs_ref[:, 2 * D : 3 * D], block(w_ref, shards, 2))
            for m in range(rhs_ref.shape[0] // length):
                hot = (lax.broadcasted_iota(jnp.int32, (length, most), 0) == pos_ref[s : s + 1, :]).astype(F32)
                spread = jnp.dot(hot, dr1_ref[s * most : (s + 1) * most, lanes], precision=EXACT, preferred_element_type=F32)
                out_ref[s * length : (s + 1) * length, lanes] = total[m * length : (m + 1) * length] + spread
                s += 1


def input_grad(rhs0, rhs1, w_attn, dr1, positions):
    tokens = rhs0.shape[0] + rhs1.shape[0]
    return pl.pallas_call(
        functools.partial(input_grad_kernel, positions.shape[0]),
        out_shape=out((tokens, D), F32),
        in_specs=[VMEM] * 5,
        out_specs=VMEM,
        compiler_params=BIG,
        cost_estimate=cost(8),
        name="input_grad",
    )(rhs0, rhs1, w_attn, dr1, positions)


def place(z, y, x, c):
    return (2 * z + y) * 4 + 2 * x + c


def grid_perm(move):
    return [
        (place(z, y, x, c), place(*move(z, y, x, c)))
        for z in range(4)
        for y in range(2)
        for x in range(2)
        for c in range(2)
    ]


MOVES = {
    "x": grid_perm(lambda z, y, x, c: (z, y, 1 - x, c)),
    "y": grid_perm(lambda z, y, x, c: (z, 1 - y, x, c)),
    "c": grid_perm(lambda z, y, x, c: (z, y, x, 1 - c)),
    1: grid_perm(lambda z, y, x, c: ((z + 1) % 4, y, x, c)),
    2: grid_perm(lambda z, y, x, c: ((z + 2) % 4, y, x, c)),
    3: grid_perm(lambda z, y, x, c: ((z + 3) % 4, y, x, c)),
    "down": [(m * 4 + q, (2 * q + m // 4) * 4 + m % 4) for m in range(8) for q in range(4)],
}


def send(value, move):
    return lax.ppermute(value, AXES, MOVES[move])


def share_dp(value):
    other = send(value, "x")
    return value, send(value, "c"), other, send(other, "c")


def after(value, *earlier):
    return lax.optimization_barrier((value, *earlier))[0]


def add(kept, got):
    return kept.astype(F32) + got.astype(F32)


def line_parts(keep, got):
    return [add(keep[r], got[r]).astype(LOW) for r in (1, 2, 3)]


def line_send(parts):
    return [send(value, r) for r, value in zip((1, 2, 3), parts)]


def line_add(keep, got, came):
    return (add(keep[0], got[0]) + came[0].astype(F32) + came[1].astype(F32) + came[2].astype(F32)).astype(LOW)


def finish_ffn_kernel(where_ref, *rest):
    pieces, (down_ref, up_ref) = rest[:QUARTERS], rest[QUARTERS:]
    mine = where_ref[4]
    for n, ref in enumerate(pieces):
        j = jnp.bitwise_xor(mine, n)
        down_ref[pl.ds(pl.multiple_of(j * ROWS, 8), ROWS), :] = ref[0].astype(F32)
        for half in (0, 1):
            up_ref[:, pl.ds(pl.multiple_of((half * QUARTERS + j) * D, D), D)] = ref[1 + half].astype(F32)


def finish_attention_kernel(where_ref, *rest):
    pieces, (qkv_ref, out_ref, held_ref) = rest[:QUARTERS], rest[QUARTERS:]
    mine = where_ref[4]
    for n, ref in enumerate(pieces):
        held_ref[jnp.bitwise_xor(mine, n)] = ref[...].astype(F32)
    for j in range(3):
        qkv_ref[:, j * D : (j + 1) * D] = held_ref[j]
    out_ref[...] = held_ref[3]


def finish_ffn(where, pieces):
    return pl.pallas_call(
        finish_ffn_kernel,
        out_shape=(out((QUARTERS * ROWS, D), F32), out((ROWS, 2 * QUARTERS * D), F32)),
        in_specs=[SMEM] + [VMEM] * QUARTERS,
        out_specs=(VMEM, VMEM),
        compiler_params=BIG,
        cost_estimate=cost(4),
        name="finish_ffn",
    )(where, *pieces)


def finish_attention(where, pieces):
    return pl.pallas_call(
        finish_attention_kernel,
        out_shape=(out((ROWS, 3 * D), F32), out((ROWS, D), F32)),
        in_specs=[SMEM] + [VMEM] * QUARTERS,
        out_specs=(VMEM, VMEM),
        scratch_shapes=[pltpu.VMEM((QUARTERS, ROWS, D), F32)],
        compiler_params=BIG,
        cost_estimate=cost(2),
        name="finish_attention",
    )(where, *pieces)


def spread(piece, order):
    got = {frozenset(): piece}
    for step in (*order, "c"):
        for key in list(got):
            got[key | {step}] = send(got[key], step)
    return [got[frozenset(n for n, b in zip("yxc", key) if b)] for key in KEYS]


def on_block(hidden_in, w_qkv, w_out, w_up, w_down, gain_attn, shift_attn, gain_ffn, shift_ffn, grad_listed, positions, counts):
    seqs, length, width = hidden_in.shape
    tokens = seqs * length
    most = positions.shape[1]
    i, j = lax.axis_index("fsdp"), lax.axis_index("dp")
    where = jnp.stack([i // 2, i % 2, j // 2, j % 2, j]).astype(jnp.int32)
    ff = w_down.shape[0] * SHARDS
    attn_piece = lax.dynamic_slice_in_dim(jnp.concatenate([w_qkv, w_out], axis=1), j * D, D, axis=1)
    norms = jnp.concatenate([gain_attn, shift_attn, gain_ffn, shift_ffn, jnp.zeros((D - 4 * ROWS,), LOW)])
    attn_piece = jnp.concatenate([attn_piece, jnp.broadcast_to(norms, (EXTRA, D))], axis=0)
    line = jnp.stack([attn_piece] + [send(attn_piece, r) for r in (1, 2, 3)])
    x = hidden_in.reshape(tokens, width)
    line, x_flip = lax.optimization_barrier((line, x.T))
    halves = [
        spread(line[:, start : start + size], order)
        for (start, size), order in zip(HALVES, (("y", "x"), ("x", "y")))
    ]
    lines = [half[n] for n in range(len(KEYS)) for half in halves]
    ffn_piece = jnp.stack(
        [
            lax.dynamic_slice_in_dim(w_up, j * D, D, axis=1),
            lax.dynamic_slice_in_dim(w_up, ff + j * D, D, axis=1),
            lax.dynamic_slice_in_dim(w_down, j * ROWS, ROWS, axis=0),
        ]
    )
    w_ffn = lax.all_gather(ffn_piece, AXES, axis=0, tiled=False).reshape(SHARDS, QUARTERS, 3, ROWS, D)
    tails = jnp.stack([halves[1][n][:, 48, : 4 * ROWS] for n in range(2)])
    tails = jnp.where(i % 2 == 0, tails, tails[::-1])
    tails = jnp.roll(tails[:, ::-1], i // 2 + 1, axis=1)
    norms = tails.transpose(1, 0, 2).reshape(SHARDS, 4, ROWS).transpose(1, 0, 2).reshape(4, D).astype(F32)
    slopes = jnp.exp2(-8.0 * (jnp.arange(HEADS, dtype=F32) + 1.0) / HEADS)
    pos = positions.reshape(seqs * most, 1)
    live = jnp.arange(most, dtype=jnp.int32)[None, :] < counts[:, None]
    dy = jnp.where(live[:, :, None], grad_listed, jnp.zeros_like(grad_listed)).reshape(seqs * most, width)

    qkv, h1, att_m, h1_m, q_m, r1_m, w_attn = attention_forward(where, x, lines, norms, pos, slopes, seqs)
    h_all = jnp.stack(share_dp(h1_m))
    h1, h_all = lax.optimization_barrier((h1, h_all))
    layer_out, dr2, e2, small_ffn = ffn_forward(h1, w_ffn, norms, pos, dy, seqs)
    act, to_gate, to_up = ffn_again(where, h_all, w_ffn)
    other = after(send(e2, "x"), act)
    e_all = jnp.stack([e2, send(e2, "c"), other, send(other, "c")])
    dgate, dup, keep, away = ffn_back(where, e_all, to_gate, to_up, w_ffn)
    part = add(keep, send(away, "c"))
    part, part_away = part[0], part[1].astype(LOW)
    keep_d, away_d = weight_grad(where, act, e_all)
    came = send(part_away, "x")
    got_d = send(away_d, "y")
    keep_g, away_g = weight_grad(where, after(h_all, (away_d, part_away)), dgate)
    got_g = send(away_g, "y")
    keep_u, away_u = weight_grad(where, after(h_all, (away_g, came)), dup)
    got_u = send(away_u, "y")
    dr1, low, datt, small_attn = norm_back_call(dr2, part, after(came, away_u), r1_m, w_attn, norms)
    rhs0 = attention_back(datt, q_m, qkv, pos, slopes, seqs, 0)
    got_d, rhs0 = lax.optimization_barrier((got_d, rhs0))
    parts_d = line_parts(keep_d, got_d)
    line_d = line_send(parts_d)
    rhs1 = attention_back(after(datt, (rhs0, parts_d)), q_m, qkv, pos, slopes, seqs, 1)
    line_d, got_g, rhs1 = lax.optimization_barrier((line_d, got_g, rhs1))
    parts_g = line_parts(keep_g, got_g)
    line_g = line_send(parts_g)
    keep0, keep1, away0, away1 = attention_grads(where, x_flip, rhs0, after(rhs1, parts_g), att_m, low, small_attn, small_ffn)
    away0, away1, line_g, got_u = lax.optimization_barrier((away0, away1, line_g, got_u))
    came0, came1 = send(away0, "c"), send(away1, "c")
    parts_u = line_parts(keep_u, got_u)
    line_u = line_send(parts_u)
    g_down = send(line_add(keep_d, got_d, line_d), "down")
    away0, away1 = add(keep0[1], came0[1]).astype(LOW), add(keep1[1], came1[1]).astype(LOW)
    got0, got1 = send(away0, "x"), send(away1, "y")
    total0 = add(keep0[0], came0[0]) + got0.astype(F32)
    total1 = add(keep1[0], came1[0]) + got1.astype(F32)
    away0, away1 = total0[1].astype(LOW), total1[1].astype(LOW)
    got0, got1 = send(away0, "y"), send(away1, "x")
    g_down, line_u = after((g_down, line_u), (away0, away1))
    g_ffn = jnp.stack([g_down, line_add(keep_g, got_g, line_g), line_add(keep_u, got_u, line_u)])
    got0, got1 = after((got0, got1), g_ffn)
    total = jnp.concatenate([add(total0[0], got0), add(total1[0], got1)], axis=1)
    parts = [total[r].astype(LOW) for r in (1, 2, 3)]
    line_a = line_send(parts)
    other = send(g_ffn, "x")
    grad_in = input_grad(rhs0, after(rhs1, parts), w_attn, dr1, positions)
    line_a, other, grad_in = lax.optimization_barrier((line_a, other, grad_in))
    g_attn = total[0] + line_a[0].astype(F32) + line_a[1].astype(F32) + line_a[2].astype(F32)
    small = g_attn[ROWS : ROWS + 4, :ROWS]
    g_attn = g_attn[:ROWS].astype(LOW)
    shared = (g_ffn, send(g_ffn, "c"), other, send(other, "c"))
    grad_down, grad_up = finish_ffn(where, after(shared, g_attn))
    other = after(send(g_attn, "x"), grad_down)
    grad_qkv, grad_out = finish_attention(where, (g_attn, send(g_attn, "c"), other, send(other, "c")))
    return (
        layer_out.reshape(seqs, length, width),
        grad_in.reshape(seqs, length, width),
        grad_qkv,
        grad_out,
        grad_up,
        grad_down,
        small[0],
        small[1],
        small[2],
        small[3],
    )


FF = 3072


def slopes():
    return jnp.exp2(-8.0 * (jnp.arange(HEADS, dtype=F32) + 1.0) / HEADS)


def pick(onehot, rows):
    if rows.dtype == LOW:
        return jnp.einsum("svj,sjd->svd", onehot.astype(LOW), rows, preferred_element_type=F32).astype(LOW)
    return jnp.einsum("svj,sjd->svd", onehot, rows, precision=lax.Precision.HIGHEST)


def gather_weights(w_qkv, w_out, w_up, w_down):
    fsdp = lax.axis_size("fsdp")
    dp = lax.axis_size("dp")
    rows, width = w_out.shape
    if rows % (8 * dp):
        return (
            lax.all_gather(w_qkv, "fsdp", axis=0, tiled=True),
            lax.all_gather(w_out, "fsdp", axis=0, tiled=True),
            lax.all_gather(w_up, "fsdp", axis=0, tiled=True),
            lax.all_gather(w_down, "fsdp", axis=0, tiled=True),
        )
    mine = lax.axis_index("dp")
    part = rows // dp
    group = w_down.shape[0] // rows
    joined = jnp.concatenate([w_qkv, w_out, w_up], axis=1)
    joined = lax.dynamic_slice_in_dim(joined, mine * part, part, axis=0)
    down = lax.dynamic_slice_in_dim(w_down, mine * part * group, part * group, axis=0)
    down = jnp.concatenate([down[k * part : (k + 1) * part] for k in range(group)], axis=1)
    full = lax.all_gather(jnp.concatenate([joined, down], axis=1), AXES, axis=0, tiled=True)
    a, b = w_qkv.shape[1], w_qkv.shape[1] + w_out.shape[1]
    c = b + w_up.shape[1]
    full_down = full[:, c:].reshape(fsdp * dp, part, group, width)
    full_down = full_down.transpose(0, 2, 1, 3).reshape(fsdp * dp * part * group, width)
    return full[:, :a], full[:, a:b], full[:, b:c], full_down


def scatter_grads(g_qkv, g_out, g_up, g_down):
    fsdp = lax.axis_size("fsdp")
    dp = lax.axis_size("dp")
    width = g_out.shape[1]
    rows = g_out.shape[0] // fsdp
    if rows % (8 * dp):
        return tuple(
            lax.psum(lax.psum_scatter(g, "fsdp", scatter_dimension=0, tiled=True), "dp")
            for g in (g_qkv, g_out, g_up, g_down)
        )
    part = rows // dp
    group = g_down.shape[0] // g_out.shape[0]
    down = g_down.reshape(fsdp * dp, group, part, width).transpose(0, 2, 1, 3)
    down = down.reshape(fsdp * rows, group * width)
    joined = jnp.concatenate([g_qkv, g_out, g_up, down], axis=1).astype(LOW)
    mine = lax.psum_scatter(joined, AXES, scatter_dimension=0, tiled=True)
    full = lax.all_gather(mine, "dp", axis=0, tiled=True).astype(F32)
    a, b = g_qkv.shape[1], g_qkv.shape[1] + width
    c = b + g_up.shape[1]
    full_down = full[:, c:].reshape(dp, part, group, width).transpose(0, 2, 1, 3)
    return full[:, :a], full[:, a:b], full[:, b:c], full_down.reshape(rows * group, width)


def on_device(hidden_in, w_qkv, w_out, w_up, w_down, gain_attn, shift_attn, gain_ffn, shift_ffn, grad_listed, positions, counts):
    seqs, length, width = hidden_in.shape
    tokens = seqs * length
    most = positions.shape[1]
    norms = jnp.stack([gain_attn, shift_attn, gain_ffn, shift_ffn])
    norms = lax.all_gather(norms, "fsdp", axis=1, tiled=True).astype(F32)
    w_qkv, w_out, w_up, w_down = gather_weights(w_qkv, w_out, w_up, w_down)
    live = jnp.arange(most, dtype=jnp.int32)[None, :] < counts[:, None]
    onehot = (positions[:, :, None] == jnp.arange(length, dtype=jnp.int32)).astype(F32)
    rows_in = hidden_in.reshape(tokens, width)
    slope = slopes()
    scale = HEAD_DIM**-0.5
    qkv = mm(rows_in, w_qkv).astype(LOW)
    split = qkv.reshape(seqs, length, 3, HEADS, HEAD_DIM)
    q, k, v = split[:, :, 0], split[:, :, 1], split[:, :, 2]
    place = jnp.arange(length, dtype=F32)
    bias = -slope[:, None, None] * jnp.abs(place[:, None] - place[None, :])
    s = jnp.einsum("sqhc,skhc->shqk", q, k, preferred_element_type=F32) * scale + bias
    p = jax.nn.softmax(s, axis=-1).astype(LOW)
    att = jnp.einsum("shqk,skhc->sqhc", p, v, preferred_element_type=F32).astype(LOW)
    att = att.reshape(tokens, width)
    r1 = rows_in.astype(F32) + mm(att, w_out)
    unit1, _ = norm_parts(r1)
    h1 = unit1 * norms[0] + norms[1]
    h1_low = h1.astype(LOW)
    u = mm(h1_low, w_up)
    act = (jax.nn.gelu(u[:, :FF], approximate=False) * u[:, FF:]).astype(LOW)
    r2 = h1 + mm(act, w_down)
    unit2, _ = norm_parts(r2)
    layer_out = (unit2 * norms[2] + norms[3]).astype(LOW).reshape(seqs, length, width)
    def listed(a):
        return pick(onehot, a.reshape(seqs, length, -1)).reshape(seqs * most, -1)

    dy = jnp.where(live[:, :, None], grad_listed, 0).astype(F32).reshape(seqs * most, width)
    unit2_m, rstd2_m = norm_parts(listed(r2))
    g_gain_ffn = jnp.sum(dy * unit2_m, axis=0)
    g_shift_ffn = jnp.sum(dy, axis=0)
    dr2 = norm_back(dy, unit2_m, rstd2_m, norms[2])
    e2 = dr2.astype(LOW)
    h1_m = listed(h1_low)
    u_m = mm(h1_m, w_up)
    gate, up = u_m[:, :FF], u_m[:, FF:]
    cdf = 0.5 * (1.0 + lax.erf(gate * (0.5**0.5)))
    pdf = jnp.exp(-0.5 * gate * gate) * ((2.0 * jnp.pi) ** -0.5)
    gelu = gate * cdf
    act_m = (gelu * up).astype(LOW)
    g_down = jnp.einsum("nf,nd->fd", act_m, e2, preferred_element_type=F32)
    dact = jnp.einsum("nd,fd->nf", e2, w_down, preferred_element_type=F32)
    du = jnp.concatenate([dact * up * (cdf + gate * pdf), dact * gelu], axis=1).astype(LOW)
    g_up = jnp.einsum("nd,nf->df", h1_m, du, preferred_element_type=F32)
    dh1 = dr2 + jnp.einsum("nf,df->nd", du, w_up, preferred_element_type=F32)
    unit1_m, rstd1_m = norm_parts(listed(r1))
    g_gain_attn = jnp.sum(dh1 * unit1_m, axis=0)
    g_shift_attn = jnp.sum(dh1, axis=0)
    dr1 = norm_back(dh1, unit1_m, rstd1_m, norms[0])
    e1 = dr1.astype(LOW)
    g_out = jnp.einsum("nd,ne->de", listed(att), e1, preferred_element_type=F32)
    datt = jnp.einsum("ne,de->nd", e1, w_out, preferred_element_type=F32).astype(LOW)
    datt = datt.reshape(seqs, most, HEADS, HEAD_DIM)
    q_m = listed(qkv[:, :width]).reshape(seqs, most, HEADS, HEAD_DIM)
    away = jnp.abs(positions[:, :, None].astype(F32) - place[None, None, :])
    s_m = jnp.einsum("sqhc,skhc->shqk", q_m, k, preferred_element_type=F32) * scale
    p_m = jax.nn.softmax(s_m - slope[None, :, None, None] * away[:, None], axis=-1)
    dv = jnp.einsum("shqk,sqhc->skhc", p_m.astype(LOW), datt, preferred_element_type=F32)
    dp = jnp.einsum("sqhc,skhc->shqk", datt, v, preferred_element_type=F32)
    ds = (p_m * (dp - jnp.sum(dp * p_m, axis=-1, keepdims=True))).astype(LOW)
    dq_m = (jnp.einsum("shqk,skhc->sqhc", ds, k, preferred_element_type=F32) * scale).astype(LOW)
    dk = (jnp.einsum("shqk,sqhc->skhc", ds, q_m, preferred_element_type=F32) * scale).astype(LOW)
    put = (onehot * live[:, :, None]).astype(LOW)
    dq = jnp.einsum("svj,svd->sjd", put, dq_m.reshape(seqs, most, width), preferred_element_type=F32)
    dqkv = jnp.concatenate(
        [dq.astype(LOW).reshape(tokens, width), dk.reshape(tokens, width), dv.astype(LOW).reshape(tokens, width)], axis=1
    )
    g_qkv = jnp.einsum("nd,ne->de", rows_in, dqkv, preferred_element_type=F32)
    dr1_all = jnp.einsum("svj,svd->sjd", onehot * live[:, :, None], dr1.reshape(seqs, most, width), precision=lax.Precision.HIGHEST)
    grad_in = dr1_all.reshape(tokens, width) + jnp.einsum("ne,de->nd", dqkv, w_qkv, preferred_element_type=F32)
    owned = scatter_grads(g_qkv, g_out, g_up, g_down)
    small = lax.psum(jnp.stack([g_gain_attn, g_shift_attn, g_gain_ffn, g_shift_ffn]), AXES)
    share = width // lax.axis_size("fsdp")
    small = lax.dynamic_slice_in_dim(small, lax.axis_index("fsdp") * share, share, axis=1)
    return (
        layer_out,
        grad_in.reshape(seqs, length, width),
        *owned,
        small[0],
        small[1],
        small[2],
        small[3],
    )


def solution(mesh):
    rows3 = P(("fsdp", "dp"), None, None)
    rows2 = P("fsdp", None)
    rows1 = P("fsdp")
    shape = dict(mesh.shape)
    step = on_block if shape == {"fsdp": SHARDS, "dp": QUARTERS} else on_device
    return jax.shard_map(
        step,
        mesh=mesh,
        in_specs=(rows3, rows2, rows2, rows2, rows2, rows1, rows1, rows1, rows1, rows3, P(("fsdp", "dp"), None), P(("fsdp", "dp"))),
        out_specs=(rows3, rows3, rows2, rows2, rows2, rows2, rows1, rows1, rows1, rows1),
        check_vma=False,
    )
```

```python
import functools

import jax
import jax.numpy as jnp
from jax import lax
from jax.experimental import pallas as pl
from jax.experimental.pallas import tpu as pltpu
from jax.sharding import PartitionSpec as P

HEADS = 12
HEAD_DIM = 64
EPS = 1e-12
F32 = jnp.float32
LOW = jnp.bfloat16
AXES = ("fsdp", "dp")
D = 768
ROWS = 96
LINE = 4
SHARDS = D // ROWS
QUARTERS = 4
EXACT = lax.Precision.HIGHEST
SCALE = HEAD_DIM**-0.5
VMEM = pl.BlockSpec(memory_space=pltpu.VMEM)
SMEM = pl.BlockSpec(memory_space=pltpu.SMEM)
BIG = pltpu.CompilerParams(vmem_limit_bytes=60 * 1024 * 1024)


def out(shape, dtype):
    return jax.ShapeDtypeStruct(shape, dtype)


def cost(us):
    return pl.CostEstimate(flops=0, bytes_accessed=int(us * 3.0e6), transcendentals=0)


def mm(a, b):
    return jnp.dot(a, b, preferred_element_type=F32)


def mm_nt(a, b):
    return lax.dot_general(a, b, (((1,), (1,)), ((), ())), preferred_element_type=F32)


def mm_tn(a, b):
    return lax.dot_general(a, b, (((0,), (0,)), ((), ())), preferred_element_type=F32)


def norm_parts(value):
    center = value - jnp.mean(value, axis=-1, keepdims=True)
    rstd = lax.rsqrt(jnp.mean(center * center, axis=-1, keepdims=True) + EPS)
    return center * rstd, rstd


def norm_back(grad, unit, rstd, gain):
    scaled = grad * gain
    return rstd * (
        scaled
        - jnp.mean(scaled, axis=-1, keepdims=True)
        - unit * jnp.mean(scaled * unit, axis=-1, keepdims=True)
    )


def onehot(pos_ref, seq, most, length):
    spots = lax.broadcasted_iota(jnp.int32, (most, length), 1)
    return spots == pos_ref[pl.ds(seq * most, most), :]


def gelu_parts(gate):
    cdf = 0.5 * (1.0 + lax.erf(gate * (0.5**0.5)))
    pdf = jnp.exp(-0.5 * gate * gate) * ((2.0 * jnp.pi) ** -0.5)
    return gate * cdf, cdf + gate * pdf


def slope_of(head):
    return 2.0 ** (-8.0 * (head + 1.0) / HEADS)


def block(ref, *index):
    value = ref[index] if index else ref[...]
    return value.reshape(-1, value.shape[-1])


EXTRA = 8
TAIL = 8
HALVES = ((0, 48), (48, 56))
KEYS = [(ry, rx, rc) for rc in (0, 1) for rx in (0, 1) for ry in (0, 1)]


def attention_kernel(seqs, most, where_ref, slope_ref, x_ref, norm_ref, pos_ref, *rest):
    lines, rest = rest[:16], rest[16:]
    qkv_ref, h1_ref, att_m_ref, h1_m_ref, q_m_ref, r1_m_ref, w_ref, att_ref, r1_ref, sem = rest
    z, y, c_x = where_ref[0], where_ref[1], where_ref[4]
    copies = []
    for n, (ry, rx, rc) in enumerate(KEYS):
        j = jnp.bitwise_xor(c_x, 2 * rx + rc)
        for r in range(LINE):
            shard = 2 * lax.rem(z + LINE - r, LINE) + jnp.bitwise_xor(y, ry)
            for half, (start, size) in enumerate(HALVES):
                size = min(size, ROWS - start)
                copies.append(
                    pltpu.make_async_copy(
                        lines[2 * n + half].at[r, pl.ds(0, size)], w_ref.at[shard, j, pl.ds(start, size)], sem
                    )
                )
    for copy in copies:
        copy.start()
    for copy in copies:
        copy.wait()
    length = x_ref.shape[0] // seqs
    step = 256

    @pl.loop(0, 3 * D // step)
    def _(n):
        j = n // (D // step)
        lane = pl.multiple_of((n - j * (D // step)) * step, step)
        w = w_ref[:, j, :, pl.ds(lane, step)].reshape(D, step)
        qkv_ref[:, pl.ds(pl.multiple_of(n * step, step), step)] = mm(x_ref[...], w).astype(LOW)

    first = lax.broadcasted_iota(jnp.int32, (length, 128), 1) < HEAD_DIM
    row = lax.broadcasted_iota(jnp.int32, (length, length), 0)
    col = lax.broadcasted_iota(jnp.int32, (length, length), 1)
    away = jnp.abs(row - col).astype(F32)

    @pl.loop(0, HEADS // 2)
    def _(t):
        lane = pl.multiple_of(t * 128, 128)
        bias = jnp.concatenate([slope_ref[2 * t] * away, slope_ref[2 * t + 1] * away], axis=0)
        for s in range(seqs):
            rows = slice(s * length, (s + 1) * length)
            q = qkv_ref[rows, pl.ds(lane, 128)]
            k = qkv_ref[rows, pl.ds(D + lane, 128)]
            v = qkv_ref[rows, pl.ds(2 * D + lane, 128)]
            zero = jnp.zeros_like(q)
            both = jnp.concatenate([jnp.where(first, q, zero), jnp.where(first, zero, q)], axis=0)
            score = mm_nt(both, k) * SCALE - bias
            e = jnp.exp(score - jnp.max(score, axis=-1, keepdims=True))
            p = (e * (1.0 / jnp.sum(e, axis=-1, keepdims=True))).astype(LOW)
            mixed = mm(p, v)
            att_ref[rows, pl.ds(lane, 128)] = jnp.where(first, mixed[:length], mixed[length:]).astype(LOW)

    @pl.loop(0, D // step)
    def _(n):
        lane = pl.multiple_of(n * step, step)
        w = w_ref[:, 3, :, pl.ds(lane, step)].reshape(D, step)
        r1_ref[:, pl.ds(lane, step)] = x_ref[:, pl.ds(lane, step)].astype(F32) + mm(att_ref[...], w)

    for s in range(seqs):
        rows = slice(s * length, (s + 1) * length)
        listed = slice(s * most, (s + 1) * most)
        unit, _ = norm_parts(r1_ref[rows, :])
        h1 = unit * norm_ref[0:1, :] + norm_ref[1:2, :]
        h1_ref[rows, :] = h1
        hot = onehot(pos_ref, s, most, length)
        hot_low = hot.astype(LOW)
        r1_m_ref[listed, :] = jnp.dot(hot.astype(F32), r1_ref[rows, :], precision=EXACT, preferred_element_type=F32)
        h1_m_ref[listed, :] = mm(hot_low, h1.astype(LOW)).astype(LOW)
        att_m_ref[listed, :] = mm(hot_low, att_ref[rows, :]).astype(LOW)
        q_m_ref[listed, :] = mm(hot_low, qkv_ref[rows, 0:D]).astype(LOW)


def attention_forward(where, x, lines, norms, pos, slopes, seqs):
    tokens = x.shape[0]
    listed = pos.shape[0]
    return pl.pallas_call(
        functools.partial(attention_kernel, seqs, listed // seqs),
        out_shape=(
            out((tokens, 3 * D), LOW),
            out((tokens, D), F32),
            out((listed, D), LOW),
            out((listed, D), LOW),
            out((listed, D), LOW),
            out((listed, D), F32),
            out((SHARDS, QUARTERS, ROWS, D), LOW),
        ),
        in_specs=[SMEM, SMEM, VMEM, VMEM, VMEM] + [pl.BlockSpec(memory_space=pl.ANY)] * 16,
        out_specs=(VMEM,) * 7,
        scratch_shapes=[pltpu.VMEM((tokens, D), LOW), pltpu.VMEM((tokens, D), F32), pltpu.SemaphoreType.DMA],
        compiler_params=BIG,
        cost_estimate=cost(20),
        name="attention_forward",
    )(where, slopes, x, norms, pos, *lines)


def ffn_kernel(seqs, most, h1_ref, gate_ref, up_ref, down_ref, norm_ref, pos_ref, dy_ref, y_ref, dr2_ref, e2_ref, small_ref, low_ref, act_ref, acc_ref):
    j = pl.program_id(0)
    tokens = h1_ref.shape[0]
    length = tokens // seqs
    step = 256

    @pl.when(j == 0)
    def _():
        low_ref[...] = h1_ref[...].astype(LOW)
        acc_ref[...] = h1_ref[...]

    def products(n):
        lanes = slice(n * step, (n + 1) * step)
        return mm(low_ref[...], gate_ref[:, :, lanes].reshape(D, step)), mm(low_ref[...], up_ref[:, :, lanes].reshape(D, step))

    gate, up = products(0)
    for n in range(D // step):
        following = products(n + 1) if (n + 1) * step < D else (None, None)
        cdf = 0.5 * (1.0 + lax.erf(gate * (0.5**0.5)))
        act_ref[:, n * step : (n + 1) * step] = (gate * cdf * up).astype(LOW)
        gate, up = following
    for n in range(D // step):
        lanes = slice(n * step, (n + 1) * step)
        acc_ref[:, lanes] += mm(act_ref[...], down_ref[:, :, :, lanes].reshape(D, step))

    @pl.when(j == QUARTERS - 1)
    def _():
        gain = norm_ref[2:3, :]
        small = [jnp.zeros((1, D), F32)] * 2
        for s in range(seqs):
            rows = slice(s * length, (s + 1) * length)
            listed = slice(s * most, (s + 1) * most)
            unit, _ = norm_parts(acc_ref[rows, :])
            y_ref[rows, :] = (unit * gain + norm_ref[3:4, :]).astype(LOW)
            hot = onehot(pos_ref, s, most, length).astype(F32)
            picked = jnp.dot(hot, acc_ref[rows, :], precision=EXACT, preferred_element_type=F32)
            unit_m, rstd_m = norm_parts(picked)
            dy = dy_ref[listed, :].astype(F32)
            small = [small[0] + jnp.sum(dy * unit_m, axis=0, keepdims=True), small[1] + jnp.sum(dy, axis=0, keepdims=True)]
            dr2 = norm_back(dy, unit_m, rstd_m, gain)
            dr2_ref[listed, :] = dr2
            e2_ref[listed, :] = dr2.astype(LOW)
        small_ref[...] = jnp.concatenate(small, axis=0)


def ffn_forward(h1, w_ffn, norms, pos, dy, seqs):
    tokens = h1.shape[0]
    listed = pos.shape[0]
    whole = lambda shape: pl.BlockSpec(shape, lambda j: (0,) * len(shape), pipeline_mode=pl.Buffered(1))
    return pl.pallas_call(
        functools.partial(ffn_kernel, seqs, listed // seqs),
        out_shape=(out((tokens, D), LOW), out((listed, D), F32), out((listed, D), LOW), out((2, D), F32)),
        grid=(QUARTERS,),
        in_specs=[
            whole((tokens, D)),
            pl.BlockSpec((SHARDS, None, None, ROWS, D), lambda j: (0, j, 0, 0, 0)),
            pl.BlockSpec((SHARDS, None, None, ROWS, D), lambda j: (0, j, 1, 0, 0)),
            pl.BlockSpec((SHARDS // QUARTERS, QUARTERS, None, ROWS, D), lambda j: (j, 0, 2, 0, 0)),
            whole(norms.shape),
            whole(pos.shape),
            whole(dy.shape),
        ],
        out_specs=(
            pl.BlockSpec((tokens, D), lambda j: (0, 0)),
            pl.BlockSpec((listed, D), lambda j: (0, 0)),
            pl.BlockSpec((listed, D), lambda j: (0, 0)),
            pl.BlockSpec((2, D), lambda j: (0, 0)),
        ),
        scratch_shapes=[pltpu.VMEM((tokens, D), LOW), pltpu.VMEM((tokens, D), LOW), pltpu.VMEM((tokens, D), F32)],
        compiler_params=BIG,
        cost_estimate=cost(16),
        name="ffn_forward",
    )(h1, w_ffn, w_ffn, w_ffn, norms, pos, dy)


def ffn_again_kernel(where_ref, h_ref, gate_ref, up_ref, act_ref, to_gate_ref, to_up_ref):
    step = 256

    rows = block(h_ref)

    def products(n):
        lanes = slice(n * step, (n + 1) * step)
        return mm(rows, gate_ref[:, :, lanes].reshape(D, step)), mm(rows, up_ref[:, :, lanes].reshape(D, step))

    gate, up = products(0)
    for n in range(D // step):
        following = products(n + 1) if (n + 1) * step < D else (None, None)
        lanes = slice(n * step, (n + 1) * step)
        value, slope = gelu_parts(gate)
        act_ref[:, lanes] = (value * up).astype(LOW)
        to_gate_ref[:, lanes] = slope * up
        to_up_ref[:, lanes] = value
        gate, up = following


def quarter_specs(which):
    specs = {
        "gate": pl.BlockSpec((SHARDS, None, None, ROWS, D), lambda g, w: (0, w[4], 0, 0, 0)),
        "up": pl.BlockSpec((SHARDS, None, None, ROWS, D), lambda g, w: (0, w[4], 1, 0, 0)),
        "down": pl.BlockSpec((SHARDS // QUARTERS, QUARTERS, None, ROWS, D), lambda g, w: (w[4], 0, 2, 0, 0)),
    }
    return [specs[name] for name in which]


def at_once(shape):
    return pl.BlockSpec(shape, lambda g, w: (0,) * len(shape))


def ffn_again(where, h_all, w_ffn):
    rows = h_all.shape[0] * h_all.shape[1]
    return pl.pallas_call(
        ffn_again_kernel,
        out_shape=(out((rows, D), LOW), out((rows, D), F32), out((rows, D), F32)),
        grid_spec=pltpu.PrefetchScalarGridSpec(
            num_scalar_prefetch=1,
            grid=(1,),
            in_specs=[at_once(h_all.shape), *quarter_specs(["gate", "up"])],
            out_specs=(at_once((rows, D)),) * 3,
        ),
        compiler_params=BIG,
        cost_estimate=cost(6),
        name="ffn_again",
    )(where, h_all, w_ffn, w_ffn)


def ffn_back_kernel(where_ref, e_ref, to_gate_ref, to_up_ref, gate_ref, up_ref, down_ref, dgate_ref, dup_ref, keep_ref, send_ref):
    listed = e_ref.shape[1]
    half = QUARTERS // 2
    for n in range(SHARDS // QUARTERS):
        lanes = slice(n * QUARTERS * ROWS, (n + 1) * QUARTERS * ROWS)
        dact = mm_nt(block(e_ref), block(down_ref, n))
        dgate_ref[:, lanes] = (dact * to_gate_ref[:, lanes]).astype(LOW)
        dup_ref[:, lanes] = (dact * to_up_ref[:, lanes]).astype(LOW)
    for n in range(2):
        shards = slice(n * SHARDS // 2, (n + 1) * SHARDS // 2)
        lanes = slice(n * D // 2, (n + 1) * D // 2)
        part = mm_nt(dgate_ref[...], block(gate_ref, shards)) + mm_nt(dup_ref[...], block(up_ref, shards))
        for r in range(half):
            keep_ref[r, :, lanes] = part[2 * r * listed : (2 * r + 1) * listed]
            send_ref[r, :, lanes] = part[(2 * r + 1) * listed : (2 * r + 2) * listed].astype(LOW)


def ffn_back(where, e_all, to_gate, to_up, w_ffn):
    count, listed, _ = e_all.shape
    rows = count * listed
    return pl.pallas_call(
        ffn_back_kernel,
        out_shape=(out((rows, D), LOW), out((rows, D), LOW), out((count // 2, listed, D), F32), out((count // 2, listed, D), LOW)),
        grid_spec=pltpu.PrefetchScalarGridSpec(
            num_scalar_prefetch=1,
            grid=(1,),
            in_specs=[at_once(e_all.shape), at_once((rows, D)), at_once((rows, D)), *quarter_specs(["gate", "up", "down"])],
            out_specs=(at_once((rows, D)), at_once((rows, D)), at_once((count // 2, listed, D)), at_once((count // 2, listed, D))),
        ),
        compiler_params=BIG,
        cost_estimate=cost(7),
        name="ffn_back",
    )(where, e_all, to_gate, to_up, w_ffn, w_ffn, w_ffn)


def weight_grad_kernel(where_ref, a_ref, b_ref, keep_ref, send_ref, full_ref):
    z, y = where_ref[0], where_ref[1]
    b = block(b_ref)
    step = 256

    for n in range(D // step):
        rows = slice(n * step, (n + 1) * step)
        full_ref[rows, :] = mm_tn(block(a_ref, *([slice(None)] * (len(a_ref.shape) - 1)), rows), b)

    for r in range(LINE):
        base = 2 * lax.rem(z + r, LINE)
        for other, ref in ((0, keep_ref), (1, send_ref)):
            start = (base + (y if other == 0 else 1 - y)) * ROWS
            ref[r] = full_ref[pl.ds(pl.multiple_of(start, 8), ROWS), :].astype(LOW)


def weight_grad(where, a, b):
    shape = (LINE, ROWS, D)
    rows = a.size // D
    return pl.pallas_call(
        weight_grad_kernel,
        out_shape=(out(shape, LOW), out(shape, LOW)),
        in_specs=[SMEM, VMEM, VMEM],
        out_specs=(VMEM, VMEM),
        scratch_shapes=[pltpu.VMEM((D, D), F32)],
        compiler_params=BIG,
        cost_estimate=cost(4),
        name="weight_grad",
    )(where, a, b)


def norm_back_kernel(dr2_ref, part_ref, came_ref, r1_ref, w_ref, norm_ref, dr1_ref, low_ref, datt_ref, small_ref):
    dh1 = dr2_ref[...] + part_ref[...] + came_ref[...].astype(F32)
    unit, rstd = norm_parts(r1_ref[...])
    small_ref[0:1, :] = jnp.sum(dh1 * unit, axis=0, keepdims=True)
    small_ref[1:2, :] = jnp.sum(dh1, axis=0, keepdims=True)
    dr1 = norm_back(dh1, unit, rstd, norm_ref[0:1, :])
    dr1_ref[...] = dr1
    low = dr1.astype(LOW)
    low_ref[...] = low
    for n in range(2):
        lanes = slice(n * D // 2, (n + 1) * D // 2)
        datt_ref[:, lanes] = mm_nt(low, block(w_ref, slice(n * SHARDS // 2, (n + 1) * SHARDS // 2))).astype(LOW)


def norm_back_call(dr2, part, came, r1_m, w_attn, norms):
    listed = dr2.shape[0]
    same = lambda shape: pl.BlockSpec(shape, lambda g: (0,) * len(shape))
    rows = same((listed, D))
    return pl.pallas_call(
        norm_back_kernel,
        out_shape=(out((listed, D), F32), out((listed, D), LOW), out((listed, D), LOW), out((2, D), F32)),
        grid=(1,),
        in_specs=[rows, rows, rows, rows, pl.BlockSpec((SHARDS, None, ROWS, D), lambda g: (0, 3, 0, 0)), same((4, D))],
        out_specs=(rows, rows, rows, same((2, D))),
        compiler_params=BIG,
        cost_estimate=cost(4),
        name="norm_back",
    )(dr2, part, came, r1_m, w_attn, norms)


def both_heads(value):
    first = lax.broadcasted_iota(jnp.int32, value.shape, 1) < HEAD_DIM
    zero = jnp.zeros_like(value)
    return jnp.concatenate([jnp.where(first, value, zero), jnp.where(first, zero, value)], axis=0)


def attention_again_kernel(seqs, slope_ref, q_ref, k_ref, pos_ref, p_ref):
    length, most = k_ref.shape[0] // seqs, q_ref.shape[0] // seqs
    spots = lax.broadcasted_iota(jnp.int32, (most, length), 1)

    @pl.loop(0, HEADS // 2)
    def _(t):
        lane = pl.multiple_of(t * 128, 128)
        for s in range(seqs):
            rows = slice(s * length, (s + 1) * length)
            mine = slice(s * most, (s + 1) * most)
            away = jnp.abs(pos_ref[mine, :] - spots).astype(F32)
            bias = jnp.concatenate([slope_ref[2 * t] * away, slope_ref[2 * t + 1] * away], axis=0)
            score = mm_nt(both_heads(q_ref[mine, pl.ds(lane, 128)]), k_ref[rows, pl.ds(lane, 128)]) * SCALE - bias
            e = jnp.exp(score - jnp.max(score, axis=-1, keepdims=True))
            p = e * (1.0 / jnp.sum(e, axis=-1, keepdims=True))
            p_ref[2 * t, mine, :] = p[:most]
            p_ref[2 * t + 1, mine, :] = p[most:]


def attention_again(q_m, qkv, pos, slopes, seqs):
    tokens, listed = qkv.shape[0], pos.shape[0]
    shape = (HEADS, listed, tokens // seqs)
    return pl.pallas_call(
        functools.partial(attention_again_kernel, seqs),
        out_shape=out(shape, F32),
        grid=(1,),
        in_specs=[SMEM, pl.BlockSpec((listed, D), lambda g: (0, 0)), pl.BlockSpec((tokens, D), lambda g: (0, 1)), pl.BlockSpec((listed, 1), lambda g: (0, 0))],
        out_specs=pl.BlockSpec(shape, lambda g: (0, 0, 0)),
        compiler_params=BIG,
        cost_estimate=cost(8),
        name="attention_again",
    )(slopes, q_m, qkv, pos)


def attention_back_kernel(seqs, datt_ref, q_ref, k_ref, v_ref, p_ref, pos_ref, rhs_ref, hot_ref):
    length, most = k_ref.shape[0] // seqs, q_ref.shape[0] // seqs
    first_m = lax.broadcasted_iota(jnp.int32, (most, 128), 1) < HEAD_DIM
    hot_ref[...] = (lax.broadcasted_iota(jnp.int32, hot_ref.shape, 1) == pos_ref[...]).astype(LOW)

    @pl.loop(0, HEADS // 4)
    def _(step):
        for n, s in ((n, s) for n in (0, 1) for s in range(seqs)):
            t = 2 * step + n
            lane = pl.multiple_of(t * 128, 128)
            rows = slice(s * length, (s + 1) * length)
            mine = slice(s * most, (s + 1) * most)
            q = both_heads(q_ref[mine, pl.ds(lane, 128)])
            da = both_heads(datt_ref[mine, pl.ds(lane, 128)])
            k = k_ref[rows, pl.ds(lane, 128)]
            v = v_ref[rows, pl.ds(lane, 128)]
            p = jnp.concatenate([p_ref[2 * t, mine, :], p_ref[2 * t + 1, mine, :]], axis=0)
            dp = mm_nt(da, v)
            ds = (p * (dp - jnp.sum(dp * p, axis=-1, keepdims=True))).astype(LOW)
            dq = mm(ds, k)
            dq = (jnp.where(first_m, dq[:most], dq[most:]) * SCALE).astype(LOW)
            rhs_ref[rows, pl.ds(lane, 128)] = mm_tn(hot_ref[mine, :], dq).astype(LOW)
            rhs_ref[rows, pl.ds(D + lane, 128)] = (mm_tn(ds, q) * SCALE).astype(LOW)
            rhs_ref[rows, pl.ds(2 * D + lane, 128)] = mm_tn(p.astype(LOW), da).astype(LOW)


def attention_back(datt, q_m, qkv, p_m, pos, seqs, part):
    tokens, listed = qkv.shape[0] // 2, pos.shape[0] // 2
    length = tokens * 2 // seqs
    mine = lambda shape, lane=0: pl.BlockSpec(shape, lambda g: (part, lane))
    return pl.pallas_call(
        functools.partial(attention_back_kernel, seqs // 2),
        out_shape=out((tokens, 3 * D), LOW),
        grid=(1,),
        in_specs=[
            mine((listed, D)),
            mine((listed, D)),
            mine((tokens, D), 1),
            mine((tokens, D), 2),
            pl.BlockSpec((HEADS, listed, length), lambda g: (0, part, 0)),
            mine((listed, 1)),
        ],
        out_specs=pl.BlockSpec((tokens, 3 * D), lambda g: (0, 0)),
        scratch_shapes=[pltpu.VMEM((listed, length), LOW)],
        compiler_params=BIG,
        cost_estimate=cost(8),
        name="attention_back",
    )(datt, q_m, qkv, qkv, p_m, pos)


def attention_grads_kernel(where_ref, flip_ref, rhs0_ref, rhs1_ref, att_ref, low_ref, small_attn_ref, small_ffn_ref, keep0_ref, keep1_ref, away0_ref, away1_ref, full_ref, tail_ref):
    z, y, mine = where_ref[0], where_ref[1], where_ref[4]
    half = ROWS // 2
    step = 256
    tail_ref[...] = jnp.zeros(tail_ref.shape, LOW)
    small = jnp.concatenate([small_attn_ref[...], small_ffn_ref[...]], axis=0).astype(LOW)
    for n in range(SHARDS):
        tail_ref[n, 0:4, 0:ROWS] = small[:, n * ROWS : (n + 1) * ROWS]
    for rc in (1, 0):
        cut0_ref, cut1_ref = (keep0_ref, keep1_ref) if rc == 0 else (away0_ref, away1_ref)
        for rx in (0, 1):
            j = jnp.bitwise_xor(mine, 2 * rx + rc)

            @pl.when(j == 3)
            def _():
                for n in range(D // step):
                    rows = slice(n * step, (n + 1) * step)
                    full_ref[rows, :] = mm_tn(att_ref[:, rows], low_ref[...])

            @pl.when(j != 3)
            def _():
                @pl.loop(0, D // step)
                def _(n):
                    lane = pl.multiple_of(n * step, step)
                    cols = pl.ds(pl.multiple_of(j * D + n * step, step), step)
                    first = rhs0_ref.shape[0]
                    full_ref[:, pl.ds(lane, step)] = mm(flip_ref[:, :first], rhs0_ref[:, cols]) + mm(flip_ref[:, first:], rhs1_ref[:, cols])

            for rz in range(LINE):
                base = 2 * lax.rem(z + rz, LINE)
                for ry in (0, 1):
                    shard = base + (y if ry == 0 else 1 - y)
                    start = shard * ROWS
                    cut0_ref[rx, ry, rz] = full_ref[pl.ds(pl.multiple_of(start, 8), half), :].astype(LOW)
                    cut1_ref[ry, rx, rz, 0:half] = full_ref[pl.ds(pl.multiple_of(start + half, 8), half), :].astype(LOW)
                    cut1_ref[ry, rx, rz, half:] = tail_ref[shard]


def attention_grads(where, x_flip, rhs0, rhs1, att_m, low, small_attn, small_ffn):
    half = ROWS // 2
    return pl.pallas_call(
        attention_grads_kernel,
        out_shape=(out((2, 2, LINE, half, D), LOW), out((2, 2, LINE, half + TAIL, D), LOW)) * 2,
        in_specs=[SMEM] + [VMEM] * 7,
        out_specs=(VMEM,) * 4,
        scratch_shapes=[pltpu.VMEM((D, D), F32), pltpu.VMEM((SHARDS, TAIL, D), LOW)],
        compiler_params=BIG,
        cost_estimate=cost(10),
        name="attention_grads",
    )(where, x_flip, rhs0, rhs1, att_m, low, small_attn, small_ffn)


def input_grad_kernel(seqs, rhs0_ref, rhs1_ref, w_ref, dr1_ref, pos_ref, out_ref):
    length = out_ref.shape[0] // seqs
    most = dr1_ref.shape[0] // seqs
    for n in range(2):
        lanes = slice(n * D // 2, (n + 1) * D // 2)
        shards = slice(n * SHARDS // 2, (n + 1) * SHARDS // 2)
        s = 0
        for rhs_ref in (rhs0_ref, rhs1_ref):
            total = mm_nt(rhs_ref[:, 0:D], block(w_ref, shards, 0))
            total += mm_nt(rhs_ref[:, D : 2 * D], block(w_ref, shards, 1))
            total += mm_nt(rhs_ref[:, 2 * D : 3 * D], block(w_ref, shards, 2))
            for m in range(rhs_ref.shape[0] // length):
                hot = (lax.broadcasted_iota(jnp.int32, (length, most), 0) == pos_ref[s : s + 1, :]).astype(F32)
                spread = jnp.dot(hot, dr1_ref[s * most : (s + 1) * most, lanes], precision=EXACT, preferred_element_type=F32)
                out_ref[s * length : (s + 1) * length, lanes] = total[m * length : (m + 1) * length] + spread
                s += 1


def input_grad(rhs0, rhs1, w_attn, dr1, positions):
    tokens = rhs0.shape[0] + rhs1.shape[0]
    return pl.pallas_call(
        functools.partial(input_grad_kernel, positions.shape[0]),
        out_shape=out((tokens, D), F32),
        in_specs=[VMEM] * 5,
        out_specs=VMEM,
        compiler_params=BIG,
        cost_estimate=cost(8),
        name="input_grad",
    )(rhs0, rhs1, w_attn, dr1, positions)


def place(z, y, x, c):
    return (2 * z + y) * 4 + 2 * x + c


def grid_perm(move):
    return [
        (place(z, y, x, c), place(*move(z, y, x, c)))
        for z in range(4)
        for y in range(2)
        for x in range(2)
        for c in range(2)
    ]


MOVES = {
    "x": grid_perm(lambda z, y, x, c: (z, y, 1 - x, c)),
    "y": grid_perm(lambda z, y, x, c: (z, 1 - y, x, c)),
    "c": grid_perm(lambda z, y, x, c: (z, y, x, 1 - c)),
    1: grid_perm(lambda z, y, x, c: ((z + 1) % 4, y, x, c)),
    2: grid_perm(lambda z, y, x, c: ((z + 2) % 4, y, x, c)),
    3: grid_perm(lambda z, y, x, c: ((z + 3) % 4, y, x, c)),
    "down": [(m * 4 + q, (2 * q + m // 4) * 4 + m % 4) for m in range(8) for q in range(4)],
}


def send(value, move):
    return lax.ppermute(value, AXES, MOVES[move])


def share_dp(value):
    other = send(value, "x")
    return value, send(value, "c"), other, send(other, "c")


def after(value, *earlier):
    return lax.optimization_barrier((value, *earlier))[0]


def add(kept, got):
    return kept.astype(F32) + got.astype(F32)


def line_parts(keep, got):
    return [add(keep[r], got[r]).astype(LOW) for r in (1, 2, 3)]


def line_send(parts):
    return [send(value, r) for r, value in zip((1, 2, 3), parts)]


def line_add(keep, got, came):
    return (add(keep[0], got[0]) + came[0].astype(F32) + came[1].astype(F32) + came[2].astype(F32)).astype(LOW)


def finish_ffn_kernel(where_ref, *rest):
    pieces, (down_ref, up_ref) = rest[:QUARTERS], rest[QUARTERS:]
    mine = where_ref[4]
    for n, ref in enumerate(pieces):
        j = jnp.bitwise_xor(mine, n)
        down_ref[pl.ds(pl.multiple_of(j * ROWS, 8), ROWS), :] = ref[0].astype(F32)
        for half in (0, 1):
            up_ref[:, pl.ds(pl.multiple_of((half * QUARTERS + j) * D, D), D)] = ref[1 + half].astype(F32)


def finish_attention_kernel(where_ref, *rest):
    pieces, (qkv_ref, out_ref, held_ref) = rest[:QUARTERS], rest[QUARTERS:]
    mine = where_ref[4]
    for n, ref in enumerate(pieces):
        held_ref[jnp.bitwise_xor(mine, n)] = ref[...].astype(F32)
    for j in range(3):
        qkv_ref[:, j * D : (j + 1) * D] = held_ref[j]
    out_ref[...] = held_ref[3]


def finish_ffn(where, pieces):
    return pl.pallas_call(
        finish_ffn_kernel,
        out_shape=(out((QUARTERS * ROWS, D), F32), out((ROWS, 2 * QUARTERS * D), F32)),
        in_specs=[SMEM] + [VMEM] * QUARTERS,
        out_specs=(VMEM, VMEM),
        compiler_params=BIG,
        cost_estimate=cost(4),
        name="finish_ffn",
    )(where, *pieces)


def finish_attention(where, pieces):
    return pl.pallas_call(
        finish_attention_kernel,
        out_shape=(out((ROWS, 3 * D), F32), out((ROWS, D), F32)),
        in_specs=[SMEM] + [VMEM] * QUARTERS,
        out_specs=(VMEM, VMEM),
        scratch_shapes=[pltpu.VMEM((QUARTERS, ROWS, D), F32)],
        compiler_params=BIG,
        cost_estimate=cost(2),
        name="finish_attention",
    )(where, *pieces)


def spread(piece, order):
    got = {frozenset(): piece}
    for step in (*order, "c"):
        for key in list(got):
            got[key | {step}] = send(got[key], step)
    return [got[frozenset(n for n, b in zip("yxc", key) if b)] for key in KEYS]


def on_block(hidden_in, w_qkv, w_out, w_up, w_down, gain_attn, shift_attn, gain_ffn, shift_ffn, grad_listed, positions, counts):
    seqs, length, width = hidden_in.shape
    tokens = seqs * length
    most = positions.shape[1]
    i, j = lax.axis_index("fsdp"), lax.axis_index("dp")
    where = jnp.stack([i // 2, i % 2, j // 2, j % 2, j]).astype(jnp.int32)
    ff = w_down.shape[0] * SHARDS
    attn_piece = lax.dynamic_slice_in_dim(jnp.concatenate([w_qkv, w_out], axis=1), j * D, D, axis=1)
    norms = jnp.concatenate([gain_attn, shift_attn, gain_ffn, shift_ffn, jnp.zeros((D - 4 * ROWS,), LOW)])
    attn_piece = jnp.concatenate([attn_piece, jnp.broadcast_to(norms, (EXTRA, D))], axis=0)
    line = jnp.stack([attn_piece] + [send(attn_piece, r) for r in (1, 2, 3)])
    x = hidden_in.reshape(tokens, width)
    line, x_flip = lax.optimization_barrier((line, x.T))
    halves = [
        spread(line[:, start : start + size], order)
        for (start, size), order in zip(HALVES, (("y", "x"), ("x", "y")))
    ]
    lines = [half[n] for n in range(len(KEYS)) for half in halves]
    ffn_piece = jnp.stack(
        [
            lax.dynamic_slice_in_dim(w_up, j * D, D, axis=1),
            lax.dynamic_slice_in_dim(w_up, ff + j * D, D, axis=1),
            lax.dynamic_slice_in_dim(w_down, j * ROWS, ROWS, axis=0),
        ]
    )
    w_ffn = lax.all_gather(ffn_piece, AXES, axis=0, tiled=False).reshape(SHARDS, QUARTERS, 3, ROWS, D)
    tails = jnp.stack([halves[1][n][:, 48, : 4 * ROWS] for n in range(2)])
    tails = jnp.where(i % 2 == 0, tails, tails[::-1])
    tails = jnp.roll(tails[:, ::-1], i // 2 + 1, axis=1)
    norms = tails.transpose(1, 0, 2).reshape(SHARDS, 4, ROWS).transpose(1, 0, 2).reshape(4, D).astype(F32)
    slopes = jnp.exp2(-8.0 * (jnp.arange(HEADS, dtype=F32) + 1.0) / HEADS)
    pos = positions.reshape(seqs * most, 1)
    live = jnp.arange(most, dtype=jnp.int32)[None, :] < counts[:, None]
    dy = jnp.where(live[:, :, None], grad_listed, jnp.zeros_like(grad_listed)).reshape(seqs * most, width)

    qkv, h1, att_m, h1_m, q_m, r1_m, w_attn = attention_forward(where, x, lines, norms, pos, slopes, seqs)
    h_all = jnp.stack(share_dp(h1_m))
    p_m = attention_again(q_m, qkv, pos, slopes, seqs)
    h1, h_all, p_m = lax.optimization_barrier((h1, h_all, p_m))
    layer_out, dr2, e2, small_ffn = ffn_forward(h1, w_ffn, norms, pos, dy, seqs)
    act, to_gate, to_up = ffn_again(where, h_all, w_ffn)
    other = after(send(e2, "x"), act)
    e_all = jnp.stack([e2, send(e2, "c"), other, send(other, "c")])
    dgate, dup, keep, away = ffn_back(where, e_all, to_gate, to_up, w_ffn)
    part = add(keep, send(away, "c"))
    part, part_away = part[0], part[1].astype(LOW)
    keep_d, away_d = weight_grad(where, act, e_all)
    came = send(part_away, "x")
    got_d = send(away_d, "y")
    keep_g, away_g = weight_grad(where, after(h_all, (away_d, part_away)), dgate)
    got_g = send(away_g, "y")
    keep_u, away_u = weight_grad(where, after(h_all, (away_g, came)), dup)
    got_u = send(away_u, "y")
    dr1, low, datt, small_attn = norm_back_call(dr2, part, after(came, away_u), r1_m, w_attn, norms)
    rhs0 = attention_back(datt, q_m, qkv, p_m, pos, seqs, 0)
    got_d, rhs0 = lax.optimization_barrier((got_d, rhs0))
    parts_d = line_parts(keep_d, got_d)
    line_d = line_send(parts_d)
    rhs1 = attention_back(after(datt, (rhs0, parts_d)), q_m, qkv, p_m, pos, seqs, 1)
    line_d, got_g, rhs1 = lax.optimization_barrier((line_d, got_g, rhs1))
    half = ROWS // 2
    parts_g = line_parts(keep_g[:, :half], got_g[:, :half])
    line_g = line_send(parts_g)
    keep0, keep1, away0, away1 = attention_grads(where, x_flip, rhs0, after(rhs1, parts_g), att_m, low, small_attn, small_ffn)
    away0, away1, line_g, got_u = lax.optimization_barrier((away0, away1, line_g, got_u))
    came0, came1 = send(away0, "c"), send(away1, "c")
    rest_g = line_parts(keep_g[:, half:], got_g[:, half:])
    parts_u = [jnp.concatenate(pair) for pair in zip(rest_g, line_parts(keep_u, got_u))]
    line_u = line_send(parts_u)
    g_down = send(line_add(keep_d, got_d, line_d), "down")
    away0, away1 = add(keep0[1], came0[1]).astype(LOW), add(keep1[1], came1[1]).astype(LOW)
    got0, got1 = send(away0, "x"), send(away1, "y")
    total0 = add(keep0[0], came0[0]) + got0.astype(F32)
    total1 = add(keep1[0], came1[0]) + got1.astype(F32)
    away0, away1 = total0[1].astype(LOW), total1[1].astype(LOW)
    got0, got1 = send(away0, "y"), send(away1, "x")
    g_down, line_u = after((g_down, line_u), (away0, away1))
    g_ffn = jnp.concatenate(
        [
            g_down,
            line_add(keep_g[:, :half], got_g[:, :half], line_g),
            line_add(keep_g[:, half:], got_g[:, half:], [value[:half] for value in line_u]),
            line_add(keep_u, got_u, [value[half:] for value in line_u]),
        ]
    ).reshape(3, ROWS, D)
    got0, got1 = after((got0, got1), g_ffn)
    total = jnp.concatenate([add(total0[0], got0), add(total1[0], got1)], axis=1)
    parts = [total[r].astype(LOW) for r in (1, 2, 3)]
    line_a = line_send(parts)
    other = send(g_ffn, "x")
    grad_in = input_grad(rhs0, after(rhs1, parts), w_attn, dr1, positions)
    line_a, other, grad_in = lax.optimization_barrier((line_a, other, grad_in))
    g_attn = total[0] + line_a[0].astype(F32) + line_a[1].astype(F32) + line_a[2].astype(F32)
    small = g_attn[ROWS : ROWS + 4, :ROWS]
    g_attn = g_attn[:ROWS].astype(LOW)
    shared = (g_ffn, send(g_ffn, "c"), other, send(other, "c"))
    grad_down, grad_up = finish_ffn(where, after(shared, g_attn))
    other = after(send(g_attn, "x"), grad_down)
    grad_qkv, grad_out = finish_attention(where, (g_attn, send(g_attn, "c"), other, send(other, "c")))
    return (
        layer_out.reshape(seqs, length, width),
        grad_in.reshape(seqs, length, width),
        grad_qkv,
        grad_out,
        grad_up,
        grad_down,
        small[0],
        small[1],
        small[2],
        small[3],
    )


FF = 3072


def slopes():
    return jnp.exp2(-8.0 * (jnp.arange(HEADS, dtype=F32) + 1.0) / HEADS)


def pick(onehot, rows):
    if rows.dtype == LOW:
        return jnp.einsum("svj,sjd->svd", onehot.astype(LOW), rows, preferred_element_type=F32).astype(LOW)
    return jnp.einsum("svj,sjd->svd", onehot, rows, precision=lax.Precision.HIGHEST)


def gather_weights(w_qkv, w_out, w_up, w_down):
    fsdp = lax.axis_size("fsdp")
    dp = lax.axis_size("dp")
    rows, width = w_out.shape
    if rows % (8 * dp):
        return (
            lax.all_gather(w_qkv, "fsdp", axis=0, tiled=True),
            lax.all_gather(w_out, "fsdp", axis=0, tiled=True),
            lax.all_gather(w_up, "fsdp", axis=0, tiled=True),
            lax.all_gather(w_down, "fsdp", axis=0, tiled=True),
        )
    mine = lax.axis_index("dp")
    part = rows // dp
    group = w_down.shape[0] // rows
    joined = jnp.concatenate([w_qkv, w_out, w_up], axis=1)
    joined = lax.dynamic_slice_in_dim(joined, mine * part, part, axis=0)
    down = lax.dynamic_slice_in_dim(w_down, mine * part * group, part * group, axis=0)
    down = jnp.concatenate([down[k * part : (k + 1) * part] for k in range(group)], axis=1)
    full = lax.all_gather(jnp.concatenate([joined, down], axis=1), AXES, axis=0, tiled=True)
    a, b = w_qkv.shape[1], w_qkv.shape[1] + w_out.shape[1]
    c = b + w_up.shape[1]
    full_down = full[:, c:].reshape(fsdp * dp, part, group, width)
    full_down = full_down.transpose(0, 2, 1, 3).reshape(fsdp * dp * part * group, width)
    return full[:, :a], full[:, a:b], full[:, b:c], full_down


def scatter_grads(g_qkv, g_out, g_up, g_down):
    fsdp = lax.axis_size("fsdp")
    dp = lax.axis_size("dp")
    width = g_out.shape[1]
    rows = g_out.shape[0] // fsdp
    if rows % (8 * dp):
        return tuple(
            lax.psum(lax.psum_scatter(g, "fsdp", scatter_dimension=0, tiled=True), "dp")
            for g in (g_qkv, g_out, g_up, g_down)
        )
    part = rows // dp
    group = g_down.shape[0] // g_out.shape[0]
    down = g_down.reshape(fsdp * dp, group, part, width).transpose(0, 2, 1, 3)
    down = down.reshape(fsdp * rows, group * width)
    joined = jnp.concatenate([g_qkv, g_out, g_up, down], axis=1).astype(LOW)
    mine = lax.psum_scatter(joined, AXES, scatter_dimension=0, tiled=True)
    full = lax.all_gather(mine, "dp", axis=0, tiled=True).astype(F32)
    a, b = g_qkv.shape[1], g_qkv.shape[1] + width
    c = b + g_up.shape[1]
    full_down = full[:, c:].reshape(dp, part, group, width).transpose(0, 2, 1, 3)
    return full[:, :a], full[:, a:b], full[:, b:c], full_down.reshape(rows * group, width)


def on_device(hidden_in, w_qkv, w_out, w_up, w_down, gain_attn, shift_attn, gain_ffn, shift_ffn, grad_listed, positions, counts):
    seqs, length, width = hidden_in.shape
    tokens = seqs * length
    most = positions.shape[1]
    norms = jnp.stack([gain_attn, shift_attn, gain_ffn, shift_ffn])
    norms = lax.all_gather(norms, "fsdp", axis=1, tiled=True).astype(F32)
    w_qkv, w_out, w_up, w_down = gather_weights(w_qkv, w_out, w_up, w_down)
    live = jnp.arange(most, dtype=jnp.int32)[None, :] < counts[:, None]
    onehot = (positions[:, :, None] == jnp.arange(length, dtype=jnp.int32)).astype(F32)
    rows_in = hidden_in.reshape(tokens, width)
    slope = slopes()
    scale = HEAD_DIM**-0.5
    qkv = mm(rows_in, w_qkv).astype(LOW)
    split = qkv.reshape(seqs, length, 3, HEADS, HEAD_DIM)
    q, k, v = split[:, :, 0], split[:, :, 1], split[:, :, 2]
    place = jnp.arange(length, dtype=F32)
    bias = -slope[:, None, None] * jnp.abs(place[:, None] - place[None, :])
    s = jnp.einsum("sqhc,skhc->shqk", q, k, preferred_element_type=F32) * scale + bias
    p = jax.nn.softmax(s, axis=-1).astype(LOW)
    att = jnp.einsum("shqk,skhc->sqhc", p, v, preferred_element_type=F32).astype(LOW)
    att = att.reshape(tokens, width)
    r1 = rows_in.astype(F32) + mm(att, w_out)
    unit1, _ = norm_parts(r1)
    h1 = unit1 * norms[0] + norms[1]
    h1_low = h1.astype(LOW)
    u = mm(h1_low, w_up)
    act = (jax.nn.gelu(u[:, :FF], approximate=False) * u[:, FF:]).astype(LOW)
    r2 = h1 + mm(act, w_down)
    unit2, _ = norm_parts(r2)
    layer_out = (unit2 * norms[2] + norms[3]).astype(LOW).reshape(seqs, length, width)
    def listed(a):
        return pick(onehot, a.reshape(seqs, length, -1)).reshape(seqs * most, -1)

    dy = jnp.where(live[:, :, None], grad_listed, 0).astype(F32).reshape(seqs * most, width)
    unit2_m, rstd2_m = norm_parts(listed(r2))
    g_gain_ffn = jnp.sum(dy * unit2_m, axis=0)
    g_shift_ffn = jnp.sum(dy, axis=0)
    dr2 = norm_back(dy, unit2_m, rstd2_m, norms[2])
    e2 = dr2.astype(LOW)
    h1_m = listed(h1_low)
    u_m = mm(h1_m, w_up)
    gate, up = u_m[:, :FF], u_m[:, FF:]
    cdf = 0.5 * (1.0 + lax.erf(gate * (0.5**0.5)))
    pdf = jnp.exp(-0.5 * gate * gate) * ((2.0 * jnp.pi) ** -0.5)
    gelu = gate * cdf
    act_m = (gelu * up).astype(LOW)
    g_down = jnp.einsum("nf,nd->fd", act_m, e2, preferred_element_type=F32)
    dact = jnp.einsum("nd,fd->nf", e2, w_down, preferred_element_type=F32)
    du = jnp.concatenate([dact * up * (cdf + gate * pdf), dact * gelu], axis=1).astype(LOW)
    g_up = jnp.einsum("nd,nf->df", h1_m, du, preferred_element_type=F32)
    dh1 = dr2 + jnp.einsum("nf,df->nd", du, w_up, preferred_element_type=F32)
    unit1_m, rstd1_m = norm_parts(listed(r1))
    g_gain_attn = jnp.sum(dh1 * unit1_m, axis=0)
    g_shift_attn = jnp.sum(dh1, axis=0)
    dr1 = norm_back(dh1, unit1_m, rstd1_m, norms[0])
    e1 = dr1.astype(LOW)
    g_out = jnp.einsum("nd,ne->de", listed(att), e1, preferred_element_type=F32)
    datt = jnp.einsum("ne,de->nd", e1, w_out, preferred_element_type=F32).astype(LOW)
    datt = datt.reshape(seqs, most, HEADS, HEAD_DIM)
    q_m = listed(qkv[:, :width]).reshape(seqs, most, HEADS, HEAD_DIM)
    away = jnp.abs(positions[:, :, None].astype(F32) - place[None, None, :])
    s_m = jnp.einsum("sqhc,skhc->shqk", q_m, k, preferred_element_type=F32) * scale
    p_m = jax.nn.softmax(s_m - slope[None, :, None, None] * away[:, None], axis=-1)
    dv = jnp.einsum("shqk,sqhc->skhc", p_m.astype(LOW), datt, preferred_element_type=F32)
    dp = jnp.einsum("sqhc,skhc->shqk", datt, v, preferred_element_type=F32)
    ds = (p_m * (dp - jnp.sum(dp * p_m, axis=-1, keepdims=True))).astype(LOW)
    dq_m = (jnp.einsum("shqk,skhc->sqhc", ds, k, preferred_element_type=F32) * scale).astype(LOW)
    dk = (jnp.einsum("shqk,sqhc->skhc", ds, q_m, preferred_element_type=F32) * scale).astype(LOW)
    put = (onehot * live[:, :, None]).astype(LOW)
    dq = jnp.einsum("svj,svd->sjd", put, dq_m.reshape(seqs, most, width), preferred_element_type=F32)
    dqkv = jnp.concatenate(
        [dq.astype(LOW).reshape(tokens, width), dk.reshape(tokens, width), dv.astype(LOW).reshape(tokens, width)], axis=1
    )
    g_qkv = jnp.einsum("nd,ne->de", rows_in, dqkv, preferred_element_type=F32)
    dr1_all = jnp.einsum("svj,svd->sjd", onehot * live[:, :, None], dr1.reshape(seqs, most, width), precision=lax.Precision.HIGHEST)
    grad_in = dr1_all.reshape(tokens, width) + jnp.einsum("ne,de->nd", dqkv, w_qkv, preferred_element_type=F32)
    owned = scatter_grads(g_qkv, g_out, g_up, g_down)
    small = lax.psum(jnp.stack([g_gain_attn, g_shift_attn, g_gain_ffn, g_shift_ffn]), AXES)
    share = width // lax.axis_size("fsdp")
    small = lax.dynamic_slice_in_dim(small, lax.axis_index("fsdp") * share, share, axis=1)
    return (
        layer_out,
        grad_in.reshape(seqs, length, width),
        *owned,
        small[0],
        small[1],
        small[2],
        small[3],
    )


def solution(mesh):
    rows3 = P(("fsdp", "dp"), None, None)
    rows2 = P("fsdp", None)
    rows1 = P("fsdp")
    shape = dict(mesh.shape)
    step = on_block if shape == {"fsdp": SHARDS, "dp": QUARTERS} else on_device
    return jax.shard_map(
        step,
        mesh=mesh,
        in_specs=(rows3, rows2, rows2, rows2, rows2, rows1, rows1, rows1, rows1, rows3, P(("fsdp", "dp"), None), P(("fsdp", "dp"))),
        out_specs=(rows3, rows3, rows2, rows2, rows2, rows2, rows1, rows1, rows1, rows1),
        check_vma=False,
    )
```

```python
import functools

import jax
import jax.numpy as jnp
from jax import lax
from jax.experimental import pallas as pl
from jax.experimental.pallas import tpu as pltpu
from jax.sharding import PartitionSpec as P

HEADS = 12
HEAD_DIM = 64
EPS = 1e-12
F32 = jnp.float32
LOW = jnp.bfloat16
AXES = ("fsdp", "dp")
D = 768
ROWS = 96
LINE = 4
SHARDS = D // ROWS
QUARTERS = 4
EXACT = lax.Precision.HIGHEST
SCALE = HEAD_DIM**-0.5
VMEM = pl.BlockSpec(memory_space=pltpu.VMEM)
SMEM = pl.BlockSpec(memory_space=pltpu.SMEM)
BIG = pltpu.CompilerParams(vmem_limit_bytes=60 * 1024 * 1024)


def out(shape, dtype):
    return jax.ShapeDtypeStruct(shape, dtype)


def cost(us):
    return pl.CostEstimate(flops=0, bytes_accessed=int(us * 3.0e6), transcendentals=0)


def mm(a, b):
    return jnp.dot(a, b, preferred_element_type=F32)


def mm_nt(a, b):
    return lax.dot_general(a, b, (((1,), (1,)), ((), ())), preferred_element_type=F32)


def mm_tn(a, b):
    return lax.dot_general(a, b, (((0,), (0,)), ((), ())), preferred_element_type=F32)


def norm_parts(value):
    center = value - jnp.mean(value, axis=-1, keepdims=True)
    rstd = lax.rsqrt(jnp.mean(center * center, axis=-1, keepdims=True) + EPS)
    return center * rstd, rstd


def norm_back(grad, unit, rstd, gain):
    scaled = grad * gain
    return rstd * (
        scaled
        - jnp.mean(scaled, axis=-1, keepdims=True)
        - unit * jnp.mean(scaled * unit, axis=-1, keepdims=True)
    )


def onehot(pos_ref, seq, most, length):
    spots = lax.broadcasted_iota(jnp.int32, (most, length), 1)
    return spots == pos_ref[pl.ds(seq * most, most), :]


def gelu_parts(gate):
    cdf = 0.5 * (1.0 + lax.erf(gate * (0.5**0.5)))
    pdf = jnp.exp(-0.5 * gate * gate) * ((2.0 * jnp.pi) ** -0.5)
    return gate * cdf, cdf + gate * pdf


def slope_of(head):
    return 2.0 ** (-8.0 * (head + 1.0) / HEADS)


def block(ref, *index):
    value = ref[index] if index else ref[...]
    return value.reshape(-1, value.shape[-1])


EXTRA = 8
TAIL = 8
HALVES = ((0, 48), (48, 56))
KEYS = [(ry, rx, rc) for rc in (0, 1) for rx in (0, 1) for ry in (0, 1)]


def attention_kernel(seqs, most, where_ref, slope_ref, x_ref, norm_ref, pos_ref, *rest):
    lines, rest = rest[:16], rest[16:]
    qkv_ref, h1_ref, att_m_ref, h1_m_ref, q_m_ref, r1_m_ref, w_ref, att_ref, r1_ref, sem = rest
    z, y, c_x = where_ref[0], where_ref[1], where_ref[4]
    copies = []
    for n, (ry, rx, rc) in enumerate(KEYS):
        j = jnp.bitwise_xor(c_x, 2 * rx + rc)
        for r in range(LINE):
            shard = 2 * lax.rem(z + LINE - r, LINE) + jnp.bitwise_xor(y, ry)
            for half, (start, size) in enumerate(HALVES):
                size = min(size, ROWS - start)
                copies.append(
                    pltpu.make_async_copy(
                        lines[2 * n + half].at[r, pl.ds(0, size)], w_ref.at[shard, j, pl.ds(start, size)], sem
                    )
                )
    for copy in copies:
        copy.start()
    for copy in copies:
        copy.wait()
    length = x_ref.shape[0] // seqs
    step = 256

    @pl.loop(0, 3 * D // step)
    def _(n):
        j = n // (D // step)
        lane = pl.multiple_of((n - j * (D // step)) * step, step)
        w = w_ref[:, j, :, pl.ds(lane, step)].reshape(D, step)
        qkv_ref[:, pl.ds(pl.multiple_of(n * step, step), step)] = mm(x_ref[...], w).astype(LOW)

    first = lax.broadcasted_iota(jnp.int32, (length, 128), 1) < HEAD_DIM
    row = lax.broadcasted_iota(jnp.int32, (length, length), 0)
    col = lax.broadcasted_iota(jnp.int32, (length, length), 1)
    away = jnp.abs(row - col).astype(F32)

    @pl.loop(0, HEADS // 2)
    def _(t):
        lane = pl.multiple_of(t * 128, 128)
        bias = jnp.concatenate([slope_ref[2 * t] * away, slope_ref[2 * t + 1] * away], axis=0)
        for s in range(seqs):
            rows = slice(s * length, (s + 1) * length)
            q = qkv_ref[rows, pl.ds(lane, 128)]
            k = qkv_ref[rows, pl.ds(D + lane, 128)]
            v = qkv_ref[rows, pl.ds(2 * D + lane, 128)]
            zero = jnp.zeros_like(q)
            both = jnp.concatenate([jnp.where(first, q, zero), jnp.where(first, zero, q)], axis=0)
            score = mm_nt(both, k) * SCALE - bias
            e = jnp.exp(score - jnp.max(score, axis=-1, keepdims=True))
            p = (e * (1.0 / jnp.sum(e, axis=-1, keepdims=True))).astype(LOW)
            mixed = mm(p, v)
            att_ref[rows, pl.ds(lane, 128)] = jnp.where(first, mixed[:length], mixed[length:]).astype(LOW)

    @pl.loop(0, D // step)
    def _(n):
        lane = pl.multiple_of(n * step, step)
        w = w_ref[:, 3, :, pl.ds(lane, step)].reshape(D, step)
        r1_ref[:, pl.ds(lane, step)] = x_ref[:, pl.ds(lane, step)].astype(F32) + mm(att_ref[...], w)

    for s in range(seqs):
        rows = slice(s * length, (s + 1) * length)
        listed = slice(s * most, (s + 1) * most)
        unit, _ = norm_parts(r1_ref[rows, :])
        h1 = unit * norm_ref[0:1, :] + norm_ref[1:2, :]
        h1_ref[rows, :] = h1
        hot = onehot(pos_ref, s, most, length)
        hot_low = hot.astype(LOW)
        r1_m_ref[listed, :] = jnp.dot(hot.astype(F32), r1_ref[rows, :], precision=EXACT, preferred_element_type=F32)
        h1_m_ref[listed, :] = mm(hot_low, h1.astype(LOW)).astype(LOW)
        att_m_ref[listed, :] = mm(hot_low, att_ref[rows, :]).astype(LOW)
        q_m_ref[listed, :] = mm(hot_low, qkv_ref[rows, 0:D]).astype(LOW)


def attention_forward(where, x, lines, norms, pos, slopes, seqs):
    tokens = x.shape[0]
    listed = pos.shape[0]
    return pl.pallas_call(
        functools.partial(attention_kernel, seqs, listed // seqs),
        out_shape=(
            out((tokens, 3 * D), LOW),
            out((tokens, D), F32),
            out((listed, D), LOW),
            out((listed, D), LOW),
            out((listed, D), LOW),
            out((listed, D), F32),
            out((SHARDS, QUARTERS, ROWS, D), LOW),
        ),
        in_specs=[SMEM, SMEM, VMEM, VMEM, VMEM] + [pl.BlockSpec(memory_space=pl.ANY)] * 16,
        out_specs=(VMEM,) * 7,
        scratch_shapes=[pltpu.VMEM((tokens, D), LOW), pltpu.VMEM((tokens, D), F32), pltpu.SemaphoreType.DMA],
        compiler_params=BIG,
        cost_estimate=cost(20),
        name="attention_forward",
    )(where, slopes, x, norms, pos, *lines)


def ffn_kernel(seqs, most, h1_ref, gate_ref, up_ref, down_ref, norm_ref, pos_ref, dy_ref, y_ref, dr2_ref, e2_ref, small_ref, low_ref, act_ref, acc_ref):
    j = pl.program_id(0)
    tokens = h1_ref.shape[0]
    length = tokens // seqs
    step = 256

    @pl.when(j == 0)
    def _():
        low_ref[...] = h1_ref[...].astype(LOW)
        acc_ref[...] = h1_ref[...]

    def products(n):
        lanes = slice(n * step, (n + 1) * step)
        return mm(low_ref[...], gate_ref[:, :, lanes].reshape(D, step)), mm(low_ref[...], up_ref[:, :, lanes].reshape(D, step))

    gate, up = products(0)
    for n in range(D // step):
        following = products(n + 1) if (n + 1) * step < D else (None, None)
        cdf = 0.5 * (1.0 + lax.erf(gate * (0.5**0.5)))
        act_ref[:, n * step : (n + 1) * step] = (gate * cdf * up).astype(LOW)
        gate, up = following
    for n in range(D // step):
        lanes = slice(n * step, (n + 1) * step)
        acc_ref[:, lanes] += mm(act_ref[...], down_ref[:, :, :, lanes].reshape(D, step))

    @pl.when(j == QUARTERS - 1)
    def _():
        gain = norm_ref[2:3, :]
        small = [jnp.zeros((1, D), F32)] * 2
        for s in range(seqs):
            rows = slice(s * length, (s + 1) * length)
            listed = slice(s * most, (s + 1) * most)
            unit, _ = norm_parts(acc_ref[rows, :])
            y_ref[rows, :] = (unit * gain + norm_ref[3:4, :]).astype(LOW)
            hot = onehot(pos_ref, s, most, length).astype(F32)
            picked = jnp.dot(hot, acc_ref[rows, :], precision=EXACT, preferred_element_type=F32)
            unit_m, rstd_m = norm_parts(picked)
            dy = dy_ref[listed, :].astype(F32)
            small = [small[0] + jnp.sum(dy * unit_m, axis=0, keepdims=True), small[1] + jnp.sum(dy, axis=0, keepdims=True)]
            dr2 = norm_back(dy, unit_m, rstd_m, gain)
            dr2_ref[listed, :] = dr2
            e2_ref[listed, :] = dr2.astype(LOW)
        small_ref[...] = jnp.concatenate(small, axis=0)


def ffn_forward(h1, w_ffn, norms, pos, dy, seqs):
    tokens = h1.shape[0]
    listed = pos.shape[0]
    whole = lambda shape: pl.BlockSpec(shape, lambda j: (0,) * len(shape), pipeline_mode=pl.Buffered(1))
    return pl.pallas_call(
        functools.partial(ffn_kernel, seqs, listed // seqs),
        out_shape=(out((tokens, D), LOW), out((listed, D), F32), out((listed, D), LOW), out((2, D), F32)),
        grid=(QUARTERS,),
        in_specs=[
            whole((tokens, D)),
            pl.BlockSpec((SHARDS, None, None, ROWS, D), lambda j: (0, j, 0, 0, 0)),
            pl.BlockSpec((SHARDS, None, None, ROWS, D), lambda j: (0, j, 1, 0, 0)),
            pl.BlockSpec((SHARDS // QUARTERS, QUARTERS, None, ROWS, D), lambda j: (j, 0, 2, 0, 0)),
            whole(norms.shape),
            whole(pos.shape),
            whole(dy.shape),
        ],
        out_specs=(
            pl.BlockSpec((tokens, D), lambda j: (0, 0)),
            pl.BlockSpec((listed, D), lambda j: (0, 0)),
            pl.BlockSpec((listed, D), lambda j: (0, 0)),
            pl.BlockSpec((2, D), lambda j: (0, 0)),
        ),
        scratch_shapes=[pltpu.VMEM((tokens, D), LOW), pltpu.VMEM((tokens, D), LOW), pltpu.VMEM((tokens, D), F32)],
        compiler_params=BIG,
        cost_estimate=cost(16),
        name="ffn_forward",
    )(h1, w_ffn, w_ffn, w_ffn, norms, pos, dy)


def ffn_again_kernel(where_ref, h_ref, gate_ref, up_ref, act_ref, to_gate_ref, to_up_ref):
    step = 256

    rows = block(h_ref)

    def products(n):
        lanes = slice(n * step, (n + 1) * step)
        return mm(rows, gate_ref[:, :, lanes].reshape(D, step)), mm(rows, up_ref[:, :, lanes].reshape(D, step))

    gate, up = products(0)
    for n in range(D // step):
        following = products(n + 1) if (n + 1) * step < D else (None, None)
        lanes = slice(n * step, (n + 1) * step)
        value, slope = gelu_parts(gate)
        act_ref[:, lanes] = (value * up).astype(LOW)
        to_gate_ref[:, lanes] = slope * up
        to_up_ref[:, lanes] = value
        gate, up = following


def quarter_specs(which):
    specs = {
        "gate": pl.BlockSpec((SHARDS, None, None, ROWS, D), lambda g, w: (0, w[4], 0, 0, 0)),
        "up": pl.BlockSpec((SHARDS, None, None, ROWS, D), lambda g, w: (0, w[4], 1, 0, 0)),
        "down": pl.BlockSpec((SHARDS // QUARTERS, QUARTERS, None, ROWS, D), lambda g, w: (w[4], 0, 2, 0, 0)),
    }
    return [specs[name] for name in which]


def at_once(shape):
    return pl.BlockSpec(shape, lambda g, w: (0,) * len(shape))


def ffn_again(where, h_all, w_ffn):
    rows = h_all.shape[0] * h_all.shape[1]
    return pl.pallas_call(
        ffn_again_kernel,
        out_shape=(out((rows, D), LOW), out((rows, D), F32), out((rows, D), F32)),
        grid_spec=pltpu.PrefetchScalarGridSpec(
            num_scalar_prefetch=1,
            grid=(1,),
            in_specs=[at_once(h_all.shape), *quarter_specs(["gate", "up"])],
            out_specs=(at_once((rows, D)),) * 3,
        ),
        compiler_params=BIG,
        cost_estimate=cost(6),
        name="ffn_again",
    )(where, h_all, w_ffn, w_ffn)


def ffn_back_kernel(where_ref, e_ref, to_gate_ref, to_up_ref, gate_ref, up_ref, down_ref, dgate_ref, dup_ref, keep_ref, send_ref):
    listed = e_ref.shape[1]
    half = QUARTERS // 2
    for n in range(SHARDS // QUARTERS):
        lanes = slice(n * QUARTERS * ROWS, (n + 1) * QUARTERS * ROWS)
        dact = mm_nt(block(e_ref), block(down_ref, n))
        dgate_ref[:, lanes] = (dact * to_gate_ref[:, lanes]).astype(LOW)
        dup_ref[:, lanes] = (dact * to_up_ref[:, lanes]).astype(LOW)
    for n in range(2):
        shards = slice(n * SHARDS // 2, (n + 1) * SHARDS // 2)
        lanes = slice(n * D // 2, (n + 1) * D // 2)
        part = mm_nt(dgate_ref[...], block(gate_ref, shards)) + mm_nt(dup_ref[...], block(up_ref, shards))
        for r in range(half):
            keep_ref[r, :, lanes] = part[2 * r * listed : (2 * r + 1) * listed]
            send_ref[r, :, lanes] = part[(2 * r + 1) * listed : (2 * r + 2) * listed].astype(LOW)


def ffn_back(where, e_all, to_gate, to_up, w_ffn):
    count, listed, _ = e_all.shape
    rows = count * listed
    return pl.pallas_call(
        ffn_back_kernel,
        out_shape=(out((rows, D), LOW), out((rows, D), LOW), out((count // 2, listed, D), F32), out((count // 2, listed, D), LOW)),
        grid_spec=pltpu.PrefetchScalarGridSpec(
            num_scalar_prefetch=1,
            grid=(1,),
            in_specs=[at_once(e_all.shape), at_once((rows, D)), at_once((rows, D)), *quarter_specs(["gate", "up", "down"])],
            out_specs=(at_once((rows, D)), at_once((rows, D)), at_once((count // 2, listed, D)), at_once((count // 2, listed, D))),
        ),
        compiler_params=BIG,
        cost_estimate=cost(7),
        name="ffn_back",
    )(where, e_all, to_gate, to_up, w_ffn, w_ffn, w_ffn)


def weight_grad_kernel(where_ref, a_ref, b_ref, keep_ref, send_ref, full_ref):
    z, y = where_ref[0], where_ref[1]
    b = block(b_ref)
    step = 256

    for n in range(D // step):
        rows = slice(n * step, (n + 1) * step)
        full_ref[rows, :] = mm_tn(block(a_ref, *([slice(None)] * (len(a_ref.shape) - 1)), rows), b)

    for r in range(LINE):
        base = 2 * lax.rem(z + r, LINE)
        for other, ref in ((0, keep_ref), (1, send_ref)):
            start = (base + (y if other == 0 else 1 - y)) * ROWS
            ref[r] = full_ref[pl.ds(pl.multiple_of(start, 8), ROWS), :].astype(LOW)


def weight_grad(where, a, b):
    shape = (LINE, ROWS, D)
    rows = a.size // D
    return pl.pallas_call(
        weight_grad_kernel,
        out_shape=(out(shape, LOW), out(shape, LOW)),
        in_specs=[SMEM, VMEM, VMEM],
        out_specs=(VMEM, VMEM),
        scratch_shapes=[pltpu.VMEM((D, D), F32)],
        compiler_params=BIG,
        cost_estimate=cost(4),
        name="weight_grad",
    )(where, a, b)


def norm_back_kernel(dr2_ref, part_ref, came_ref, r1_ref, w_ref, norm_ref, dr1_ref, low_ref, datt_ref, small_ref):
    dh1 = dr2_ref[...] + part_ref[...] + came_ref[...].astype(F32)
    unit, rstd = norm_parts(r1_ref[...])
    small_ref[0:1, :] = jnp.sum(dh1 * unit, axis=0, keepdims=True)
    small_ref[1:2, :] = jnp.sum(dh1, axis=0, keepdims=True)
    dr1 = norm_back(dh1, unit, rstd, norm_ref[0:1, :])
    dr1_ref[...] = dr1
    low = dr1.astype(LOW)
    low_ref[...] = low
    for n in range(2):
        lanes = slice(n * D // 2, (n + 1) * D // 2)
        datt_ref[:, lanes] = mm_nt(low, block(w_ref, slice(n * SHARDS // 2, (n + 1) * SHARDS // 2))).astype(LOW)


def norm_back_call(dr2, part, came, r1_m, w_attn, norms):
    listed = dr2.shape[0]
    same = lambda shape: pl.BlockSpec(shape, lambda g: (0,) * len(shape))
    rows = same((listed, D))
    return pl.pallas_call(
        norm_back_kernel,
        out_shape=(out((listed, D), F32), out((listed, D), LOW), out((listed, D), LOW), out((2, D), F32)),
        grid=(1,),
        in_specs=[rows, rows, rows, rows, pl.BlockSpec((SHARDS, None, ROWS, D), lambda g: (0, 3, 0, 0)), same((4, D))],
        out_specs=(rows, rows, rows, same((2, D))),
        compiler_params=BIG,
        cost_estimate=cost(4),
        name="norm_back",
    )(dr2, part, came, r1_m, w_attn, norms)


def both_heads(value):
    first = lax.broadcasted_iota(jnp.int32, value.shape, 1) < HEAD_DIM
    zero = jnp.zeros_like(value)
    return jnp.concatenate([jnp.where(first, value, zero), jnp.where(first, zero, value)], axis=0)


def attention_again_kernel(seqs, slope_ref, q_ref, k_ref, pos_ref, p_ref):
    length, most = k_ref.shape[0] // seqs, q_ref.shape[0] // seqs
    spots = lax.broadcasted_iota(jnp.int32, (most, length), 1)

    @pl.loop(0, HEADS // 2)
    def _(t):
        lane = pl.multiple_of(t * 128, 128)
        for s in range(seqs):
            rows = slice(s * length, (s + 1) * length)
            mine = slice(s * most, (s + 1) * most)
            away = jnp.abs(pos_ref[mine, :] - spots).astype(F32)
            bias = jnp.concatenate([slope_ref[2 * t] * away, slope_ref[2 * t + 1] * away], axis=0)
            score = mm_nt(both_heads(q_ref[mine, pl.ds(lane, 128)]), k_ref[rows, pl.ds(lane, 128)]) * SCALE - bias
            e = jnp.exp(score - jnp.max(score, axis=-1, keepdims=True))
            p = e * (1.0 / jnp.sum(e, axis=-1, keepdims=True))
            p_ref[2 * t, mine, :] = p[:most]
            p_ref[2 * t + 1, mine, :] = p[most:]


def attention_again(q_m, qkv, pos, slopes, seqs):
    tokens, listed = qkv.shape[0], pos.shape[0]
    shape = (HEADS, listed, tokens // seqs)
    return pl.pallas_call(
        functools.partial(attention_again_kernel, seqs),
        out_shape=out(shape, F32),
        grid=(1,),
        in_specs=[SMEM, pl.BlockSpec((listed, D), lambda g: (0, 0)), pl.BlockSpec((tokens, D), lambda g: (0, 1)), pl.BlockSpec((listed, 1), lambda g: (0, 0))],
        out_specs=pl.BlockSpec(shape, lambda g: (0, 0, 0)),
        compiler_params=BIG,
        cost_estimate=cost(8),
        name="attention_again",
    )(slopes, q_m, qkv, pos)


def attention_back_kernel(seqs, datt_ref, q_ref, k_ref, v_ref, p_ref, pos_ref, rhs_ref, hot_ref):
    length, most = k_ref.shape[0] // seqs, q_ref.shape[0] // seqs
    first_m = lax.broadcasted_iota(jnp.int32, (most, 128), 1) < HEAD_DIM
    hot_ref[...] = (lax.broadcasted_iota(jnp.int32, hot_ref.shape, 1) == pos_ref[...]).astype(LOW)

    @pl.loop(0, HEADS // 4)
    def _(step):
        for n, s in ((n, s) for n in (0, 1) for s in range(seqs)):
            t = 2 * step + n
            lane = pl.multiple_of(t * 128, 128)
            rows = slice(s * length, (s + 1) * length)
            mine = slice(s * most, (s + 1) * most)
            q = both_heads(q_ref[mine, pl.ds(lane, 128)])
            da = both_heads(datt_ref[mine, pl.ds(lane, 128)])
            k = k_ref[rows, pl.ds(lane, 128)]
            v = v_ref[rows, pl.ds(lane, 128)]
            p = jnp.concatenate([p_ref[2 * t, mine, :], p_ref[2 * t + 1, mine, :]], axis=0)
            dp = mm_nt(da, v)
            ds = (p * (dp - jnp.sum(dp * p, axis=-1, keepdims=True))).astype(LOW)
            dq = mm(ds, k)
            dq = (jnp.where(first_m, dq[:most], dq[most:]) * SCALE).astype(LOW)
            rhs_ref[rows, pl.ds(lane, 128)] = mm_tn(hot_ref[mine, :], dq).astype(LOW)
            rhs_ref[rows, pl.ds(D + lane, 128)] = (mm_tn(ds, q) * SCALE).astype(LOW)
            rhs_ref[rows, pl.ds(2 * D + lane, 128)] = mm_tn(p.astype(LOW), da).astype(LOW)


def attention_back(datt, q_m, qkv, p_m, pos, seqs):
    tokens, listed = qkv.shape[0], pos.shape[0]
    length = tokens // seqs
    whole = lambda shape, lane=0: pl.BlockSpec(shape, lambda g: (0, lane))
    return pl.pallas_call(
        functools.partial(attention_back_kernel, seqs),
        out_shape=out((tokens, 3 * D), LOW),
        grid=(1,),
        in_specs=[
            whole((listed, D)),
            whole((listed, D)),
            whole((tokens, D), 1),
            whole((tokens, D), 2),
            pl.BlockSpec((HEADS, listed, length), lambda g: (0, 0, 0)),
            whole((listed, 1)),
        ],
        out_specs=pl.BlockSpec((tokens, 3 * D), lambda g: (0, 0)),
        scratch_shapes=[pltpu.VMEM((listed, length), LOW)],
        compiler_params=BIG,
        cost_estimate=cost(12),
        name="attention_back",
    )(datt, q_m, qkv, qkv, p_m, pos)


def attention_grads_kernel(where_ref, flip_ref, rhs_ref, att_ref, low_ref, small_attn_ref, small_ffn_ref, keep0_ref, keep1_ref, away0_ref, away1_ref, full_ref, tail_ref):
    z, y, mine = where_ref[0], where_ref[1], where_ref[4]
    half = ROWS // 2
    step = 256
    tail_ref[...] = jnp.zeros(tail_ref.shape, LOW)
    small = jnp.concatenate([small_attn_ref[...], small_ffn_ref[...]], axis=0).astype(LOW)
    for n in range(SHARDS):
        tail_ref[n, 0:4, 0:ROWS] = small[:, n * ROWS : (n + 1) * ROWS]
    for rc in (1, 0):
        cut0_ref, cut1_ref = (keep0_ref, keep1_ref) if rc == 0 else (away0_ref, away1_ref)
        for rx in (0, 1):
            j = jnp.bitwise_xor(mine, 2 * rx + rc)

            @pl.when(j == 3)
            def _():
                for n in range(D // step):
                    rows = slice(n * step, (n + 1) * step)
                    full_ref[rows, :] = mm_tn(att_ref[:, rows], low_ref[...])

            @pl.when(j != 3)
            def _():
                @pl.loop(0, D // step)
                def _(n):
                    lane = pl.multiple_of(n * step, step)
                    cols = pl.ds(pl.multiple_of(j * D + n * step, step), step)
                    full_ref[:, pl.ds(lane, step)] = mm(flip_ref[...], rhs_ref[:, cols])

            for rz in range(LINE):
                base = 2 * lax.rem(z + rz, LINE)
                for ry in (0, 1):
                    shard = base + (y if ry == 0 else 1 - y)
                    start = shard * ROWS
                    cut0_ref[rx, ry, rz] = full_ref[pl.ds(pl.multiple_of(start, 8), half), :].astype(LOW)
                    cut1_ref[ry, rx, rz, 0:half] = full_ref[pl.ds(pl.multiple_of(start + half, 8), half), :].astype(LOW)
                    cut1_ref[ry, rx, rz, half:] = tail_ref[shard]


def attention_grads(where, x_flip, rhs, att_m, low, small_attn, small_ffn):
    half = ROWS // 2
    return pl.pallas_call(
        attention_grads_kernel,
        out_shape=(out((2, 2, LINE, half, D), LOW), out((2, 2, LINE, half + TAIL, D), LOW)) * 2,
        in_specs=[SMEM] + [VMEM] * 6,
        out_specs=(VMEM,) * 4,
        scratch_shapes=[pltpu.VMEM((D, D), F32), pltpu.VMEM((SHARDS, TAIL, D), LOW)],
        compiler_params=BIG,
        cost_estimate=cost(10),
        name="attention_grads",
    )(where, x_flip, rhs, att_m, low, small_attn, small_ffn)


def input_grad_kernel(seqs, rhs_ref, w_ref, dr1_ref, pos_ref, out_ref):
    length = out_ref.shape[0] // seqs
    most = dr1_ref.shape[0] // seqs
    for n in range(2):
        lanes = slice(n * D // 2, (n + 1) * D // 2)
        shards = slice(n * SHARDS // 2, (n + 1) * SHARDS // 2)
        total = mm_nt(rhs_ref[:, 0:D], block(w_ref, shards, 0))
        total += mm_nt(rhs_ref[:, D : 2 * D], block(w_ref, shards, 1))
        total += mm_nt(rhs_ref[:, 2 * D : 3 * D], block(w_ref, shards, 2))
        for s in range(seqs):
            rows = slice(s * length, (s + 1) * length)
            hot = (lax.broadcasted_iota(jnp.int32, (length, most), 0) == pos_ref[s : s + 1, :]).astype(F32)
            spread = jnp.dot(hot, dr1_ref[s * most : (s + 1) * most, lanes], precision=EXACT, preferred_element_type=F32)
            out_ref[rows, lanes] = total[rows] + spread


def input_grad(rhs, w_attn, dr1, positions):
    tokens = rhs.shape[0]
    return pl.pallas_call(
        functools.partial(input_grad_kernel, positions.shape[0]),
        out_shape=out((tokens, D), F32),
        in_specs=[VMEM] * 4,
        out_specs=VMEM,
        compiler_params=BIG,
        cost_estimate=cost(8),
        name="input_grad",
    )(rhs, w_attn, dr1, positions)


def place(z, y, x, c):
    return (2 * z + y) * 4 + 2 * x + c


def grid_perm(move):
    return [
        (place(z, y, x, c), place(*move(z, y, x, c)))
        for z in range(4)
        for y in range(2)
        for x in range(2)
        for c in range(2)
    ]


MOVES = {
    "x": grid_perm(lambda z, y, x, c: (z, y, 1 - x, c)),
    "y": grid_perm(lambda z, y, x, c: (z, 1 - y, x, c)),
    "c": grid_perm(lambda z, y, x, c: (z, y, x, 1 - c)),
    1: grid_perm(lambda z, y, x, c: ((z + 1) % 4, y, x, c)),
    2: grid_perm(lambda z, y, x, c: ((z + 2) % 4, y, x, c)),
    3: grid_perm(lambda z, y, x, c: ((z + 3) % 4, y, x, c)),
    "down": [(m * 4 + q, (2 * q + m // 4) * 4 + m % 4) for m in range(8) for q in range(4)],
}


def send(value, move):
    return lax.ppermute(value, AXES, MOVES[move])


def share_dp(value):
    other = send(value, "x")
    return value, send(value, "c"), other, send(other, "c")


def after(value, *earlier):
    return lax.optimization_barrier((value, *earlier))[0]


def add(kept, got):
    return kept.astype(F32) + got.astype(F32)


def line_parts(keep, got):
    return [add(keep[r], got[r]).astype(LOW) for r in (1, 2, 3)]


def line_send(parts):
    return [send(value, r) for r, value in zip((1, 2, 3), parts)]


def line_add(keep, got, came):
    return (add(keep[0], got[0]) + came[0].astype(F32) + came[1].astype(F32) + came[2].astype(F32)).astype(LOW)


def finish_ffn_kernel(where_ref, *rest):
    pieces, (down_ref, up_ref) = rest[:QUARTERS], rest[QUARTERS:]
    mine = where_ref[4]
    for n, ref in enumerate(pieces):
        j = jnp.bitwise_xor(mine, n)
        down_ref[pl.ds(pl.multiple_of(j * ROWS, 8), ROWS), :] = ref[0].astype(F32)
        for half in (0, 1):
            up_ref[:, pl.ds(pl.multiple_of((half * QUARTERS + j) * D, D), D)] = ref[1 + half].astype(F32)


def finish_attention_kernel(where_ref, *rest):
    pieces, (qkv_ref, out_ref, held_ref) = rest[:QUARTERS], rest[QUARTERS:]
    mine = where_ref[4]
    for n, ref in enumerate(pieces):
        held_ref[jnp.bitwise_xor(mine, n)] = ref[...].astype(F32)
    for j in range(3):
        qkv_ref[:, j * D : (j + 1) * D] = held_ref[j]
    out_ref[...] = held_ref[3]


def finish_ffn(where, pieces):
    return pl.pallas_call(
        finish_ffn_kernel,
        out_shape=(out((QUARTERS * ROWS, D), F32), out((ROWS, 2 * QUARTERS * D), F32)),
        in_specs=[SMEM] + [VMEM] * QUARTERS,
        out_specs=(VMEM, VMEM),
        compiler_params=BIG,
        cost_estimate=cost(4),
        name="finish_ffn",
    )(where, *pieces)


def finish_attention(where, pieces):
    return pl.pallas_call(
        finish_attention_kernel,
        out_shape=(out((ROWS, 3 * D), F32), out((ROWS, D), F32)),
        in_specs=[SMEM] + [VMEM] * QUARTERS,
        out_specs=(VMEM, VMEM),
        scratch_shapes=[pltpu.VMEM((QUARTERS, ROWS, D), F32)],
        compiler_params=BIG,
        cost_estimate=cost(2),
        name="finish_attention",
    )(where, *pieces)


def spread(piece, order):
    got = {frozenset(): piece}
    for step in (*order, "c"):
        for key in list(got):
            got[key | {step}] = send(got[key], step)
    return [got[frozenset(n for n, b in zip("yxc", key) if b)] for key in KEYS]


def on_block(hidden_in, w_qkv, w_out, w_up, w_down, gain_attn, shift_attn, gain_ffn, shift_ffn, grad_listed, positions, counts):
    seqs, length, width = hidden_in.shape
    tokens = seqs * length
    most = positions.shape[1]
    i, j = lax.axis_index("fsdp"), lax.axis_index("dp")
    where = jnp.stack([i // 2, i % 2, j // 2, j % 2, j]).astype(jnp.int32)
    ff = w_down.shape[0] * SHARDS
    attn_piece = lax.dynamic_slice_in_dim(jnp.concatenate([w_qkv, w_out], axis=1), j * D, D, axis=1)
    norms = jnp.concatenate([gain_attn, shift_attn, gain_ffn, shift_ffn, jnp.zeros((D - 4 * ROWS,), LOW)])
    attn_piece = jnp.concatenate([attn_piece, jnp.broadcast_to(norms, (EXTRA, D))], axis=0)
    line = jnp.stack([attn_piece] + [send(attn_piece, r) for r in (1, 2, 3)])
    x = hidden_in.reshape(tokens, width)
    line, x_flip = lax.optimization_barrier((line, x.T))
    halves = [
        spread(line[:, start : start + size], order)
        for (start, size), order in zip(HALVES, (("y", "x"), ("x", "y")))
    ]
    lines = [half[n] for n in range(len(KEYS)) for half in halves]
    ffn_piece = jnp.stack(
        [
            lax.dynamic_slice_in_dim(w_up, j * D, D, axis=1),
            lax.dynamic_slice_in_dim(w_up, ff + j * D, D, axis=1),
            lax.dynamic_slice_in_dim(w_down, j * ROWS, ROWS, axis=0),
        ]
    )
    w_ffn = lax.all_gather(ffn_piece, AXES, axis=0, tiled=False).reshape(SHARDS, QUARTERS, 3, ROWS, D)
    tails = jnp.stack([halves[1][n][:, 48, : 4 * ROWS] for n in range(2)])
    tails = jnp.where(i % 2 == 0, tails, tails[::-1])
    tails = jnp.roll(tails[:, ::-1], i // 2 + 1, axis=1)
    norms = tails.transpose(1, 0, 2).reshape(SHARDS, 4, ROWS).transpose(1, 0, 2).reshape(4, D).astype(F32)
    slopes = jnp.exp2(-8.0 * (jnp.arange(HEADS, dtype=F32) + 1.0) / HEADS)
    pos = positions.reshape(seqs * most, 1)
    live = jnp.arange(most, dtype=jnp.int32)[None, :] < counts[:, None]
    dy = jnp.where(live[:, :, None], grad_listed, jnp.zeros_like(grad_listed)).reshape(seqs * most, width)

    qkv, h1, att_m, h1_m, q_m, r1_m, w_attn = attention_forward(where, x, lines, norms, pos, slopes, seqs)
    h_all = jnp.stack(share_dp(h1_m))
    p_m = attention_again(q_m, qkv, pos, slopes, seqs)
    h1, h_all, p_m = lax.optimization_barrier((h1, h_all, p_m))
    layer_out, dr2, e2, small_ffn = ffn_forward(h1, w_ffn, norms, pos, dy, seqs)
    act, to_gate, to_up = ffn_again(where, h_all, w_ffn)
    other = after(send(e2, "x"), act)
    e_all = jnp.stack([e2, send(e2, "c"), other, send(other, "c")])
    dgate, dup, keep, away = ffn_back(where, e_all, to_gate, to_up, w_ffn)
    part = add(keep, send(away, "c"))
    part, part_away = part[0], part[1].astype(LOW)
    keep_d, away_d = weight_grad(where, act, e_all)
    came = send(part_away, "x")
    got_d = send(away_d, "y")
    keep_g, away_g = weight_grad(where, after(h_all, (away_d, part_away)), dgate)
    got_g = send(away_g, "y")
    keep_u, away_u = weight_grad(where, after(h_all, (away_g, came)), dup)
    got_u = send(away_u, "y")
    dr1, low, datt, small_attn = norm_back_call(dr2, part, after(came, away_u), r1_m, w_attn, norms)
    rhs = attention_back(datt, q_m, qkv, p_m, pos, seqs)
    got_d, rhs = lax.optimization_barrier((got_d, rhs))
    parts_d = line_parts(keep_d, got_d)
    line_d = line_send(parts_d)
    keep0, keep1, away0, away1 = attention_grads(where, x_flip, after(rhs, parts_d), att_m, low, small_attn, small_ffn)
    away0, away1, line_d, got_g, got_u = lax.optimization_barrier((away0, away1, line_d, got_g, got_u))
    came0, came1 = send(away0, "c"), send(away1, "c")
    parts_gu = [jnp.concatenate(pair) for pair in zip(line_parts(keep_g, got_g), line_parts(keep_u, got_u))]
    line_gu = line_send(parts_gu)
    g_down = send(line_add(keep_d, got_d, line_d), "down")
    away0, away1 = add(keep0[1], came0[1]).astype(LOW), add(keep1[1], came1[1]).astype(LOW)
    got0, got1 = send(away0, "x"), send(away1, "y")
    total0 = add(keep0[0], came0[0]) + got0.astype(F32)
    total1 = add(keep1[0], came1[0]) + got1.astype(F32)
    away0, away1 = total0[1].astype(LOW), total1[1].astype(LOW)
    got0, got1 = send(away0, "y"), send(away1, "x")
    g_down, line_gu = after((g_down, line_gu), (away0, away1))
    g_ffn = jnp.stack(
        [
            g_down,
            line_add(keep_g, got_g, [value[:ROWS] for value in line_gu]),
            line_add(keep_u, got_u, [value[ROWS:] for value in line_gu]),
        ]
    )
    got0, got1 = after((got0, got1), g_ffn)
    total = jnp.concatenate([add(total0[0], got0), add(total1[0], got1)], axis=1)
    parts = [total[r].astype(LOW) for r in (1, 2, 3)]
    line_a = line_send(parts)
    other = send(g_ffn, "x")
    grad_in = input_grad(after(rhs, parts), w_attn, dr1, positions)
    line_a, other, grad_in = lax.optimization_barrier((line_a, other, grad_in))
    g_attn = total[0] + line_a[0].astype(F32) + line_a[1].astype(F32) + line_a[2].astype(F32)
    small = g_attn[ROWS : ROWS + 4, :ROWS]
    g_attn = g_attn[:ROWS].astype(LOW)
    shared = (g_ffn, send(g_ffn, "c"), other, send(other, "c"))
    grad_down, grad_up = finish_ffn(where, after(shared, g_attn))
    other = after(send(g_attn, "x"), grad_down)
    grad_qkv, grad_out = finish_attention(where, (g_attn, send(g_attn, "c"), other, send(other, "c")))
    return (
        layer_out.reshape(seqs, length, width),
        grad_in.reshape(seqs, length, width),
        grad_qkv,
        grad_out,
        grad_up,
        grad_down,
        small[0],
        small[1],
        small[2],
        small[3],
    )


FF = 3072


def slopes():
    return jnp.exp2(-8.0 * (jnp.arange(HEADS, dtype=F32) + 1.0) / HEADS)


def pick(onehot, rows):
    if rows.dtype == LOW:
        return jnp.einsum("svj,sjd->svd", onehot.astype(LOW), rows, preferred_element_type=F32).astype(LOW)
    return jnp.einsum("svj,sjd->svd", onehot, rows, precision=lax.Precision.HIGHEST)


def gather_weights(w_qkv, w_out, w_up, w_down):
    fsdp = lax.axis_size("fsdp")
    dp = lax.axis_size("dp")
    rows, width = w_out.shape
    if rows % (8 * dp):
        return (
            lax.all_gather(w_qkv, "fsdp", axis=0, tiled=True),
            lax.all_gather(w_out, "fsdp", axis=0, tiled=True),
            lax.all_gather(w_up, "fsdp", axis=0, tiled=True),
            lax.all_gather(w_down, "fsdp", axis=0, tiled=True),
        )
    mine = lax.axis_index("dp")
    part = rows // dp
    group = w_down.shape[0] // rows
    joined = jnp.concatenate([w_qkv, w_out, w_up], axis=1)
    joined = lax.dynamic_slice_in_dim(joined, mine * part, part, axis=0)
    down = lax.dynamic_slice_in_dim(w_down, mine * part * group, part * group, axis=0)
    down = jnp.concatenate([down[k * part : (k + 1) * part] for k in range(group)], axis=1)
    full = lax.all_gather(jnp.concatenate([joined, down], axis=1), AXES, axis=0, tiled=True)
    a, b = w_qkv.shape[1], w_qkv.shape[1] + w_out.shape[1]
    c = b + w_up.shape[1]
    full_down = full[:, c:].reshape(fsdp * dp, part, group, width)
    full_down = full_down.transpose(0, 2, 1, 3).reshape(fsdp * dp * part * group, width)
    return full[:, :a], full[:, a:b], full[:, b:c], full_down


def scatter_grads(g_qkv, g_out, g_up, g_down):
    fsdp = lax.axis_size("fsdp")
    dp = lax.axis_size("dp")
    width = g_out.shape[1]
    rows = g_out.shape[0] // fsdp
    if rows % (8 * dp):
        return tuple(
            lax.psum(lax.psum_scatter(g, "fsdp", scatter_dimension=0, tiled=True), "dp")
            for g in (g_qkv, g_out, g_up, g_down)
        )
    part = rows // dp
    group = g_down.shape[0] // g_out.shape[0]
    down = g_down.reshape(fsdp * dp, group, part, width).transpose(0, 2, 1, 3)
    down = down.reshape(fsdp * rows, group * width)
    joined = jnp.concatenate([g_qkv, g_out, g_up, down], axis=1).astype(LOW)
    mine = lax.psum_scatter(joined, AXES, scatter_dimension=0, tiled=True)
    full = lax.all_gather(mine, "dp", axis=0, tiled=True).astype(F32)
    a, b = g_qkv.shape[1], g_qkv.shape[1] + width
    c = b + g_up.shape[1]
    full_down = full[:, c:].reshape(dp, part, group, width).transpose(0, 2, 1, 3)
    return full[:, :a], full[:, a:b], full[:, b:c], full_down.reshape(rows * group, width)


def on_device(hidden_in, w_qkv, w_out, w_up, w_down, gain_attn, shift_attn, gain_ffn, shift_ffn, grad_listed, positions, counts):
    seqs, length, width = hidden_in.shape
    tokens = seqs * length
    most = positions.shape[1]
    norms = jnp.stack([gain_attn, shift_attn, gain_ffn, shift_ffn])
    norms = lax.all_gather(norms, "fsdp", axis=1, tiled=True).astype(F32)
    w_qkv, w_out, w_up, w_down = gather_weights(w_qkv, w_out, w_up, w_down)
    live = jnp.arange(most, dtype=jnp.int32)[None, :] < counts[:, None]
    onehot = (positions[:, :, None] == jnp.arange(length, dtype=jnp.int32)).astype(F32)
    rows_in = hidden_in.reshape(tokens, width)
    slope = slopes()
    scale = HEAD_DIM**-0.5
    qkv = mm(rows_in, w_qkv).astype(LOW)
    split = qkv.reshape(seqs, length, 3, HEADS, HEAD_DIM)
    q, k, v = split[:, :, 0], split[:, :, 1], split[:, :, 2]
    place = jnp.arange(length, dtype=F32)
    bias = -slope[:, None, None] * jnp.abs(place[:, None] - place[None, :])
    s = jnp.einsum("sqhc,skhc->shqk", q, k, preferred_element_type=F32) * scale + bias
    p = jax.nn.softmax(s, axis=-1).astype(LOW)
    att = jnp.einsum("shqk,skhc->sqhc", p, v, preferred_element_type=F32).astype(LOW)
    att = att.reshape(tokens, width)
    r1 = rows_in.astype(F32) + mm(att, w_out)
    unit1, _ = norm_parts(r1)
    h1 = unit1 * norms[0] + norms[1]
    h1_low = h1.astype(LOW)
    u = mm(h1_low, w_up)
    act = (jax.nn.gelu(u[:, :FF], approximate=False) * u[:, FF:]).astype(LOW)
    r2 = h1 + mm(act, w_down)
    unit2, _ = norm_parts(r2)
    layer_out = (unit2 * norms[2] + norms[3]).astype(LOW).reshape(seqs, length, width)
    def listed(a):
        return pick(onehot, a.reshape(seqs, length, -1)).reshape(seqs * most, -1)

    dy = jnp.where(live[:, :, None], grad_listed, 0).astype(F32).reshape(seqs * most, width)
    unit2_m, rstd2_m = norm_parts(listed(r2))
    g_gain_ffn = jnp.sum(dy * unit2_m, axis=0)
    g_shift_ffn = jnp.sum(dy, axis=0)
    dr2 = norm_back(dy, unit2_m, rstd2_m, norms[2])
    e2 = dr2.astype(LOW)
    h1_m = listed(h1_low)
    u_m = mm(h1_m, w_up)
    gate, up = u_m[:, :FF], u_m[:, FF:]
    cdf = 0.5 * (1.0 + lax.erf(gate * (0.5**0.5)))
    pdf = jnp.exp(-0.5 * gate * gate) * ((2.0 * jnp.pi) ** -0.5)
    gelu = gate * cdf
    act_m = (gelu * up).astype(LOW)
    g_down = jnp.einsum("nf,nd->fd", act_m, e2, preferred_element_type=F32)
    dact = jnp.einsum("nd,fd->nf", e2, w_down, preferred_element_type=F32)
    du = jnp.concatenate([dact * up * (cdf + gate * pdf), dact * gelu], axis=1).astype(LOW)
    g_up = jnp.einsum("nd,nf->df", h1_m, du, preferred_element_type=F32)
    dh1 = dr2 + jnp.einsum("nf,df->nd", du, w_up, preferred_element_type=F32)
    unit1_m, rstd1_m = norm_parts(listed(r1))
    g_gain_attn = jnp.sum(dh1 * unit1_m, axis=0)
    g_shift_attn = jnp.sum(dh1, axis=0)
    dr1 = norm_back(dh1, unit1_m, rstd1_m, norms[0])
    e1 = dr1.astype(LOW)
    g_out = jnp.einsum("nd,ne->de", listed(att), e1, preferred_element_type=F32)
    datt = jnp.einsum("ne,de->nd", e1, w_out, preferred_element_type=F32).astype(LOW)
    datt = datt.reshape(seqs, most, HEADS, HEAD_DIM)
    q_m = listed(qkv[:, :width]).reshape(seqs, most, HEADS, HEAD_DIM)
    away = jnp.abs(positions[:, :, None].astype(F32) - place[None, None, :])
    s_m = jnp.einsum("sqhc,skhc->shqk", q_m, k, preferred_element_type=F32) * scale
    p_m = jax.nn.softmax(s_m - slope[None, :, None, None] * away[:, None], axis=-1)
    dv = jnp.einsum("shqk,sqhc->skhc", p_m.astype(LOW), datt, preferred_element_type=F32)
    dp = jnp.einsum("sqhc,skhc->shqk", datt, v, preferred_element_type=F32)
    ds = (p_m * (dp - jnp.sum(dp * p_m, axis=-1, keepdims=True))).astype(LOW)
    dq_m = (jnp.einsum("shqk,skhc->sqhc", ds, k, preferred_element_type=F32) * scale).astype(LOW)
    dk = (jnp.einsum("shqk,sqhc->skhc", ds, q_m, preferred_element_type=F32) * scale).astype(LOW)
    put = (onehot * live[:, :, None]).astype(LOW)
    dq = jnp.einsum("svj,svd->sjd", put, dq_m.reshape(seqs, most, width), preferred_element_type=F32)
    dqkv = jnp.concatenate(
        [dq.astype(LOW).reshape(tokens, width), dk.reshape(tokens, width), dv.astype(LOW).reshape(tokens, width)], axis=1
    )
    g_qkv = jnp.einsum("nd,ne->de", rows_in, dqkv, preferred_element_type=F32)
    dr1_all = jnp.einsum("svj,svd->sjd", onehot * live[:, :, None], dr1.reshape(seqs, most, width), precision=lax.Precision.HIGHEST)
    grad_in = dr1_all.reshape(tokens, width) + jnp.einsum("ne,de->nd", dqkv, w_qkv, preferred_element_type=F32)
    owned = scatter_grads(g_qkv, g_out, g_up, g_down)
    small = lax.psum(jnp.stack([g_gain_attn, g_shift_attn, g_gain_ffn, g_shift_ffn]), AXES)
    share = width // lax.axis_size("fsdp")
    small = lax.dynamic_slice_in_dim(small, lax.axis_index("fsdp") * share, share, axis=1)
    return (
        layer_out,
        grad_in.reshape(seqs, length, width),
        *owned,
        small[0],
        small[1],
        small[2],
        small[3],
    )


def solution(mesh):
    rows3 = P(("fsdp", "dp"), None, None)
    rows2 = P("fsdp", None)
    rows1 = P("fsdp")
    shape = dict(mesh.shape)
    step = on_block if shape == {"fsdp": SHARDS, "dp": QUARTERS} else on_device
    return jax.shard_map(
        step,
        mesh=mesh,
        in_specs=(rows3, rows2, rows2, rows2, rows2, rows1, rows1, rows1, rows1, rows3, P(("fsdp", "dp"), None), P(("fsdp", "dp"))),
        out_specs=(rows3, rows3, rows2, rows2, rows2, rows2, rows1, rows1, rows1, rows1),
        check_vma=False,
    )
```

```python
import functools

import jax
import jax.numpy as jnp
from jax import lax
from jax.experimental import pallas as pl
from jax.experimental.pallas import tpu as pltpu
from jax.sharding import PartitionSpec as P

HEADS = 12
HEAD_DIM = 64
EPS = 1e-12
F32 = jnp.float32
LOW = jnp.bfloat16
AXES = ("fsdp", "dp")
D = 768
ROWS = 96
LINE = 4
SHARDS = D // ROWS
QUARTERS = 4
EXACT = lax.Precision.HIGHEST
SCALE = HEAD_DIM**-0.5
VMEM = pl.BlockSpec(memory_space=pltpu.VMEM)
SMEM = pl.BlockSpec(memory_space=pltpu.SMEM)
BIG = pltpu.CompilerParams(vmem_limit_bytes=60 * 1024 * 1024)


def out(shape, dtype):
    return jax.ShapeDtypeStruct(shape, dtype)


def cost(us):
    return pl.CostEstimate(flops=0, bytes_accessed=int(us * 3.0e6), transcendentals=0)


def mm(a, b):
    return jnp.dot(a, b, preferred_element_type=F32)


def mm_nt(a, b):
    return lax.dot_general(a, b, (((1,), (1,)), ((), ())), preferred_element_type=F32)


def mm_tn(a, b):
    return lax.dot_general(a, b, (((0,), (0,)), ((), ())), preferred_element_type=F32)


def norm_parts(value):
    center = value - jnp.mean(value, axis=-1, keepdims=True)
    rstd = lax.rsqrt(jnp.mean(center * center, axis=-1, keepdims=True) + EPS)
    return center * rstd, rstd


def norm_back(grad, unit, rstd, gain):
    scaled = grad * gain
    return rstd * (
        scaled
        - jnp.mean(scaled, axis=-1, keepdims=True)
        - unit * jnp.mean(scaled * unit, axis=-1, keepdims=True)
    )


def onehot(pos_ref, seq, most, length):
    spots = lax.broadcasted_iota(jnp.int32, (most, length), 1)
    return spots == pos_ref[pl.ds(seq * most, most), :]


def gelu_parts(gate):
    cdf = 0.5 * (1.0 + lax.erf(gate * (0.5**0.5)))
    pdf = jnp.exp(-0.5 * gate * gate) * ((2.0 * jnp.pi) ** -0.5)
    return gate * cdf, cdf + gate * pdf


def slope_of(head):
    return 2.0 ** (-8.0 * (head + 1.0) / HEADS)


def block(ref, *index):
    value = ref[index] if index else ref[...]
    return value.reshape(-1, value.shape[-1])


EXTRA = 8
TAIL = 8
HALVES = ((0, 48), (48, 56))
KEYS = [(ry, rx, rc) for rc in (0, 1) for rx in (0, 1) for ry in (0, 1)]


def attention_kernel(seqs, most, where_ref, slope_ref, x_ref, norm_ref, pos_ref, *rest):
    lines, rest = rest[:16], rest[16:]
    qkv_ref, h1_ref, att_m_ref, h1_m_ref, q_m_ref, r1_m_ref, w_ref, att_ref, r1_ref, sem = rest
    z, y, c_x = where_ref[0], where_ref[1], where_ref[4]
    copies = []
    for n, (ry, rx, rc) in enumerate(KEYS):
        j = jnp.bitwise_xor(c_x, 2 * rx + rc)
        for r in range(LINE):
            shard = 2 * lax.rem(z + LINE - r, LINE) + jnp.bitwise_xor(y, ry)
            for half, (start, size) in enumerate(HALVES):
                size = min(size, ROWS - start)
                copies.append(
                    pltpu.make_async_copy(
                        lines[2 * n + half].at[r, pl.ds(0, size)], w_ref.at[shard, j, pl.ds(start, size)], sem
                    )
                )
    for copy in copies:
        copy.start()
    for copy in copies:
        copy.wait()
    length = x_ref.shape[0] // seqs
    step = 256

    @pl.loop(0, 3 * D // step)
    def _(n):
        j = n // (D // step)
        lane = pl.multiple_of((n - j * (D // step)) * step, step)
        w = w_ref[:, j, :, pl.ds(lane, step)].reshape(D, step)
        qkv_ref[:, pl.ds(pl.multiple_of(n * step, step), step)] = mm(x_ref[...], w).astype(LOW)

    first = lax.broadcasted_iota(jnp.int32, (length, 128), 1) < HEAD_DIM
    row = lax.broadcasted_iota(jnp.int32, (length, length), 0)
    col = lax.broadcasted_iota(jnp.int32, (length, length), 1)
    away = jnp.abs(row - col).astype(F32)

    @pl.loop(0, HEADS // 2)
    def _(t):
        lane = pl.multiple_of(t * 128, 128)
        bias = jnp.concatenate([slope_ref[2 * t] * away, slope_ref[2 * t + 1] * away], axis=0)
        for s in range(seqs):
            rows = slice(s * length, (s + 1) * length)
            q = qkv_ref[rows, pl.ds(lane, 128)]
            k = qkv_ref[rows, pl.ds(D + lane, 128)]
            v = qkv_ref[rows, pl.ds(2 * D + lane, 128)]
            zero = jnp.zeros_like(q)
            both = jnp.concatenate([jnp.where(first, q, zero), jnp.where(first, zero, q)], axis=0)
            score = mm_nt(both, k) * SCALE - bias
            e = jnp.exp(score - jnp.max(score, axis=-1, keepdims=True))
            p = (e * (1.0 / jnp.sum(e, axis=-1, keepdims=True))).astype(LOW)
            mixed = mm(p, v)
            att_ref[rows, pl.ds(lane, 128)] = jnp.where(first, mixed[:length], mixed[length:]).astype(LOW)

    @pl.loop(0, D // step)
    def _(n):
        lane = pl.multiple_of(n * step, step)
        w = w_ref[:, 3, :, pl.ds(lane, step)].reshape(D, step)
        r1_ref[:, pl.ds(lane, step)] = x_ref[:, pl.ds(lane, step)].astype(F32) + mm(att_ref[...], w)

    for s in range(seqs):
        rows = slice(s * length, (s + 1) * length)
        listed = slice(s * most, (s + 1) * most)
        unit, _ = norm_parts(r1_ref[rows, :])
        h1 = unit * norm_ref[0:1, :] + norm_ref[1:2, :]
        h1_ref[rows, :] = h1
        hot = onehot(pos_ref, s, most, length)
        hot_low = hot.astype(LOW)
        r1_m_ref[listed, :] = jnp.dot(hot.astype(F32), r1_ref[rows, :], precision=EXACT, preferred_element_type=F32)
        h1_m_ref[listed, :] = mm(hot_low, h1.astype(LOW)).astype(LOW)
        att_m_ref[listed, :] = mm(hot_low, att_ref[rows, :]).astype(LOW)
        q_m_ref[listed, :] = mm(hot_low, qkv_ref[rows, 0:D]).astype(LOW)


def attention_forward(where, x, lines, norms, pos, slopes, seqs):
    tokens = x.shape[0]
    listed = pos.shape[0]
    return pl.pallas_call(
        functools.partial(attention_kernel, seqs, listed // seqs),
        out_shape=(
            out((tokens, 3 * D), LOW),
            out((tokens, D), F32),
            out((listed, D), LOW),
            out((listed, D), LOW),
            out((listed, D), LOW),
            out((listed, D), F32),
            out((SHARDS, QUARTERS, ROWS, D), LOW),
        ),
        in_specs=[SMEM, SMEM, VMEM, VMEM, VMEM] + [pl.BlockSpec(memory_space=pl.ANY)] * 16,
        out_specs=(VMEM,) * 7,
        scratch_shapes=[pltpu.VMEM((tokens, D), LOW), pltpu.VMEM((tokens, D), F32), pltpu.SemaphoreType.DMA],
        compiler_params=BIG,
        cost_estimate=cost(20),
        name="attention_forward",
    )(where, slopes, x, norms, pos, *lines)


def ffn_kernel(seqs, most, h1_ref, gate_ref, up_ref, down_ref, norm_ref, pos_ref, dy_ref, y_ref, dr2_ref, e2_ref, small_ref, low_ref, act_ref, acc_ref):
    j = pl.program_id(0)
    tokens = h1_ref.shape[0]
    length = tokens // seqs
    step = 256

    @pl.when(j == 0)
    def _():
        low_ref[...] = h1_ref[...].astype(LOW)
        acc_ref[...] = h1_ref[...]

    def products(n):
        lanes = slice(n * step, (n + 1) * step)
        return mm(low_ref[...], gate_ref[:, :, lanes].reshape(D, step)), mm(low_ref[...], up_ref[:, :, lanes].reshape(D, step))

    gate, up = products(0)
    for n in range(D // step):
        following = products(n + 1) if (n + 1) * step < D else (None, None)
        cdf = 0.5 * (1.0 + lax.erf(gate * (0.5**0.5)))
        act_ref[:, n * step : (n + 1) * step] = (gate * cdf * up).astype(LOW)
        gate, up = following
    for n in range(D // step):
        lanes = slice(n * step, (n + 1) * step)
        acc_ref[:, lanes] += mm(act_ref[...], down_ref[:, :, :, lanes].reshape(D, step))

    @pl.when(j == QUARTERS - 1)
    def _():
        gain = norm_ref[2:3, :]
        small = [jnp.zeros((1, D), F32)] * 2
        for s in range(seqs):
            rows = slice(s * length, (s + 1) * length)
            listed = slice(s * most, (s + 1) * most)
            unit, _ = norm_parts(acc_ref[rows, :])
            y_ref[rows, :] = (unit * gain + norm_ref[3:4, :]).astype(LOW)
            hot = onehot(pos_ref, s, most, length).astype(F32)
            picked = jnp.dot(hot, acc_ref[rows, :], precision=EXACT, preferred_element_type=F32)
            unit_m, rstd_m = norm_parts(picked)
            dy = dy_ref[listed, :].astype(F32)
            small = [small[0] + jnp.sum(dy * unit_m, axis=0, keepdims=True), small[1] + jnp.sum(dy, axis=0, keepdims=True)]
            dr2 = norm_back(dy, unit_m, rstd_m, gain)
            dr2_ref[listed, :] = dr2
            e2_ref[listed, :] = dr2.astype(LOW)
        small_ref[...] = jnp.concatenate(small, axis=0)


def ffn_forward(h1, w_ffn, norms, pos, dy, seqs):
    tokens = h1.shape[0]
    listed = pos.shape[0]
    whole = lambda shape: pl.BlockSpec(shape, lambda j: (0,) * len(shape), pipeline_mode=pl.Buffered(1))
    return pl.pallas_call(
        functools.partial(ffn_kernel, seqs, listed // seqs),
        out_shape=(out((tokens, D), LOW), out((listed, D), F32), out((listed, D), LOW), out((2, D), F32)),
        grid=(QUARTERS,),
        in_specs=[
            whole((tokens, D)),
            pl.BlockSpec((SHARDS, None, None, ROWS, D), lambda j: (0, j, 0, 0, 0)),
            pl.BlockSpec((SHARDS, None, None, ROWS, D), lambda j: (0, j, 1, 0, 0)),
            pl.BlockSpec((SHARDS // QUARTERS, QUARTERS, None, ROWS, D), lambda j: (j, 0, 2, 0, 0)),
            whole(norms.shape),
            whole(pos.shape),
            whole(dy.shape),
        ],
        out_specs=(
            pl.BlockSpec((tokens, D), lambda j: (0, 0)),
            pl.BlockSpec((listed, D), lambda j: (0, 0)),
            pl.BlockSpec((listed, D), lambda j: (0, 0)),
            pl.BlockSpec((2, D), lambda j: (0, 0)),
        ),
        scratch_shapes=[pltpu.VMEM((tokens, D), LOW), pltpu.VMEM((tokens, D), LOW), pltpu.VMEM((tokens, D), F32)],
        compiler_params=BIG,
        cost_estimate=cost(16),
        name="ffn_forward",
    )(h1, w_ffn, w_ffn, w_ffn, norms, pos, dy)


def ffn_again_kernel(where_ref, h_ref, gate_ref, up_ref, act_ref, to_gate_ref, to_up_ref):
    step = 256

    rows = block(h_ref)

    def products(n):
        lanes = slice(n * step, (n + 1) * step)
        return mm(rows, gate_ref[:, :, lanes].reshape(D, step)), mm(rows, up_ref[:, :, lanes].reshape(D, step))

    gate, up = products(0)
    for n in range(D // step):
        following = products(n + 1) if (n + 1) * step < D else (None, None)
        lanes = slice(n * step, (n + 1) * step)
        value, slope = gelu_parts(gate)
        act_ref[:, lanes] = (value * up).astype(LOW)
        to_gate_ref[:, lanes] = (slope * up).astype(LOW)
        to_up_ref[:, lanes] = value.astype(LOW)
        gate, up = following


def quarter_specs(which):
    specs = {
        "gate": pl.BlockSpec((SHARDS, None, None, ROWS, D), lambda g, w: (0, w[4], 0, 0, 0)),
        "up": pl.BlockSpec((SHARDS, None, None, ROWS, D), lambda g, w: (0, w[4], 1, 0, 0)),
        "down": pl.BlockSpec((SHARDS // QUARTERS, QUARTERS, None, ROWS, D), lambda g, w: (w[4], 0, 2, 0, 0)),
    }
    return [specs[name] for name in which]


def at_once(shape):
    return pl.BlockSpec(shape, lambda g, w: (0,) * len(shape))


def ffn_again(where, h_all, w_ffn):
    rows = h_all.shape[0] * h_all.shape[1]
    return pl.pallas_call(
        ffn_again_kernel,
        out_shape=(out((rows, D), LOW),) * 3,
        grid_spec=pltpu.PrefetchScalarGridSpec(
            num_scalar_prefetch=1,
            grid=(1,),
            in_specs=[at_once(h_all.shape), *quarter_specs(["gate", "up"])],
            out_specs=(at_once((rows, D)),) * 3,
        ),
        compiler_params=BIG,
        cost_estimate=cost(6),
        name="ffn_again",
    )(where, h_all, w_ffn, w_ffn)


def ffn_back_kernel(where_ref, *rest):
    pieces, rest = rest[:QUARTERS], rest[QUARTERS:]
    to_gate_ref, to_up_ref, gate_ref, up_ref, down_ref, dgate_ref, dup_ref, keep_ref, send_ref, e_ref = rest
    listed = pieces[0].shape[0]
    for n, piece in enumerate(pieces):
        e_ref[n * listed : (n + 1) * listed, :] = piece[...]
    half = QUARTERS // 2
    for n in range(SHARDS // QUARTERS):
        lanes = slice(n * QUARTERS * ROWS, (n + 1) * QUARTERS * ROWS)
        dact = mm_nt(e_ref[...], block(down_ref, n))
        dgate_ref[:, lanes] = (dact * to_gate_ref[:, lanes].astype(F32)).astype(LOW)
        dup_ref[:, lanes] = (dact * to_up_ref[:, lanes].astype(F32)).astype(LOW)
    for n in range(2):
        shards = slice(n * SHARDS // 2, (n + 1) * SHARDS // 2)
        lanes = slice(n * D // 2, (n + 1) * D // 2)
        part = mm_nt(dgate_ref[...], block(gate_ref, shards)) + mm_nt(dup_ref[...], block(up_ref, shards))
        for r in range(half):
            keep_ref[r, :, lanes] = part[2 * r * listed : (2 * r + 1) * listed]
            send_ref[r, :, lanes] = part[(2 * r + 1) * listed : (2 * r + 2) * listed].astype(LOW)


def ffn_back(where, pieces, to_gate, to_up, w_ffn):
    count, listed = len(pieces), pieces[0].shape[0]
    rows = count * listed
    return pl.pallas_call(
        ffn_back_kernel,
        out_shape=(out((rows, D), LOW), out((rows, D), LOW), out((count // 2, listed, D), F32), out((count // 2, listed, D), LOW), out((rows, D), LOW)),
        grid_spec=pltpu.PrefetchScalarGridSpec(
            num_scalar_prefetch=1,
            grid=(1,),
            in_specs=[*[at_once((listed, D))] * count, at_once((rows, D)), at_once((rows, D)), *quarter_specs(["gate", "up", "down"])],
            out_specs=(at_once((rows, D)), at_once((rows, D)), at_once((count // 2, listed, D)), at_once((count // 2, listed, D)), at_once((rows, D))),
        ),
        compiler_params=BIG,
        cost_estimate=cost(7),
        name="ffn_back",
    )(where, *pieces, to_gate, to_up, w_ffn, w_ffn, w_ffn)


def weight_grad_kernel(where_ref, a_ref, b_ref, keep_ref, send_ref, full_ref):
    z, y = where_ref[0], where_ref[1]
    b = block(b_ref)
    step = 256

    for n in range(D // step):
        rows = slice(n * step, (n + 1) * step)
        full_ref[rows, :] = mm_tn(block(a_ref, *([slice(None)] * (len(a_ref.shape) - 1)), rows), b)

    for r in range(LINE):
        base = 2 * lax.rem(z + r, LINE)
        for other, ref in ((0, keep_ref), (1, send_ref)):
            start = (base + (y if other == 0 else 1 - y)) * ROWS
            ref[r] = full_ref[pl.ds(pl.multiple_of(start, 8), ROWS), :].astype(LOW)


def weight_grad(where, a, b):
    shape = (LINE, ROWS, D)
    rows = a.size // D
    return pl.pallas_call(
        weight_grad_kernel,
        out_shape=(out(shape, LOW), out(shape, LOW)),
        in_specs=[SMEM, VMEM, VMEM],
        out_specs=(VMEM, VMEM),
        scratch_shapes=[pltpu.VMEM((D, D), F32)],
        compiler_params=BIG,
        cost_estimate=cost(4),
        name="weight_grad",
    )(where, a, b)


def norm_back_kernel(dr2_ref, part_ref, came_ref, r1_ref, w_ref, norm_ref, dr1_ref, low_ref, datt_ref, small_ref):
    dh1 = dr2_ref[...] + part_ref[...] + came_ref[...].astype(F32)
    unit, rstd = norm_parts(r1_ref[...])
    small_ref[0:1, :] = jnp.sum(dh1 * unit, axis=0, keepdims=True)
    small_ref[1:2, :] = jnp.sum(dh1, axis=0, keepdims=True)
    dr1 = norm_back(dh1, unit, rstd, norm_ref[0:1, :])
    dr1_ref[...] = dr1
    low = dr1.astype(LOW)
    low_ref[...] = low
    for n in range(2):
        lanes = slice(n * D // 2, (n + 1) * D // 2)
        datt_ref[:, lanes] = mm_nt(low, block(w_ref, slice(n * SHARDS // 2, (n + 1) * SHARDS // 2))).astype(LOW)


def norm_back_call(dr2, part, came, r1_m, w_attn, norms):
    listed = dr2.shape[0]
    same = lambda shape: pl.BlockSpec(shape, lambda g: (0,) * len(shape))
    rows = same((listed, D))
    return pl.pallas_call(
        norm_back_kernel,
        out_shape=(out((listed, D), F32), out((listed, D), LOW), out((listed, D), LOW), out((2, D), F32)),
        grid=(1,),
        in_specs=[rows, rows, rows, rows, pl.BlockSpec((SHARDS, None, ROWS, D), lambda g: (0, 3, 0, 0)), same((4, D))],
        out_specs=(rows, rows, rows, same((2, D))),
        compiler_params=BIG,
        cost_estimate=cost(4),
        name="norm_back",
    )(dr2, part, came, r1_m, w_attn, norms)


def both_heads(value):
    first = lax.broadcasted_iota(jnp.int32, value.shape, 1) < HEAD_DIM
    zero = jnp.zeros_like(value)
    return jnp.concatenate([jnp.where(first, value, zero), jnp.where(first, zero, value)], axis=0)


def attention_again_kernel(seqs, slope_ref, q_ref, k_ref, pos_ref, p_ref):
    length, most = k_ref.shape[0] // seqs, q_ref.shape[0] // seqs
    spots = lax.broadcasted_iota(jnp.int32, (most, length), 1)

    @pl.loop(0, HEADS // 2)
    def _(t):
        lane = pl.multiple_of(t * 128, 128)
        for s in range(seqs):
            rows = slice(s * length, (s + 1) * length)
            mine = slice(s * most, (s + 1) * most)
            away = jnp.abs(pos_ref[mine, :] - spots).astype(F32)
            bias = jnp.concatenate([slope_ref[2 * t] * away, slope_ref[2 * t + 1] * away], axis=0)
            score = mm_nt(both_heads(q_ref[mine, pl.ds(lane, 128)]), k_ref[rows, pl.ds(lane, 128)]) * SCALE - bias
            e = jnp.exp(score - jnp.max(score, axis=-1, keepdims=True))
            p = e * (1.0 / jnp.sum(e, axis=-1, keepdims=True))
            p_ref[2 * t, mine, :] = p[:most]
            p_ref[2 * t + 1, mine, :] = p[most:]


def attention_again(q_m, qkv, pos, slopes, seqs):
    tokens, listed = qkv.shape[0], pos.shape[0]
    shape = (HEADS, listed, tokens // seqs)
    return pl.pallas_call(
        functools.partial(attention_again_kernel, seqs),
        out_shape=out(shape, F32),
        grid=(1,),
        in_specs=[SMEM, pl.BlockSpec((listed, D), lambda g: (0, 0)), pl.BlockSpec((tokens, D), lambda g: (0, 1)), pl.BlockSpec((listed, 1), lambda g: (0, 0))],
        out_specs=pl.BlockSpec(shape, lambda g: (0, 0, 0)),
        compiler_params=BIG,
        cost_estimate=cost(8),
        name="attention_again",
    )(slopes, q_m, qkv, pos)


def attention_back_kernel(seqs, datt_ref, q_ref, k_ref, v_ref, p_ref, pos_ref, rhs_ref, hot_ref):
    length, most = k_ref.shape[0] // seqs, q_ref.shape[0] // seqs
    first_m = lax.broadcasted_iota(jnp.int32, (most, 128), 1) < HEAD_DIM
    hot_ref[...] = (lax.broadcasted_iota(jnp.int32, hot_ref.shape, 1) == pos_ref[...]).astype(LOW)

    @pl.loop(0, HEADS // 4)
    def _(step):
        for n, s in ((n, s) for n in (0, 1) for s in range(seqs)):
            t = 2 * step + n
            lane = pl.multiple_of(t * 128, 128)
            rows = slice(s * length, (s + 1) * length)
            mine = slice(s * most, (s + 1) * most)
            q = both_heads(q_ref[mine, pl.ds(lane, 128)])
            da = both_heads(datt_ref[mine, pl.ds(lane, 128)])
            k = k_ref[rows, pl.ds(lane, 128)]
            v = v_ref[rows, pl.ds(lane, 128)]
            p = jnp.concatenate([p_ref[2 * t, mine, :], p_ref[2 * t + 1, mine, :]], axis=0)
            dp = mm_nt(da, v)
            ds = (p * (dp - jnp.sum(dp * p, axis=-1, keepdims=True))).astype(LOW)
            dq = mm(ds, k)
            dq = (jnp.where(first_m, dq[:most], dq[most:]) * SCALE).astype(LOW)
            rhs_ref[rows, pl.ds(lane, 128)] = mm_tn(hot_ref[mine, :], dq).astype(LOW)
            rhs_ref[rows, pl.ds(D + lane, 128)] = (mm_tn(ds, q) * SCALE).astype(LOW)
            rhs_ref[rows, pl.ds(2 * D + lane, 128)] = mm_tn(p.astype(LOW), da).astype(LOW)


def attention_back(datt, q_m, qkv, p_m, pos, seqs):
    tokens, listed = qkv.shape[0], pos.shape[0]
    length = tokens // seqs
    whole = lambda shape, lane=0: pl.BlockSpec(shape, lambda g: (0, lane))
    return pl.pallas_call(
        functools.partial(attention_back_kernel, seqs),
        out_shape=out((tokens, 3 * D), LOW),
        grid=(1,),
        in_specs=[
            whole((listed, D)),
            whole((listed, D)),
            whole((tokens, D), 1),
            whole((tokens, D), 2),
            pl.BlockSpec((HEADS, listed, length), lambda g: (0, 0, 0)),
            whole((listed, 1)),
        ],
        out_specs=pl.BlockSpec((tokens, 3 * D), lambda g: (0, 0)),
        scratch_shapes=[pltpu.VMEM((listed, length), LOW)],
        compiler_params=BIG,
        cost_estimate=cost(12),
        name="attention_back",
    )(datt, q_m, qkv, qkv, p_m, pos)


def attention_grads_kernel(where_ref, flip_ref, rhs_ref, att_ref, low_ref, small_attn_ref, small_ffn_ref, keep0_ref, keep1_ref, away0_ref, away1_ref, full_ref, tail_ref):
    z, y, mine = where_ref[0], where_ref[1], where_ref[4]
    half = ROWS // 2
    step = 256
    tail_ref[...] = jnp.zeros(tail_ref.shape, LOW)
    small = jnp.concatenate([small_attn_ref[...], small_ffn_ref[...]], axis=0).astype(LOW)
    for n in range(SHARDS):
        tail_ref[n, 0:4, 0:ROWS] = small[:, n * ROWS : (n + 1) * ROWS]
    for rc in (1, 0):
        cut0_ref, cut1_ref = (keep0_ref, keep1_ref) if rc == 0 else (away0_ref, away1_ref)
        for rx in (0, 1):
            j = jnp.bitwise_xor(mine, 2 * rx + rc)

            @pl.when(j == 3)
            def _():
                for n in range(D // step):
                    rows = slice(n * step, (n + 1) * step)
                    full_ref[rows, :] = mm_tn(att_ref[:, rows], low_ref[...])

            @pl.when(j != 3)
            def _():
                @pl.loop(0, D // step)
                def _(n):
                    lane = pl.multiple_of(n * step, step)
                    cols = pl.ds(pl.multiple_of(j * D + n * step, step), step)
                    full_ref[:, pl.ds(lane, step)] = mm(flip_ref[...], rhs_ref[:, cols])

            for rz in range(LINE):
                base = 2 * lax.rem(z + rz, LINE)
                for ry in (0, 1):
                    shard = base + (y if ry == 0 else 1 - y)
                    start = shard * ROWS
                    cut0_ref[rx, ry, rz] = full_ref[pl.ds(pl.multiple_of(start, 8), half), :].astype(LOW)
                    cut1_ref[ry, rx, rz, 0:half] = full_ref[pl.ds(pl.multiple_of(start + half, 8), half), :].astype(LOW)
                    cut1_ref[ry, rx, rz, half:] = tail_ref[shard]


def attention_grads(where, x_flip, rhs, att_m, low, small_attn, small_ffn):
    half = ROWS // 2
    return pl.pallas_call(
        attention_grads_kernel,
        out_shape=(out((2, 2, LINE, half, D), LOW), out((2, 2, LINE, half + TAIL, D), LOW)) * 2,
        in_specs=[SMEM] + [VMEM] * 6,
        out_specs=(VMEM,) * 4,
        scratch_shapes=[pltpu.VMEM((D, D), F32), pltpu.VMEM((SHARDS, TAIL, D), LOW)],
        compiler_params=BIG,
        cost_estimate=cost(10),
        name="attention_grads",
    )(where, x_flip, rhs, att_m, low, small_attn, small_ffn)


def input_grad_kernel(seqs, rhs_ref, w_ref, dr1_ref, pos_ref, out_ref):
    length = out_ref.shape[0] // seqs
    most = dr1_ref.shape[0] // seqs
    for n in range(2):
        lanes = slice(n * D // 2, (n + 1) * D // 2)
        shards = slice(n * SHARDS // 2, (n + 1) * SHARDS // 2)
        total = mm_nt(rhs_ref[:, 0:D], block(w_ref, shards, 0))
        total += mm_nt(rhs_ref[:, D : 2 * D], block(w_ref, shards, 1))
        total += mm_nt(rhs_ref[:, 2 * D : 3 * D], block(w_ref, shards, 2))
        for s in range(seqs):
            rows = slice(s * length, (s + 1) * length)
            hot = (lax.broadcasted_iota(jnp.int32, (length, most), 0) == pos_ref[s : s + 1, :]).astype(F32)
            spread = jnp.dot(hot, dr1_ref[s * most : (s + 1) * most, lanes], precision=EXACT, preferred_element_type=F32)
            out_ref[rows, lanes] = total[rows] + spread


def input_grad(rhs, w_attn, dr1, positions):
    tokens = rhs.shape[0]
    return pl.pallas_call(
        functools.partial(input_grad_kernel, positions.shape[0]),
        out_shape=out((tokens, D), F32),
        in_specs=[VMEM] * 4,
        out_specs=VMEM,
        compiler_params=BIG,
        cost_estimate=cost(8),
        name="input_grad",
    )(rhs, w_attn, dr1, positions)


def place(z, y, x, c):
    return (2 * z + y) * 4 + 2 * x + c


def grid_perm(move):
    return [
        (place(z, y, x, c), place(*move(z, y, x, c)))
        for z in range(4)
        for y in range(2)
        for x in range(2)
        for c in range(2)
    ]


MOVES = {
    "x": grid_perm(lambda z, y, x, c: (z, y, 1 - x, c)),
    "y": grid_perm(lambda z, y, x, c: (z, 1 - y, x, c)),
    "c": grid_perm(lambda z, y, x, c: (z, y, x, 1 - c)),
    1: grid_perm(lambda z, y, x, c: ((z + 1) % 4, y, x, c)),
    2: grid_perm(lambda z, y, x, c: ((z + 2) % 4, y, x, c)),
    3: grid_perm(lambda z, y, x, c: ((z + 3) % 4, y, x, c)),
    "down": [(m * 4 + q, (2 * q + m // 4) * 4 + m % 4) for m in range(8) for q in range(4)],
}


def send(value, move):
    return lax.ppermute(value, AXES, MOVES[move])


def share_dp(value):
    other = send(value, "x")
    return value, send(value, "c"), other, send(other, "c")


def after(value, *earlier):
    return lax.optimization_barrier((value, *earlier))[0]


def add(kept, got):
    return kept.astype(F32) + got.astype(F32)


def line_parts(keep, got):
    return [add(keep[r], got[r]).astype(LOW) for r in (1, 2, 3)]


def line_send(parts):
    return [send(value, r) for r, value in zip((1, 2, 3), parts)]


def line_add(keep, got, came):
    return (add(keep[0], got[0]) + came[0].astype(F32) + came[1].astype(F32) + came[2].astype(F32)).astype(LOW)


def finish_ffn_kernel(where_ref, *rest):
    pieces, (down_ref, up_ref) = rest[:QUARTERS], rest[QUARTERS:]
    mine = where_ref[4]
    for n, ref in enumerate(pieces):
        j = jnp.bitwise_xor(mine, n)
        down_ref[pl.ds(pl.multiple_of(j * ROWS, 8), ROWS), :] = ref[0].astype(F32)
        for half in (0, 1):
            up_ref[:, pl.ds(pl.multiple_of((half * QUARTERS + j) * D, D), D)] = ref[1 + half].astype(F32)


def finish_attention_kernel(where_ref, *rest):
    pieces, (qkv_ref, out_ref, held_ref) = rest[:QUARTERS], rest[QUARTERS:]
    mine = where_ref[4]
    for n, ref in enumerate(pieces):
        held_ref[jnp.bitwise_xor(mine, n)] = ref[...].astype(F32)
    for j in range(3):
        qkv_ref[:, j * D : (j + 1) * D] = held_ref[j]
    out_ref[...] = held_ref[3]


def finish_ffn(where, pieces):
    return pl.pallas_call(
        finish_ffn_kernel,
        out_shape=(out((QUARTERS * ROWS, D), F32), out((ROWS, 2 * QUARTERS * D), F32)),
        in_specs=[SMEM] + [VMEM] * QUARTERS,
        out_specs=(VMEM, VMEM),
        compiler_params=BIG,
        cost_estimate=cost(4),
        name="finish_ffn",
    )(where, *pieces)


def finish_attention(where, pieces):
    return pl.pallas_call(
        finish_attention_kernel,
        out_shape=(out((ROWS, 3 * D), F32), out((ROWS, D), F32)),
        in_specs=[SMEM] + [VMEM] * QUARTERS,
        out_specs=(VMEM, VMEM),
        scratch_shapes=[pltpu.VMEM((QUARTERS, ROWS, D), F32)],
        compiler_params=BIG,
        cost_estimate=cost(2),
        name="finish_attention",
    )(where, *pieces)


def spread(piece, order):
    got = {frozenset(): piece}
    for step in (*order, "c"):
        for key in list(got):
            got[key | {step}] = send(got[key], step)
    return [got[frozenset(n for n, b in zip("yxc", key) if b)] for key in KEYS]


def on_block(hidden_in, w_qkv, w_out, w_up, w_down, gain_attn, shift_attn, gain_ffn, shift_ffn, grad_listed, positions, counts):
    seqs, length, width = hidden_in.shape
    tokens = seqs * length
    most = positions.shape[1]
    i, j = lax.axis_index("fsdp"), lax.axis_index("dp")
    where = jnp.stack([i // 2, i % 2, j // 2, j % 2, j]).astype(jnp.int32)
    ff = w_down.shape[0] * SHARDS
    attn_piece = lax.dynamic_slice_in_dim(jnp.concatenate([w_qkv, w_out], axis=1), j * D, D, axis=1)
    norms = jnp.concatenate([gain_attn, shift_attn, gain_ffn, shift_ffn, jnp.zeros((D - 4 * ROWS,), LOW)])
    attn_piece = jnp.concatenate([attn_piece, jnp.broadcast_to(norms, (EXTRA, D))], axis=0)
    line = jnp.stack([attn_piece] + [send(attn_piece, r) for r in (1, 2, 3)])
    x = hidden_in.reshape(tokens, width)
    line, x_flip = lax.optimization_barrier((line, x.T))
    halves = [
        spread(line[:, start : start + size], order)
        for (start, size), order in zip(HALVES, (("y", "x"), ("x", "y")))
    ]
    lines = [half[n] for n in range(len(KEYS)) for half in halves]
    ffn_piece = jnp.stack(
        [
            lax.dynamic_slice_in_dim(w_up, j * D, D, axis=1),
            lax.dynamic_slice_in_dim(w_up, ff + j * D, D, axis=1),
            lax.dynamic_slice_in_dim(w_down, j * ROWS, ROWS, axis=0),
        ]
    )
    w_ffn = lax.all_gather(ffn_piece, AXES, axis=0, tiled=False).reshape(SHARDS, QUARTERS, 3, ROWS, D)
    tails = jnp.stack([halves[1][n][:, 48, : 4 * ROWS] for n in range(2)])
    tails = jnp.where(i % 2 == 0, tails, tails[::-1])
    tails = jnp.roll(tails[:, ::-1], i // 2 + 1, axis=1)
    norms = tails.transpose(1, 0, 2).reshape(SHARDS, 4, ROWS).transpose(1, 0, 2).reshape(4, D).astype(F32)
    slopes = jnp.exp2(-8.0 * (jnp.arange(HEADS, dtype=F32) + 1.0) / HEADS)
    pos = positions.reshape(seqs * most, 1)
    live = jnp.arange(most, dtype=jnp.int32)[None, :] < counts[:, None]
    dy = jnp.where(live[:, :, None], grad_listed, jnp.zeros_like(grad_listed)).reshape(seqs * most, width)

    qkv, h1, att_m, h1_m, q_m, r1_m, w_attn = attention_forward(where, x, lines, norms, pos, slopes, seqs)
    h_all = jnp.stack(share_dp(h1_m))
    p_m = attention_again(q_m, qkv, pos, slopes, seqs)
    h1, h_all, p_m = lax.optimization_barrier((h1, h_all, p_m))
    layer_out, dr2, e2, small_ffn = ffn_forward(h1, w_ffn, norms, pos, dy, seqs)
    act, to_gate, to_up = ffn_again(where, h_all, w_ffn)
    other = after(send(e2, "x"), act)
    pieces = (e2, send(e2, "c"), other, send(other, "c"))
    dgate, dup, keep, away, e_all = ffn_back(where, pieces, to_gate, to_up, w_ffn)
    part = add(keep, send(away, "c"))
    part, part_away = part[0], part[1].astype(LOW)
    keep_d, away_d = weight_grad(where, act, e_all)
    came = send(part_away, "x")
    got_d = send(away_d, "y")
    keep_g, away_g = weight_grad(where, after(h_all, (away_d, part_away)), dgate)
    got_g = send(away_g, "y")
    keep_u, away_u = weight_grad(where, after(h_all, (away_g, came)), dup)
    got_u = send(away_u, "y")
    dr1, low, datt, small_attn = norm_back_call(dr2, part, after(came, away_u), r1_m, w_attn, norms)
    rhs = attention_back(datt, q_m, qkv, p_m, pos, seqs)
    got_d, rhs = lax.optimization_barrier((got_d, rhs))
    parts_d = line_parts(keep_d, got_d)
    line_d = line_send(parts_d)
    keep0, keep1, away0, away1 = attention_grads(where, x_flip, after(rhs, parts_d), att_m, low, small_attn, small_ffn)
    away0, away1, line_d, got_g, got_u = lax.optimization_barrier((away0, away1, line_d, got_g, got_u))
    came0, came1 = send(away0, "c"), send(away1, "c")
    parts_gu = [jnp.concatenate(pair) for pair in zip(line_parts(keep_g, got_g), line_parts(keep_u, got_u))]
    line_gu = line_send(parts_gu)
    g_down = send(line_add(keep_d, got_d, line_d), "down")
    away0, away1 = add(keep0[1], came0[1]).astype(LOW), add(keep1[1], came1[1]).astype(LOW)
    got0, got1 = send(away0, "x"), send(away1, "y")
    total0 = add(keep0[0], came0[0]) + got0.astype(F32)
    total1 = add(keep1[0], came1[0]) + got1.astype(F32)
    away0, away1 = total0[1].astype(LOW), total1[1].astype(LOW)
    got0, got1 = send(away0, "y"), send(away1, "x")
    g_down, line_gu = after((g_down, line_gu), (away0, away1))
    g_ffn = jnp.stack(
        [
            g_down,
            line_add(keep_g, got_g, [value[:ROWS] for value in line_gu]),
            line_add(keep_u, got_u, [value[ROWS:] for value in line_gu]),
        ]
    )
    got0, got1 = after((got0, got1), g_ffn)
    total = jnp.concatenate([add(total0[0], got0), add(total1[0], got1)], axis=1)
    parts = [total[r].astype(LOW) for r in (1, 2, 3)]
    line_a = line_send(parts)
    other = send(g_ffn, "x")
    grad_in = input_grad(after(rhs, parts), w_attn, dr1, positions)
    line_a, other, grad_in = lax.optimization_barrier((line_a, other, grad_in))
    g_attn = total[0] + line_a[0].astype(F32) + line_a[1].astype(F32) + line_a[2].astype(F32)
    small = g_attn[ROWS : ROWS + 4, :ROWS]
    g_attn = g_attn[:ROWS].astype(LOW)
    shared = (g_ffn, send(g_ffn, "c"), other, send(other, "c"))
    grad_down, grad_up = finish_ffn(where, after(shared, g_attn))
    other = after(send(g_attn, "x"), grad_down)
    grad_qkv, grad_out = finish_attention(where, (g_attn, send(g_attn, "c"), other, send(other, "c")))
    return (
        layer_out.reshape(seqs, length, width),
        grad_in.reshape(seqs, length, width),
        grad_qkv,
        grad_out,
        grad_up,
        grad_down,
        small[0],
        small[1],
        small[2],
        small[3],
    )


FF = 3072


def slopes():
    return jnp.exp2(-8.0 * (jnp.arange(HEADS, dtype=F32) + 1.0) / HEADS)


def pick(onehot, rows):
    if rows.dtype == LOW:
        return jnp.einsum("svj,sjd->svd", onehot.astype(LOW), rows, preferred_element_type=F32).astype(LOW)
    return jnp.einsum("svj,sjd->svd", onehot, rows, precision=lax.Precision.HIGHEST)


def gather_weights(w_qkv, w_out, w_up, w_down):
    fsdp = lax.axis_size("fsdp")
    dp = lax.axis_size("dp")
    rows, width = w_out.shape
    if rows % (8 * dp):
        return (
            lax.all_gather(w_qkv, "fsdp", axis=0, tiled=True),
            lax.all_gather(w_out, "fsdp", axis=0, tiled=True),
            lax.all_gather(w_up, "fsdp", axis=0, tiled=True),
            lax.all_gather(w_down, "fsdp", axis=0, tiled=True),
        )
    mine = lax.axis_index("dp")
    part = rows // dp
    group = w_down.shape[0] // rows
    joined = jnp.concatenate([w_qkv, w_out, w_up], axis=1)
    joined = lax.dynamic_slice_in_dim(joined, mine * part, part, axis=0)
    down = lax.dynamic_slice_in_dim(w_down, mine * part * group, part * group, axis=0)
    down = jnp.concatenate([down[k * part : (k + 1) * part] for k in range(group)], axis=1)
    full = lax.all_gather(jnp.concatenate([joined, down], axis=1), AXES, axis=0, tiled=True)
    a, b = w_qkv.shape[1], w_qkv.shape[1] + w_out.shape[1]
    c = b + w_up.shape[1]
    full_down = full[:, c:].reshape(fsdp * dp, part, group, width)
    full_down = full_down.transpose(0, 2, 1, 3).reshape(fsdp * dp * part * group, width)
    return full[:, :a], full[:, a:b], full[:, b:c], full_down


def scatter_grads(g_qkv, g_out, g_up, g_down):
    fsdp = lax.axis_size("fsdp")
    dp = lax.axis_size("dp")
    width = g_out.shape[1]
    rows = g_out.shape[0] // fsdp
    if rows % (8 * dp):
        return tuple(
            lax.psum(lax.psum_scatter(g, "fsdp", scatter_dimension=0, tiled=True), "dp")
            for g in (g_qkv, g_out, g_up, g_down)
        )
    part = rows // dp
    group = g_down.shape[0] // g_out.shape[0]
    down = g_down.reshape(fsdp * dp, group, part, width).transpose(0, 2, 1, 3)
    down = down.reshape(fsdp * rows, group * width)
    joined = jnp.concatenate([g_qkv, g_out, g_up, down], axis=1).astype(LOW)
    mine = lax.psum_scatter(joined, AXES, scatter_dimension=0, tiled=True)
    full = lax.all_gather(mine, "dp", axis=0, tiled=True).astype(F32)
    a, b = g_qkv.shape[1], g_qkv.shape[1] + width
    c = b + g_up.shape[1]
    full_down = full[:, c:].reshape(dp, part, group, width).transpose(0, 2, 1, 3)
    return full[:, :a], full[:, a:b], full[:, b:c], full_down.reshape(rows * group, width)


def on_device(hidden_in, w_qkv, w_out, w_up, w_down, gain_attn, shift_attn, gain_ffn, shift_ffn, grad_listed, positions, counts):
    seqs, length, width = hidden_in.shape
    tokens = seqs * length
    most = positions.shape[1]
    norms = jnp.stack([gain_attn, shift_attn, gain_ffn, shift_ffn])
    norms = lax.all_gather(norms, "fsdp", axis=1, tiled=True).astype(F32)
    w_qkv, w_out, w_up, w_down = gather_weights(w_qkv, w_out, w_up, w_down)
    live = jnp.arange(most, dtype=jnp.int32)[None, :] < counts[:, None]
    onehot = (positions[:, :, None] == jnp.arange(length, dtype=jnp.int32)).astype(F32)
    rows_in = hidden_in.reshape(tokens, width)
    slope = slopes()
    scale = HEAD_DIM**-0.5
    qkv = mm(rows_in, w_qkv).astype(LOW)
    split = qkv.reshape(seqs, length, 3, HEADS, HEAD_DIM)
    q, k, v = split[:, :, 0], split[:, :, 1], split[:, :, 2]
    place = jnp.arange(length, dtype=F32)
    bias = -slope[:, None, None] * jnp.abs(place[:, None] - place[None, :])
    s = jnp.einsum("sqhc,skhc->shqk", q, k, preferred_element_type=F32) * scale + bias
    p = jax.nn.softmax(s, axis=-1).astype(LOW)
    att = jnp.einsum("shqk,skhc->sqhc", p, v, preferred_element_type=F32).astype(LOW)
    att = att.reshape(tokens, width)
    r1 = rows_in.astype(F32) + mm(att, w_out)
    unit1, _ = norm_parts(r1)
    h1 = unit1 * norms[0] + norms[1]
    h1_low = h1.astype(LOW)
    u = mm(h1_low, w_up)
    act = (jax.nn.gelu(u[:, :FF], approximate=False) * u[:, FF:]).astype(LOW)
    r2 = h1 + mm(act, w_down)
    unit2, _ = norm_parts(r2)
    layer_out = (unit2 * norms[2] + norms[3]).astype(LOW).reshape(seqs, length, width)
    def listed(a):
        return pick(onehot, a.reshape(seqs, length, -1)).reshape(seqs * most, -1)

    dy = jnp.where(live[:, :, None], grad_listed, 0).astype(F32).reshape(seqs * most, width)
    unit2_m, rstd2_m = norm_parts(listed(r2))
    g_gain_ffn = jnp.sum(dy * unit2_m, axis=0)
    g_shift_ffn = jnp.sum(dy, axis=0)
    dr2 = norm_back(dy, unit2_m, rstd2_m, norms[2])
    e2 = dr2.astype(LOW)
    h1_m = listed(h1_low)
    u_m = mm(h1_m, w_up)
    gate, up = u_m[:, :FF], u_m[:, FF:]
    cdf = 0.5 * (1.0 + lax.erf(gate * (0.5**0.5)))
    pdf = jnp.exp(-0.5 * gate * gate) * ((2.0 * jnp.pi) ** -0.5)
    gelu = gate * cdf
    act_m = (gelu * up).astype(LOW)
    g_down = jnp.einsum("nf,nd->fd", act_m, e2, preferred_element_type=F32)
    dact = jnp.einsum("nd,fd->nf", e2, w_down, preferred_element_type=F32)
    du = jnp.concatenate([dact * up * (cdf + gate * pdf), dact * gelu], axis=1).astype(LOW)
    g_up = jnp.einsum("nd,nf->df", h1_m, du, preferred_element_type=F32)
    dh1 = dr2 + jnp.einsum("nf,df->nd", du, w_up, preferred_element_type=F32)
    unit1_m, rstd1_m = norm_parts(listed(r1))
    g_gain_attn = jnp.sum(dh1 * unit1_m, axis=0)
    g_shift_attn = jnp.sum(dh1, axis=0)
    dr1 = norm_back(dh1, unit1_m, rstd1_m, norms[0])
    e1 = dr1.astype(LOW)
    g_out = jnp.einsum("nd,ne->de", listed(att), e1, preferred_element_type=F32)
    datt = jnp.einsum("ne,de->nd", e1, w_out, preferred_element_type=F32).astype(LOW)
    datt = datt.reshape(seqs, most, HEADS, HEAD_DIM)
    q_m = listed(qkv[:, :width]).reshape(seqs, most, HEADS, HEAD_DIM)
    away = jnp.abs(positions[:, :, None].astype(F32) - place[None, None, :])
    s_m = jnp.einsum("sqhc,skhc->shqk", q_m, k, preferred_element_type=F32) * scale
    p_m = jax.nn.softmax(s_m - slope[None, :, None, None] * away[:, None], axis=-1)
    dv = jnp.einsum("shqk,sqhc->skhc", p_m.astype(LOW), datt, preferred_element_type=F32)
    dp = jnp.einsum("sqhc,skhc->shqk", datt, v, preferred_element_type=F32)
    ds = (p_m * (dp - jnp.sum(dp * p_m, axis=-1, keepdims=True))).astype(LOW)
    dq_m = (jnp.einsum("shqk,skhc->sqhc", ds, k, preferred_element_type=F32) * scale).astype(LOW)
    dk = (jnp.einsum("shqk,sqhc->skhc", ds, q_m, preferred_element_type=F32) * scale).astype(LOW)
    put = (onehot * live[:, :, None]).astype(LOW)
    dq = jnp.einsum("svj,svd->sjd", put, dq_m.reshape(seqs, most, width), preferred_element_type=F32)
    dqkv = jnp.concatenate(
        [dq.astype(LOW).reshape(tokens, width), dk.reshape(tokens, width), dv.astype(LOW).reshape(tokens, width)], axis=1
    )
    g_qkv = jnp.einsum("nd,ne->de", rows_in, dqkv, preferred_element_type=F32)
    dr1_all = jnp.einsum("svj,svd->sjd", onehot * live[:, :, None], dr1.reshape(seqs, most, width), precision=lax.Precision.HIGHEST)
    grad_in = dr1_all.reshape(tokens, width) + jnp.einsum("ne,de->nd", dqkv, w_qkv, preferred_element_type=F32)
    owned = scatter_grads(g_qkv, g_out, g_up, g_down)
    small = lax.psum(jnp.stack([g_gain_attn, g_shift_attn, g_gain_ffn, g_shift_ffn]), AXES)
    share = width // lax.axis_size("fsdp")
    small = lax.dynamic_slice_in_dim(small, lax.axis_index("fsdp") * share, share, axis=1)
    return (
        layer_out,
        grad_in.reshape(seqs, length, width),
        *owned,
        small[0],
        small[1],
        small[2],
        small[3],
    )


def solution(mesh):
    rows3 = P(("fsdp", "dp"), None, None)
    rows2 = P("fsdp", None)
    rows1 = P("fsdp")
    shape = dict(mesh.shape)
    step = on_block if shape == {"fsdp": SHARDS, "dp": QUARTERS} else on_device
    return jax.shard_map(
        step,
        mesh=mesh,
        in_specs=(rows3, rows2, rows2, rows2, rows2, rows1, rows1, rows1, rows1, rows3, P(("fsdp", "dp"), None), P(("fsdp", "dp"))),
        out_specs=(rows3, rows3, rows2, rows2, rows2, rows2, rows1, rows1, rows1, rows1),
        check_vma=False,
    )
```
